32 devices in a mesh: ep: 8 (over z, x), ws: 4 (over y, core).
Axes of the slice: x: 2, y: 2, z: 4, core: 2. Of those that a mesh axis runs over, the one named last changes fastest.
Arguments:
- x_in: bfloat16 [4096, 2048], P(('ep', 'ws')), may hold values from -6 to 6
- gain_attn: bfloat16 [2048], P(('ep', 'ws')), may hold values from 0.5 to 1.5
- gain_ffn: bfloat16 [2048], P(('ep', 'ws')), may hold values from 0.5 to 1.5
- key_value_weight: bfloat16 [2048, 4096], P(None, ('ep', 'ws')), may hold values from -0.125 to 0.125
- w_query: bfloat16 [8, 2048, 2048], P('ep', None, 'ws'), may hold values from -0.125 to 0.125
- w_output: bfloat16 [8, 2048, 2048], P('ep', 'ws'), may hold values from -0.5 to 0.5
- w_in: bfloat16 [8, 2048, 2, 5632], P('ep', None, None, 'ws'), may hold values from -0.125 to 0.125
- w_out: bfloat16 [8, 5632, 2048], P('ep', 'ws'), may hold values from -0.078125 to 0.078125
- gate_attn: float32 [4096, 2], P(('ep', 'ws')), may hold values from 0.3 to 1
- gate_ffn: float32 [4096, 2], P(('ep', 'ws')), may hold values from 0.3 to 1
- route_attn: int32 [4096, 2], P(('ep', 'ws')), may hold values from 0 to 7, as said below
- slot_attn: int32 [4096, 2], P(('ep', 'ws')), may hold values from 0 to 127, as said below
- route_ffn: int32 [4096, 2], P(('ep', 'ws')), may hold values from 0 to 7, as said below
- slot_ffn: int32 [4096, 2], P(('ep', 'ws')), may hold values from 0 to 127, as said below
- cotangent: bfloat16 [4096, 2048], P(('ep', 'ws')), may hold values from -6 to 6
Outputs:
- out: bfloat16 [4096, 2048], P(('ep', 'ws'))
- grad_input: float32 [4096, 2048], P(('ep', 'ws'))
- grad_gain_attn: float32 [2048], P(('ep', 'ws'))
- grad_gain_ffn: float32 [2048], P(('ep', 'ws'))
- grad_w_kv: float32 [2048, 4096], P(None, ('ep', 'ws'))
- grad_w_query: float32 [8, 2048, 2048], P('ep', None, 'ws')
- grad_w_output: float32 [8, 2048, 2048], P('ep', 'ws')
- grad_w_in: float32 [8, 2048, 2, 5632], P('ep', None, None, 'ws')
- grad_w_out: float32 [8, 5632, 2048], P('ep', 'ws')
The draws below stay inside these ranges and needn't reach their ends.
Inputs may be any that keep to these rules, and one draw needn't show every extreme that they name: `route_attn`: each token names 2 different experts. `route_ffn`: each token names 2 different experts. `slot_attn`: a pair's rank, in an order drawn for each device's 128 tokens, among that device's pairs of the same expert. `slot_ffn`: a pair's rank, in an order drawn for each device's 128 tokens, among that device's pairs of the same expert.
All inputs are finite; a program needn't handle non-finite values.
Results may differ from the reference program's by a relative error of at most 0.018.
Values may be sent and summed in bfloat16 or wider, within the bound.
A program may use at most 384 MiB of HBM per device.

```python
from functools import partial
import jax
import jax.numpy as jnp
from jax import lax

MODEL_WIDTH = 2048
KEY_VALUE_HEADS = 16
HQE = 16
HEAD_SIZE = 128
FF = 5632
MIXTURE_EXPERTS = 8
CHOSEN_EXPERTS = 2
BLOCK = 256
TOK_DEV = 128
GROUP = 1
CAP = 36
SEQUENCE_LENGTH = 512
TOKENS = 4096


def route_draw(key, salt):
    key = jax.random.fold_in(key, salt)
    key_bias, key_noise, key_order, key_force = jax.random.split(key, 4)
    favour_bias = jax.random.randint(key_bias, (MIXTURE_EXPERTS,), 0, 6) * 60
    router_noise = jax.random.randint(key_noise, (TOKENS, MIXTURE_EXPERTS), 0, 400)
    forced = jax.random.randint(key_force, (), 0, MIXTURE_EXPERTS)
    leading_block = (jnp.arange(TOKENS, dtype=jnp.int32) < TOK_DEV)[:, None]
    forced_flag = (jnp.arange(MIXTURE_EXPERTS, dtype=jnp.int32) == forced)[None, :]
    extra_bias = jnp.where(leading_block & forced_flag, 1 << 16, 0).astype(jnp.int32)
    attention_scores = (router_noise + favour_bias[None, :]) * MIXTURE_EXPERTS + jnp.arange(MIXTURE_EXPERTS, dtype=jnp.int32)[None, :] + extra_bias
    chosen = lax.top_k(attention_scores, CHOSEN_EXPERTS)[1].astype(jnp.int32)
    order = jax.random.randint(key_order, (TOKENS,), 0, 1 << 20) * TOK_DEV + jnp.arange(TOKENS, dtype=jnp.int32) % TOK_DEV
    member = jnp.sum((chosen[:, :, None] == jnp.arange(MIXTURE_EXPERTS, dtype=jnp.int32)[None, None, :]).astype(jnp.int32), 1)
    blocks = TOKENS // TOK_DEV
    order_blocks = order.reshape(blocks, TOK_DEV)
    member_blocks = member.reshape(blocks, TOK_DEV, MIXTURE_EXPERTS)
    earlier = (order_blocks[:, None, :] < order_blocks[:, :, None]).astype(jnp.int32)
    ahead = jnp.einsum('bts,bse->bte', earlier, member_blocks).reshape(TOKENS, MIXTURE_EXPERTS)
    slots = jnp.take_along_axis(ahead, chosen, axis=1).astype(jnp.int32)
    return (chosen, slots)


def draw_route_attn(key, part):
    return route_draw(key, 1)[0]


def draw_slot_attn(key, part):
    return route_draw(key, 1)[1]


def draw_route_ffn(key, part):
    return route_draw(key, 2)[0]


def draw_slot_ffn(key, part):
    return route_draw(key, 2)[1]


def shard_levels(rng, extent, cuts, low, largest):
    level, own = 1.0, jax.random.fold_in(rng, 6)
    for position, parts in cuts:
        steps = jnp.exp(jax.random.uniform(jax.random.fold_in(own, position), (parts,), jnp.float32, low / len(cuts), largest / len(cuts)))
        level = level * jnp.repeat(steps, extent[position] // parts).reshape([-1 if axis == position else 1 for axis in range(len(extent))])
    return level


def normal_values(stream_key, shape, scale, bound, cuts=(), kind=jnp.bfloat16):
    level = shard_levels(stream_key, shape, cuts, -0.22, 0.18) if cuts else 1.0
    entries = jax.random.normal(stream_key, shape, jnp.float32) * scale * level
    return jnp.minimum(jnp.maximum(entries, -bound), bound).astype(kind)


def setup_inputs(seed: int = 0) -> dict:
    streams_of = jax.random.split(jax.random.key(seed), 16)
    return {
        "x_in": normal_values(streams_of[0], (TOKENS, MODEL_WIDTH), 1.0, 6.0, ((0, 32),)),
        "gain_attn": jnp.clip(1.0 + 0.1 * jax.random.normal(streams_of[1], (MODEL_WIDTH,), jnp.float32), 0.5, 1.5).astype(jnp.bfloat16),
        "gain_ffn": jnp.clip(1.0 + 0.1 * jax.random.normal(streams_of[2], (MODEL_WIDTH,), jnp.float32), 0.5, 1.5).astype(jnp.bfloat16),
        "key_value_weight": normal_values(streams_of[3], (MODEL_WIDTH, 2 * KEY_VALUE_HEADS * HEAD_SIZE), MODEL_WIDTH ** -0.5, 0.125, ((1, 32),)),
        "w_query": normal_values(streams_of[4], (MIXTURE_EXPERTS * GROUP, MODEL_WIDTH, HQE * HEAD_SIZE // GROUP), MODEL_WIDTH ** -0.5, 0.125, ((0, 8), (2, 4))),
        "w_output": normal_values(streams_of[5], (MIXTURE_EXPERTS * GROUP, HQE * HEAD_SIZE // GROUP, MODEL_WIDTH), (HQE * HEAD_SIZE // 16) ** -0.5, 0.5, ((0, 8), (1, 4))),
        "w_in": normal_values(streams_of[6], (MIXTURE_EXPERTS * GROUP, MODEL_WIDTH, 2, FF // GROUP), MODEL_WIDTH ** -0.5, 0.125, ((0, 8), (3, 4))),
        "w_out": normal_values(streams_of[7], (MIXTURE_EXPERTS * GROUP, FF // GROUP, MODEL_WIDTH), FF ** -0.5, 0.078125, ((0, 8), (1, 4))),
        "gate_attn": jnp.clip(0.3 + 0.7 * jax.random.uniform(streams_of[8], (TOKENS, CHOSEN_EXPERTS), jnp.float32) ** shard_levels(streams_of[8], (TOKENS, CHOSEN_EXPERTS), ((0, 32),), -0.2, 0.2), 0.3, 1.0),
        "gate_ffn": jnp.clip(0.3 + 0.7 * jax.random.uniform(streams_of[9], (TOKENS, CHOSEN_EXPERTS), jnp.float32) ** shard_levels(streams_of[9], (TOKENS, CHOSEN_EXPERTS), ((0, 32),), -0.2, 0.2), 0.3, 1.0),
        "route_attn": draw_route_attn(jax.random.fold_in(streams_of[15], 71), 0),
        "slot_attn": draw_slot_attn(jax.random.fold_in(streams_of[15], 71), 0),
        "route_ffn": draw_route_ffn(jax.random.fold_in(streams_of[15], 71), 0),
        "slot_ffn": draw_slot_ffn(jax.random.fold_in(streams_of[15], 71), 0),
        "cotangent": normal_values(streams_of[14], (TOKENS, MODEL_WIDTH), 1.0, 6.0, ((0, 32),)),
    }


EPS = 1e-06
exact_precision = lax.Precision.HIGHEST

@jax.custom_vjp
def low(v):
    return lax.optimization_barrier(v.astype(jnp.bfloat16)).astype(jnp.float32)

@jax.custom_vjp
def low_back(v):
    return v

def low_keep(v):
    return (low(v), None)

def low_pass(kept, grad):
    return (grad,)

def back_keep(v):
    return (v, None)

def back_low(kept, grad):
    return (low(grad),)
low.defvjp(low_keep, low_pass)
low_back.defvjp(back_keep, back_low)

def normalize(value_rows, gain):
    inverse = lax.rsqrt(lax.optimization_barrier(jnp.mean(value_rows * value_rows, -1, keepdims=True)) + EPS)
    return value_rows * inverse * gain

def slot_tables(routes, slots):
    blocks = routes.shape[0] // TOK_DEV
    target = jnp.where(slots < CAP, routes * CAP + slots, -1).astype(jnp.int32)
    target = target.reshape(blocks, 1, TOK_DEV * CHOSEN_EXPERTS)
    places = lax.broadcasted_iota(jnp.int32, (blocks, MIXTURE_EXPERTS * CAP, TOK_DEV * CHOSEN_EXPERTS), 1)
    return (places == target).astype(jnp.float32)

def query_block(rows, weights):
    part_q = weights.shape[2]
    spread = low_back(jnp.broadcast_to(rows.reshape(MIXTURE_EXPERTS, 1, CAP, MODEL_WIDTH), (MIXTURE_EXPERTS, GROUP, CAP, MODEL_WIDTH)))
    query = low(jnp.einsum('egcd,egdq->egcq', spread, weights.reshape(MIXTURE_EXPERTS, GROUP, MODEL_WIDTH, part_q), precision=exact_precision))
    return query.transpose(0, 2, 1, 3).reshape(MIXTURE_EXPERTS * CAP, GROUP * part_q)

def output_block(rows, weights):
    part_q = weights.shape[1]
    split = rows.reshape(MIXTURE_EXPERTS, CAP, GROUP, part_q).transpose(0, 2, 1, 3)
    pieces = low(jnp.einsum('egcq,egqd->egcd', split, weights.reshape(MIXTURE_EXPERTS, GROUP, part_q, MODEL_WIDTH), precision=exact_precision))
    return low_back(lax.optimization_barrier(jnp.sum(pieces, 1))).reshape(MIXTURE_EXPERTS * CAP, MODEL_WIDTH)

def expert_block(rows, first_weight, second_weight):
    part_f = second_weight.shape[1]
    spread = low_back(jnp.broadcast_to(rows.reshape(MIXTURE_EXPERTS, 1, CAP, MODEL_WIDTH), (MIXTURE_EXPERTS, GROUP, CAP, MODEL_WIDTH)))
    hidden = low_back(jnp.einsum('egcd,egdjf->egcjf', spread, first_weight.reshape(MIXTURE_EXPERTS, GROUP, MODEL_WIDTH, 2, part_f), precision=exact_precision))
    active = low(jax.nn.silu(hidden[:, :, :, 0, :]) * hidden[:, :, :, 1, :])
    pieces = low(jnp.einsum('egcf,egfd->egcd', active, second_weight.reshape(MIXTURE_EXPERTS, GROUP, part_f, MODEL_WIDTH), precision=exact_precision))
    return low_back(lax.optimization_barrier(jnp.sum(pieces, 1))).reshape(MIXTURE_EXPERTS * CAP, MODEL_WIDTH)

def reference(x_in, gain_attn, gain_ffn, key_value_weight, w_query, w_output, w_in, w_out, gate_attn, gate_ffn, route_attn, slot_attn, route_ffn, slot_ffn, cotangent):
    blocks = TOKENS // TOK_DEV
    sequence_count = TOKENS // SEQUENCE_LENGTH
    key_value_width = KEY_VALUE_HEADS * HEAD_SIZE
    attn_table = slot_tables(route_attn, slot_attn)
    ffn_table = slot_tables(route_ffn, slot_ffn)
    attn_tokens = lax.optimization_barrier(jnp.sum(attn_table.reshape(blocks, MIXTURE_EXPERTS * CAP, TOK_DEV, CHOSEN_EXPERTS), -1))
    ffn_tokens = lax.optimization_barrier(jnp.sum(ffn_table.reshape(blocks, MIXTURE_EXPERTS * CAP, TOK_DEV, CHOSEN_EXPERTS), -1))
    gates_attn = gate_attn.astype(jnp.float32).reshape(TOKENS, CHOSEN_EXPERTS, 1)
    gates_ffn = gate_ffn.astype(jnp.float32).reshape(TOKENS, CHOSEN_EXPERTS, 1)
    positions = jnp.arange(SEQUENCE_LENGTH) // BLOCK
    allowed = positions[None, :] <= positions[:, None]

    def to_slots(table, value_rows):
        return jnp.einsum('bst,btx->bsx', table, value_rows.reshape(blocks, TOK_DEV, -1), precision=exact_precision)

    def from_slots(table, slot_values):
        picked = jnp.einsum('bsp,bsx->bpx', table, slot_values, precision=exact_precision)
        return picked.reshape(TOKENS, CHOSEN_EXPERTS, -1)

    def attend_heads(items):
        query_rows, key_rows, value_rows = items
        attention_scores = low_back(jnp.einsum('tkhd,shd->htks', query_rows, key_rows, precision=exact_precision) * HEAD_SIZE ** (-0.5))
        attention_scores = jnp.where(allowed[None, :, None, :], attention_scores, -1e+30)
        probs = jnp.exp(attention_scores - jax.scipy.special.logsumexp(attention_scores, axis=-1, keepdims=True))
        mixed_output = jnp.einsum('htks,shd->tkhd', low(probs), value_rows, precision=exact_precision)
        return low_back(low(mixed_output))

    def forward(inputs, gain_one, gain_two, kv_weight, query_weight, output_weight, first_weight, second_weight):
        normed = low(normalize(inputs, gain_one))
        key_value_rows = low_back(low(jnp.dot(normed, kv_weight, precision=exact_precision)))
        query_slots = lax.map(jax.checkpoint(partial(query_block, weights=query_weight)), to_slots(attn_tokens, normed))
        query_rows = low_back(from_slots(attn_table, query_slots))
        key_rows = key_value_rows[:, :key_value_width].reshape(sequence_count, SEQUENCE_LENGTH, KEY_VALUE_HEADS, HEAD_SIZE)
        value_rows = key_value_rows[:, key_value_width:].reshape(sequence_count, SEQUENCE_LENGTH, KEY_VALUE_HEADS, HEAD_SIZE)
        mixed_output = lax.map(jax.checkpoint(attend_heads), (query_rows.reshape(sequence_count, SEQUENCE_LENGTH, CHOSEN_EXPERTS, KEY_VALUE_HEADS, HEAD_SIZE), key_rows, value_rows))
        mixed_pairs = mixed_output.reshape(blocks, TOK_DEV * CHOSEN_EXPERTS, HQE * HEAD_SIZE)
        attn_rows = jnp.einsum('bsp,bpx->bsx', attn_table, mixed_pairs, precision=exact_precision)
        attn_slots = lax.map(jax.checkpoint(partial(output_block, weights=output_weight)), attn_rows)
        hidden_state = inputs + lax.optimization_barrier(jnp.sum(gates_attn * from_slots(attn_table, attn_slots), 1))
        normed_two = low(normalize(hidden_state, gain_two))
        ffn_slots = lax.map(jax.checkpoint(partial(expert_block, first_weight=first_weight, second_weight=second_weight)), to_slots(ffn_tokens, normed_two))
        return hidden_state + lax.optimization_barrier(jnp.sum(gates_ffn * from_slots(ffn_table, ffn_slots), 1))
    primals = (x_in.astype(jnp.float32), gain_attn.astype(jnp.float32), gain_ffn.astype(jnp.float32), key_value_weight.astype(jnp.float32), w_query.astype(jnp.float32), w_output.astype(jnp.float32), w_in.astype(jnp.float32), w_out.astype(jnp.float32))
    result, pullback = jax.vjp(forward, *primals)
    grads = pullback(cotangent.astype(jnp.float32))
    return (result.astype(jnp.bfloat16), grads[0], grads[1], grads[2], grads[3], grads[4], grads[5], grads[6], grads[7])
```

```python
import jax
import jax.numpy as jnp
from jax import lax
from jax.sharding import PartitionSpec as P

KEY_VALUE_HEADS = 16
HEAD_SIZE = 128
MIXTURE_EXPERTS = 8
CHOSEN_EXPERTS = 2
BLOCK = 256
CAP = 36
ROWS = 40

EPS = 1e-06
very_negative = -1e30
f32 = jnp.float32
bf16 = jnp.bfloat16


def dot(a, b):
    return jnp.dot(a, b, preferred_element_type=f32)


def dot_t(a, b):
    return lax.dot_general(a, b, (((1,), (1,)), ((), ())), preferred_element_type=f32)


def t_dot(a, b):
    return lax.dot_general(a, b, (((0,), (0,)), ((), ())), preferred_element_type=f32)


def exchange(send):
    return lax.all_to_all(send, "ep", split_axis=0, concat_axis=0, tiled=True)


def spread(rows, group):
    width = rows.shape[-1]
    blocks = rows.reshape(MIXTURE_EXPERTS, 1, ROWS, width)
    return jnp.broadcast_to(blocks, (MIXTURE_EXPERTS, group, ROWS, width)).reshape(
        MIXTURE_EXPERTS * group, ROWS, width
    )


def dispatch(rows, group):
    got = exchange(spread(rows, group))
    return lax.all_gather(got, "ws", axis=1, tiled=False)


def combine(partial, group, n_ep, n_ws):
    width = partial.shape[-1]
    part = partial.reshape(n_ep, n_ws, ROWS, width).transpose(1, 0, 2, 3)
    part = part.reshape(n_ws * n_ep * ROWS, width)
    own = lax.psum_scatter(part, "ws", scatter_dimension=0, tiled=True)
    own = own.reshape(n_ep, ROWS, width)
    back = exchange(own)
    if group == 1:
        return back.reshape(MIXTURE_EXPERTS * ROWS, width)
    total = jnp.sum(back.reshape(MIXTURE_EXPERTS, group, ROWS, width).astype(f32), 1)
    return total.astype(bf16).reshape(MIXTURE_EXPERTS * ROWS, width)


def slot_tables(routes, slots):
    target = jnp.where(slots < CAP, routes * ROWS + slots, -1)
    places = lax.broadcasted_iota(jnp.int32, (MIXTURE_EXPERTS * ROWS, target.shape[0]), 0)
    return [(places == target[None, :, k]).astype(bf16) for k in range(CHOSEN_EXPERTS)]


def norm_back(grad, unit, inverse, gain):
    gain_grad = jnp.sum(grad * unit, 0)
    scaled = grad * gain
    return (inverse * (scaled - unit * jnp.mean(scaled * unit, -1, keepdims=True)), gain_grad)


def heads_of(rows):
    return rows.reshape(rows.shape[0], -1, HEAD_SIZE)


def local(
    x_in,
    gain_attn,
    gain_ffn,
    key_value_weight,
    w_query,
    w_output,
    w_in,
    w_out,
    gate_attn,
    gate_ffn,
    route_attn,
    slot_attn,
    route_ffn,
    slot_ffn,
    cotangent,
):
    n_ep = lax.axis_size("ep")
    n_ws = lax.axis_size("ws")
    group = n_ep // MIXTURE_EXPERTS
    local_tokens, width = x_in.shape
    key_value_width = KEY_VALUE_HEADS * HEAD_SIZE
    part = w_query.shape[2]
    own_width = group * part
    sequence = n_ws * local_tokens
    place = lax.axis_index("ws")
    scale = HEAD_SIZE ** (-0.5)

    gain_one = lax.all_gather(gain_attn, ("ep", "ws"), axis=0, tiled=True).astype(f32)
    gain_two = lax.all_gather(gain_ffn, ("ep", "ws"), axis=0, tiled=True).astype(f32)
    plain = group == 1 and key_value_weight.shape[1] == HEAD_SIZE
    if plain:
        half = n_ep // 2
        there = [
            (e * n_ws + w, (w + n_ws * (e // half)) * n_ws + e % half)
            for e in range(n_ep)
            for w in range(n_ws)
        ]
        mine = lax.ppermute(key_value_weight, ("ep", "ws"), there)
        kv_own = lax.all_gather(mine, "ep", axis=1, tiled=True)
    else:
        whole = lax.all_gather(key_value_weight, ("ep", "ws"), axis=1, tiled=True)
        whole = whole.reshape(width, 2 * group, n_ws, part)
        kv_own = lax.dynamic_index_in_dim(whole, place, 2, keepdims=False).reshape(width, -1)

    inputs = x_in.astype(f32)
    inverse_one = lax.rsqrt(jnp.mean(inputs * inputs, -1, keepdims=True) + EPS)
    unit_one = inputs * inverse_one
    normed = (unit_one * gain_one).astype(bf16)
    attn_pairs = slot_tables(route_attn, slot_attn)
    ffn_pairs = slot_tables(route_ffn, slot_ffn)
    attn_tokens = attn_pairs[0] + attn_pairs[1]
    ffn_tokens = ffn_pairs[0] + ffn_pairs[1]

    normed_sequence = lax.all_gather(normed, "ws", axis=0, tiled=True)
    rows_one = dispatch(dot(attn_tokens, normed).astype(bf16), group).reshape(-1, width)
    kv = dot(normed_sequence, kv_own).astype(bf16)
    keys = kv[:, :own_width].reshape(sequence, -1, HEAD_SIZE)
    values = kv[:, own_width:].reshape(sequence, -1, HEAD_SIZE)

    owner_query = dot(rows_one, w_query[0]).astype(bf16)
    queries = exchange(owner_query.reshape(n_ep, n_ws * ROWS, part))
    queries = queries.reshape(MIXTURE_EXPERTS, group, n_ws, ROWS, part)

    def by_block(rows):
        rows = rows.reshape(MIXTURE_EXPERTS, group, n_ws, ROWS, part)
        return [
            rows[:, :, w].transpose(0, 2, 1, 3).reshape(-1, own_width // HEAD_SIZE, HEAD_SIZE)
            for w in range(n_ws)
        ]

    def to_experts(pieces):
        rows = jnp.stack(
            [
                piece.reshape(MIXTURE_EXPERTS, ROWS, group, part).transpose(0, 2, 1, 3)
                for piece in pieces
            ],
            2,
        )
        return rows.reshape(n_ep, n_ws * ROWS, part)

    spans = [(w * local_tokens // BLOCK + 1) * BLOCK for w in range(n_ws)]
    kept = []
    mixed_pieces = []
    for q, span in zip(by_block(queries), spans):
        scores = (
            jnp.einsum("rhd,shd->hrs", q, keys[:span], preferred_element_type=f32) * scale
        )
        probs = jax.nn.softmax(scores, axis=-1)
        mixed = jnp.einsum(
            "hrs,shd->rhd", probs.astype(bf16), values[:span], preferred_element_type=f32
        )
        kept.append((q, probs))
        mixed_pieces.append(mixed.astype(bf16))
    owner_mixed = exchange(to_experts(mixed_pieces)).reshape(-1, part)
    attn_slots = combine(dot(owner_mixed, w_output[0]).astype(bf16), group, n_ep, n_ws)

    def weighted(pairs, gates, slot_values):
        return sum(gates[:, k : k + 1] * t_dot(pairs[k], slot_values) for k in range(2))

    def to_slots(pairs, gates, values):
        return sum(
            dot(pairs[k], (gates[:, k : k + 1] * values).astype(bf16)) for k in range(2)
        ).astype(bf16)

    hidden_state = inputs + weighted(attn_pairs, gate_attn, attn_slots)
    inverse_two = lax.rsqrt(jnp.mean(hidden_state * hidden_state, -1, keepdims=True) + EPS)
    unit_two = hidden_state * inverse_two
    normed_two = (unit_two * gain_two).astype(bf16)

    grad_out = cotangent.astype(f32)
    expert_grad = dispatch(to_slots(ffn_pairs, gate_ffn, grad_out), group).reshape(-1, width)
    expert_rows = dispatch(dot(ffn_tokens, normed_two).astype(bf16), group).reshape(-1, width)
    gate_weight, up_weight = w_in[0, :, 0], w_in[0, :, 1]
    gate_pre = dot(expert_rows, gate_weight)
    up_pre = dot(expert_rows, up_weight)
    sigmoid_gate = jax.nn.sigmoid(gate_pre)
    silu_gate = gate_pre * sigmoid_gate
    activated = (silu_gate * up_pre).astype(bf16)
    grad_act = dot_t(expert_grad, w_out[0])
    grad_up = (grad_act * silu_gate).astype(bf16)
    grad_gate = (
        grad_act * up_pre * sigmoid_gate * (1.0 + gate_pre * (1.0 - sigmoid_gate))
    ).astype(bf16)
    back_two = (dot_t(grad_gate, gate_weight) + dot_t(grad_up, up_weight)).astype(bf16)
    back_slots = combine(back_two, group, n_ep, n_ws)
    ffn_slots = combine(dot(activated, w_out[0]).astype(bf16), group, n_ep, n_ws)
    result = hidden_state + weighted(ffn_pairs, gate_ffn, ffn_slots)
    grad_second = t_dot(activated, expert_grad)
    grad_first = jnp.stack([t_dot(expert_rows, grad_gate), t_dot(expert_rows, grad_up)], 1)

    grad_normed_two = t_dot(ffn_tokens, back_slots)
    grad_hidden_norm, grad_gain_two = norm_back(grad_normed_two, unit_two, inverse_two, gain_two)
    grad_hidden = grad_out + grad_hidden_norm
    owner_grad = dispatch(to_slots(attn_pairs, gate_attn, grad_hidden), group).reshape(-1, width)
    grad_output = t_dot(owner_mixed, owner_grad)
    back_mixed = dot_t(owner_grad, w_output[0]).astype(bf16)
    mixed_grads = exchange(back_mixed.reshape(n_ep, n_ws * ROWS, part))

    grad_keys, grad_values, query_pieces = 0.0, 0.0, []
    for (q, probs), grad, span in zip(kept, by_block(mixed_grads), spans):
        grad_probs = jnp.einsum("rhd,shd->hrs", grad, values[:span], preferred_element_type=f32)
        centred = jnp.sum(probs * grad_probs, -1, keepdims=True)
        grad_scores = (probs * (grad_probs - centred)).astype(bf16)
        grad_q = (
            jnp.einsum("hrs,shd->rhd", grad_scores, keys[:span], preferred_element_type=f32)
            * scale
        )
        query_pieces.append(grad_q.astype(bf16))
        pad = ((0, sequence - span), (0, 0), (0, 0))
        piece = jnp.einsum("hrs,rhd->shd", grad_scores, q, preferred_element_type=f32) * scale
        grad_keys = grad_keys + jnp.pad(piece, pad)
        piece = jnp.einsum(
            "hrs,rhd->shd", probs.astype(bf16), grad, preferred_element_type=f32
        )
        grad_values = grad_values + jnp.pad(piece, pad)
    grad_kv_rows = jnp.concatenate(
        [grad_keys.reshape(sequence, -1), grad_values.reshape(sequence, -1)], 1
    ).astype(bf16)
    owner_grad_query = exchange(to_experts(query_pieces)).reshape(-1, part)
    grad_query = t_dot(rows_one, owner_grad_query)
    back_normed = dot_t(owner_grad_query, w_query[0]).astype(bf16)
    normed_back = combine(back_normed, group, n_ep, n_ws)

    grad_kv = t_dot(normed_sequence, grad_kv_rows)
    if plain:
        pieces = grad_kv.reshape(width, n_ep, HEAD_SIZE).transpose(1, 0, 2).astype(bf16)
        piece = lax.psum_scatter(pieces, "ep", scatter_dimension=0, tiled=False)
        grad_kv_shard = lax.ppermute(piece, ("ep", "ws"), [(b, a) for a, b in there]).astype(f32)
    else:
        mask = (jnp.arange(n_ws) == place)[None, None, :, None]
        pieces = jnp.where(mask, grad_kv.reshape(width, 2 * group, 1, part), 0.0)
        pieces = pieces.reshape(width, 2 * key_value_width).astype(bf16)
        grad_kv_shard = lax.psum_scatter(
            pieces, ("ep", "ws"), scatter_dimension=1, tiled=True
        ).astype(f32)
    from_kv = lax.psum_scatter(
        dot_t(grad_kv_rows, kv_own).astype(bf16), "ws", scatter_dimension=0, tiled=True
    )
    grad_normed = t_dot(attn_tokens, normed_back) + from_kv.astype(f32)
    grad_input_norm, grad_gain_one = norm_back(grad_normed, unit_one, inverse_one, gain_one)
    grad_input = grad_hidden + grad_input_norm
    gain_shards = lax.psum_scatter(
        jnp.stack([grad_gain_one, grad_gain_two], 0), ("ep", "ws"), scatter_dimension=1, tiled=True
    )
    return (
        result.astype(bf16),
        grad_input,
        gain_shards[0],
        gain_shards[1],
        grad_kv_shard,
        grad_query[None],
        grad_output[None],
        grad_first[None],
        grad_second[None],
    )


def solution(mesh):
    both = ("ep", "ws")
    rows, vector, columns = P(both, None), P(both), P(None, both)
    return jax.shard_map(
        local,
        mesh=mesh,
        in_specs=(
            rows,
            vector,
            vector,
            columns,
            P("ep", None, "ws"),
            P("ep", "ws", None),
            P("ep", None, None, "ws"),
            P("ep", "ws", None),
            rows,
            rows,
            rows,
            rows,
            rows,
            rows,
            rows,
        ),
        out_specs=(
            rows,
            rows,
            vector,
            vector,
            columns,
            P("ep", None, "ws"),
            P("ep", "ws", None),
            P("ep", None, None, "ws"),
            P("ep", "ws", None),
        ),
        check_vma=False,
    )
```

```python
import functools

import jax
import jax.numpy as jnp
from jax import lax
from jax.experimental import pallas as pl
from jax.experimental.pallas import tpu as pltpu
from jax.sharding import PartitionSpec as P

KEY_VALUE_HEADS = 16
HEAD_SIZE = 128
MIXTURE_EXPERTS = 8
CHOSEN_EXPERTS = 2
BLOCK = 256
CAP = 36
ROWS = 40

EPS = 1e-06
very_negative = -1e30
f32 = jnp.float32
bf16 = jnp.bfloat16
MESH = pl.DeviceIdType.MESH
ANY = pl.BlockSpec(memory_space=pl.ANY)
VM = pl.BlockSpec(memory_space=pltpu.VMEM)
DMA = pltpu.SemaphoreType.DMA


def dot(a, b):
    return jnp.dot(a, b, preferred_element_type=f32)


def dot_t(a, b):
    return lax.dot_general(a, b, (((1,), (1,)), ((), ())), preferred_element_type=f32)


def t_dot(a, b):
    return lax.dot_general(a, b, (((0,), (0,)), ((), ())), preferred_element_type=f32)


def flip(index, bits):
    out, bit = index, 1
    while bit <= bits:
        if bits & bit:
            out = out + bit - 2 * bit * ((index // bit) % 2)
        bit *= 2
    return out


def far_first(n):
    return sorted(range(1, n), key=lambda k: (-((k // 2).bit_length()), k))


def greet(partners):
    barrier = pltpu.get_barrier_semaphore()
    for partner in partners:
        pl.semaphore_signal(barrier, inc=1, device_id=partner, device_id_type=MESH)
    pl.semaphore_wait(barrier, len(partners))


def remote(src, dst, send, recv, device):
    return pltpu.make_async_remote_copy(
        src_ref=src, dst_ref=dst, send_sem=send, recv_sem=recv, device_id=device, device_id_type=MESH
    )


def dispatch_kernel(n, rows, out, own, load_sem, ep_s, ep_r, y_s, y_r, c_s, c_r, x_s, x_r):
    e, w = lax.axis_index("ep"), lax.axis_index("ws")
    twin, other = flip(w, 1), flip(w, 2)
    hops = range(1, n)
    sources = [e] + [flip(e, k) for k in hops]
    greet([(s, w) for s in sources[1:]] + [(e, twin), (e, other)])
    first = []
    for i, s in enumerate(sources[1:]):
        first.append(remote(rows.at[s], out.at[e, w], ep_s.at[i], ep_r.at[i], (s, w)))
        first[-1].start()
    load = pltpu.make_async_copy(rows.at[e], own, load_sem.at[0])
    load.start()
    over_y, to_twin, relayed = [], [], []

    def relay(j):
        over_y[j].wait_recv()
        block = out.at[sources[j], other]
        relayed.append(remote(block, block, x_s.at[j], x_r.at[j], (e, twin)))
        relayed[-1].start()

    for j, s in enumerate(sources):
        place = out.at[s, w]
        block = rows.at[e] if j == 0 else place
        if j:
            first[j - 1].wait_recv()
        over_y.append(remote(block, place, y_s.at[j], y_r.at[j], (e, other)))
        over_y[-1].start()
        to_twin.append(remote(block, place, c_s.at[j], c_r.at[j], (e, twin)))
        to_twin[-1].start()
        if j == 0:
            load.wait()
            store = pltpu.make_async_copy(own, out.at[e, w], load_sem.at[1])
            store.start()
        else:
            relay(j - 1)
    relay(n - 1)
    store.wait()
    for copy in first + over_y:
        copy.wait_send()
    for copy in to_twin + relayed:
        copy.wait()


def dispatch_call(rows, n_ws):
    n, count, width = rows.shape
    return pl.pallas_call(
        functools.partial(dispatch_kernel, n),
        out_shape=jax.ShapeDtypeStruct((n, n_ws, count, width), rows.dtype),
        in_specs=[ANY],
        out_specs=ANY,
        scratch_shapes=[
            pltpu.VMEM((count, width), rows.dtype),
            DMA((2,)),
            DMA((n - 1,)),
            DMA((n - 1,)),
        ]
        + [DMA((n,)) for _ in range(6)],
        compiler_params=pltpu.CompilerParams(collective_id=0, has_side_effects=True),
        name="dispatch",
    )(rows)


def combine_kernel(
    n, part, out, mine, core, sum_y, from_y, total, load_sem, c_s, c_r, y_s, y_r, ep_s, ep_r, own_sem
):
    e, w = lax.axis_index("ep"), lax.axis_index("ws")
    twin, other, last = flip(w, 1), flip(w, 2), flip(w, 3)
    hops = far_first(n)
    targets = [flip(e, k) for k in hops] + [e]
    greet([(s, w) for s in targets[:-1]] + [(e, twin), (e, other)])
    loads, cores = {}, {}
    for half, near, far in ((1, other, last), (0, w, twin)):
        for j, s in enumerate(targets):
            cores[half, j] = remote(
                part.at[s, far], core.at[half, j], c_s.at[half, j], c_r.at[half, j], (e, twin)
            )
            cores[half, j].start()
            loads[half, j] = pltpu.make_async_copy(
                part.at[s, near], mine.at[half, j], load_sem.at[half, j]
            )
            loads[half, j].start()
    over_y, back = [], []

    def send_y(j):
        over_y.append(remote(sum_y.at[j], from_y.at[j], y_s.at[j], y_r.at[j], (e, other)))
        over_y[-1].start()

    def send_back(j):
        back.append(remote(total.at[j], out.at[e], ep_s.at[j], ep_r.at[j], (targets[j], w)))
        back[-1].start()

    for j in range(n):
        loads[1, j].wait()
        cores[1, j].wait_recv()
        sum_y[j] = (mine[1, j].astype(f32) + core[1, j].astype(f32)).astype(bf16)
        if j:
            send_y(j - 1)
    loads[0, 0].wait()
    cores[0, 0].wait_recv()
    send_y(n - 1)
    for j in range(n):
        if j:
            loads[0, j].wait()
            cores[0, j].wait_recv()
        over_y[j].wait_recv()
        total[j] = (
            mine[0, j].astype(f32) + core[0, j].astype(f32) + from_y[j].astype(f32)
        ).astype(bf16)
        if j:
            send_back(j - 1)
    for copy in over_y + list(cores.values()):
        copy.wait_send()
    keep = pltpu.make_async_copy(total.at[n - 1], out.at[e], own_sem)
    keep.start()
    for copy in back:
        copy.wait()
    keep.wait()


def combine_call(part):
    n, n_ws, count, width = part.shape
    block = (n, count, width)
    return pl.pallas_call(
        functools.partial(combine_kernel, n),
        out_shape=jax.ShapeDtypeStruct(block, part.dtype),
        in_specs=[ANY],
        out_specs=ANY,
        scratch_shapes=[
            pltpu.VMEM((2,) + block, part.dtype),
            pltpu.VMEM((2,) + block, part.dtype),
            pltpu.VMEM(block, part.dtype),
            pltpu.VMEM(block, part.dtype),
            pltpu.VMEM(block, part.dtype),
            DMA((2, n)),
            DMA((2, n)),
            DMA((2, n)),
            DMA((n,)),
            DMA((n,)),
            DMA((n - 1,)),
            DMA((n - 1,)),
            DMA,
        ],
        compiler_params=pltpu.CompilerParams(collective_id=1, has_side_effects=True),
        name="combine",
    )(part)


def exchange_kernel(n, rows, out, own, load_sem, ep_s, ep_r):
    e, w = lax.axis_index("ep"), lax.axis_index("ws")
    targets = [flip(e, k) for k in far_first(n)]
    greet([(s, w) for s in targets])
    copies = []
    for i, s in enumerate(targets):
        copies.append(remote(rows.at[s], out.at[e], ep_s.at[i], ep_r.at[i], (s, w)))
        copies[-1].start()
    load = pltpu.make_async_copy(rows.at[e], own, load_sem.at[0])
    load.start()
    load.wait()
    store = pltpu.make_async_copy(own, out.at[e], load_sem.at[1])
    store.start()
    store.wait()
    for copy in copies:
        copy.wait()


def exchange_call(rows):
    n = rows.shape[0]
    return pl.pallas_call(
        functools.partial(exchange_kernel, n),
        out_shape=jax.ShapeDtypeStruct(rows.shape, rows.dtype),
        in_specs=[ANY],
        out_specs=ANY,
        scratch_shapes=[
            pltpu.VMEM(rows.shape[1:], rows.dtype),
            DMA((2,)),
            DMA((n - 1,)),
            DMA((n - 1,)),
        ],
        compiler_params=pltpu.CompilerParams(collective_id=2, has_side_effects=True),
        name="exchange",
    )(rows)


def gather_kernel(n, n_ws, own, out, load_sem, w_s, w_r, ep_s, ep_r):
    e, w = lax.axis_index("ep"), lax.axis_index("ws")
    beside = [flip(w, k) for k in range(1, n_ws)]
    across = [flip(e, k) for k in far_first(n)]
    greet([(e, p) for p in beside] + [(s, w) for s in across])
    keep = pltpu.make_async_copy(own, out.at[e, w], load_sem)
    keep.start()
    first = []
    for i, p in enumerate(beside):
        first.append(remote(own, out.at[e, w], w_s.at[i], w_r.at[i], (e, p)))
        first[-1].start()
    keep.wait()
    for copy in first:
        copy.wait()
    second = []
    for i, s in enumerate(across):
        second.append(remote(out.at[e], out.at[e], ep_s.at[i], ep_r.at[i], (s, w)))
        second[-1].start()
    for copy in second:
        copy.wait()


def gather_call(own, n, n_ws):
    return pl.pallas_call(
        functools.partial(gather_kernel, n, n_ws),
        out_shape=jax.ShapeDtypeStruct((n, n_ws) + own.shape, own.dtype),
        in_specs=[VM],
        out_specs=VM,
        scratch_shapes=[DMA, DMA((n_ws - 1,)), DMA((n_ws - 1,)), DMA((n - 1,)), DMA((n - 1,))],
        compiler_params=pltpu.CompilerParams(collective_id=3, has_side_effects=True),
        name="gather_gains",
    )(own)


def reduce_kernel(n, n_ws, parts, out, held, all_parts, load_sem, w_s, w_r, ep_s, ep_r):
    e, w = lax.axis_index("ep"), lax.axis_index("ws")
    beside = [flip(w, k) for k in range(1, n_ws)]
    across = [flip(e, k) for k in far_first(n)]
    greet([(e, p) for p in beside] + [(s, w) for s in across])
    keep = pltpu.make_async_copy(parts.at[:, w], held.at[:, w], load_sem.at[0])
    keep.start()
    first = []
    for i, p in enumerate(beside):
        first.append(remote(parts.at[:, p], held.at[:, w], w_s.at[i], w_r.at[i], (e, p)))
        first[-1].start()
    keep.wait()
    for copy in first:
        copy.wait()
    keep = pltpu.make_async_copy(held.at[e], all_parts.at[e], load_sem.at[1])
    keep.start()
    second = []
    for i, s in enumerate(across):
        second.append(remote(held.at[s], all_parts.at[e], ep_s.at[i], ep_r.at[i], (s, w)))
        second[-1].start()
    keep.wait()
    for copy in second:
        copy.wait()
    out[...] = jnp.sum(jnp.sum(all_parts[...], 0), 0)


def reduce_call(parts):
    n, n_ws = parts.shape[:2]
    return pl.pallas_call(
        functools.partial(reduce_kernel, n, n_ws),
        out_shape=jax.ShapeDtypeStruct(parts.shape[2:], parts.dtype),
        in_specs=[VM],
        out_specs=VM,
        scratch_shapes=[
            pltpu.VMEM(parts.shape, parts.dtype),
            pltpu.VMEM(parts.shape, parts.dtype),
            DMA((2,)),
            DMA((n_ws - 1,)),
            DMA((n_ws - 1,)),
            DMA((n - 1,)),
            DMA((n - 1,)),
        ],
        compiler_params=pltpu.CompilerParams(collective_id=4, has_side_effects=True),
        name="reduce_gains",
    )(parts)


def small(n_ep):
    return n_ep == MIXTURE_EXPERTS and lax.axis_size("ws") == 4


def exchange(send):
    if small(send.shape[0]):
        return exchange_call(send)
    return lax.all_to_all(send, "ep", split_axis=0, concat_axis=0, tiled=True)


def spread(rows, group):
    width = rows.shape[-1]
    blocks = rows.reshape(MIXTURE_EXPERTS, 1, ROWS, width)
    return jnp.broadcast_to(blocks, (MIXTURE_EXPERTS, group, ROWS, width)).reshape(
        MIXTURE_EXPERTS * group, ROWS, width
    )


def dispatch(rows, group):
    if small(group * MIXTURE_EXPERTS):
        return dispatch_call(rows.reshape(MIXTURE_EXPERTS, ROWS, -1), lax.axis_size("ws"))
    got = exchange(spread(rows, group))
    return lax.all_gather(got, "ws", axis=1, tiled=False)


def combine(partial, group, n_ep, n_ws):
    width = partial.shape[-1]
    if small(n_ep):
        back = combine_call(partial.reshape(n_ep, n_ws, ROWS, width))
        return back.reshape(MIXTURE_EXPERTS * ROWS, width)
    part = partial.reshape(n_ep, n_ws, ROWS, width).transpose(1, 0, 2, 3)
    part = part.reshape(n_ws * n_ep * ROWS, width)
    own = lax.psum_scatter(part, "ws", scatter_dimension=0, tiled=True)
    own = own.reshape(n_ep, ROWS, width)
    back = exchange(own)
    if group == 1:
        return back.reshape(MIXTURE_EXPERTS * ROWS, width)
    total = jnp.sum(back.reshape(MIXTURE_EXPERTS, group, ROWS, width).astype(f32), 1)
    return total.astype(bf16).reshape(MIXTURE_EXPERTS * ROWS, width)


def slot_tables(routes, slots):
    target = jnp.where(slots < CAP, routes * ROWS + slots, -1)
    places = lax.broadcasted_iota(jnp.int32, (MIXTURE_EXPERTS * ROWS, target.shape[0]), 0)
    return [(places == target[None, :, k]).astype(bf16) for k in range(CHOSEN_EXPERTS)]


def norm_back(grad, unit, inverse, gain):
    gain_grad = jnp.sum(grad * unit, 0)
    scaled = grad * gain
    return (inverse * (scaled - unit * jnp.mean(scaled * unit, -1, keepdims=True)), gain_grad)


def heads_of(rows):
    return rows.reshape(rows.shape[0], -1, HEAD_SIZE)


def local(
    x_in,
    gain_attn,
    gain_ffn,
    key_value_weight,
    w_query,
    w_output,
    w_in,
    w_out,
    gate_attn,
    gate_ffn,
    route_attn,
    slot_attn,
    route_ffn,
    slot_ffn,
    cotangent,
):
    n_ep = lax.axis_size("ep")
    n_ws = lax.axis_size("ws")
    group = n_ep // MIXTURE_EXPERTS
    local_tokens, width = x_in.shape
    key_value_width = KEY_VALUE_HEADS * HEAD_SIZE
    part = w_query.shape[2]
    own_width = group * part
    sequence = n_ws * local_tokens
    place = lax.axis_index("ws")
    scale = HEAD_SIZE ** (-0.5)

    short = small(n_ep) and gain_attn.shape[0] == 64
    if short:
        gains = jnp.concatenate([gain_attn, gain_ffn], 0).astype(f32)[None]
        gains = gather_call(gains, n_ep, n_ws).reshape(n_ep * n_ws, 2, -1)
        gain_one, gain_two = gains[:, 0].reshape(-1), gains[:, 1].reshape(-1)
    else:
        gain_one = lax.all_gather(gain_attn, ("ep", "ws"), axis=0, tiled=True).astype(f32)
        gain_two = lax.all_gather(gain_ffn, ("ep", "ws"), axis=0, tiled=True).astype(f32)
    plain = group == 1 and key_value_weight.shape[1] == HEAD_SIZE
    if plain:
        half = n_ep // 2
        there = [
            (e * n_ws + w, (w + n_ws * (e // half)) * n_ws + e % half)
            for e in range(n_ep)
            for w in range(n_ws)
        ]
        mine = lax.ppermute(key_value_weight, ("ep", "ws"), there)
        kv_own = lax.all_gather(mine, "ep", axis=1, tiled=True)
    else:
        whole = lax.all_gather(key_value_weight, ("ep", "ws"), axis=1, tiled=True)
        whole = whole.reshape(width, 2 * group, n_ws, part)
        kv_own = lax.dynamic_index_in_dim(whole, place, 2, keepdims=False).reshape(width, -1)

    inputs = x_in.astype(f32)
    inverse_one = lax.rsqrt(jnp.mean(inputs * inputs, -1, keepdims=True) + EPS)
    unit_one = inputs * inverse_one
    normed = (unit_one * gain_one).astype(bf16)
    attn_pairs = slot_tables(route_attn, slot_attn)
    ffn_pairs = slot_tables(route_ffn, slot_ffn)
    attn_tokens = attn_pairs[0] + attn_pairs[1]
    ffn_tokens = ffn_pairs[0] + ffn_pairs[1]

    normed_sequence = lax.all_gather(normed, "ws", axis=0, tiled=True)
    rows_one = dispatch(dot(attn_tokens, normed).astype(bf16), group).reshape(-1, width)
    kv = dot(normed_sequence, kv_own).astype(bf16)
    keys = kv[:, :own_width].reshape(sequence, -1, HEAD_SIZE)
    values = kv[:, own_width:].reshape(sequence, -1, HEAD_SIZE)

    owner_query = dot(rows_one, w_query[0]).astype(bf16)
    queries = exchange(owner_query.reshape(n_ep, n_ws * ROWS, part))
    queries = queries.reshape(MIXTURE_EXPERTS, group, n_ws, ROWS, part)

    def by_block(rows):
        rows = rows.reshape(MIXTURE_EXPERTS, group, n_ws, ROWS, part)
        return [
            rows[:, :, w].transpose(0, 2, 1, 3).reshape(-1, own_width // HEAD_SIZE, HEAD_SIZE)
            for w in range(n_ws)
        ]

    def to_experts(pieces):
        rows = jnp.stack(
            [
                piece.reshape(MIXTURE_EXPERTS, ROWS, group, part).transpose(0, 2, 1, 3)
                for piece in pieces
            ],
            2,
        )
        return rows.reshape(n_ep, n_ws * ROWS, part)

    spans = [(w * local_tokens // BLOCK + 1) * BLOCK for w in range(n_ws)]
    kept = []
    mixed_pieces = []
    for q, span in zip(by_block(queries), spans):
        scores = (
            jnp.einsum("rhd,shd->hrs", q, keys[:span], preferred_element_type=f32) * scale
        )
        probs = jax.nn.softmax(scores, axis=-1)
        mixed = jnp.einsum(
            "hrs,shd->rhd", probs.astype(bf16), values[:span], preferred_element_type=f32
        )
        kept.append((q, probs))
        mixed_pieces.append(mixed.astype(bf16))
    owner_mixed = exchange(to_experts(mixed_pieces)).reshape(-1, part)
    attn_slots = combine(dot(owner_mixed, w_output[0]).astype(bf16), group, n_ep, n_ws)

    def weighted(pairs, gates, slot_values):
        return sum(gates[:, k : k + 1] * t_dot(pairs[k], slot_values) for k in range(2))

    def to_slots(pairs, gates, values):
        return sum(
            dot(pairs[k], (gates[:, k : k + 1] * values).astype(bf16)) for k in range(2)
        ).astype(bf16)

    hidden_state = inputs + weighted(attn_pairs, gate_attn, attn_slots)
    inverse_two = lax.rsqrt(jnp.mean(hidden_state * hidden_state, -1, keepdims=True) + EPS)
    unit_two = hidden_state * inverse_two
    normed_two = (unit_two * gain_two).astype(bf16)

    grad_out = cotangent.astype(f32)
    expert_grad = dispatch(to_slots(ffn_pairs, gate_ffn, grad_out), group).reshape(-1, width)
    expert_rows = dispatch(dot(ffn_tokens, normed_two).astype(bf16), group).reshape(-1, width)
    gate_weight, up_weight = w_in[0, :, 0], w_in[0, :, 1]
    gate_pre = dot(expert_rows, gate_weight)
    up_pre = dot(expert_rows, up_weight)
    sigmoid_gate = jax.nn.sigmoid(gate_pre)
    silu_gate = gate_pre * sigmoid_gate
    activated = (silu_gate * up_pre).astype(bf16)
    grad_act = dot_t(expert_grad, w_out[0])
    grad_up = (grad_act * silu_gate).astype(bf16)
    grad_gate = (
        grad_act * up_pre * sigmoid_gate * (1.0 + gate_pre * (1.0 - sigmoid_gate))
    ).astype(bf16)
    back_two = (dot_t(grad_gate, gate_weight) + dot_t(grad_up, up_weight)).astype(bf16)
    back_slots = combine(back_two, group, n_ep, n_ws)
    ffn_slots = combine(dot(activated, w_out[0]).astype(bf16), group, n_ep, n_ws)
    result = hidden_state + weighted(ffn_pairs, gate_ffn, ffn_slots)
    grad_second = t_dot(activated, expert_grad)
    grad_first = jnp.stack([t_dot(expert_rows, grad_gate), t_dot(expert_rows, grad_up)], 1)

    grad_normed_two = t_dot(ffn_tokens, back_slots)
    grad_hidden_norm, grad_gain_two = norm_back(grad_normed_two, unit_two, inverse_two, gain_two)
    grad_hidden = grad_out + grad_hidden_norm
    owner_grad = dispatch(to_slots(attn_pairs, gate_attn, grad_hidden), group).reshape(-1, width)
    grad_output = t_dot(owner_mixed, owner_grad)
    back_mixed = dot_t(owner_grad, w_output[0]).astype(bf16)
    mixed_grads = exchange(back_mixed.reshape(n_ep, n_ws * ROWS, part))

    grad_keys, grad_values, query_pieces = 0.0, 0.0, []
    for (q, probs), grad, span in zip(kept, by_block(mixed_grads), spans):
        grad_probs = jnp.einsum("rhd,shd->hrs", grad, values[:span], preferred_element_type=f32)
        centred = jnp.sum(probs * grad_probs, -1, keepdims=True)
        grad_scores = (probs * (grad_probs - centred)).astype(bf16)
        grad_q = (
            jnp.einsum("hrs,shd->rhd", grad_scores, keys[:span], preferred_element_type=f32)
            * scale
        )
        query_pieces.append(grad_q.astype(bf16))
        pad = ((0, sequence - span), (0, 0), (0, 0))
        piece = jnp.einsum("hrs,rhd->shd", grad_scores, q, preferred_element_type=f32) * scale
        grad_keys = grad_keys + jnp.pad(piece, pad)
        piece = jnp.einsum(
            "hrs,rhd->shd", probs.astype(bf16), grad, preferred_element_type=f32
        )
        grad_values = grad_values + jnp.pad(piece, pad)
    grad_kv_rows = jnp.concatenate(
        [grad_keys.reshape(sequence, -1), grad_values.reshape(sequence, -1)], 1
    ).astype(bf16)
    owner_grad_query = exchange(to_experts(query_pieces)).reshape(-1, part)
    grad_query = t_dot(rows_one, owner_grad_query)
    back_normed = dot_t(owner_grad_query, w_query[0]).astype(bf16)
    normed_back = combine(back_normed, group, n_ep, n_ws)

    grad_kv = t_dot(normed_sequence, grad_kv_rows)
    if plain:
        pieces = grad_kv.reshape(width, n_ep, HEAD_SIZE).transpose(1, 0, 2).astype(bf16)
        piece = lax.psum_scatter(pieces, "ep", scatter_dimension=0, tiled=False)
        grad_kv_shard = lax.ppermute(piece, ("ep", "ws"), [(b, a) for a, b in there]).astype(f32)
    else:
        mask = (jnp.arange(n_ws) == place)[None, None, :, None]
        pieces = jnp.where(mask, grad_kv.reshape(width, 2 * group, 1, part), 0.0)
        pieces = pieces.reshape(width, 2 * key_value_width).astype(bf16)
        grad_kv_shard = lax.psum_scatter(
            pieces, ("ep", "ws"), scatter_dimension=1, tiled=True
        ).astype(f32)
    from_kv = lax.psum_scatter(
        dot_t(grad_kv_rows, kv_own).astype(bf16), "ws", scatter_dimension=0, tiled=True
    )
    grad_normed = t_dot(attn_tokens, normed_back) + from_kv.astype(f32)
    grad_input_norm, grad_gain_one = norm_back(grad_normed, unit_one, inverse_one, gain_one)
    grad_input = grad_hidden + grad_input_norm
    gain_grads = jnp.stack([grad_gain_one, grad_gain_two], 0)
    if short:
        parts = gain_grads.reshape(2, n_ep, n_ws, -1).transpose(1, 2, 0, 3)
        gain_shards = reduce_call(parts.reshape(n_ep, n_ws, 1, -1)).reshape(2, -1)
    else:
        gain_shards = lax.psum_scatter(
            gain_grads, ("ep", "ws"), scatter_dimension=1, tiled=True
        )
    return (
        result.astype(bf16),
        grad_input,
        gain_shards[0],
        gain_shards[1],
        grad_kv_shard,
        grad_query[None],
        grad_output[None],
        grad_first[None],
        grad_second[None],
    )


def solution(mesh):
    both = ("ep", "ws")
    rows, vector, columns = P(both, None), P(both), P(None, both)
    return jax.shard_map(
        local,
        mesh=mesh,
        in_specs=(
            rows,
            vector,
            vector,
            columns,
            P("ep", None, "ws"),
            P("ep", "ws", None),
            P("ep", None, None, "ws"),
            P("ep", "ws", None),
            rows,
            rows,
            rows,
            rows,
            rows,
            rows,
            rows,
        ),
        out_specs=(
            rows,
            rows,
            vector,
            vector,
            columns,
            P("ep", None, "ws"),
            P("ep", "ws", None),
            P("ep", None, None, "ws"),
            P("ep", "ws", None),
        ),
        check_vma=False,
    )
```

```python
import functools

import jax
import jax.numpy as jnp
from jax import lax
from jax.experimental import pallas as pl
from jax.experimental.pallas import tpu as pltpu
from jax.sharding import PartitionSpec as P

KEY_VALUE_HEADS = 16
HEAD_SIZE = 128
MIXTURE_EXPERTS = 8
CHOSEN_EXPERTS = 2
BLOCK = 256
CAP = 36
ROWS = 40

EPS = 1e-06
very_negative = -1e30
f32 = jnp.float32
bf16 = jnp.bfloat16
MESH = pl.DeviceIdType.MESH
ANY = pl.BlockSpec(memory_space=pl.ANY)
VM = pl.BlockSpec(memory_space=pltpu.VMEM)
DMA = pltpu.SemaphoreType.DMA
STEP = 256
VMEM_LIMIT = 60 << 20


def dot(a, b):
    return jnp.dot(a, b, preferred_element_type=f32)


def dot_t(a, b):
    return lax.dot_general(a, b, (((1,), (1,)), ((), ())), preferred_element_type=f32)


def t_dot(a, b):
    return lax.dot_general(a, b, (((0,), (0,)), ((), ())), preferred_element_type=f32)


def flip(index, bits):
    out, bit = index, 1
    while bit <= bits:
        if bits & bit:
            out = out + bit - 2 * bit * ((index // bit) % 2)
        bit *= 2
    return out


def far_first(n):
    return sorted(range(1, n), key=lambda k: (-((k // 2).bit_length()), k))


def greet(partners):
    barrier = pltpu.get_barrier_semaphore()
    for partner in partners:
        pl.semaphore_signal(barrier, inc=1, device_id=partner, device_id_type=MESH)
    pl.semaphore_wait(barrier, len(partners))


def remote(src, dst, send, recv, device):
    return pltpu.make_async_remote_copy(
        src_ref=src, dst_ref=dst, send_sem=send, recv_sem=recv, device_id=device, device_id_type=MESH
    )


class Job:
    def __init__(self, args, outs, scratch, steps, body):
        self.args, self.outs, self.scratch, self.steps, self.body = args, outs, scratch, steps, body


def run_jobs(exchange_job, fills, collective_id, name):
    jobs = [exchange_job] + fills
    args = [a for job in jobs for a in job.args]
    outs = [o for job in jobs for o in job.outs]
    scratch = [x for job in jobs for x in job.scratch]

    def kernel(*refs):
        bodies, at = [], [0, len(args), len(args) + len(outs)]
        for job in jobs:
            own = []
            for k, part in enumerate((job.args, job.outs, job.scratch)):
                own.append(refs[at[k] : at[k] + len(part)])
                at[k] += len(part)
            bodies.append(job.body(*own[0], *own[1], *own[2]))
        work = [bodies[k + 1] for k in range(len(fills))]
        queue = [g for g, job in zip(work, fills) for _ in range(job.steps)]
        for g in work:
            next(g)
        done = 0
        for k, _ in enumerate(bodies[0]):
            target = (k + 1) * len(queue) // exchange_job.steps
            while done < target:
                next(queue[done])
                done += 1
        for g in work:
            for _ in g:
                pass

    return pl.pallas_call(
        kernel,
        out_shape=outs,
        in_specs=[ANY] * len(args),
        out_specs=[ANY] * len(outs),
        scratch_shapes=scratch,
        compiler_params=pltpu.CompilerParams(
            collective_id=collective_id, has_side_effects=True, vmem_limit_bytes=VMEM_LIMIT
        ),
        name=name,
    )(*args)


def fetch(pairs, sem):
    copies = [
        pltpu.make_async_copy(src, dst, sem.at[i]) for i, (src, dst) in enumerate(pairs)
    ]
    for copy in copies:
        copy.start()
    return copies


def blocks_of(size):
    return [(start, min(STEP, size - start)) for start in range(0, size, STEP)]


def column_tiles(width, tile):
    def body(c, carry):
        tile(pl.multiple_of(c * STEP, STEP), STEP)
        return carry

    lax.fori_loop(0, width // STEP, body, 0)
    if width % STEP:
        tile(width // STEP * STEP, width % STEP)


def grad_job(a, b):
    depth, rows = a.shape
    width = b.shape[1]

    def body(a_hbm, b_hbm, out, a_ref, b_ref, turned, held, load_sem, sem):
        loads = fetch(((a_hbm, a_ref), (b_hbm, b_ref)), load_sem)
        yield
        for load in loads:
            load.wait()
        copies = []
        for i, (start, size) in enumerate(blocks_of(rows)):
            if i >= 2:
                copies[i - 2].wait()
            turned[:size] = a_ref[:, start : start + size].T

            def tile(at, columns, slot=i % 2, size=size):
                held[slot, :size, pl.ds(at, columns)] = jnp.dot(
                    turned[:size], b_ref[:, pl.ds(at, columns)], preferred_element_type=f32
                )

            column_tiles(width, tile)
            copies.append(
                pltpu.make_async_copy(
                    held.at[i % 2, pl.ds(0, size)], out.at[pl.ds(start, size)], sem.at[i % 2]
                )
            )
            copies[i].start()
            yield
        for copy in copies[-2:]:
            copy.wait()

    return Job(
        [a, b],
        [jax.ShapeDtypeStruct((rows, width), f32)],
        [
            pltpu.VMEM(a.shape, bf16),
            pltpu.VMEM(b.shape, bf16),
            pltpu.VMEM((STEP, depth), bf16),
            pltpu.VMEM((2, STEP, width), f32),
            DMA((2,)),
            DMA((2,)),
        ],
        len(blocks_of(rows)),
        body,
    )


def pair_grad_job(a, first, second):
    depth, rows = a.shape
    tiles = first.shape[1] // 128

    def body(a_hbm, f_hbm, s_hbm, out, a_ref, f_ref, s_ref, turned, held, load_sem, sem):
        loads = fetch(((a_hbm, a_ref), (f_hbm, f_ref), (s_hbm, s_ref)), load_sem)
        flat = held.reshape(2 * tiles * STEP * 2, 128)
        yield
        for load in loads:
            load.wait()
        copies = []
        for i, (start, size) in enumerate(blocks_of(rows)):
            if i >= 2:
                for copy in copies[i - 2]:
                    copy.wait()
            turned[:size] = a_ref[:, start : start + size].T

            def tile(at, columns, slot=i % 2, size=size):
                for j, b_ref in enumerate((f_ref, s_ref)):
                    r = jnp.dot(
                        turned[:size], b_ref[:, pl.ds(at, columns)], preferred_element_type=f32
                    )
                    for half in range(columns // 128):
                        base = (slot * tiles + at // 128 + half) * (2 * STEP) + j
                        flat[pl.ds(base, size, stride=2), :] = r[:, half * 128 : half * 128 + 128]

            column_tiles(tiles * 128, tile)
            copies.append(
                [
                    pltpu.make_async_copy(
                        held.at[i % 2, c, pl.ds(0, size)],
                        out.at[pl.ds(start, size), :, pl.ds(c * 128, 128)],
                        sem.at[i % 2, c],
                    )
                    for c in range(tiles)
                ]
            )
            for copy in copies[i]:
                copy.start()
            yield
        for copy in copies[-2] + copies[-1]:
            copy.wait()

    return Job(
        [a, first, second],
        [jax.ShapeDtypeStruct((rows, 2, tiles * 128), f32)],
        [
            pltpu.VMEM(a.shape, bf16),
            pltpu.VMEM(first.shape, bf16),
            pltpu.VMEM(second.shape, bf16),
            pltpu.VMEM((STEP, depth), bf16),
            pltpu.VMEM((2, tiles, STEP, 2, 128), f32),
            DMA((3,)),
            DMA((2, tiles)),
        ],
        len(blocks_of(rows)),
        body,
    )


def product_job(a, b, dtype):
    rows, width = a.shape[0], b.shape[1]

    def body(a_hbm, b_hbm, out, a_ref, b_ref, held, load_sem, sem):
        loads = fetch(((a_hbm, a_ref), (b_hbm, b_ref)), load_sem)
        yield
        for load in loads:
            load.wait()
        copies = []
        for i, (start, size) in enumerate(blocks_of(rows)):
            if i >= 2:
                copies[i - 2].wait()

            def tile(at, columns, slot=i % 2, start=start, size=size):
                held[slot, :size, pl.ds(at, columns)] = jnp.dot(
                    a_ref[start : start + size],
                    b_ref[:, pl.ds(at, columns)],
                    preferred_element_type=f32,
                ).astype(dtype)

            column_tiles(width, tile)
            copies.append(
                pltpu.make_async_copy(
                    held.at[i % 2, pl.ds(0, size)], out.at[pl.ds(start, size)], sem.at[i % 2]
                )
            )
            copies[i].start()
            yield
        for copy in copies[-2:]:
            copy.wait()

    return Job(
        [a, b],
        [jax.ShapeDtypeStruct((rows, width), dtype)],
        [
            pltpu.VMEM(a.shape, bf16),
            pltpu.VMEM(b.shape, bf16),
            pltpu.VMEM((2, STEP, width), dtype),
            DMA((2,)),
            DMA((2,)),
        ],
        len(blocks_of(rows)),
        body,
    )


def dispatch_job(rows, n_ws):
    n, count, width = rows.shape

    def body(rows, out, own, load_sem, ep_s, ep_r, y_s, y_r, c_s, c_r, x_s, x_r):
        e, w = lax.axis_index("ep"), lax.axis_index("ws")
        twin, other = flip(w, 1), flip(w, 2)
        sources = [e] + [flip(e, k) for k in range(1, n)]
        greet([(s, w) for s in sources[1:]] + [(e, twin), (e, other)])
        first = []
        for i, s in enumerate(sources[1:]):
            first.append(remote(rows.at[s], out.at[e, w], ep_s.at[i], ep_r.at[i], (s, w)))
            first[-1].start()
        load = pltpu.make_async_copy(rows.at[e], own, load_sem.at[0])
        load.start()
        over_y, to_twin, relayed = [], [], []

        def relay(j):
            over_y[j].wait_recv()
            block = out.at[sources[j], other]
            relayed.append(remote(block, block, x_s.at[j], x_r.at[j], (e, twin)))
            relayed[-1].start()

        for j, s in enumerate(sources):
            place = out.at[s, w]
            block = rows.at[e] if j == 0 else place
            if j:
                first[j - 1].wait_recv()
            over_y.append(remote(block, place, y_s.at[j], y_r.at[j], (e, other)))
            over_y[-1].start()
            to_twin.append(remote(block, place, c_s.at[j], c_r.at[j], (e, twin)))
            to_twin[-1].start()
            if j == 0:
                load.wait()
                store = pltpu.make_async_copy(own, out.at[e, w], load_sem.at[1])
                store.start()
            else:
                relay(j - 1)
            yield
        relay(n - 1)
        store.wait()
        for copy in first + over_y:
            copy.wait_send()
        for copy in to_twin + relayed:
            copy.wait()

    return Job(
        [rows],
        [jax.ShapeDtypeStruct((n, n_ws, count, width), rows.dtype)],
        [pltpu.VMEM((count, width), rows.dtype), DMA((2,)), DMA((n - 1,)), DMA((n - 1,))]
        + [DMA((n,)) for _ in range(6)],
        n,
        body,
    )


def combine_job(part):
    n, _, count, width = part.shape
    block = (n, count, width)

    def body(
        part, out, mine, core, sum_y, from_y, total, load_sem, c_s, c_r, y_s, y_r, ep_s, ep_r, own_sem
    ):
        e, w = lax.axis_index("ep"), lax.axis_index("ws")
        twin, other, last = flip(w, 1), flip(w, 2), flip(w, 3)
        targets = [flip(e, k) for k in far_first(n)] + [e]
        greet([(s, w) for s in targets[:-1]] + [(e, twin), (e, other)])
        loads, cores = {}, {}
        for half, near, far in ((1, other, last), (0, w, twin)):
            for j, s in enumerate(targets):
                cores[half, j] = remote(
                    part.at[s, far], core.at[half, j], c_s.at[half, j], c_r.at[half, j], (e, twin)
                )
                cores[half, j].start()
                loads[half, j] = pltpu.make_async_copy(
                    part.at[s, near], mine.at[half, j], load_sem.at[half, j]
                )
                loads[half, j].start()
        over_y, back = [], []

        def send_y(j):
            over_y.append(remote(sum_y.at[j], from_y.at[j], y_s.at[j], y_r.at[j], (e, other)))
            over_y[-1].start()

        def send_back(j):
            back.append(remote(total.at[j], out.at[e], ep_s.at[j], ep_r.at[j], (targets[j], w)))
            back[-1].start()

        for j in range(n):
            loads[1, j].wait()
            cores[1, j].wait_recv()
            sum_y[j] = (mine[1, j].astype(f32) + core[1, j].astype(f32)).astype(bf16)
            if j:
                send_y(j - 1)
        loads[0, 0].wait()
        cores[0, 0].wait_recv()
        send_y(n - 1)
        for j in range(n):
            if j:
                loads[0, j].wait()
                cores[0, j].wait_recv()
            over_y[j].wait_recv()
            total[j] = (
                mine[0, j].astype(f32) + core[0, j].astype(f32) + from_y[j].astype(f32)
            ).astype(bf16)
            if j:
                send_back(j - 1)
            yield
        for copy in over_y + list(cores.values()):
            copy.wait_send()
        keep = pltpu.make_async_copy(total.at[n - 1], out.at[e], own_sem)
        keep.start()
        for copy in back:
            copy.wait()
        keep.wait()

    return Job(
        [part],
        [jax.ShapeDtypeStruct(block, part.dtype)],
        [
            pltpu.VMEM((2,) + block, part.dtype),
            pltpu.VMEM((2,) + block, part.dtype),
            pltpu.VMEM(block, part.dtype),
            pltpu.VMEM(block, part.dtype),
            pltpu.VMEM(block, part.dtype),
            DMA((2, n)),
            DMA((2, n)),
            DMA((2, n)),
            DMA((n,)),
            DMA((n,)),
            DMA((n - 1,)),
            DMA((n - 1,)),
            DMA,
        ],
        n,
        body,
    )


def exchange_job(rows):
    n = rows.shape[0]

    def body(rows, out, own, load_sem, ep_s, ep_r):
        e, w = lax.axis_index("ep"), lax.axis_index("ws")
        targets = [flip(e, k) for k in far_first(n)]
        greet([(s, w) for s in targets])
        copies = []
        for i, s in enumerate(targets):
            copies.append(remote(rows.at[s], out.at[e], ep_s.at[i], ep_r.at[i], (s, w)))
            copies[-1].start()
        load = pltpu.make_async_copy(rows.at[e], own, load_sem.at[0])
        load.start()
        load.wait()
        store = pltpu.make_async_copy(own, out.at[e], load_sem.at[1])
        store.start()
        yield
        store.wait()
        for copy in copies:
            copy.wait()

    return Job(
        [rows],
        [jax.ShapeDtypeStruct(rows.shape, rows.dtype)],
        [pltpu.VMEM(rows.shape[1:], rows.dtype), DMA((2,)), DMA((n - 1,)), DMA((n - 1,))],
        1,
        body,
    )


def attend_kernel(spans, q_ref, kv_ref, out):
    count, _, slots, part = q_ref.shape
    for w, span in enumerate(spans):

        def head(h, carry, w=w, span=span):
            at = pl.multiple_of(h * HEAD_SIZE, HEAD_SIZE)
            columns = pl.ds(at, HEAD_SIZE)
            q, probs, _, values = head_probs(q_ref, kv_ref, w, span, at)
            mixed = dot(probs.astype(bf16), values)
            out[:, w, :, columns] = mixed.reshape(count, slots, HEAD_SIZE).astype(bf16)
            return carry

        lax.fori_loop(0, part // HEAD_SIZE, head, 0)


def slot_rows(ref, w, at):
    count, _, slots, _ = ref.shape
    rows = ref[:, w, :, pl.ds(at, HEAD_SIZE)].astype(f32)
    return rows.reshape(count * slots, HEAD_SIZE).astype(bf16)


def head_probs(q_ref, kv_ref, w, span, at):
    half = kv_ref.shape[1] // 2
    q = slot_rows(q_ref, w, at)
    keys = kv_ref[:span, pl.ds(at, HEAD_SIZE)]
    values = kv_ref[:span, pl.ds(pl.multiple_of(half + at, HEAD_SIZE), HEAD_SIZE)]
    scores = dot_t(q, keys) * HEAD_SIZE ** (-0.5)
    weight = jnp.exp(scores - jnp.max(scores, -1, keepdims=True))
    probs = weight / jnp.sum(weight, -1, keepdims=True)
    return q, probs, keys, values


def attend_call(queries, kv, spans):
    return pl.pallas_call(
        functools.partial(attend_kernel, spans),
        out_shape=jax.ShapeDtypeStruct(queries.shape, bf16),
        in_specs=[VM, VM],
        out_specs=VM,
        compiler_params=pltpu.CompilerParams(vmem_limit_bytes=VMEM_LIMIT),
        name="attend",
    )(queries, kv)


def attend_back_kernel(spans, q_ref, g_ref, kv_ref, grad_q, grad_kv, total):
    count, _, slots, part = q_ref.shape
    total[...] = jnp.zeros_like(total)
    for w, span in enumerate(spans):

        def head(h, carry, w=w, span=span):
            at = pl.multiple_of(h * HEAD_SIZE, HEAD_SIZE)
            columns = pl.ds(at, HEAD_SIZE)
            q, probs, keys, values = head_probs(q_ref, kv_ref, w, span, at)
            grad = slot_rows(g_ref, w, at)
            grad_probs = dot_t(grad, values)
            centred = jnp.sum(probs * grad_probs, -1, keepdims=True)
            grad_scores = (probs * (grad_probs - centred)).astype(bf16)
            grad_rows = dot(grad_scores, keys) * HEAD_SIZE ** (-0.5)
            grad_q[:, w, :, columns] = grad_rows.reshape(count, slots, HEAD_SIZE).astype(bf16)
            total[:span, columns] += t_dot(grad_scores, q) * HEAD_SIZE ** (-0.5)
            at_value = pl.ds(pl.multiple_of(part + at, HEAD_SIZE), HEAD_SIZE)
            total[:span, at_value] += t_dot(probs.astype(bf16), grad)
            return carry

        lax.fori_loop(0, part // HEAD_SIZE, head, 0)
    grad_kv[...] = total[...].astype(bf16)


def attend_back_call(queries, grads, kv, spans):
    return pl.pallas_call(
        functools.partial(attend_back_kernel, spans),
        out_shape=[
            jax.ShapeDtypeStruct(queries.shape, bf16),
            jax.ShapeDtypeStruct(kv.shape, bf16),
        ],
        in_specs=[VM, VM, VM],
        out_specs=[VM, VM],
        scratch_shapes=[pltpu.VMEM(kv.shape, f32)],
        compiler_params=pltpu.CompilerParams(vmem_limit_bytes=VMEM_LIMIT),
        name="attend_back",
    )(queries, grads, kv)


def gather_kernel(n, n_ws, own, out, load_sem, w_s, w_r, ep_s, ep_r):
    e, w = lax.axis_index("ep"), lax.axis_index("ws")
    beside = [flip(w, k) for k in range(1, n_ws)]
    across = [flip(e, k) for k in far_first(n)]
    greet([(e, p) for p in beside] + [(s, w) for s in across])
    keep = pltpu.make_async_copy(own, out.at[e, w], load_sem)
    keep.start()
    first = []
    for i, p in enumerate(beside):
        first.append(remote(own, out.at[e, w], w_s.at[i], w_r.at[i], (e, p)))
        first[-1].start()
    keep.wait()
    for copy in first:
        copy.wait()
    second = []
    for i, s in enumerate(across):
        second.append(remote(out.at[e], out.at[e], ep_s.at[i], ep_r.at[i], (s, w)))
        second[-1].start()
    for copy in second:
        copy.wait()


def gather_call(own, n, n_ws):
    return pl.pallas_call(
        functools.partial(gather_kernel, n, n_ws),
        out_shape=jax.ShapeDtypeStruct((n, n_ws) + own.shape, own.dtype),
        in_specs=[VM],
        out_specs=VM,
        scratch_shapes=[DMA, DMA((n_ws - 1,)), DMA((n_ws - 1,)), DMA((n - 1,)), DMA((n - 1,))],
        compiler_params=pltpu.CompilerParams(collective_id=3, has_side_effects=True),
        name="gather_gains",
    )(own)


def reduce_kernel(n, n_ws, parts, out, held, all_parts, load_sem, w_s, w_r, ep_s, ep_r):
    e, w = lax.axis_index("ep"), lax.axis_index("ws")
    beside = [flip(w, k) for k in range(1, n_ws)]
    across = [flip(e, k) for k in far_first(n)]
    greet([(e, p) for p in beside] + [(s, w) for s in across])
    keep = pltpu.make_async_copy(parts.at[:, w], held.at[:, w], load_sem.at[0])
    keep.start()
    first = []
    for i, p in enumerate(beside):
        first.append(remote(parts.at[:, p], held.at[:, w], w_s.at[i], w_r.at[i], (e, p)))
        first[-1].start()
    keep.wait()
    for copy in first:
        copy.wait()
    keep = pltpu.make_async_copy(held.at[e], all_parts.at[e], load_sem.at[1])
    keep.start()
    second = []
    for i, s in enumerate(across):
        second.append(remote(held.at[s], all_parts.at[e], ep_s.at[i], ep_r.at[i], (s, w)))
        second[-1].start()
    keep.wait()
    for copy in second:
        copy.wait()
    out[...] = jnp.sum(jnp.sum(all_parts[...], 0), 0)


def reduce_call(parts):
    n, n_ws = parts.shape[:2]
    return pl.pallas_call(
        functools.partial(reduce_kernel, n, n_ws),
        out_shape=jax.ShapeDtypeStruct(parts.shape[2:], parts.dtype),
        in_specs=[VM],
        out_specs=VM,
        scratch_shapes=[
            pltpu.VMEM(parts.shape, parts.dtype),
            pltpu.VMEM(parts.shape, parts.dtype),
            DMA((2,)),
            DMA((n_ws - 1,)),
            DMA((n_ws - 1,)),
            DMA((n - 1,)),
            DMA((n - 1,)),
        ],
        compiler_params=pltpu.CompilerParams(collective_id=4, has_side_effects=True),
        name="reduce_gains",
    )(parts)


def small(n_ep):
    return n_ep == MIXTURE_EXPERTS and lax.axis_size("ws") == 4


PLAIN = {
    grad_job: t_dot,
    pair_grad_job: lambda a, b, c: jnp.stack([t_dot(a, b), t_dot(a, c)], 1),
    product_job: lambda a, b, dtype: dot(a, b).astype(dtype),
}


def beside(job, plain, arg, fills, collective_id, name):
    if job is None:
        return [plain(arg)] + [PLAIN[make](*rest) for make, *rest in fills]
    return run_jobs(job(arg), [make(*rest) for make, *rest in fills], collective_id, name)


def exchange_plain(send):
    return lax.all_to_all(send, "ep", split_axis=0, concat_axis=0, tiled=True)


def exchange(send, *fills, collective_id=2, name="exchange"):
    job = exchange_job if small(send.shape[0]) else None
    return beside(job, exchange_plain, send, fills, collective_id, name)


def spread(rows, group):
    width = rows.shape[-1]
    blocks = rows.reshape(MIXTURE_EXPERTS, 1, ROWS, width)
    return jnp.broadcast_to(blocks, (MIXTURE_EXPERTS, group, ROWS, width)).reshape(
        MIXTURE_EXPERTS * group, ROWS, width
    )


def dispatch(rows, group, *fills, collective_id=0, name="dispatch"):
    width = rows.shape[-1]

    def plain(blocks):
        return lax.all_gather(exchange_plain(blocks), "ws", axis=1, tiled=False)

    job = functools.partial(dispatch_job, n_ws=4) if small(MIXTURE_EXPERTS * group) else None
    out = beside(job, plain, spread(rows, group), fills, collective_id, name)
    return [out[0].reshape(-1, width)] + list(out[1:])


def combine(partial, group, n_ep, n_ws, *fills, collective_id=1, name="combine"):
    width = partial.shape[-1]

    def plain(part):
        part = part.transpose(1, 0, 2, 3).reshape(n_ws * n_ep * ROWS, width)
        own = lax.psum_scatter(part, "ws", scatter_dimension=0, tiled=True)
        return exchange_plain(own.reshape(n_ep, ROWS, width))

    part = partial.reshape(n_ep, n_ws, ROWS, width)
    job = combine_job if small(n_ep) else None
    back, *rest = beside(job, plain, part, fills, collective_id, name)
    if group > 1:
        back = jnp.sum(back.reshape(MIXTURE_EXPERTS, group, ROWS, width).astype(f32), 1).astype(bf16)
    return [back.reshape(MIXTURE_EXPERTS * ROWS, width)] + rest


def slot_tables(routes, slots):
    target = jnp.where(slots < CAP, routes * ROWS + slots, -1)
    places = lax.broadcasted_iota(jnp.int32, (MIXTURE_EXPERTS * ROWS, target.shape[0]), 0)
    return [(places == target[None, :, k]).astype(bf16) for k in range(CHOSEN_EXPERTS)]


def norm_back(grad, unit, inverse, gain):
    gain_grad = jnp.sum(grad * unit, 0)
    scaled = grad * gain
    return (inverse * (scaled - unit * jnp.mean(scaled * unit, -1, keepdims=True)), gain_grad)


def heads_of(rows):
    return rows.reshape(rows.shape[0], -1, HEAD_SIZE)


def local(
    x_in,
    gain_attn,
    gain_ffn,
    key_value_weight,
    w_query,
    w_output,
    w_in,
    w_out,
    gate_attn,
    gate_ffn,
    route_attn,
    slot_attn,
    route_ffn,
    slot_ffn,
    cotangent,
):
    n_ep = lax.axis_size("ep")
    n_ws = lax.axis_size("ws")
    group = n_ep // MIXTURE_EXPERTS
    local_tokens, width = x_in.shape
    key_value_width = KEY_VALUE_HEADS * HEAD_SIZE
    part = w_query.shape[2]
    own_width = group * part
    sequence = n_ws * local_tokens
    place = lax.axis_index("ws")
    scale = HEAD_SIZE ** (-0.5)

    short = small(n_ep) and gain_attn.shape[0] == 64
    if short:
        gains = jnp.concatenate([gain_attn, gain_ffn], 0).astype(f32)[None]
        gains = gather_call(gains, n_ep, n_ws).reshape(n_ep * n_ws, 2, -1)
        gain_one, gain_two = gains[:, 0].reshape(-1), gains[:, 1].reshape(-1)
    else:
        gain_one = lax.all_gather(gain_attn, ("ep", "ws"), axis=0, tiled=True).astype(f32)
        gain_two = lax.all_gather(gain_ffn, ("ep", "ws"), axis=0, tiled=True).astype(f32)
    plain = group == 1 and key_value_weight.shape[1] == HEAD_SIZE
    if plain:
        half = n_ep // 2
        there = [
            (e * n_ws + w, (w + n_ws * (e // half)) * n_ws + e % half)
            for e in range(n_ep)
            for w in range(n_ws)
        ]
        mine = lax.ppermute(key_value_weight, ("ep", "ws"), there)
        kv_own = lax.all_gather(mine, "ep", axis=1, tiled=True)
    else:
        whole = lax.all_gather(key_value_weight, ("ep", "ws"), axis=1, tiled=True)
        whole = whole.reshape(width, 2 * group, n_ws, part)
        kv_own = lax.dynamic_index_in_dim(whole, place, 2, keepdims=False).reshape(width, -1)

    inputs = x_in.astype(f32)
    inverse_one = lax.rsqrt(jnp.mean(inputs * inputs, -1, keepdims=True) + EPS)
    unit_one = inputs * inverse_one
    normed = (unit_one * gain_one).astype(bf16)
    attn_pairs = slot_tables(route_attn, slot_attn)
    ffn_pairs = slot_tables(route_ffn, slot_ffn)
    attn_tokens = attn_pairs[0] + attn_pairs[1]
    ffn_tokens = ffn_pairs[0] + ffn_pairs[1]

    normed_sequence = lax.all_gather(normed, "ws", axis=0, tiled=True)
    rows_one = dispatch(dot(attn_tokens, normed).astype(bf16), group)[0]
    kv = dot(normed_sequence, kv_own).astype(bf16)
    keys = kv[:, :own_width].reshape(sequence, -1, HEAD_SIZE)
    values = kv[:, own_width:].reshape(sequence, -1, HEAD_SIZE)

    owner_query = dot(rows_one, w_query[0]).astype(bf16)
    queries = exchange(owner_query.reshape(n_ep, n_ws * ROWS, part))[0]
    spans = [(w * local_tokens // BLOCK + 1) * BLOCK for w in range(n_ws)]
    fused = small(n_ep)
    queries = queries.reshape(MIXTURE_EXPERTS, group, n_ws, ROWS, part)

    def by_block(rows):
        rows = rows.reshape(MIXTURE_EXPERTS, group, n_ws, ROWS, part)
        return [
            rows[:, :, w].transpose(0, 2, 1, 3).reshape(-1, own_width // HEAD_SIZE, HEAD_SIZE)
            for w in range(n_ws)
        ]

    def to_experts(pieces):
        rows = jnp.stack(
            [
                piece.reshape(MIXTURE_EXPERTS, ROWS, group, part).transpose(0, 2, 1, 3)
                for piece in pieces
            ],
            2,
        )
        return rows.reshape(n_ep, n_ws * ROWS, part)

    if fused:
        queries = queries.reshape(n_ep, n_ws, ROWS, part)
        mixed = attend_call(queries, kv, spans).reshape(n_ep, n_ws * ROWS, part)
    else:
        kept = []
        mixed_pieces = []
        for q, span in zip(by_block(queries), spans):
            scores = (
                jnp.einsum("rhd,shd->hrs", q, keys[:span], preferred_element_type=f32) * scale
            )
            probs = jax.nn.softmax(scores, axis=-1)
            mixed = jnp.einsum(
                "hrs,shd->rhd", probs.astype(bf16), values[:span], preferred_element_type=f32
            )
            kept.append((q, probs))
            mixed_pieces.append(mixed.astype(bf16))
        mixed = to_experts(mixed_pieces)
    owner_mixed = exchange(mixed)[0].reshape(-1, part)
    attn_slots = combine(dot(owner_mixed, w_output[0]).astype(bf16), group, n_ep, n_ws)[0]

    def weighted(pairs, gates, slot_values):
        return sum(gates[:, k : k + 1] * t_dot(pairs[k], slot_values) for k in range(2))

    def to_slots(pairs, gates, values):
        return sum(
            dot(pairs[k], (gates[:, k : k + 1] * values).astype(bf16)) for k in range(2)
        ).astype(bf16)

    hidden_state = inputs + weighted(attn_pairs, gate_attn, attn_slots)
    inverse_two = lax.rsqrt(jnp.mean(hidden_state * hidden_state, -1, keepdims=True) + EPS)
    unit_two = hidden_state * inverse_two
    normed_two = (unit_two * gain_two).astype(bf16)

    grad_out = cotangent.astype(f32)
    grad_slots = to_slots(ffn_pairs, gate_ffn, grad_out)
    gate_weight, up_weight = w_in[0, :, 0], w_in[0, :, 1]
    expert_rows = dispatch(dot(ffn_tokens, normed_two).astype(bf16), group)[0]
    expert_grad, gate_pre, up_pre = dispatch(
        grad_slots,
        group,
        (product_job, expert_rows, gate_weight, f32),
        (product_job, expert_rows, up_weight, f32),
        collective_id=5,
        name="dispatch_ffn_in",
    )
    sigmoid_gate = jax.nn.sigmoid(gate_pre)
    silu_gate = gate_pre * sigmoid_gate
    activated = (silu_gate * up_pre).astype(bf16)
    grad_act = dot_t(expert_grad, w_out[0])
    grad_up = (grad_act * silu_gate).astype(bf16)
    grad_gate = (
        grad_act * up_pre * sigmoid_gate * (1.0 + gate_pre * (1.0 - sigmoid_gate))
    ).astype(bf16)
    back_two = (dot_t(grad_gate, gate_weight) + dot_t(grad_up, up_weight)).astype(bf16)
    back_slots, forward_part, grad_second = combine(
        back_two,
        group,
        n_ep,
        n_ws,
        (product_job, activated, w_out[0], bf16),
        (grad_job, activated, expert_grad),
        collective_id=6,
        name="combine_ffn_out",
    )

    grad_normed_two = t_dot(ffn_tokens, back_slots)
    grad_hidden_norm, grad_gain_two = norm_back(grad_normed_two, unit_two, inverse_two, gain_two)
    grad_hidden = grad_out + grad_hidden_norm
    owner_grad, grad_first = dispatch(
        to_slots(attn_pairs, gate_attn, grad_hidden),
        group,
        (pair_grad_job, expert_rows, grad_gate, grad_up),
        collective_id=7,
        name="dispatch_grad_in",
    )
    back_mixed = dot_t(owner_grad, w_output[0]).astype(bf16)
    mixed_grads, grad_output = exchange(
        back_mixed.reshape(n_ep, n_ws * ROWS, part),
        (grad_job, owner_mixed, owner_grad),
        collective_id=8,
        name="exchange_grad_output",
    )

    if fused:
        mixed_grads = mixed_grads.reshape(n_ep, n_ws, ROWS, part)
        query_grads, grad_kv_rows = attend_back_call(queries, mixed_grads, kv, spans)
        query_grads = query_grads.reshape(n_ep, n_ws * ROWS, part)
    else:
        grad_keys, grad_values, query_pieces = 0.0, 0.0, []
        for (q, probs), grad, span in zip(kept, by_block(mixed_grads), spans):
            grad_probs = jnp.einsum("rhd,shd->hrs", grad, values[:span], preferred_element_type=f32)
            centred = jnp.sum(probs * grad_probs, -1, keepdims=True)
            grad_scores = (probs * (grad_probs - centred)).astype(bf16)
            grad_q = (
                jnp.einsum("hrs,shd->rhd", grad_scores, keys[:span], preferred_element_type=f32)
                * scale
            )
            query_pieces.append(grad_q.astype(bf16))
            pad = ((0, sequence - span), (0, 0), (0, 0))
            piece = jnp.einsum("hrs,rhd->shd", grad_scores, q, preferred_element_type=f32) * scale
            grad_keys = grad_keys + jnp.pad(piece, pad)
            piece = jnp.einsum(
                "hrs,rhd->shd", probs.astype(bf16), grad, preferred_element_type=f32
            )
            grad_values = grad_values + jnp.pad(piece, pad)
        grad_kv_rows = jnp.concatenate(
            [grad_keys.reshape(sequence, -1), grad_values.reshape(sequence, -1)], 1
        ).astype(bf16)
        query_grads = to_experts(query_pieces)
    owner_grad_query = exchange(query_grads)[0].reshape(-1, part)
    back_normed = dot_t(owner_grad_query, w_query[0]).astype(bf16)
    normed_back, grad_query = combine(
        back_normed,
        group,
        n_ep,
        n_ws,
        (grad_job, rows_one, owner_grad_query),
        collective_id=9,
        name="combine_grad_query",
    )
    ffn_slots = combine(forward_part, group, n_ep, n_ws)[0]
    result = hidden_state + weighted(ffn_pairs, gate_ffn, ffn_slots)

    grad_kv = t_dot(normed_sequence, grad_kv_rows)
    if plain:
        pieces = grad_kv.reshape(width, n_ep, HEAD_SIZE).transpose(1, 0, 2).astype(bf16)
        piece = lax.psum_scatter(pieces, "ep", scatter_dimension=0, tiled=False)
        grad_kv_shard = lax.ppermute(piece, ("ep", "ws"), [(b, a) for a, b in there]).astype(f32)
    else:
        mask = (jnp.arange(n_ws) == place)[None, None, :, None]
        pieces = jnp.where(mask, grad_kv.reshape(width, 2 * group, 1, part), 0.0)
        pieces = pieces.reshape(width, 2 * key_value_width).astype(bf16)
        grad_kv_shard = lax.psum_scatter(
            pieces, ("ep", "ws"), scatter_dimension=1, tiled=True
        ).astype(f32)
    from_kv = lax.psum_scatter(
        dot_t(grad_kv_rows, kv_own).astype(bf16), "ws", scatter_dimension=0, tiled=True
    )
    grad_normed = t_dot(attn_tokens, normed_back) + from_kv.astype(f32)
    grad_input_norm, grad_gain_one = norm_back(grad_normed, unit_one, inverse_one, gain_one)
    grad_input = grad_hidden + grad_input_norm
    gain_grads = jnp.stack([grad_gain_one, grad_gain_two], 0)
    if short:
        parts = gain_grads.reshape(2, n_ep, n_ws, -1).transpose(1, 2, 0, 3)
        gain_shards = reduce_call(parts.reshape(n_ep, n_ws, 1, -1)).reshape(2, -1)
    else:
        gain_shards = lax.psum_scatter(
            gain_grads, ("ep", "ws"), scatter_dimension=1, tiled=True
        )
    return (
        result.astype(bf16),
        grad_input,
        gain_shards[0],
        gain_shards[1],
        grad_kv_shard,
        grad_query[None],
        grad_output[None],
        grad_first[None],
        grad_second[None],
    )


def solution(mesh):
    both = ("ep", "ws")
    rows, vector, columns = P(both, None), P(both), P(None, both)
    return jax.shard_map(
        local,
        mesh=mesh,
        in_specs=(
            rows,
            vector,
            vector,
            columns,
            P("ep", None, "ws"),
            P("ep", "ws", None),
            P("ep", None, None, "ws"),
            P("ep", "ws", None),
            rows,
            rows,
            rows,
            rows,
            rows,
            rows,
            rows,
        ),
        out_specs=(
            rows,
            rows,
            vector,
            vector,
            columns,
            P("ep", None, "ws"),
            P("ep", "ws", None),
            P("ep", None, None, "ws"),
            P("ep", "ws", None),
        ),
        check_vma=False,
    )
```

```python
import functools

import jax
import jax.numpy as jnp
from jax import lax
from jax.experimental import pallas as pl
from jax.experimental.pallas import tpu as pltpu
from jax.sharding import PartitionSpec as P

KEY_VALUE_HEADS = 16
HEAD_SIZE = 128
MIXTURE_EXPERTS = 8
CHOSEN_EXPERTS = 2
BLOCK = 256
CAP = 36
ROWS = 40

EPS = 1e-06
very_negative = -1e30
f32 = jnp.float32
bf16 = jnp.bfloat16
MESH = pl.DeviceIdType.MESH
ANY = pl.BlockSpec(memory_space=pl.ANY)
VM = pl.BlockSpec(memory_space=pltpu.VMEM)
DMA = pltpu.SemaphoreType.DMA
STEP = 256
VMEM_LIMIT = 60 << 20


def dot(a, b):
    return jnp.dot(a, b, preferred_element_type=f32)


def dot_t(a, b):
    return lax.dot_general(a, b, (((1,), (1,)), ((), ())), preferred_element_type=f32)


def t_dot(a, b):
    return lax.dot_general(a, b, (((0,), (0,)), ((), ())), preferred_element_type=f32)


def flip(index, bits):
    out, bit = index, 1
    while bit <= bits:
        if bits & bit:
            out = out + bit - 2 * bit * ((index // bit) % 2)
        bit *= 2
    return out


def far_first(n):
    return sorted(range(1, n), key=lambda k: (-((k // 2).bit_length()), k))


def greet(partners):
    barrier = pltpu.get_barrier_semaphore()
    for partner in partners:
        pl.semaphore_signal(barrier, inc=1, device_id=partner, device_id_type=MESH)
    pl.semaphore_wait(barrier, len(partners))


def remote(src, dst, send, recv, device):
    return pltpu.make_async_remote_copy(
        src_ref=src, dst_ref=dst, send_sem=send, recv_sem=recv, device_id=device, device_id_type=MESH
    )


class Job:
    def __init__(self, args, outs, scratch, steps, body):
        self.args, self.outs, self.scratch, self.steps, self.body = args, outs, scratch, steps, body


def run_jobs(exchange_job, fills, collective_id, name):
    jobs = [exchange_job] + fills
    args = [a for job in jobs for a in job.args]
    outs = [o for job in jobs for o in job.outs]
    scratch = [x for job in jobs for x in job.scratch]

    def kernel(*refs):
        bodies, at = [], [0, len(args), len(args) + len(outs)]
        for job in jobs:
            own = []
            for k, part in enumerate((job.args, job.outs, job.scratch)):
                own.append(refs[at[k] : at[k] + len(part)])
                at[k] += len(part)
            bodies.append(job.body(*own[0], *own[1], *own[2]))
        work = [bodies[k + 1] for k in range(len(fills))]
        queue = [g for g, job in zip(work, fills) for _ in range(job.steps)]
        for g in work:
            next(g)
        done = 0
        for k, _ in enumerate(bodies[0]):
            target = (k + 1) * len(queue) // exchange_job.steps
            while done < target:
                next(queue[done])
                done += 1
        for g in work:
            for _ in g:
                pass

    return pl.pallas_call(
        kernel,
        out_shape=outs,
        in_specs=[ANY] * len(args),
        out_specs=[ANY] * len(outs),
        scratch_shapes=scratch,
        compiler_params=pltpu.CompilerParams(
            collective_id=collective_id, has_side_effects=True, vmem_limit_bytes=VMEM_LIMIT
        ),
        name=name,
    )(*args)


def fetch(pairs, sem):
    copies = [
        pltpu.make_async_copy(src, dst, sem.at[i]) for i, (src, dst) in enumerate(pairs)
    ]
    for copy in copies:
        copy.start()
    return copies


def blocks_of(size):
    return [(start, min(STEP, size - start)) for start in range(0, size, STEP)]


def column_tiles(width, tile):
    def body(c, carry):
        tile(pl.multiple_of(c * STEP, STEP), STEP)
        return carry

    lax.fori_loop(0, width // STEP, body, 0)
    if width % STEP:
        tile(width // STEP * STEP, width % STEP)


def grad_job(a, b):
    depth, rows = a.shape
    width = b.shape[1]

    def body(a_hbm, b_hbm, out, a_ref, b_ref, turned, held, load_sem, sem):
        loads = fetch(((a_hbm, a_ref), (b_hbm, b_ref)), load_sem)
        yield
        for load in loads:
            load.wait()
        copies = []
        for i, (start, size) in enumerate(blocks_of(rows)):
            if i >= 2:
                copies[i - 2].wait()
            turned[:size] = a_ref[:, start : start + size].T

            def tile(at, columns, slot=i % 2, size=size):
                held[slot, :size, pl.ds(at, columns)] = jnp.dot(
                    turned[:size], b_ref[:, pl.ds(at, columns)], preferred_element_type=f32
                )

            column_tiles(width, tile)
            copies.append(
                pltpu.make_async_copy(
                    held.at[i % 2, pl.ds(0, size)], out.at[pl.ds(start, size)], sem.at[i % 2]
                )
            )
            copies[i].start()
            yield
        for copy in copies[-2:]:
            copy.wait()

    return Job(
        [a, b],
        [jax.ShapeDtypeStruct((rows, width), f32)],
        [
            pltpu.VMEM(a.shape, bf16),
            pltpu.VMEM(b.shape, bf16),
            pltpu.VMEM((STEP, depth), bf16),
            pltpu.VMEM((2, STEP, width), f32),
            DMA((2,)),
            DMA((2,)),
        ],
        len(blocks_of(rows)),
        body,
    )


def pair_grad_job(a, first, second):
    depth, rows = a.shape
    tiles = first.shape[1] // 128

    def body(a_hbm, f_hbm, s_hbm, out, a_ref, f_ref, s_ref, turned, held, load_sem, sem):
        loads = fetch(((a_hbm, a_ref), (f_hbm, f_ref), (s_hbm, s_ref)), load_sem)
        flat = held.reshape(2 * tiles * STEP * 2, 128)
        yield
        for load in loads:
            load.wait()
        copies = []
        for i, (start, size) in enumerate(blocks_of(rows)):
            if i >= 2:
                for copy in copies[i - 2]:
                    copy.wait()
            turned[:size] = a_ref[:, start : start + size].T

            def tile(at, columns, slot=i % 2, size=size):
                for j, b_ref in enumerate((f_ref, s_ref)):
                    r = jnp.dot(
                        turned[:size], b_ref[:, pl.ds(at, columns)], preferred_element_type=f32
                    )
                    for half in range(columns // 128):
                        base = (slot * tiles + at // 128 + half) * (2 * STEP) + j
                        flat[pl.ds(base, size, stride=2), :] = r[:, half * 128 : half * 128 + 128]

            column_tiles(tiles * 128, tile)
            copies.append(
                [
                    pltpu.make_async_copy(
                        held.at[i % 2, c, pl.ds(0, size)],
                        out.at[pl.ds(start, size), :, pl.ds(c * 128, 128)],
                        sem.at[i % 2, c],
                    )
                    for c in range(tiles)
                ]
            )
            for copy in copies[i]:
                copy.start()
            yield
        for copy in copies[-2] + copies[-1]:
            copy.wait()

    return Job(
        [a, first, second],
        [jax.ShapeDtypeStruct((rows, 2, tiles * 128), f32)],
        [
            pltpu.VMEM(a.shape, bf16),
            pltpu.VMEM(first.shape, bf16),
            pltpu.VMEM(second.shape, bf16),
            pltpu.VMEM((STEP, depth), bf16),
            pltpu.VMEM((2, tiles, STEP, 2, 128), f32),
            DMA((3,)),
            DMA((2, tiles)),
        ],
        len(blocks_of(rows)),
        body,
    )


def split_job(weight):
    rows, _, width = weight.shape

    def body(w_hbm, first, second, block, wide, held, load_sem, sem):
        flat = wide.reshape(2 * STEP, 128)
        steps = rows // STEP

        def load(i):
            return pltpu.make_async_copy(
                w_hbm.at[pl.ds(i * STEP, STEP)], block.at[i % 2], load_sem.at[i % 2]
            )

        load(0).start()
        yield
        copies = []
        for i in range(steps):
            slot = i % 2
            if i + 1 < steps:
                load(i + 1).start()
            load(i).wait()
            if i >= 2:
                for copy in copies[i - 2]:
                    copy.wait()

            def tile(c, carry, slot=slot):
                at = pl.ds(pl.multiple_of(c * 128, 128), 128)
                wide[...] = block[slot, :, :, at].astype(f32)
                for j in range(2):
                    held[slot, j, :, at] = flat[pl.ds(j, STEP, stride=2), :].astype(bf16)
                return carry

            lax.fori_loop(0, width // 128, tile, 0)
            copies.append(
                [
                    pltpu.make_async_copy(
                        held.at[slot, j], out.at[pl.ds(i * STEP, STEP)], sem.at[slot, j]
                    )
                    for j, out in enumerate((first, second))
                ]
            )
            for copy in copies[i]:
                copy.start()
            yield
        for copy in copies[-2] + copies[-1]:
            copy.wait()

    return Job(
        [weight],
        [jax.ShapeDtypeStruct((rows, width), bf16)] * 2,
        [
            pltpu.VMEM((2, STEP, 2, width), bf16),
            pltpu.VMEM((STEP, 2, 128), f32),
            pltpu.VMEM((2, 2, STEP, width), bf16),
            DMA((2,)),
            DMA((2, 2)),
        ],
        rows // STEP,
        body,
    )


def ffn_job(x, gate_weight, up_weight, down_weight):
    rows, width = x.shape
    hidden = gate_weight.shape[1]

    def body(
        x_hbm, g_hbm, u_hbm, d_hbm, gate_out, up_out, act_out, out, x_ref, g_ref, u_ref, d_ref, pre, act, res,
        load_sem, sem
    ):
        loads = fetch(((x_hbm, x_ref), (g_hbm, g_ref), (u_hbm, u_ref), (d_hbm, d_ref)), load_sem)
        yield
        for load in loads:
            load.wait()
        copies = []
        for i, (start, size) in enumerate(blocks_of(rows)):
            slot = i % 2
            here = pl.ds(start, size)
            if i >= 2:
                for copy in copies[i - 2]:
                    copy.wait()

            def tile(at, columns, slot=slot, start=start, size=size):
                part = pl.ds(at, columns)
                left = x_ref[start : start + size]
                gate = dot(left, g_ref[:, part])
                up = dot(left, u_ref[:, part])
                pre[slot, 0, :, part] = gate
                pre[slot, 1, :, part] = up
                act[slot, :, part] = (gate * jax.nn.sigmoid(gate) * up).astype(bf16)

            column_tiles(hidden, tile)
            yield

            def last(at, columns, slot=slot):
                part = pl.ds(at, columns)
                res[slot, :, part] = dot(act[slot], d_ref[:, part]).astype(bf16)

            column_tiles(width, last)
            copies.append(
                [
                    pltpu.make_async_copy(src.at[slot], dst.at[here], sem.at[slot, k])
                    for k, (src, dst) in enumerate(((act, act_out), (res, out)))
                ]
                + [
                    pltpu.make_async_copy(pre.at[slot, k], dst.at[here], sem.at[slot, 2 + k])
                    for k, dst in enumerate((gate_out, up_out))
                ]
            )
            for copy in copies[i]:
                copy.start()
            yield
        for copy in copies[-2] + copies[-1]:
            copy.wait()

    return Job(
        [x, gate_weight, up_weight, down_weight],
        [jax.ShapeDtypeStruct((rows, hidden), f32)] * 2
        + [jax.ShapeDtypeStruct((rows, hidden), bf16), jax.ShapeDtypeStruct((rows, width), bf16)],
        [
            pltpu.VMEM(x.shape, bf16),
            pltpu.VMEM(gate_weight.shape, bf16),
            pltpu.VMEM(up_weight.shape, bf16),
            pltpu.VMEM(down_weight.shape, bf16),
            pltpu.VMEM((2, 2, STEP, hidden), f32),
            pltpu.VMEM((2, STEP, hidden), bf16),
            pltpu.VMEM((2, STEP, width), bf16),
            DMA((4,)),
            DMA((2, 4)),
        ],
        2 * (rows // STEP),
        body,
    )


def ffn_plain(x, gate_weight, up_weight, down_weight):
    gate_pre, up_pre = dot(x, gate_weight), dot(x, up_weight)
    activated = (gate_pre * jax.nn.sigmoid(gate_pre) * up_pre).astype(bf16)
    return gate_pre, up_pre, activated, dot(activated, down_weight).astype(bf16)


def before_activation(grad_act, gate_pre, up_pre):
    sigmoid_gate = jax.nn.sigmoid(gate_pre)
    grad_up = (grad_act * gate_pre * sigmoid_gate).astype(bf16)
    grad_gate = (
        grad_act * up_pre * sigmoid_gate * (1.0 + gate_pre * (1.0 - sigmoid_gate))
    ).astype(bf16)
    return grad_gate, grad_up


def ffn_back_job(grad, gate_pre, up_pre, gate_weight, up_weight, down_weight):
    rows, width = grad.shape
    hidden = gate_weight.shape[1]

    def body(
        x_hbm, gp_hbm, up_hbm, g_hbm, u_hbm, d_hbm, gate_out, up_out, out, x_ref, g_ref, u_ref, d_ref, pre, hid,
        res, load_sem, pre_sem, sem
    ):
        loads = fetch(((x_hbm, x_ref), (g_hbm, g_ref), (u_hbm, u_ref), (d_hbm, d_ref)), load_sem)

        def load_pre(i):
            here = pl.ds(i * STEP, STEP)
            return [
                pltpu.make_async_copy(src.at[here], pre.at[i % 2, k], pre_sem.at[i % 2, k])
                for k, src in enumerate((gp_hbm, up_hbm))
            ]

        for copy in load_pre(0):
            copy.start()
        yield
        for load in loads:
            load.wait()
        copies = []
        steps = rows // STEP
        for i in range(steps):
            slot, start = i % 2, i * STEP
            here = pl.ds(start, STEP)
            if i + 1 < steps:
                for copy in load_pre(i + 1):
                    copy.start()
            for copy in load_pre(i):
                copy.wait()
            if i >= 2:
                for copy in copies[i - 2]:
                    copy.wait()

            def tile(at, columns, slot=slot, start=start):
                part = pl.ds(at, columns)
                grad_act = dot_t(x_ref[start : start + STEP], d_ref[part, :])
                pair = before_activation(grad_act, pre[slot, 0, :, part], pre[slot, 1, :, part])
                hid[slot, 0, :, part], hid[slot, 1, :, part] = pair

            column_tiles(hidden, tile)
            yield

            def last(at, columns, slot=slot):
                part = pl.ds(at, columns)
                total = dot_t(hid[slot, 0], g_ref[part, :]) + dot_t(hid[slot, 1], u_ref[part, :])
                res[slot, :, part] = total.astype(bf16)

            column_tiles(width, last)
            copies.append(
                [pltpu.make_async_copy(res.at[slot], out.at[here], sem.at[slot, 2])]
                + [
                    pltpu.make_async_copy(hid.at[slot, k], dst.at[here], sem.at[slot, k])
                    for k, dst in enumerate((gate_out, up_out))
                ]
            )
            for copy in copies[i]:
                copy.start()
            yield
        for copy in copies[-2] + copies[-1]:
            copy.wait()

    return Job(
        [grad, gate_pre, up_pre, gate_weight, up_weight, down_weight],
        [jax.ShapeDtypeStruct((rows, hidden), bf16)] * 2 + [jax.ShapeDtypeStruct((rows, width), bf16)],
        [
            pltpu.VMEM(grad.shape, bf16),
            pltpu.VMEM(gate_weight.shape, bf16),
            pltpu.VMEM(up_weight.shape, bf16),
            pltpu.VMEM(down_weight.shape, bf16),
            pltpu.VMEM((2, 2, STEP, hidden), f32),
            pltpu.VMEM((2, 2, STEP, hidden), bf16),
            pltpu.VMEM((2, STEP, width), bf16),
            DMA((4,)),
            DMA((2, 2)),
            DMA((2, 3)),
        ],
        2 * (rows // STEP),
        body,
    )


def ffn_back_plain(grad, gate_pre, up_pre, gate_weight, up_weight, down_weight):
    grad_gate, grad_up = before_activation(dot_t(grad, down_weight), gate_pre, up_pre)
    back = dot_t(grad_gate, gate_weight) + dot_t(grad_up, up_weight)
    return grad_gate, grad_up, back.astype(bf16)


def dispatch_job(rows, n_ws):
    n, count, width = rows.shape

    def body(rows, out, own, load_sem, ep_s, ep_r, y_s, y_r, c_s, c_r, x_s, x_r):
        e, w = lax.axis_index("ep"), lax.axis_index("ws")
        twin, other = flip(w, 1), flip(w, 2)
        sources = [e] + [flip(e, k) for k in range(1, n)]
        greet([(s, w) for s in sources[1:]] + [(e, twin), (e, other)])
        first = []
        for i, s in enumerate(sources[1:]):
            first.append(remote(rows.at[s], out.at[e, w], ep_s.at[i], ep_r.at[i], (s, w)))
            first[-1].start()
        load = pltpu.make_async_copy(rows.at[e], own, load_sem.at[0])
        load.start()
        over_y, to_twin, relayed = [], [], []

        def relay(j):
            over_y[j].wait_recv()
            block = out.at[sources[j], other]
            relayed.append(remote(block, block, x_s.at[j], x_r.at[j], (e, twin)))
            relayed[-1].start()

        for j, s in enumerate(sources):
            place = out.at[s, w]
            block = rows.at[e] if j == 0 else place
            if j:
                first[j - 1].wait_recv()
            over_y.append(remote(block, place, y_s.at[j], y_r.at[j], (e, other)))
            over_y[-1].start()
            to_twin.append(remote(block, place, c_s.at[j], c_r.at[j], (e, twin)))
            to_twin[-1].start()
            if j == 0:
                load.wait()
                store = pltpu.make_async_copy(own, out.at[e, w], load_sem.at[1])
                store.start()
            else:
                relay(j - 1)
            yield
        relay(n - 1)
        store.wait()
        for copy in first + over_y:
            copy.wait_send()
        for copy in to_twin + relayed:
            copy.wait()

    return Job(
        [rows],
        [jax.ShapeDtypeStruct((n, n_ws, count, width), rows.dtype)],
        [pltpu.VMEM((count, width), rows.dtype), DMA((2,)), DMA((n - 1,)), DMA((n - 1,))]
        + [DMA((n,)) for _ in range(6)],
        n,
        body,
    )


def combine_job(part):
    n, _, count, width = part.shape
    block = (n, count, width)

    def body(
        part, out, mine, core, sum_y, from_y, total, load_sem, c_s, c_r, y_s, y_r, ep_s, ep_r, own_sem
    ):
        e, w = lax.axis_index("ep"), lax.axis_index("ws")
        twin, other, last = flip(w, 1), flip(w, 2), flip(w, 3)
        targets = [flip(e, k) for k in far_first(n)] + [e]
        greet([(s, w) for s in targets[:-1]] + [(e, twin), (e, other)])
        loads, cores = {}, {}
        for half, near, far in ((1, other, last), (0, w, twin)):
            for j, s in enumerate(targets):
                cores[half, j] = remote(
                    part.at[s, far], core.at[half, j], c_s.at[half, j], c_r.at[half, j], (e, twin)
                )
                cores[half, j].start()
                loads[half, j] = pltpu.make_async_copy(
                    part.at[s, near], mine.at[half, j], load_sem.at[half, j]
                )
                loads[half, j].start()
        over_y, back = [], []

        def send_y(j):
            over_y.append(remote(sum_y.at[j], from_y.at[j], y_s.at[j], y_r.at[j], (e, other)))
            over_y[-1].start()

        def send_back(j):
            back.append(remote(total.at[j], out.at[e], ep_s.at[j], ep_r.at[j], (targets[j], w)))
            back[-1].start()

        for j in range(n):
            loads[1, j].wait()
            cores[1, j].wait_recv()
            sum_y[j] = (mine[1, j].astype(f32) + core[1, j].astype(f32)).astype(bf16)
            if j:
                send_y(j - 1)
        loads[0, 0].wait()
        cores[0, 0].wait_recv()
        send_y(n - 1)
        for j in range(n):
            if j:
                loads[0, j].wait()
                cores[0, j].wait_recv()
            over_y[j].wait_recv()
            total[j] = (
                mine[0, j].astype(f32) + core[0, j].astype(f32) + from_y[j].astype(f32)
            ).astype(bf16)
            if j:
                send_back(j - 1)
            yield
        for copy in over_y + list(cores.values()):
            copy.wait_send()
        keep = pltpu.make_async_copy(total.at[n - 1], out.at[e], own_sem)
        keep.start()
        for copy in back:
            copy.wait()
        keep.wait()

    return Job(
        [part],
        [jax.ShapeDtypeStruct(block, part.dtype)],
        [
            pltpu.VMEM((2,) + block, part.dtype),
            pltpu.VMEM((2,) + block, part.dtype),
            pltpu.VMEM(block, part.dtype),
            pltpu.VMEM(block, part.dtype),
            pltpu.VMEM(block, part.dtype),
            DMA((2, n)),
            DMA((2, n)),
            DMA((2, n)),
            DMA((n,)),
            DMA((n,)),
            DMA((n - 1,)),
            DMA((n - 1,)),
            DMA,
        ],
        n,
        body,
    )


def exchange_job(rows):
    n = rows.shape[0]

    def body(rows, out, own, load_sem, ep_s, ep_r):
        e, w = lax.axis_index("ep"), lax.axis_index("ws")
        targets = [flip(e, k) for k in far_first(n)]
        greet([(s, w) for s in targets])
        copies = []
        for i, s in enumerate(targets):
            copies.append(remote(rows.at[s], out.at[e], ep_s.at[i], ep_r.at[i], (s, w)))
            copies[-1].start()
        load = pltpu.make_async_copy(rows.at[e], own, load_sem.at[0])
        load.start()
        load.wait()
        store = pltpu.make_async_copy(own, out.at[e], load_sem.at[1])
        store.start()
        yield
        store.wait()
        for copy in copies:
            copy.wait()

    return Job(
        [rows],
        [jax.ShapeDtypeStruct(rows.shape, rows.dtype)],
        [pltpu.VMEM(rows.shape[1:], rows.dtype), DMA((2,)), DMA((n - 1,)), DMA((n - 1,))],
        1,
        body,
    )


def attend_kernel(spans, q_ref, kv_ref, out):
    count, _, slots, part = q_ref.shape
    for w, span in enumerate(spans):

        def head(h, carry, w=w, span=span):
            at = pl.multiple_of(h * HEAD_SIZE, HEAD_SIZE)
            columns = pl.ds(at, HEAD_SIZE)
            q, probs, _, values = head_probs(q_ref, kv_ref, w, span, at)
            mixed = dot(probs.astype(bf16), values)
            out[:, w, :, columns] = mixed.reshape(count, slots, HEAD_SIZE).astype(bf16)
            return carry

        lax.fori_loop(0, part // HEAD_SIZE, head, 0)


def slot_rows(ref, w, at):
    count, _, slots, _ = ref.shape
    rows = ref[:, w, :, pl.ds(at, HEAD_SIZE)].astype(f32)
    return rows.reshape(count * slots, HEAD_SIZE).astype(bf16)


def head_probs(q_ref, kv_ref, w, span, at):
    half = kv_ref.shape[1] // 2
    q = slot_rows(q_ref, w, at)
    keys = kv_ref[:span, pl.ds(at, HEAD_SIZE)]
    values = kv_ref[:span, pl.ds(pl.multiple_of(half + at, HEAD_SIZE), HEAD_SIZE)]
    scores = dot_t(q, keys) * HEAD_SIZE ** (-0.5)
    weight = jnp.exp(scores - jnp.max(scores, -1, keepdims=True))
    probs = weight / jnp.sum(weight, -1, keepdims=True)
    return q, probs, keys, values


def attend_call(queries, kv, spans):
    return pl.pallas_call(
        functools.partial(attend_kernel, spans),
        out_shape=jax.ShapeDtypeStruct(queries.shape, bf16),
        in_specs=[VM, VM],
        out_specs=VM,
        compiler_params=pltpu.CompilerParams(vmem_limit_bytes=VMEM_LIMIT),
        name="attend",
    )(queries, kv)


def attend_back_kernel(spans, q_ref, g_ref, kv_ref, grad_q, grad_kv, total):
    count, _, slots, part = q_ref.shape
    total[...] = jnp.zeros_like(total)
    for w, span in enumerate(spans):

        def head(h, carry, w=w, span=span):
            at = pl.multiple_of(h * HEAD_SIZE, HEAD_SIZE)
            columns = pl.ds(at, HEAD_SIZE)
            q, probs, keys, values = head_probs(q_ref, kv_ref, w, span, at)
            grad = slot_rows(g_ref, w, at)
            grad_probs = dot_t(grad, values)
            centred = jnp.sum(probs * grad_probs, -1, keepdims=True)
            grad_scores = (probs * (grad_probs - centred)).astype(bf16)
            grad_rows = dot(grad_scores, keys) * HEAD_SIZE ** (-0.5)
            grad_q[:, w, :, columns] = grad_rows.reshape(count, slots, HEAD_SIZE).astype(bf16)
            total[:span, columns] += t_dot(grad_scores, q) * HEAD_SIZE ** (-0.5)
            at_value = pl.ds(pl.multiple_of(part + at, HEAD_SIZE), HEAD_SIZE)
            total[:span, at_value] += t_dot(probs.astype(bf16), grad)
            return carry

        lax.fori_loop(0, part // HEAD_SIZE, head, 0)
    grad_kv[...] = total[...].astype(bf16)


def attend_back_call(queries, grads, kv, spans):
    return pl.pallas_call(
        functools.partial(attend_back_kernel, spans),
        out_shape=[
            jax.ShapeDtypeStruct(queries.shape, bf16),
            jax.ShapeDtypeStruct(kv.shape, bf16),
        ],
        in_specs=[VM, VM, VM],
        out_specs=[VM, VM],
        scratch_shapes=[pltpu.VMEM(kv.shape, f32)],
        compiler_params=pltpu.CompilerParams(vmem_limit_bytes=VMEM_LIMIT),
        name="attend_back",
    )(queries, grads, kv)


def gather_kernel(n, n_ws, own, out, load_sem, w_s, w_r, ep_s, ep_r):
    e, w = lax.axis_index("ep"), lax.axis_index("ws")
    beside = [flip(w, k) for k in range(1, n_ws)]
    across = [flip(e, k) for k in far_first(n)]
    greet([(e, p) for p in beside] + [(s, w) for s in across])
    keep = pltpu.make_async_copy(own, out.at[e, w], load_sem)
    keep.start()
    first = []
    for i, p in enumerate(beside):
        first.append(remote(own, out.at[e, w], w_s.at[i], w_r.at[i], (e, p)))
        first[-1].start()
    keep.wait()
    for copy in first:
        copy.wait()
    second = []
    for i, s in enumerate(across):
        second.append(remote(out.at[e], out.at[e], ep_s.at[i], ep_r.at[i], (s, w)))
        second[-1].start()
    for copy in second:
        copy.wait()


def gather_call(own, n, n_ws):
    return pl.pallas_call(
        functools.partial(gather_kernel, n, n_ws),
        out_shape=jax.ShapeDtypeStruct((n, n_ws) + own.shape, own.dtype),
        in_specs=[VM],
        out_specs=VM,
        scratch_shapes=[DMA, DMA((n_ws - 1,)), DMA((n_ws - 1,)), DMA((n - 1,)), DMA((n - 1,))],
        compiler_params=pltpu.CompilerParams(collective_id=3, has_side_effects=True),
        name="gather_gains",
    )(own)


def reduce_kernel(n, n_ws, parts, out, held, all_parts, load_sem, w_s, w_r, ep_s, ep_r):
    e, w = lax.axis_index("ep"), lax.axis_index("ws")
    beside = [flip(w, k) for k in range(1, n_ws)]
    across = [flip(e, k) for k in far_first(n)]
    greet([(e, p) for p in beside] + [(s, w) for s in across])
    keep = pltpu.make_async_copy(parts.at[:, w], held.at[:, w], load_sem.at[0])
    keep.start()
    first = []
    for i, p in enumerate(beside):
        first.append(remote(parts.at[:, p], held.at[:, w], w_s.at[i], w_r.at[i], (e, p)))
        first[-1].start()
    keep.wait()
    for copy in first:
        copy.wait()
    keep = pltpu.make_async_copy(held.at[e], all_parts.at[e], load_sem.at[1])
    keep.start()
    second = []
    for i, s in enumerate(across):
        second.append(remote(held.at[s], all_parts.at[e], ep_s.at[i], ep_r.at[i], (s, w)))
        second[-1].start()
    keep.wait()
    for copy in second:
        copy.wait()
    out[...] = jnp.sum(jnp.sum(all_parts[...], 0), 0)


def reduce_call(parts):
    n, n_ws = parts.shape[:2]
    return pl.pallas_call(
        functools.partial(reduce_kernel, n, n_ws),
        out_shape=jax.ShapeDtypeStruct(parts.shape[2:], parts.dtype),
        in_specs=[VM],
        out_specs=VM,
        scratch_shapes=[
            pltpu.VMEM(parts.shape, parts.dtype),
            pltpu.VMEM(parts.shape, parts.dtype),
            DMA((2,)),
            DMA((n_ws - 1,)),
            DMA((n_ws - 1,)),
            DMA((n - 1,)),
            DMA((n - 1,)),
        ],
        compiler_params=pltpu.CompilerParams(collective_id=4, has_side_effects=True),
        name="reduce_gains",
    )(parts)


def small(n_ep):
    return n_ep == MIXTURE_EXPERTS and lax.axis_size("ws") == 4


PLAIN = {
    grad_job: lambda a, b: [t_dot(a, b)],
    pair_grad_job: lambda a, b, c: [jnp.stack([t_dot(a, b), t_dot(a, c)], 1)],
    split_job: lambda weight: [weight[:, 0], weight[:, 1]],
    ffn_job: ffn_plain,
    ffn_back_job: ffn_back_plain,
}


def beside(job, plain, arg, fills, collective_id, name):
    if job is None:
        return [plain(arg)] + [out for make, *rest in fills for out in PLAIN[make](*rest)]
    return run_jobs(job(arg), [make(*rest) for make, *rest in fills], collective_id, name)


def exchange_plain(send):
    return lax.all_to_all(send, "ep", split_axis=0, concat_axis=0, tiled=True)


def exchange(send, *fills, collective_id=2, name="exchange"):
    job = exchange_job if small(send.shape[0]) else None
    return beside(job, exchange_plain, send, fills, collective_id, name)


def spread(rows, group):
    width = rows.shape[-1]
    blocks = rows.reshape(MIXTURE_EXPERTS, 1, ROWS, width)
    return jnp.broadcast_to(blocks, (MIXTURE_EXPERTS, group, ROWS, width)).reshape(
        MIXTURE_EXPERTS * group, ROWS, width
    )


def dispatch(rows, group, *fills, collective_id=0, name="dispatch"):
    width = rows.shape[-1]

    def plain(blocks):
        return lax.all_gather(exchange_plain(blocks), "ws", axis=1, tiled=False)

    job = functools.partial(dispatch_job, n_ws=4) if small(MIXTURE_EXPERTS * group) else None
    out = beside(job, plain, spread(rows, group), fills, collective_id, name)
    return [out[0].reshape(-1, width)] + list(out[1:])


def combine(partial, group, n_ep, n_ws, *fills, collective_id=1, name="combine"):
    width = partial.shape[-1]

    def plain(part):
        part = part.transpose(1, 0, 2, 3).reshape(n_ws * n_ep * ROWS, width)
        own = lax.psum_scatter(part, "ws", scatter_dimension=0, tiled=True)
        return exchange_plain(own.reshape(n_ep, ROWS, width))

    part = partial.reshape(n_ep, n_ws, ROWS, width)
    job = combine_job if small(n_ep) else None
    back, *rest = beside(job, plain, part, fills, collective_id, name)
    if group > 1:
        back = jnp.sum(back.reshape(MIXTURE_EXPERTS, group, ROWS, width).astype(f32), 1).astype(bf16)
    return [back.reshape(MIXTURE_EXPERTS * ROWS, width)] + rest


def slot_tables(routes, slots):
    target = jnp.where(slots < CAP, routes * ROWS + slots, -1)
    places = lax.broadcasted_iota(jnp.int32, (MIXTURE_EXPERTS * ROWS, target.shape[0]), 0)
    return [(places == target[None, :, k]).astype(bf16) for k in range(CHOSEN_EXPERTS)]


def norm_back(grad, unit, inverse, gain):
    gain_grad = jnp.sum(grad * unit, 0)
    scaled = grad * gain
    return (inverse * (scaled - unit * jnp.mean(scaled * unit, -1, keepdims=True)), gain_grad)


def heads_of(rows):
    return rows.reshape(rows.shape[0], -1, HEAD_SIZE)


def local(
    x_in,
    gain_attn,
    gain_ffn,
    key_value_weight,
    w_query,
    w_output,
    w_in,
    w_out,
    gate_attn,
    gate_ffn,
    route_attn,
    slot_attn,
    route_ffn,
    slot_ffn,
    cotangent,
):
    n_ep = lax.axis_size("ep")
    n_ws = lax.axis_size("ws")
    group = n_ep // MIXTURE_EXPERTS
    local_tokens, width = x_in.shape
    key_value_width = KEY_VALUE_HEADS * HEAD_SIZE
    part = w_query.shape[2]
    own_width = group * part
    sequence = n_ws * local_tokens
    place = lax.axis_index("ws")
    scale = HEAD_SIZE ** (-0.5)

    short = small(n_ep) and gain_attn.shape[0] == 64
    if short:
        gains = jnp.concatenate([gain_attn, gain_ffn], 0).astype(f32)[None]
        gains = gather_call(gains, n_ep, n_ws).reshape(n_ep * n_ws, 2, -1)
        gain_one, gain_two = gains[:, 0].reshape(-1), gains[:, 1].reshape(-1)
    else:
        gain_one = lax.all_gather(gain_attn, ("ep", "ws"), axis=0, tiled=True).astype(f32)
        gain_two = lax.all_gather(gain_ffn, ("ep", "ws"), axis=0, tiled=True).astype(f32)
    plain = group == 1 and key_value_weight.shape[1] == HEAD_SIZE
    if plain:
        half = n_ep // 2
        there = [
            (e * n_ws + w, (w + n_ws * (e // half)) * n_ws + e % half)
            for e in range(n_ep)
            for w in range(n_ws)
        ]
        mine = lax.ppermute(key_value_weight, ("ep", "ws"), there)
        kv_own = lax.all_gather(mine, "ep", axis=1, tiled=True)
    else:
        whole = lax.all_gather(key_value_weight, ("ep", "ws"), axis=1, tiled=True)
        whole = whole.reshape(width, 2 * group, n_ws, part)
        kv_own = lax.dynamic_index_in_dim(whole, place, 2, keepdims=False).reshape(width, -1)

    inputs = x_in.astype(f32)
    inverse_one = lax.rsqrt(jnp.mean(inputs * inputs, -1, keepdims=True) + EPS)
    unit_one = inputs * inverse_one
    normed = (unit_one * gain_one).astype(bf16)
    attn_pairs = slot_tables(route_attn, slot_attn)
    ffn_pairs = slot_tables(route_ffn, slot_ffn)
    attn_tokens = attn_pairs[0] + attn_pairs[1]
    ffn_tokens = ffn_pairs[0] + ffn_pairs[1]

    normed_sequence = lax.all_gather(normed, "ws", axis=0, tiled=True)
    rows_one, gate_weight, up_weight = dispatch(
        dot(attn_tokens, normed).astype(bf16),
        group,
        (split_job, w_in[0]),
        collective_id=10,
        name="dispatch_split",
    )
    kv = dot(normed_sequence, kv_own).astype(bf16)
    keys = kv[:, :own_width].reshape(sequence, -1, HEAD_SIZE)
    values = kv[:, own_width:].reshape(sequence, -1, HEAD_SIZE)

    owner_query = dot(rows_one, w_query[0]).astype(bf16)
    queries = exchange(owner_query.reshape(n_ep, n_ws * ROWS, part))[0]
    spans = [(w * local_tokens // BLOCK + 1) * BLOCK for w in range(n_ws)]
    fused = small(n_ep)
    queries = queries.reshape(MIXTURE_EXPERTS, group, n_ws, ROWS, part)

    def by_block(rows):
        rows = rows.reshape(MIXTURE_EXPERTS, group, n_ws, ROWS, part)
        return [
            rows[:, :, w].transpose(0, 2, 1, 3).reshape(-1, own_width // HEAD_SIZE, HEAD_SIZE)
            for w in range(n_ws)
        ]

    def to_experts(pieces):
        rows = jnp.stack(
            [
                piece.reshape(MIXTURE_EXPERTS, ROWS, group, part).transpose(0, 2, 1, 3)
                for piece in pieces
            ],
            2,
        )
        return rows.reshape(n_ep, n_ws * ROWS, part)

    if fused:
        queries = queries.reshape(n_ep, n_ws, ROWS, part)
        mixed = attend_call(queries, kv, spans).reshape(n_ep, n_ws * ROWS, part)
    else:
        kept = []
        mixed_pieces = []
        for q, span in zip(by_block(queries), spans):
            scores = (
                jnp.einsum("rhd,shd->hrs", q, keys[:span], preferred_element_type=f32) * scale
            )
            probs = jax.nn.softmax(scores, axis=-1)
            mixed = jnp.einsum(
                "hrs,shd->rhd", probs.astype(bf16), values[:span], preferred_element_type=f32
            )
            kept.append((q, probs))
            mixed_pieces.append(mixed.astype(bf16))
        mixed = to_experts(mixed_pieces)
    owner_mixed = exchange(mixed)[0].reshape(-1, part)
    attn_slots = combine(dot(owner_mixed, w_output[0]).astype(bf16), group, n_ep, n_ws, collective_id=11)[0]

    def weighted(pairs, gates, slot_values):
        return sum(gates[:, k : k + 1] * t_dot(pairs[k], slot_values) for k in range(2))

    def to_slots(pairs, gates, values):
        return sum(
            dot(pairs[k], (gates[:, k : k + 1] * values).astype(bf16)) for k in range(2)
        ).astype(bf16)

    hidden_state = inputs + weighted(attn_pairs, gate_attn, attn_slots)
    inverse_two = lax.rsqrt(jnp.mean(hidden_state * hidden_state, -1, keepdims=True) + EPS)
    unit_two = hidden_state * inverse_two
    normed_two = (unit_two * gain_two).astype(bf16)

    grad_out = cotangent.astype(f32)
    grad_slots = to_slots(ffn_pairs, gate_ffn, grad_out)
    expert_rows = dispatch(dot(ffn_tokens, normed_two).astype(bf16), group)[0]
    expert_grad, gate_pre, up_pre, activated, forward_part = dispatch(
        grad_slots,
        group,
        (ffn_job, expert_rows, gate_weight, up_weight, w_out[0]),
        collective_id=5,
        name="dispatch_ffn",
    )
    ffn_slots, grad_gate, grad_up, back_two = combine(
        forward_part,
        group,
        n_ep,
        n_ws,
        (ffn_back_job, expert_grad, gate_pre, up_pre, gate_weight, up_weight, w_out[0]),
        collective_id=1,
        name="combine_ffn_back",
    )
    result = hidden_state + weighted(ffn_pairs, gate_ffn, ffn_slots)
    back_slots, grad_second = combine(
        back_two,
        group,
        n_ep,
        n_ws,
        (grad_job, activated, expert_grad),
        collective_id=6,
        name="combine_grad_out",
    )

    grad_normed_two = t_dot(ffn_tokens, back_slots)
    grad_hidden_norm, grad_gain_two = norm_back(grad_normed_two, unit_two, inverse_two, gain_two)
    grad_hidden = grad_out + grad_hidden_norm
    owner_grad, grad_first = dispatch(
        to_slots(attn_pairs, gate_attn, grad_hidden),
        group,
        (pair_grad_job, expert_rows, grad_gate, grad_up),
        collective_id=7,
        name="dispatch_grad_in",
    )
    back_mixed = dot_t(owner_grad, w_output[0]).astype(bf16)
    mixed_grads, grad_output = exchange(
        back_mixed.reshape(n_ep, n_ws * ROWS, part),
        (grad_job, owner_mixed, owner_grad),
        collective_id=8,
        name="exchange_grad_output",
    )

    if fused:
        mixed_grads = mixed_grads.reshape(n_ep, n_ws, ROWS, part)
        query_grads, grad_kv_rows = attend_back_call(queries, mixed_grads, kv, spans)
        query_grads = query_grads.reshape(n_ep, n_ws * ROWS, part)
    else:
        grad_keys, grad_values, query_pieces = 0.0, 0.0, []
        for (q, probs), grad, span in zip(kept, by_block(mixed_grads), spans):
            grad_probs = jnp.einsum("rhd,shd->hrs", grad, values[:span], preferred_element_type=f32)
            centred = jnp.sum(probs * grad_probs, -1, keepdims=True)
            grad_scores = (probs * (grad_probs - centred)).astype(bf16)
            grad_q = (
                jnp.einsum("hrs,shd->rhd", grad_scores, keys[:span], preferred_element_type=f32)
                * scale
            )
            query_pieces.append(grad_q.astype(bf16))
            pad = ((0, sequence - span), (0, 0), (0, 0))
            piece = jnp.einsum("hrs,rhd->shd", grad_scores, q, preferred_element_type=f32) * scale
            grad_keys = grad_keys + jnp.pad(piece, pad)
            piece = jnp.einsum(
                "hrs,rhd->shd", probs.astype(bf16), grad, preferred_element_type=f32
            )
            grad_values = grad_values + jnp.pad(piece, pad)
        grad_kv_rows = jnp.concatenate(
            [grad_keys.reshape(sequence, -1), grad_values.reshape(sequence, -1)], 1
        ).astype(bf16)
        query_grads = to_experts(query_pieces)
    owner_grad_query = exchange(query_grads)[0].reshape(-1, part)
    back_normed = dot_t(owner_grad_query, w_query[0]).astype(bf16)
    normed_back, grad_query = combine(
        back_normed,
        group,
        n_ep,
        n_ws,
        (grad_job, rows_one, owner_grad_query),
        collective_id=9,
        name="combine_grad_query",
    )

    grad_kv = t_dot(normed_sequence, grad_kv_rows)
    if plain:
        pieces = grad_kv.reshape(width, n_ep, HEAD_SIZE).transpose(1, 0, 2).astype(bf16)
        piece = lax.psum_scatter(pieces, "ep", scatter_dimension=0, tiled=False)
        grad_kv_shard = lax.ppermute(piece, ("ep", "ws"), [(b, a) for a, b in there]).astype(f32)
    else:
        mask = (jnp.arange(n_ws) == place)[None, None, :, None]
        pieces = jnp.where(mask, grad_kv.reshape(width, 2 * group, 1, part), 0.0)
        pieces = pieces.reshape(width, 2 * key_value_width).astype(bf16)
        grad_kv_shard = lax.psum_scatter(
            pieces, ("ep", "ws"), scatter_dimension=1, tiled=True
        ).astype(f32)
    from_kv = lax.psum_scatter(
        dot_t(grad_kv_rows, kv_own).astype(bf16), "ws", scatter_dimension=0, tiled=True
    )
    grad_normed = t_dot(attn_tokens, normed_back) + from_kv.astype(f32)
    grad_input_norm, grad_gain_one = norm_back(grad_normed, unit_one, inverse_one, gain_one)
    grad_input = grad_hidden + grad_input_norm
    gain_grads = jnp.stack([grad_gain_one, grad_gain_two], 0)
    if short:
        parts = gain_grads.reshape(2, n_ep, n_ws, -1).transpose(1, 2, 0, 3)
        gain_shards = reduce_call(parts.reshape(n_ep, n_ws, 1, -1)).reshape(2, -1)
    else:
        gain_shards = lax.psum_scatter(
            gain_grads, ("ep", "ws"), scatter_dimension=1, tiled=True
        )
    return (
        result.astype(bf16),
        grad_input,
        gain_shards[0],
        gain_shards[1],
        grad_kv_shard,
        grad_query[None],
        grad_output[None],
        grad_first[None],
        grad_second[None],
    )


def solution(mesh):
    both = ("ep", "ws")
    rows, vector, columns = P(both, None), P(both), P(None, both)
    return jax.shard_map(
        local,
        mesh=mesh,
        in_specs=(
            rows,
            vector,
            vector,
            columns,
            P("ep", None, "ws"),
            P("ep", "ws", None),
            P("ep", None, None, "ws"),
            P("ep", "ws", None),
            rows,
            rows,
            rows,
            rows,
            rows,
            rows,
            rows,
        ),
        out_specs=(
            rows,
            rows,
            vector,
            vector,
            columns,
            P("ep", None, "ws"),
            P("ep", "ws", None),
            P("ep", None, None, "ws"),
            P("ep", "ws", None),
        ),
        check_vma=False,
    )
```

```python
import functools

import jax
import jax.numpy as jnp
from jax import lax
from jax.experimental import pallas as pl
from jax.experimental.pallas import tpu as pltpu
from jax.sharding import PartitionSpec as P

KEY_VALUE_HEADS = 16
HEAD_SIZE = 128
MIXTURE_EXPERTS = 8
CHOSEN_EXPERTS = 2
BLOCK = 256
CAP = 36
ROWS = 40

EPS = 1e-06
very_negative = -1e30
f32 = jnp.float32
bf16 = jnp.bfloat16
MESH = pl.DeviceIdType.MESH
ANY = pl.BlockSpec(memory_space=pl.ANY)
VM = pl.BlockSpec(memory_space=pltpu.VMEM)
DMA = pltpu.SemaphoreType.DMA
STEP = 256
VMEM_LIMIT = 60 << 20


def dot(a, b):
    return jnp.dot(a, b, preferred_element_type=f32)


def dot_t(a, b):
    return lax.dot_general(a, b, (((1,), (1,)), ((), ())), preferred_element_type=f32)


def t_dot(a, b):
    return lax.dot_general(a, b, (((0,), (0,)), ((), ())), preferred_element_type=f32)


def flip(index, bits):
    out, bit = index, 1
    while bit <= bits:
        if bits & bit:
            out = out + bit - 2 * bit * ((index // bit) % 2)
        bit *= 2
    return out


def far_first(n):
    return sorted(range(1, n), key=lambda k: (-((k // 2).bit_length()), k))


def greet(partners):
    barrier = pltpu.get_barrier_semaphore()
    for partner in partners:
        pl.semaphore_signal(barrier, inc=1, device_id=partner, device_id_type=MESH)
    pl.semaphore_wait(barrier, len(partners))


def remote(src, dst, send, recv, device):
    return pltpu.make_async_remote_copy(
        src_ref=src, dst_ref=dst, send_sem=send, recv_sem=recv, device_id=device, device_id_type=MESH
    )


class Job:
    def __init__(self, args, outs, scratch, steps, body, partners=()):
        self.args, self.outs, self.scratch, self.steps, self.body = args, outs, scratch, steps, body
        self.partners = partners


def run_jobs(jobs, fills, collective_id, name):
    whole = jobs + fills
    args = [a for job in whole for a in job.args]
    outs = [o for job in whole for o in job.outs]
    scratch = [x for job in whole for x in job.scratch]
    turns = sorted((k / job.steps, i) for i, job in enumerate(jobs) for k in range(job.steps))
    partners = sorted({p for job in jobs for p in job.partners})

    def kernel(*refs):
        bodies, at = [], [0, len(args), len(args) + len(outs)]
        for job in whole:
            own = []
            for k, part in enumerate((job.args, job.outs, job.scratch)):
                own.append(refs[at[k] : at[k] + len(part)])
                at[k] += len(part)
            bodies.append(job.body(*own[0], *own[1], *own[2]))
        moves, work = bodies[: len(jobs)], bodies[len(jobs) :]
        queue = [g for g, job in zip(work, fills) for _ in range(job.steps)]
        for g in work:
            next(g)
        e, w = lax.axis_index("ep"), lax.axis_index("ws")
        greet([(flip(e, p), flip(w, q)) for p, q in partners])
        done = 0
        for k, (_, i) in enumerate(turns):
            next(moves[i])
            target = (k + 1) * len(queue) // len(turns)
            while done < target:
                next(queue[done])
                done += 1
        for g in moves + work:
            for _ in g:
                pass

    return pl.pallas_call(
        kernel,
        out_shape=outs,
        in_specs=[ANY] * len(args),
        out_specs=[ANY] * len(outs),
        scratch_shapes=scratch,
        compiler_params=pltpu.CompilerParams(
            collective_id=collective_id, has_side_effects=True, vmem_limit_bytes=VMEM_LIMIT
        ),
        name=name,
    )(*args)


def fetch(pairs, sem):
    copies = [
        pltpu.make_async_copy(src, dst, sem.at[i]) for i, (src, dst) in enumerate(pairs)
    ]
    for copy in copies:
        copy.start()
    return copies


def blocks_of(size):
    return [(start, min(STEP, size - start)) for start in range(0, size, STEP)]


def column_tiles(width, tile):
    def body(c, carry):
        tile(pl.multiple_of(c * STEP, STEP), STEP)
        return carry

    lax.fori_loop(0, width // STEP, body, 0)
    if width % STEP:
        tile(width // STEP * STEP, width % STEP)


def grad_job(a, b):
    depth, rows = a.shape
    width = b.shape[1]

    def body(a_hbm, b_hbm, out, a_ref, b_ref, turned, held, load_sem, sem):
        loads = fetch(((a_hbm, a_ref), (b_hbm, b_ref)), load_sem)
        yield
        for load in loads:
            load.wait()
        copies = []
        for i, (start, size) in enumerate(blocks_of(rows)):
            if i >= 2:
                copies[i - 2].wait()
            turned[:size] = a_ref[:, start : start + size].T

            def tile(at, columns, slot=i % 2, size=size):
                held[slot, :size, pl.ds(at, columns)] = jnp.dot(
                    turned[:size], b_ref[:, pl.ds(at, columns)], preferred_element_type=f32
                )

            column_tiles(width, tile)
            copies.append(
                pltpu.make_async_copy(
                    held.at[i % 2, pl.ds(0, size)], out.at[pl.ds(start, size)], sem.at[i % 2]
                )
            )
            copies[i].start()
            yield
        for copy in copies[-2:]:
            copy.wait()

    return Job(
        [a, b],
        [jax.ShapeDtypeStruct((rows, width), f32)],
        [
            pltpu.VMEM(a.shape, bf16),
            pltpu.VMEM(b.shape, bf16),
            pltpu.VMEM((STEP, depth), bf16),
            pltpu.VMEM((2, STEP, width), f32),
            DMA((2,)),
            DMA((2,)),
        ],
        len(blocks_of(rows)),
        body,
    )


def pair_grad_job(a, first, second):
    depth, rows = a.shape
    tiles = first.shape[1] // 128

    def body(a_hbm, f_hbm, s_hbm, out, a_ref, f_ref, s_ref, turned, held, load_sem, sem):
        loads = fetch(((a_hbm, a_ref), (f_hbm, f_ref), (s_hbm, s_ref)), load_sem)
        flat = held.reshape(2 * tiles * STEP * 2, 128)
        yield
        for load in loads:
            load.wait()
        copies = []
        for i, (start, size) in enumerate(blocks_of(rows)):
            if i >= 2:
                for copy in copies[i - 2]:
                    copy.wait()
            turned[:size] = a_ref[:, start : start + size].T

            def tile(at, columns, slot=i % 2, size=size):
                for j, b_ref in enumerate((f_ref, s_ref)):
                    r = jnp.dot(
                        turned[:size], b_ref[:, pl.ds(at, columns)], preferred_element_type=f32
                    )
                    for half in range(columns // 128):
                        base = (slot * tiles + at // 128 + half) * (2 * STEP) + j
                        flat[pl.ds(base, size, stride=2), :] = r[:, half * 128 : half * 128 + 128]

            column_tiles(tiles * 128, tile)
            copies.append(
                [
                    pltpu.make_async_copy(
                        held.at[i % 2, c, pl.ds(0, size)],
                        out.at[pl.ds(start, size), :, pl.ds(c * 128, 128)],
                        sem.at[i % 2, c],
                    )
                    for c in range(tiles)
                ]
            )
            for copy in copies[i]:
                copy.start()
            yield
        for copy in copies[-2] + copies[-1]:
            copy.wait()

    return Job(
        [a, first, second],
        [jax.ShapeDtypeStruct((rows, 2, tiles * 128), f32)],
        [
            pltpu.VMEM(a.shape, bf16),
            pltpu.VMEM(first.shape, bf16),
            pltpu.VMEM(second.shape, bf16),
            pltpu.VMEM((STEP, depth), bf16),
            pltpu.VMEM((2, tiles, STEP, 2, 128), f32),
            DMA((3,)),
            DMA((2, tiles)),
        ],
        len(blocks_of(rows)),
        body,
    )


def split_job(weight):
    rows, _, width = weight.shape

    def body(w_hbm, first, second, block, wide, held, load_sem, sem):
        flat = wide.reshape(2 * STEP, 128)
        steps = rows // STEP

        def load(i):
            return pltpu.make_async_copy(
                w_hbm.at[pl.ds(i * STEP, STEP)], block.at[i % 2], load_sem.at[i % 2]
            )

        load(0).start()
        yield
        copies = []
        for i in range(steps):
            slot = i % 2
            if i + 1 < steps:
                load(i + 1).start()
            load(i).wait()
            if i >= 2:
                for copy in copies[i - 2]:
                    copy.wait()

            def tile(c, carry, slot=slot):
                at = pl.ds(pl.multiple_of(c * 128, 128), 128)
                wide[...] = block[slot, :, :, at].astype(f32)
                for j in range(2):
                    held[slot, j, :, at] = flat[pl.ds(j, STEP, stride=2), :].astype(bf16)
                return carry

            lax.fori_loop(0, width // 128, tile, 0)
            copies.append(
                [
                    pltpu.make_async_copy(
                        held.at[slot, j], out.at[pl.ds(i * STEP, STEP)], sem.at[slot, j]
                    )
                    for j, out in enumerate((first, second))
                ]
            )
            for copy in copies[i]:
                copy.start()
            yield
        for copy in copies[-2] + copies[-1]:
            copy.wait()

    return Job(
        [weight],
        [jax.ShapeDtypeStruct((rows, width), bf16)] * 2,
        [
            pltpu.VMEM((2, STEP, 2, width), bf16),
            pltpu.VMEM((STEP, 2, 128), f32),
            pltpu.VMEM((2, 2, STEP, width), bf16),
            DMA((2,)),
            DMA((2, 2)),
        ],
        rows // STEP,
        body,
    )


def ffn_job(x, gate_weight, up_weight, down_weight):
    rows, width = x.shape
    hidden = gate_weight.shape[1]

    def body(
        x_hbm, g_hbm, u_hbm, d_hbm, gate_out, up_out, act_out, out, x_ref, g_ref, u_ref, d_ref, pre, act, res,
        load_sem, sem
    ):
        loads = fetch(((x_hbm, x_ref), (g_hbm, g_ref), (u_hbm, u_ref), (d_hbm, d_ref)), load_sem)
        yield
        for load in loads:
            load.wait()
        copies = []
        for i, (start, size) in enumerate(blocks_of(rows)):
            slot = i % 2
            here = pl.ds(start, size)
            if i >= 2:
                for copy in copies[i - 2]:
                    copy.wait()

            def tile(at, columns, slot=slot, start=start, size=size):
                part = pl.ds(at, columns)
                left = x_ref[start : start + size]
                gate = dot(left, g_ref[:, part])
                up = dot(left, u_ref[:, part])
                pre[slot, 0, :, part] = gate
                pre[slot, 1, :, part] = up
                act[slot, :, part] = (gate * jax.nn.sigmoid(gate) * up).astype(bf16)

            column_tiles(hidden, tile)
            yield

            def last(at, columns, slot=slot):
                part = pl.ds(at, columns)
                res[slot, :, part] = dot(act[slot], d_ref[:, part]).astype(bf16)

            column_tiles(width, last)
            copies.append(
                [
                    pltpu.make_async_copy(src.at[slot], dst.at[here], sem.at[slot, k])
                    for k, (src, dst) in enumerate(((act, act_out), (res, out)))
                ]
                + [
                    pltpu.make_async_copy(pre.at[slot, k], dst.at[here], sem.at[slot, 2 + k])
                    for k, dst in enumerate((gate_out, up_out))
                ]
            )
            for copy in copies[i]:
                copy.start()
            yield
        for copy in copies[-2] + copies[-1]:
            copy.wait()

    return Job(
        [x, gate_weight, up_weight, down_weight],
        [jax.ShapeDtypeStruct((rows, hidden), f32)] * 2
        + [jax.ShapeDtypeStruct((rows, hidden), bf16), jax.ShapeDtypeStruct((rows, width), bf16)],
        [
            pltpu.VMEM(x.shape, bf16),
            pltpu.VMEM(gate_weight.shape, bf16),
            pltpu.VMEM(up_weight.shape, bf16),
            pltpu.VMEM(down_weight.shape, bf16),
            pltpu.VMEM((2, 2, STEP, hidden), f32),
            pltpu.VMEM((2, STEP, hidden), bf16),
            pltpu.VMEM((2, STEP, width), bf16),
            DMA((4,)),
            DMA((2, 4)),
        ],
        2 * (rows // STEP),
        body,
    )


def ffn_plain(x, gate_weight, up_weight, down_weight):
    gate_pre, up_pre = dot(x, gate_weight), dot(x, up_weight)
    activated = (gate_pre * jax.nn.sigmoid(gate_pre) * up_pre).astype(bf16)
    return gate_pre, up_pre, activated, dot(activated, down_weight).astype(bf16)


def before_activation(grad_act, gate_pre, up_pre):
    sigmoid_gate = jax.nn.sigmoid(gate_pre)
    grad_up = (grad_act * gate_pre * sigmoid_gate).astype(bf16)
    grad_gate = (
        grad_act * up_pre * sigmoid_gate * (1.0 + gate_pre * (1.0 - sigmoid_gate))
    ).astype(bf16)
    return grad_gate, grad_up


def ffn_back_job(grad, gate_pre, up_pre, gate_weight, up_weight, down_weight):
    rows, width = grad.shape
    hidden = gate_weight.shape[1]

    def body(
        x_hbm, gp_hbm, up_hbm, g_hbm, u_hbm, d_hbm, gate_out, up_out, out, x_ref, g_ref, u_ref, d_ref, pre, hid,
        res, load_sem, pre_sem, sem
    ):
        loads = fetch(((x_hbm, x_ref), (g_hbm, g_ref), (u_hbm, u_ref), (d_hbm, d_ref)), load_sem)

        def load_pre(i):
            here = pl.ds(i * STEP, STEP)
            return [
                pltpu.make_async_copy(src.at[here], pre.at[i % 2, k], pre_sem.at[i % 2, k])
                for k, src in enumerate((gp_hbm, up_hbm))
            ]

        for copy in load_pre(0):
            copy.start()
        yield
        for load in loads:
            load.wait()
        copies = []
        steps = rows // STEP
        for i in range(steps):
            slot, start = i % 2, i * STEP
            here = pl.ds(start, STEP)
            if i + 1 < steps:
                for copy in load_pre(i + 1):
                    copy.start()
            for copy in load_pre(i):
                copy.wait()
            if i >= 2:
                for copy in copies[i - 2]:
                    copy.wait()

            def tile(at, columns, slot=slot, start=start):
                part = pl.ds(at, columns)
                grad_act = dot_t(x_ref[start : start + STEP], d_ref[part, :])
                pair = before_activation(grad_act, pre[slot, 0, :, part], pre[slot, 1, :, part])
                hid[slot, 0, :, part], hid[slot, 1, :, part] = pair

            column_tiles(hidden, tile)
            yield

            def last(at, columns, slot=slot):
                part = pl.ds(at, columns)
                total = dot_t(hid[slot, 0], g_ref[part, :]) + dot_t(hid[slot, 1], u_ref[part, :])
                res[slot, :, part] = total.astype(bf16)

            column_tiles(width, last)
            copies.append(
                [pltpu.make_async_copy(res.at[slot], out.at[here], sem.at[slot, 2])]
                + [
                    pltpu.make_async_copy(hid.at[slot, k], dst.at[here], sem.at[slot, k])
                    for k, dst in enumerate((gate_out, up_out))
                ]
            )
            for copy in copies[i]:
                copy.start()
            yield
        for copy in copies[-2] + copies[-1]:
            copy.wait()

    return Job(
        [grad, gate_pre, up_pre, gate_weight, up_weight, down_weight],
        [jax.ShapeDtypeStruct((rows, hidden), bf16)] * 2 + [jax.ShapeDtypeStruct((rows, width), bf16)],
        [
            pltpu.VMEM(grad.shape, bf16),
            pltpu.VMEM(gate_weight.shape, bf16),
            pltpu.VMEM(up_weight.shape, bf16),
            pltpu.VMEM(down_weight.shape, bf16),
            pltpu.VMEM((2, 2, STEP, hidden), f32),
            pltpu.VMEM((2, 2, STEP, hidden), bf16),
            pltpu.VMEM((2, STEP, width), bf16),
            DMA((4,)),
            DMA((2, 2)),
            DMA((2, 3)),
        ],
        2 * (rows // STEP),
        body,
    )


def ffn_back_plain(grad, gate_pre, up_pre, gate_weight, up_weight, down_weight):
    grad_gate, grad_up = before_activation(dot_t(grad, down_weight), gate_pre, up_pre)
    back = dot_t(grad_gate, gate_weight) + dot_t(grad_up, up_weight)
    return grad_gate, grad_up, back.astype(bf16)


def dispatch_job(rows, n_ws):
    n, count, width = rows.shape

    def body(rows, out, own, load_sem, ep_s, ep_r, y_s, y_r, c_s, c_r, x_s, x_r):
        e, w = lax.axis_index("ep"), lax.axis_index("ws")
        twin, other = flip(w, 1), flip(w, 2)
        sources = [e] + [flip(e, k) for k in range(1, n)]
        first = []
        for i, s in enumerate(sources[1:]):
            first.append(remote(rows.at[s], out.at[e, w], ep_s.at[i], ep_r.at[i], (s, w)))
            first[-1].start()
        load = pltpu.make_async_copy(rows.at[e], own, load_sem.at[0])
        load.start()
        over_y, to_twin, relayed = [], [], []

        def relay(j):
            over_y[j].wait_recv()
            block = out.at[sources[j], other]
            relayed.append(remote(block, block, x_s.at[j], x_r.at[j], (e, twin)))
            relayed[-1].start()

        for j, s in enumerate(sources):
            place = out.at[s, w]
            block = rows.at[e] if j == 0 else place
            if j:
                first[j - 1].wait_recv()
            over_y.append(remote(block, place, y_s.at[j], y_r.at[j], (e, other)))
            over_y[-1].start()
            to_twin.append(remote(block, place, c_s.at[j], c_r.at[j], (e, twin)))
            to_twin[-1].start()
            if j == 0:
                load.wait()
                store = pltpu.make_async_copy(own, out.at[e, w], load_sem.at[1])
                store.start()
            else:
                relay(j - 1)
            yield
        relay(n - 1)
        store.wait()
        for copy in first + over_y:
            copy.wait_send()
        for copy in to_twin + relayed:
            copy.wait()

    return Job(
        [rows],
        [jax.ShapeDtypeStruct((n, n_ws, count, width), rows.dtype)],
        [pltpu.VMEM((count, width), rows.dtype), DMA((2,)), DMA((n - 1,)), DMA((n - 1,))]
        + [DMA((n,)) for _ in range(6)],
        n,
        body,
        [(k, 0) for k in range(1, n)] + [(0, 1), (0, 2)],
    )


def combine_job(part):
    n, _, count, width = part.shape
    block = (n, count, width)

    def body(
        part, out, mine, core, sum_y, from_y, total, load_sem, c_s, c_r, y_s, y_r, ep_s, ep_r, own_sem
    ):
        e, w = lax.axis_index("ep"), lax.axis_index("ws")
        twin, other, last = flip(w, 1), flip(w, 2), flip(w, 3)
        targets = [flip(e, k) for k in far_first(n)] + [e]
        loads, cores = {}, {}
        for half, near, far in ((1, other, last), (0, w, twin)):
            for j, s in enumerate(targets):
                cores[half, j] = remote(
                    part.at[s, far], core.at[half, j], c_s.at[half, j], c_r.at[half, j], (e, twin)
                )
                cores[half, j].start()
                loads[half, j] = pltpu.make_async_copy(
                    part.at[s, near], mine.at[half, j], load_sem.at[half, j]
                )
                loads[half, j].start()
        over_y, back = [], []

        def send_y(j):
            over_y.append(remote(sum_y.at[j], from_y.at[j], y_s.at[j], y_r.at[j], (e, other)))
            over_y[-1].start()

        def send_back(j):
            back.append(remote(total.at[j], out.at[e], ep_s.at[j], ep_r.at[j], (targets[j], w)))
            back[-1].start()

        for j in range(n):
            loads[1, j].wait()
            cores[1, j].wait_recv()
            sum_y[j] = (mine[1, j].astype(f32) + core[1, j].astype(f32)).astype(bf16)
            if j:
                send_y(j - 1)
        loads[0, 0].wait()
        cores[0, 0].wait_recv()
        send_y(n - 1)
        for j in range(n):
            if j:
                loads[0, j].wait()
                cores[0, j].wait_recv()
            over_y[j].wait_recv()
            total[j] = (
                mine[0, j].astype(f32) + core[0, j].astype(f32) + from_y[j].astype(f32)
            ).astype(bf16)
            if j:
                send_back(j - 1)
            yield
        for copy in over_y + list(cores.values()):
            copy.wait_send()
        keep = pltpu.make_async_copy(total.at[n - 1], out.at[e], own_sem)
        keep.start()
        for copy in back:
            copy.wait()
        keep.wait()

    return Job(
        [part],
        [jax.ShapeDtypeStruct(block, part.dtype)],
        [
            pltpu.VMEM((2,) + block, part.dtype),
            pltpu.VMEM((2,) + block, part.dtype),
            pltpu.VMEM(block, part.dtype),
            pltpu.VMEM(block, part.dtype),
            pltpu.VMEM(block, part.dtype),
            DMA((2, n)),
            DMA((2, n)),
            DMA((2, n)),
            DMA((n,)),
            DMA((n,)),
            DMA((n - 1,)),
            DMA((n - 1,)),
            DMA,
        ],
        n,
        body,
        [(k, 0) for k in range(1, n)] + [(0, 1), (0, 2)],
    )


def exchange_job(rows):
    n = rows.shape[0]

    def body(rows, out, own, load_sem, ep_s, ep_r):
        e, w = lax.axis_index("ep"), lax.axis_index("ws")
        targets = [flip(e, k) for k in far_first(n)]
        copies = []
        for i, s in enumerate(targets):
            copies.append(remote(rows.at[s], out.at[e], ep_s.at[i], ep_r.at[i], (s, w)))
            copies[-1].start()
        load = pltpu.make_async_copy(rows.at[e], own, load_sem.at[0])
        load.start()
        load.wait()
        store = pltpu.make_async_copy(own, out.at[e], load_sem.at[1])
        store.start()
        yield
        store.wait()
        for copy in copies:
            copy.wait()

    return Job(
        [rows],
        [jax.ShapeDtypeStruct(rows.shape, rows.dtype)],
        [pltpu.VMEM(rows.shape[1:], rows.dtype), DMA((2,)), DMA((n - 1,)), DMA((n - 1,))],
        1,
        body,
        [(k, 0) for k in range(1, n)],
    )


def gather_weights_job(mine, normed, n, n_ws):
    rows, block = mine.shape
    routes = [(4, 0), (1, 0), (2, 0), (2, 4), (1, 4), (1, 2), (1, 6)]

    def body(mine, normed, out, seq, held, held_rows, load_sem, s_sem, r_sem, w_s, w_r):
        e, w = lax.axis_index("ep"), lax.axis_index("ws")
        twin, other = flip(w, 1), flip(w, 2)
        copies = {}

        def send(hop, offset, half):
            k = routes.index((hop, offset))
            s = flip(e, offset)
            part = pl.ds(half * (rows // 2), rows // 2)
            place = out.at[part, pl.ds(pl.multiple_of(s * block, block), block)]
            copies[hop, offset, half] = remote(
                place if offset else mine.at[part],
                place,
                s_sem.at[k, half],
                r_sem.at[k, half],
                (flip(e, hop), w),
            )
            copies[hop, offset, half].start()

        for half in range(2):
            for route in routes[:3]:
                send(*route, half)
        over_y = remote(normed, seq.at[w], w_s.at[0], w_r.at[0], (e, other))
        over_y.start()
        to_twin = remote(normed, seq.at[w], w_s.at[1], w_r.at[1], (e, twin))
        to_twin.start()
        loads = fetch(((mine, held), (normed, held_rows)), load_sem)
        for load in loads:
            load.wait()
        own = out.at[:, pl.ds(pl.multiple_of(e * block, block), block)]
        stores = fetch(((held, own), (held_rows, seq.at[w])), load_sem)
        yield
        over_y.wait_recv()
        relay = remote(seq.at[other], seq.at[other], w_s.at[2], w_r.at[2], (e, twin))
        relay.start()
        for arrival, onward in (
            ((4, 0), ((2, 4), (1, 4))),
            ((2, 0), ((1, 2),)),
            ((2, 4), ((1, 6),)),
        ):
            for half in range(2):
                copies[(*arrival, half)].wait_recv()
                for route in onward:
                    send(*route, half)
                yield
        for store in stores:
            store.wait()
        for (hop, offset, _), copy in copies.items():
            copy.wait_send()
            if hop == 1:
                copy.wait_recv()
        over_y.wait_send()
        to_twin.wait()
        relay.wait()

    return Job(
        [mine, normed],
        [
            jax.ShapeDtypeStruct((rows, n * block), bf16),
            jax.ShapeDtypeStruct((n_ws,) + normed.shape, bf16),
        ],
        [
            pltpu.VMEM(mine.shape, bf16),
            pltpu.VMEM(normed.shape, bf16),
            DMA((2,)),
            DMA((7, 2)),
            DMA((7, 2)),
            DMA((3,)),
            DMA((3,)),
        ],
        7,
        body,
        [(1, 0), (2, 0), (4, 0), (0, 1), (0, 2)],
    )


def add_blocks(out, *refs):
    step = 64 if out.shape[1] > 1024 else 256

    def body(i, carry):
        at = pl.ds(pl.multiple_of(i * step, step), step)
        total = refs[0][at].astype(f32)
        for ref in refs[1:]:
            total = total + ref[at].astype(f32)
        out[at] = total.astype(bf16)
        return carry

    lax.fori_loop(0, out.shape[0] // step, body, 0)


def reduce_weights_job(pieces, part, n):
    rows = pieces.shape[0]
    block = pieces.shape[1] // n
    offsets = (6, 4, 2, 0)

    def body(
        pieces, part, out, out_rows, mine, from_x, sums, from_z, last_z, fourth, total, own, core, sum_y, from_y,
        total_rows, load_sem, x_s, x_r, z_s, z_r, w_load, w_s, w_r, sem
    ):
        e, w = lax.axis_index("ep"), lax.axis_index("ws")
        twin, other, last = flip(w, 1), flip(w, 2), flip(w, 3)

        def columns(s):
            return pieces.at[:, pl.ds(pl.multiple_of(s * block, block), block)]

        across = []
        for i, offset in enumerate(offsets):
            across.append(
                remote(columns(flip(e, offset + 1)), from_x.at[i], x_s.at[i], x_r.at[i], (flip(e, 1), w))
            )
            across[i].start()
        cores = [
            remote(part.at[to], core.at[k], w_s.at[k], w_r.at[k], (e, twin))
            for k, to in enumerate((last, twin))
        ]
        for copy in cores:
            copy.start()
        loads = fetch([(columns(flip(e, o)), mine.at[i]) for i, o in enumerate(offsets)], load_sem)
        own_loads = fetch(((part.at[other], own.at[0]), (part.at[w], own.at[1])), w_load)
        yield

        def add(i):
            loads[i].wait()
            across[i].wait_recv()
            add_blocks(sums.at[i], mine.at[i], from_x.at[i])

        own_loads[0].wait()
        cores[0].wait_recv()
        add_blocks(sum_y, own.at[0], core.at[0])
        add(0)
        over_y = remote(sum_y, from_y, w_s.at[2], w_r.at[2], (e, other))
        over_y.start()
        yield
        add(1)
        first = remote(sums.at[0], from_z.at[0], z_s.at[0], z_r.at[0], (flip(e, 2), w))
        first.start()
        yield
        add(2)
        first.wait_recv()
        add_blocks(fourth, sums.at[1], from_z.at[0])
        second = remote(sums.at[2], from_z.at[1], z_s.at[1], z_r.at[1], (flip(e, 2), w))
        second.start()
        yield
        add(3)
        third = remote(fourth, last_z, z_s.at[2], z_r.at[2], (flip(e, 4), w))
        third.start()
        yield
        own_loads[1].wait()
        cores[1].wait_recv()
        over_y.wait_recv()
        add_blocks(total_rows, own.at[1], core.at[1], from_y)
        second.wait_recv()
        third.wait_recv()
        add_blocks(total, sums.at[3], from_z.at[1], last_z)
        stores = fetch(((total_rows, out_rows), (total, out)), sem)
        for copy in across + cores + [over_y, first, second, third]:
            copy.wait_send()
        for store in stores:
            store.wait()

    one, rows_one = (rows, block), part.shape[1:]
    return Job(
        [pieces, part],
        [jax.ShapeDtypeStruct(one, bf16), jax.ShapeDtypeStruct(rows_one, bf16)],
        [pltpu.VMEM((4,) + one, bf16) for _ in range(3)]
        + [pltpu.VMEM((2,) + one, bf16)]
        + [pltpu.VMEM(one, bf16) for _ in range(3)]
        + [pltpu.VMEM((2,) + rows_one, bf16) for _ in range(2)]
        + [pltpu.VMEM(rows_one, bf16) for _ in range(3)]
        + [DMA((4,)), DMA((4,)), DMA((4,)), DMA((3,)), DMA((3,)), DMA((2,)), DMA((3,)), DMA((3,)), DMA((2,))],
        5,
        body,
        [(1, 0), (2, 0), (4, 0), (0, 1), (0, 2)],
    )


def attend_kernel(spans, q_ref, kv_ref, out):
    count, _, slots, part = q_ref.shape
    for w, span in enumerate(spans):

        def head(h, carry, w=w, span=span):
            at = pl.multiple_of(h * HEAD_SIZE, HEAD_SIZE)
            columns = pl.ds(at, HEAD_SIZE)
            q, probs, _, values = head_probs(q_ref, kv_ref, w, span, at)
            mixed = dot(probs.astype(bf16), values)
            out[:, w, :, columns] = mixed.reshape(count, slots, HEAD_SIZE).astype(bf16)
            return carry

        lax.fori_loop(0, part // HEAD_SIZE, head, 0)


def slot_rows(ref, w, at):
    count, _, slots, _ = ref.shape
    rows = ref[:, w, :, pl.ds(at, HEAD_SIZE)].astype(f32)
    return rows.reshape(count * slots, HEAD_SIZE).astype(bf16)


def head_probs(q_ref, kv_ref, w, span, at):
    half = kv_ref.shape[1] // 2
    q = slot_rows(q_ref, w, at)
    keys = kv_ref[:span, pl.ds(at, HEAD_SIZE)]
    values = kv_ref[:span, pl.ds(pl.multiple_of(half + at, HEAD_SIZE), HEAD_SIZE)]
    scores = dot_t(q, keys) * HEAD_SIZE ** (-0.5)
    weight = jnp.exp(scores - jnp.max(scores, -1, keepdims=True))
    probs = weight / jnp.sum(weight, -1, keepdims=True)
    return q, probs, keys, values


def attend_call(queries, kv, spans):
    return pl.pallas_call(
        functools.partial(attend_kernel, spans),
        out_shape=jax.ShapeDtypeStruct(queries.shape, bf16),
        in_specs=[VM, VM],
        out_specs=VM,
        compiler_params=pltpu.CompilerParams(vmem_limit_bytes=VMEM_LIMIT),
        name="attend",
    )(queries, kv)


def attend_back_kernel(spans, q_ref, g_ref, kv_ref, grad_q, grad_kv, total):
    count, _, slots, part = q_ref.shape
    total[...] = jnp.zeros_like(total)
    for w, span in enumerate(spans):

        def head(h, carry, w=w, span=span):
            at = pl.multiple_of(h * HEAD_SIZE, HEAD_SIZE)
            columns = pl.ds(at, HEAD_SIZE)
            q, probs, keys, values = head_probs(q_ref, kv_ref, w, span, at)
            grad = slot_rows(g_ref, w, at)
            grad_probs = dot_t(grad, values)
            centred = jnp.sum(probs * grad_probs, -1, keepdims=True)
            grad_scores = (probs * (grad_probs - centred)).astype(bf16)
            grad_rows = dot(grad_scores, keys) * HEAD_SIZE ** (-0.5)
            grad_q[:, w, :, columns] = grad_rows.reshape(count, slots, HEAD_SIZE).astype(bf16)
            total[:span, columns] += t_dot(grad_scores, q) * HEAD_SIZE ** (-0.5)
            at_value = pl.ds(pl.multiple_of(part + at, HEAD_SIZE), HEAD_SIZE)
            total[:span, at_value] += t_dot(probs.astype(bf16), grad)
            return carry

        lax.fori_loop(0, part // HEAD_SIZE, head, 0)
    grad_kv[...] = total[...].astype(bf16)


def attend_back_call(queries, grads, kv, spans):
    return pl.pallas_call(
        functools.partial(attend_back_kernel, spans),
        out_shape=[
            jax.ShapeDtypeStruct(queries.shape, bf16),
            jax.ShapeDtypeStruct(kv.shape, bf16),
        ],
        in_specs=[VM, VM, VM],
        out_specs=[VM, VM],
        scratch_shapes=[pltpu.VMEM(kv.shape, f32)],
        compiler_params=pltpu.CompilerParams(vmem_limit_bytes=VMEM_LIMIT),
        name="attend_back",
    )(queries, grads, kv)


def gather_kernel(n, n_ws, own, out, load_sem, w_s, w_r, ep_s, ep_r):
    e, w = lax.axis_index("ep"), lax.axis_index("ws")
    beside = [flip(w, k) for k in range(1, n_ws)]
    across = [flip(e, k) for k in far_first(n)]
    greet([(e, p) for p in beside] + [(s, w) for s in across])
    keep = pltpu.make_async_copy(own, out.at[e, w], load_sem)
    keep.start()
    first = []
    for i, p in enumerate(beside):
        first.append(remote(own, out.at[e, w], w_s.at[i], w_r.at[i], (e, p)))
        first[-1].start()
    keep.wait()
    for copy in first:
        copy.wait()
    second = []
    for i, s in enumerate(across):
        second.append(remote(out.at[e], out.at[e], ep_s.at[i], ep_r.at[i], (s, w)))
        second[-1].start()
    for copy in second:
        copy.wait()


def gather_call(own, n, n_ws):
    return pl.pallas_call(
        functools.partial(gather_kernel, n, n_ws),
        out_shape=jax.ShapeDtypeStruct((n, n_ws) + own.shape, own.dtype),
        in_specs=[VM],
        out_specs=VM,
        scratch_shapes=[DMA, DMA((n_ws - 1,)), DMA((n_ws - 1,)), DMA((n - 1,)), DMA((n - 1,))],
        compiler_params=pltpu.CompilerParams(collective_id=3, has_side_effects=True),
        name="gather_gains",
    )(own)


def reduce_kernel(n, n_ws, parts, out, held, all_parts, load_sem, w_s, w_r, ep_s, ep_r):
    e, w = lax.axis_index("ep"), lax.axis_index("ws")
    beside = [flip(w, k) for k in range(1, n_ws)]
    across = [flip(e, k) for k in far_first(n)]
    greet([(e, p) for p in beside] + [(s, w) for s in across])
    keep = pltpu.make_async_copy(parts.at[:, w], held.at[:, w], load_sem.at[0])
    keep.start()
    first = []
    for i, p in enumerate(beside):
        first.append(remote(parts.at[:, p], held.at[:, w], w_s.at[i], w_r.at[i], (e, p)))
        first[-1].start()
    keep.wait()
    for copy in first:
        copy.wait()
    keep = pltpu.make_async_copy(held.at[e], all_parts.at[e], load_sem.at[1])
    keep.start()
    second = []
    for i, s in enumerate(across):
        second.append(remote(held.at[s], all_parts.at[e], ep_s.at[i], ep_r.at[i], (s, w)))
        second[-1].start()
    keep.wait()
    for copy in second:
        copy.wait()
    out[...] = jnp.sum(jnp.sum(all_parts[...], 0), 0)


def reduce_call(parts):
    n, n_ws = parts.shape[:2]
    return pl.pallas_call(
        functools.partial(reduce_kernel, n, n_ws),
        out_shape=jax.ShapeDtypeStruct(parts.shape[2:], parts.dtype),
        in_specs=[VM],
        out_specs=VM,
        scratch_shapes=[
            pltpu.VMEM(parts.shape, parts.dtype),
            pltpu.VMEM(parts.shape, parts.dtype),
            DMA((2,)),
            DMA((n_ws - 1,)),
            DMA((n_ws - 1,)),
            DMA((n - 1,)),
            DMA((n - 1,)),
        ],
        compiler_params=pltpu.CompilerParams(collective_id=4, has_side_effects=True),
        name="reduce_gains",
    )(parts)


def small(n_ep):
    return n_ep == MIXTURE_EXPERTS and lax.axis_size("ws") == 4


PLAIN = {
    grad_job: lambda a, b: [t_dot(a, b)],
    pair_grad_job: lambda a, b, c: [jnp.stack([t_dot(a, b), t_dot(a, c)], 1)],
    split_job: lambda weight: [weight[:, 0], weight[:, 1]],
    ffn_job: ffn_plain,
    ffn_back_job: ffn_back_plain,
}


def beside(job, plain, arg, fills, collective_id, name):
    if job is None:
        return [plain(arg)] + [out for make, *rest in fills for out in PLAIN[make](*rest)]
    return run_jobs([job(arg)], [make(*rest) for make, *rest in fills], collective_id, name)


def exchange_plain(send):
    return lax.all_to_all(send, "ep", split_axis=0, concat_axis=0, tiled=True)


def exchange(send, *fills, collective_id=2, name="exchange"):
    job = exchange_job if small(send.shape[0]) else None
    return beside(job, exchange_plain, send, fills, collective_id, name)


def spread(rows, group):
    width = rows.shape[-1]
    blocks = rows.reshape(MIXTURE_EXPERTS, 1, ROWS, width)
    return jnp.broadcast_to(blocks, (MIXTURE_EXPERTS, group, ROWS, width)).reshape(
        MIXTURE_EXPERTS * group, ROWS, width
    )


def dispatch(rows, group, *fills, collective_id=0, name="dispatch"):
    width = rows.shape[-1]

    def plain(blocks):
        return lax.all_gather(exchange_plain(blocks), "ws", axis=1, tiled=False)

    job = functools.partial(dispatch_job, n_ws=4) if small(MIXTURE_EXPERTS * group) else None
    out = beside(job, plain, spread(rows, group), fills, collective_id, name)
    return [out[0].reshape(-1, width)] + list(out[1:])


def combine(partial, group, n_ep, n_ws, *fills, collective_id=1, name="combine"):
    width = partial.shape[-1]

    def plain(part):
        part = part.transpose(1, 0, 2, 3).reshape(n_ws * n_ep * ROWS, width)
        own = lax.psum_scatter(part, "ws", scatter_dimension=0, tiled=True)
        return exchange_plain(own.reshape(n_ep, ROWS, width))

    part = partial.reshape(n_ep, n_ws, ROWS, width)
    job = combine_job if small(n_ep) else None
    back, *rest = beside(job, plain, part, fills, collective_id, name)
    if group > 1:
        back = jnp.sum(back.reshape(MIXTURE_EXPERTS, group, ROWS, width).astype(f32), 1).astype(bf16)
    return [back.reshape(MIXTURE_EXPERTS * ROWS, width)] + rest


def slot_tables(routes, slots):
    target = jnp.where(slots < CAP, routes * ROWS + slots, -1)
    places = lax.broadcasted_iota(jnp.int32, (MIXTURE_EXPERTS * ROWS, target.shape[0]), 0)
    return [(places == target[None, :, k]).astype(bf16) for k in range(CHOSEN_EXPERTS)]


def norm_back(grad, unit, inverse, gain):
    gain_grad = jnp.sum(grad * unit, 0)
    scaled = grad * gain
    return (inverse * (scaled - unit * jnp.mean(scaled * unit, -1, keepdims=True)), gain_grad)


def heads_of(rows):
    return rows.reshape(rows.shape[0], -1, HEAD_SIZE)


def local(
    x_in,
    gain_attn,
    gain_ffn,
    key_value_weight,
    w_query,
    w_output,
    w_in,
    w_out,
    gate_attn,
    gate_ffn,
    route_attn,
    slot_attn,
    route_ffn,
    slot_ffn,
    cotangent,
):
    n_ep = lax.axis_size("ep")
    n_ws = lax.axis_size("ws")
    group = n_ep // MIXTURE_EXPERTS
    local_tokens, width = x_in.shape
    key_value_width = KEY_VALUE_HEADS * HEAD_SIZE
    part = w_query.shape[2]
    own_width = group * part
    sequence = n_ws * local_tokens
    place = lax.axis_index("ws")
    scale = HEAD_SIZE ** (-0.5)

    fused = small(n_ep) and key_value_weight.shape[1] == HEAD_SIZE
    short = fused and gain_attn.shape[0] == 64
    if short:
        gains = jnp.concatenate([gain_attn, gain_ffn], 0).astype(f32)[None]
        gains = gather_call(gains, n_ep, n_ws).reshape(n_ep * n_ws, 2, -1)
        gain_one, gain_two = gains[:, 0].reshape(-1), gains[:, 1].reshape(-1)
    else:
        gain_one = lax.all_gather(gain_attn, ("ep", "ws"), axis=0, tiled=True).astype(f32)
        gain_two = lax.all_gather(gain_ffn, ("ep", "ws"), axis=0, tiled=True).astype(f32)
    plain = group == 1 and key_value_weight.shape[1] == HEAD_SIZE
    if plain:
        half = n_ep // 2
        there = [
            (e * n_ws + w, (w + n_ws * (e // half)) * n_ws + e % half)
            for e in range(n_ep)
            for w in range(n_ws)
        ]
        mine = lax.ppermute(key_value_weight, ("ep", "ws"), there)
    else:
        whole = lax.all_gather(key_value_weight, ("ep", "ws"), axis=1, tiled=True)
        whole = whole.reshape(width, 2 * group, n_ws, part)
        kv_own = lax.dynamic_index_in_dim(whole, place, 2, keepdims=False).reshape(width, -1)

    inputs = x_in.astype(f32)
    inverse_one = lax.rsqrt(jnp.mean(inputs * inputs, -1, keepdims=True) + EPS)
    unit_one = inputs * inverse_one
    normed = (unit_one * gain_one).astype(bf16)
    attn_pairs = slot_tables(route_attn, slot_attn)
    ffn_pairs = slot_tables(route_ffn, slot_ffn)
    attn_tokens = attn_pairs[0] + attn_pairs[1]
    ffn_tokens = ffn_pairs[0] + ffn_pairs[1]

    slots_one = dot(attn_tokens, normed).astype(bf16)
    if fused:
        rows_one, kv_own, normed_sequence, gate_weight, up_weight = run_jobs(
            [
                dispatch_job(slots_one.reshape(n_ep, ROWS, width), n_ws),
                gather_weights_job(mine, normed, n_ep, n_ws),
            ],
            [split_job(w_in[0])],
            10,
            "dispatch_weights",
        )
        rows_one = rows_one.reshape(-1, width)
        normed_sequence = normed_sequence.reshape(sequence, width)
    else:
        if plain:
            kv_own = lax.all_gather(mine, "ep", axis=1, tiled=True)
        normed_sequence = lax.all_gather(normed, "ws", axis=0, tiled=True)
        rows_one, gate_weight, up_weight = dispatch(slots_one, group, (split_job, w_in[0]))
    kv = dot(normed_sequence, kv_own).astype(bf16)
    keys = kv[:, :own_width].reshape(sequence, -1, HEAD_SIZE)
    values = kv[:, own_width:].reshape(sequence, -1, HEAD_SIZE)

    owner_query = dot(rows_one, w_query[0]).astype(bf16)
    queries = exchange(owner_query.reshape(n_ep, n_ws * ROWS, part))[0]
    spans = [(w * local_tokens // BLOCK + 1) * BLOCK for w in range(n_ws)]
    queries = queries.reshape(MIXTURE_EXPERTS, group, n_ws, ROWS, part)

    def by_block(rows):
        rows = rows.reshape(MIXTURE_EXPERTS, group, n_ws, ROWS, part)
        return [
            rows[:, :, w].transpose(0, 2, 1, 3).reshape(-1, own_width // HEAD_SIZE, HEAD_SIZE)
            for w in range(n_ws)
        ]

    def to_experts(pieces):
        rows = jnp.stack(
            [
                piece.reshape(MIXTURE_EXPERTS, ROWS, group, part).transpose(0, 2, 1, 3)
                for piece in pieces
            ],
            2,
        )
        return rows.reshape(n_ep, n_ws * ROWS, part)

    if fused:
        queries = queries.reshape(n_ep, n_ws, ROWS, part)
        mixed = attend_call(queries, kv, spans).reshape(n_ep, n_ws * ROWS, part)
    else:
        kept = []
        mixed_pieces = []
        for q, span in zip(by_block(queries), spans):
            scores = (
                jnp.einsum("rhd,shd->hrs", q, keys[:span], preferred_element_type=f32) * scale
            )
            probs = jax.nn.softmax(scores, axis=-1)
            mixed = jnp.einsum(
                "hrs,shd->rhd", probs.astype(bf16), values[:span], preferred_element_type=f32
            )
            kept.append((q, probs))
            mixed_pieces.append(mixed.astype(bf16))
        mixed = to_experts(mixed_pieces)
    owner_mixed = exchange(mixed)[0].reshape(-1, part)
    attn_slots = combine(dot(owner_mixed, w_output[0]).astype(bf16), group, n_ep, n_ws, collective_id=11)[0]

    def weighted(pairs, gates, slot_values):
        return sum(gates[:, k : k + 1] * t_dot(pairs[k], slot_values) for k in range(2))

    def to_slots(pairs, gates, values):
        return sum(
            dot(pairs[k], (gates[:, k : k + 1] * values).astype(bf16)) for k in range(2)
        ).astype(bf16)

    hidden_state = inputs + weighted(attn_pairs, gate_attn, attn_slots)
    inverse_two = lax.rsqrt(jnp.mean(hidden_state * hidden_state, -1, keepdims=True) + EPS)
    unit_two = hidden_state * inverse_two
    normed_two = (unit_two * gain_two).astype(bf16)

    grad_out = cotangent.astype(f32)
    grad_slots = to_slots(ffn_pairs, gate_ffn, grad_out)
    expert_rows = dispatch(dot(ffn_tokens, normed_two).astype(bf16), group)[0]
    expert_grad, gate_pre, up_pre, activated, forward_part = dispatch(
        grad_slots,
        group,
        (ffn_job, expert_rows, gate_weight, up_weight, w_out[0]),
        collective_id=5,
        name="dispatch_ffn",
    )
    ffn_slots, grad_gate, grad_up, back_two = combine(
        forward_part,
        group,
        n_ep,
        n_ws,
        (ffn_back_job, expert_grad, gate_pre, up_pre, gate_weight, up_weight, w_out[0]),
        collective_id=1,
        name="combine_ffn_back",
    )
    result = hidden_state + weighted(ffn_pairs, gate_ffn, ffn_slots)
    back_slots, grad_second = combine(
        back_two,
        group,
        n_ep,
        n_ws,
        (grad_job, activated, expert_grad),
        collective_id=6,
        name="combine_grad_out",
    )

    grad_normed_two = t_dot(ffn_tokens, back_slots)
    grad_hidden_norm, grad_gain_two = norm_back(grad_normed_two, unit_two, inverse_two, gain_two)
    grad_hidden = grad_out + grad_hidden_norm
    owner_grad, grad_first = dispatch(
        to_slots(attn_pairs, gate_attn, grad_hidden),
        group,
        (pair_grad_job, expert_rows, grad_gate, grad_up),
        collective_id=7,
        name="dispatch_grad_in",
    )
    back_mixed = dot_t(owner_grad, w_output[0]).astype(bf16)
    mixed_grads, grad_output = exchange(
        back_mixed.reshape(n_ep, n_ws * ROWS, part),
        (grad_job, owner_mixed, owner_grad),
        collective_id=8,
        name="exchange_grad_output",
    )

    if fused:
        mixed_grads = mixed_grads.reshape(n_ep, n_ws, ROWS, part)
        query_grads, grad_kv_rows = attend_back_call(queries, mixed_grads, kv, spans)
        query_grads = query_grads.reshape(n_ep, n_ws * ROWS, part)
    else:
        grad_keys, grad_values, query_pieces = 0.0, 0.0, []
        for (q, probs), grad, span in zip(kept, by_block(mixed_grads), spans):
            grad_probs = jnp.einsum("rhd,shd->hrs", grad, values[:span], preferred_element_type=f32)
            centred = jnp.sum(probs * grad_probs, -1, keepdims=True)
            grad_scores = (probs * (grad_probs - centred)).astype(bf16)
            grad_q = (
                jnp.einsum("hrs,shd->rhd", grad_scores, keys[:span], preferred_element_type=f32)
                * scale
            )
            query_pieces.append(grad_q.astype(bf16))
            pad = ((0, sequence - span), (0, 0), (0, 0))
            piece = jnp.einsum("hrs,rhd->shd", grad_scores, q, preferred_element_type=f32) * scale
            grad_keys = grad_keys + jnp.pad(piece, pad)
            piece = jnp.einsum(
                "hrs,rhd->shd", probs.astype(bf16), grad, preferred_element_type=f32
            )
            grad_values = grad_values + jnp.pad(piece, pad)
        grad_kv_rows = jnp.concatenate(
            [grad_keys.reshape(sequence, -1), grad_values.reshape(sequence, -1)], 1
        ).astype(bf16)
        query_grads = to_experts(query_pieces)
    grad_kv = t_dot(normed_sequence, grad_kv_rows)
    from_kv = dot_t(grad_kv_rows, kv_own).astype(bf16)
    if fused:
        owner_grad_query, piece, from_kv = run_jobs(
            [
                exchange_job(query_grads),
                reduce_weights_job(
                    grad_kv.astype(bf16), from_kv.reshape(n_ws, local_tokens, width), n_ep
                ),
            ],
            [],
            12,
            "exchange_weights",
        )
        owner_grad_query = owner_grad_query.reshape(-1, part)
    else:
        owner_grad_query = exchange(query_grads)[0].reshape(-1, part)
    back_normed = dot_t(owner_grad_query, w_query[0]).astype(bf16)
    normed_back, grad_query = combine(
        back_normed,
        group,
        n_ep,
        n_ws,
        (grad_job, rows_one, owner_grad_query),
        collective_id=9,
        name="combine_grad_query",
    )

    if fused:
        back = [(b, a) for a, b in there]
        grad_kv_shard = lax.ppermute(piece, ("ep", "ws"), back).astype(f32)
    elif plain:
        pieces = grad_kv.reshape(width, n_ep, HEAD_SIZE).transpose(1, 0, 2).astype(bf16)
        piece = lax.psum_scatter(pieces, "ep", scatter_dimension=0, tiled=False)
        grad_kv_shard = lax.ppermute(piece, ("ep", "ws"), [(b, a) for a, b in there]).astype(f32)
    else:
        mask = (jnp.arange(n_ws) == place)[None, None, :, None]
        pieces = jnp.where(mask, grad_kv.reshape(width, 2 * group, 1, part), 0.0)
        pieces = pieces.reshape(width, 2 * key_value_width).astype(bf16)
        grad_kv_shard = lax.psum_scatter(
            pieces, ("ep", "ws"), scatter_dimension=1, tiled=True
        ).astype(f32)
    if not fused:
        from_kv = lax.psum_scatter(from_kv, "ws", scatter_dimension=0, tiled=True)
    grad_normed = t_dot(attn_tokens, normed_back) + from_kv.astype(f32)
    grad_input_norm, grad_gain_one = norm_back(grad_normed, unit_one, inverse_one, gain_one)
    grad_input = grad_hidden + grad_input_norm
    gain_grads = jnp.stack([grad_gain_one, grad_gain_two], 0)
    if short:
        parts = gain_grads.reshape(2, n_ep, n_ws, -1).transpose(1, 2, 0, 3)
        gain_shards = reduce_call(parts.reshape(n_ep, n_ws, 1, -1)).reshape(2, -1)
    else:
        gain_shards = lax.psum_scatter(
            gain_grads, ("ep", "ws"), scatter_dimension=1, tiled=True
        )
    return (
        result.astype(bf16),
        grad_input,
        gain_shards[0],
        gain_shards[1],
        grad_kv_shard,
        grad_query[None],
        grad_output[None],
        grad_first[None],
        grad_second[None],
    )


def solution(mesh):
    both = ("ep", "ws")
    rows, vector, columns = P(both, None), P(both), P(None, both)
    return jax.shard_map(
        local,
        mesh=mesh,
        in_specs=(
            rows,
            vector,
            vector,
            columns,
            P("ep", None, "ws"),
            P("ep", "ws", None),
            P("ep", None, None, "ws"),
            P("ep", "ws", None),
            rows,
            rows,
            rows,
            rows,
            rows,
            rows,
            rows,
        ),
        out_specs=(
            rows,
            rows,
            vector,
            vector,
            columns,
            P("ep", None, "ws"),
            P("ep", "ws", None),
            P("ep", None, None, "ws"),
            P("ep", "ws", None),
        ),
        check_vma=False,
    )
```

```python
import functools

import jax
import jax.numpy as jnp
from jax import lax
from jax.experimental import pallas as pl
from jax.experimental.pallas import tpu as pltpu
from jax.sharding import PartitionSpec as P

KEY_VALUE_HEADS = 16
HEAD_SIZE = 128
MIXTURE_EXPERTS = 8
CHOSEN_EXPERTS = 2
BLOCK = 256
CAP = 36
ROWS = 40

EPS = 1e-06
very_negative = -1e30
f32 = jnp.float32
bf16 = jnp.bfloat16
MESH = pl.DeviceIdType.MESH
ANY = pl.BlockSpec(memory_space=pl.ANY)
VM = pl.BlockSpec(memory_space=pltpu.VMEM)
DMA = pltpu.SemaphoreType.DMA
STEP = 256
VMEM_LIMIT = 60 << 20


def dot(a, b):
    return jnp.dot(a, b, preferred_element_type=f32)


def dot_t(a, b):
    return lax.dot_general(a, b, (((1,), (1,)), ((), ())), preferred_element_type=f32)


def t_dot(a, b):
    return lax.dot_general(a, b, (((0,), (0,)), ((), ())), preferred_element_type=f32)


def flip(index, bits):
    out, bit = index, 1
    while bit <= bits:
        if bits & bit:
            out = out + bit - 2 * bit * ((index // bit) % 2)
        bit *= 2
    return out


def far_first(n):
    return sorted(range(1, n), key=lambda k: (-((k // 2).bit_length()), k))


def greet(partners):
    barrier = pltpu.get_barrier_semaphore()
    for partner in partners:
        pl.semaphore_signal(barrier, inc=1, device_id=partner, device_id_type=MESH)
    pl.semaphore_wait(barrier, len(partners))


def remote(src, dst, send, recv, device):
    return pltpu.make_async_remote_copy(
        src_ref=src, dst_ref=dst, send_sem=send, recv_sem=recv, device_id=device, device_id_type=MESH
    )


class Job:
    def __init__(self, args, outs, scratch, steps, body, partners=()):
        self.args, self.outs, self.scratch, self.steps, self.body = args, outs, scratch, steps, body
        self.partners = partners


def run_jobs(jobs, fills, collective_id, name):
    whole = jobs + fills
    args = [a for job in whole for a in job.args]
    outs = [o for job in whole for o in job.outs]
    scratch = [x for job in whole for x in job.scratch]
    turns = sorted((k / job.steps, i) for i, job in enumerate(jobs) for k in range(job.steps))
    partners = sorted({p for job in jobs for p in job.partners})

    def kernel(*refs):
        bodies, at = [], [0, len(args), len(args) + len(outs)]
        for job in whole:
            own = []
            for k, part in enumerate((job.args, job.outs, job.scratch)):
                own.append(refs[at[k] : at[k] + len(part)])
                at[k] += len(part)
            bodies.append(job.body(*own[0], *own[1], *own[2]))
        moves, work = bodies[: len(jobs)], bodies[len(jobs) :]
        queue = [g for g, job in zip(work, fills) for _ in range(job.steps)]
        for g in work:
            next(g)
        e, w = lax.axis_index("ep"), lax.axis_index("ws")
        greet([(flip(e, p), flip(w, q)) for p, q in partners])
        done = 0
        for k, (_, i) in enumerate(turns):
            next(moves[i])
            target = (k + 1) * len(queue) // len(turns)
            while done < target:
                next(queue[done])
                done += 1
        for g in moves + work:
            for _ in g:
                pass

    return pl.pallas_call(
        kernel,
        out_shape=outs,
        in_specs=[ANY] * len(args),
        out_specs=[ANY] * len(outs),
        scratch_shapes=scratch,
        compiler_params=pltpu.CompilerParams(
            collective_id=collective_id, has_side_effects=True, vmem_limit_bytes=VMEM_LIMIT
        ),
        name=name,
    )(*args)


def fetch(pairs, sem):
    copies = [
        pltpu.make_async_copy(src, dst, sem.at[i]) for i, (src, dst) in enumerate(pairs)
    ]
    for copy in copies:
        copy.start()
    return copies


def blocks_of(size):
    return [(start, min(STEP, size - start)) for start in range(0, size, STEP)]


def column_tiles(width, tile):
    def body(c, carry):
        tile(pl.multiple_of(c * STEP, STEP), STEP)
        return carry

    lax.fori_loop(0, width // STEP, body, 0)
    if width % STEP:
        tile(width // STEP * STEP, width % STEP)


def grad_job(a, b):
    depth, rows = a.shape
    width = b.shape[1]

    def body(a_hbm, b_hbm, out, a_ref, b_ref, turned, held, load_sem, sem):
        loads = fetch(((a_hbm, a_ref), (b_hbm, b_ref)), load_sem)
        yield
        for load in loads:
            load.wait()
        copies = []
        for i, (start, size) in enumerate(blocks_of(rows)):
            if i >= 2:
                copies[i - 2].wait()
            turned[:size] = a_ref[:, start : start + size].T

            def tile(at, columns, slot=i % 2, size=size):
                held[slot, :size, pl.ds(at, columns)] = jnp.dot(
                    turned[:size], b_ref[:, pl.ds(at, columns)], preferred_element_type=f32
                )

            column_tiles(width, tile)
            copies.append(
                pltpu.make_async_copy(
                    held.at[i % 2, pl.ds(0, size)], out.at[pl.ds(start, size)], sem.at[i % 2]
                )
            )
            copies[i].start()
            yield
        for copy in copies[-2:]:
            copy.wait()

    return Job(
        [a, b],
        [jax.ShapeDtypeStruct((rows, width), f32)],
        [
            pltpu.VMEM(a.shape, bf16),
            pltpu.VMEM(b.shape, bf16),
            pltpu.VMEM((STEP, depth), bf16),
            pltpu.VMEM((2, STEP, width), f32),
            DMA((2,)),
            DMA((2,)),
        ],
        len(blocks_of(rows)),
        body,
    )


def pair_grad_job(a, first, second):
    depth, rows = a.shape
    tiles = first.shape[1] // 128

    def body(a_hbm, f_hbm, s_hbm, out, a_ref, f_ref, s_ref, turned, held, load_sem, sem):
        loads = fetch(((a_hbm, a_ref), (f_hbm, f_ref), (s_hbm, s_ref)), load_sem)
        flat = held.reshape(2 * tiles * STEP * 2, 128)
        yield
        for load in loads:
            load.wait()
        copies = []
        for i, (start, size) in enumerate(blocks_of(rows)):
            if i >= 2:
                for copy in copies[i - 2]:
                    copy.wait()
            turned[:size] = a_ref[:, start : start + size].T

            def tile(at, columns, slot=i % 2, size=size):
                for j, b_ref in enumerate((f_ref, s_ref)):
                    r = jnp.dot(
                        turned[:size], b_ref[:, pl.ds(at, columns)], preferred_element_type=f32
                    )
                    for half in range(columns // 128):
                        base = (slot * tiles + at // 128 + half) * (2 * STEP) + j
                        flat[pl.ds(base, size, stride=2), :] = r[:, half * 128 : half * 128 + 128]

            column_tiles(tiles * 128, tile)
            copies.append(
                [
                    pltpu.make_async_copy(
                        held.at[i % 2, c, pl.ds(0, size)],
                        out.at[pl.ds(start, size), :, pl.ds(c * 128, 128)],
                        sem.at[i % 2, c],
                    )
                    for c in range(tiles)
                ]
            )
            for copy in copies[i]:
                copy.start()
            yield
        for copy in copies[-2] + copies[-1]:
            copy.wait()

    return Job(
        [a, first, second],
        [jax.ShapeDtypeStruct((rows, 2, tiles * 128), f32)],
        [
            pltpu.VMEM(a.shape, bf16),
            pltpu.VMEM(first.shape, bf16),
            pltpu.VMEM(second.shape, bf16),
            pltpu.VMEM((STEP, depth), bf16),
            pltpu.VMEM((2, tiles, STEP, 2, 128), f32),
            DMA((3,)),
            DMA((2, tiles)),
        ],
        len(blocks_of(rows)),
        body,
    )


def split_job(weight):
    rows, _, width = weight.shape

    def body(w_hbm, first, second, block, wide, held, load_sem, sem):
        flat = wide.reshape(2 * STEP, 128)
        steps = rows // STEP

        def load(i):
            return pltpu.make_async_copy(
                w_hbm.at[pl.ds(i * STEP, STEP)], block.at[i % 2], load_sem.at[i % 2]
            )

        load(0).start()
        yield
        copies = []
        for i in range(steps):
            slot = i % 2
            if i + 1 < steps:
                load(i + 1).start()
            load(i).wait()
            if i >= 2:
                for copy in copies[i - 2]:
                    copy.wait()

            def tile(c, carry, slot=slot):
                at = pl.ds(pl.multiple_of(c * 128, 128), 128)
                wide[...] = block[slot, :, :, at].astype(f32)
                for j in range(2):
                    held[slot, j, :, at] = flat[pl.ds(j, STEP, stride=2), :].astype(bf16)
                return carry

            lax.fori_loop(0, width // 128, tile, 0)
            copies.append(
                [
                    pltpu.make_async_copy(
                        held.at[slot, j], out.at[pl.ds(i * STEP, STEP)], sem.at[slot, j]
                    )
                    for j, out in enumerate((first, second))
                ]
            )
            for copy in copies[i]:
                copy.start()
            yield
        for copy in copies[-2] + copies[-1]:
            copy.wait()

    return Job(
        [weight],
        [jax.ShapeDtypeStruct((rows, width), bf16)] * 2,
        [
            pltpu.VMEM((2, STEP, 2, width), bf16),
            pltpu.VMEM((STEP, 2, 128), f32),
            pltpu.VMEM((2, 2, STEP, width), bf16),
            DMA((2,)),
            DMA((2, 2)),
        ],
        rows // STEP,
        body,
    )


def ffn_job(x, gate_weight, up_weight, down_weight):
    rows, width = x.shape
    hidden = gate_weight.shape[1]

    def body(
        x_hbm, g_hbm, u_hbm, d_hbm, gate_out, up_out, act_out, out, x_ref, g_ref, u_ref, d_ref, pre, act, res,
        load_sem, sem
    ):
        loads = fetch(((x_hbm, x_ref), (g_hbm, g_ref), (u_hbm, u_ref), (d_hbm, d_ref)), load_sem)
        yield
        for load in loads:
            load.wait()
        copies = []
        for i, (start, size) in enumerate(blocks_of(rows)):
            slot = i % 2
            here = pl.ds(start, size)
            if i >= 2:
                for copy in copies[i - 2]:
                    copy.wait()

            def tile(at, columns, slot=slot, start=start, size=size):
                part = pl.ds(at, columns)
                left = x_ref[start : start + size]
                gate = dot(left, g_ref[:, part])
                up = dot(left, u_ref[:, part])
                pre[slot, 0, :, part] = gate
                pre[slot, 1, :, part] = up
                act[slot, :, part] = (gate * jax.nn.sigmoid(gate) * up).astype(bf16)

            column_tiles(hidden, tile)
            yield

            def last(at, columns, slot=slot):
                part = pl.ds(at, columns)
                res[slot, :, part] = dot(act[slot], d_ref[:, part]).astype(bf16)

            column_tiles(width, last)
            copies.append(
                [
                    pltpu.make_async_copy(src.at[slot], dst.at[here], sem.at[slot, k])
                    for k, (src, dst) in enumerate(((act, act_out), (res, out)))
                ]
                + [
                    pltpu.make_async_copy(pre.at[slot, k], dst.at[here], sem.at[slot, 2 + k])
                    for k, dst in enumerate((gate_out, up_out))
                ]
            )
            for copy in copies[i]:
                copy.start()
            yield
        for copy in copies[-2] + copies[-1]:
            copy.wait()

    return Job(
        [x, gate_weight, up_weight, down_weight],
        [jax.ShapeDtypeStruct((rows, hidden), f32)] * 2
        + [jax.ShapeDtypeStruct((rows, hidden), bf16), jax.ShapeDtypeStruct((rows, width), bf16)],
        [
            pltpu.VMEM(x.shape, bf16),
            pltpu.VMEM(gate_weight.shape, bf16),
            pltpu.VMEM(up_weight.shape, bf16),
            pltpu.VMEM(down_weight.shape, bf16),
            pltpu.VMEM((2, 2, STEP, hidden), f32),
            pltpu.VMEM((2, STEP, hidden), bf16),
            pltpu.VMEM((2, STEP, width), bf16),
            DMA((4,)),
            DMA((2, 4)),
        ],
        2 * (rows // STEP),
        body,
    )


def ffn_plain(x, gate_weight, up_weight, down_weight):
    gate_pre, up_pre = dot(x, gate_weight), dot(x, up_weight)
    activated = (gate_pre * jax.nn.sigmoid(gate_pre) * up_pre).astype(bf16)
    return gate_pre, up_pre, activated, dot(activated, down_weight).astype(bf16)


def before_activation(grad_act, gate_pre, up_pre):
    sigmoid_gate = jax.nn.sigmoid(gate_pre)
    grad_up = (grad_act * gate_pre * sigmoid_gate).astype(bf16)
    grad_gate = (
        grad_act * up_pre * sigmoid_gate * (1.0 + gate_pre * (1.0 - sigmoid_gate))
    ).astype(bf16)
    return grad_gate, grad_up


def ffn_back_job(grad, gate_pre, up_pre, gate_weight, up_weight, down_weight):
    rows, width = grad.shape
    hidden = gate_weight.shape[1]

    def body(
        x_hbm, gp_hbm, up_hbm, g_hbm, u_hbm, d_hbm, gate_out, up_out, out, x_ref, g_ref, u_ref, d_ref, pre, hid,
        res, load_sem, pre_sem, sem
    ):
        loads = fetch(((x_hbm, x_ref), (g_hbm, g_ref), (u_hbm, u_ref), (d_hbm, d_ref)), load_sem)

        def load_pre(i):
            here = pl.ds(i * STEP, STEP)
            return [
                pltpu.make_async_copy(src.at[here], pre.at[i % 2, k], pre_sem.at[i % 2, k])
                for k, src in enumerate((gp_hbm, up_hbm))
            ]

        for copy in load_pre(0):
            copy.start()
        yield
        for load in loads:
            load.wait()
        copies = []
        steps = rows // STEP
        for i in range(steps):
            slot, start = i % 2, i * STEP
            here = pl.ds(start, STEP)
            if i + 1 < steps:
                for copy in load_pre(i + 1):
                    copy.start()
            for copy in load_pre(i):
                copy.wait()
            if i >= 2:
                for copy in copies[i - 2]:
                    copy.wait()

            def tile(at, columns, slot=slot, start=start):
                part = pl.ds(at, columns)
                grad_act = dot_t(x_ref[start : start + STEP], d_ref[part, :])
                pair = before_activation(grad_act, pre[slot, 0, :, part], pre[slot, 1, :, part])
                hid[slot, 0, :, part], hid[slot, 1, :, part] = pair

            column_tiles(hidden, tile)
            yield

            def last(at, columns, slot=slot):
                part = pl.ds(at, columns)
                total = dot_t(hid[slot, 0], g_ref[part, :]) + dot_t(hid[slot, 1], u_ref[part, :])
                res[slot, :, part] = total.astype(bf16)

            column_tiles(width, last)
            copies.append(
                [pltpu.make_async_copy(res.at[slot], out.at[here], sem.at[slot, 2])]
                + [
                    pltpu.make_async_copy(hid.at[slot, k], dst.at[here], sem.at[slot, k])
                    for k, dst in enumerate((gate_out, up_out))
                ]
            )
            for copy in copies[i]:
                copy.start()
            yield
        for copy in copies[-2] + copies[-1]:
            copy.wait()

    return Job(
        [grad, gate_pre, up_pre, gate_weight, up_weight, down_weight],
        [jax.ShapeDtypeStruct((rows, hidden), bf16)] * 2 + [jax.ShapeDtypeStruct((rows, width), bf16)],
        [
            pltpu.VMEM(grad.shape, bf16),
            pltpu.VMEM(gate_weight.shape, bf16),
            pltpu.VMEM(up_weight.shape, bf16),
            pltpu.VMEM(down_weight.shape, bf16),
            pltpu.VMEM((2, 2, STEP, hidden), f32),
            pltpu.VMEM((2, 2, STEP, hidden), bf16),
            pltpu.VMEM((2, STEP, width), bf16),
            DMA((4,)),
            DMA((2, 2)),
            DMA((2, 3)),
        ],
        2 * (rows // STEP),
        body,
    )


def ffn_back_plain(grad, gate_pre, up_pre, gate_weight, up_weight, down_weight):
    grad_gate, grad_up = before_activation(dot_t(grad, down_weight), gate_pre, up_pre)
    back = dot_t(grad_gate, gate_weight) + dot_t(grad_up, up_weight)
    return grad_gate, grad_up, back.astype(bf16)


def dispatch_job(rows, n_ws):
    n, count, width = rows.shape

    def body(rows, out, own, load_sem, ep_s, ep_r, y_s, y_r, c_s, c_r, x_s, x_r):
        e, w = lax.axis_index("ep"), lax.axis_index("ws")
        twin, other = flip(w, 1), flip(w, 2)
        sources = [e] + [flip(e, k) for k in range(1, n)]
        first = []
        for i, s in enumerate(sources[1:]):
            first.append(remote(rows.at[s], out.at[e, w], ep_s.at[i], ep_r.at[i], (s, w)))
            first[-1].start()
        load = pltpu.make_async_copy(rows.at[e], own, load_sem.at[0])
        load.start()
        over_y, to_twin, relayed = [], [], []

        def relay(j):
            over_y[j].wait_recv()
            block = out.at[sources[j], other]
            relayed.append(remote(block, block, x_s.at[j], x_r.at[j], (e, twin)))
            relayed[-1].start()

        for j, s in enumerate(sources):
            place = out.at[s, w]
            block = rows.at[e] if j == 0 else place
            if j:
                first[j - 1].wait_recv()
            over_y.append(remote(block, place, y_s.at[j], y_r.at[j], (e, other)))
            over_y[-1].start()
            to_twin.append(remote(block, place, c_s.at[j], c_r.at[j], (e, twin)))
            to_twin[-1].start()
            if j == 0:
                load.wait()
                store = pltpu.make_async_copy(own, out.at[e, w], load_sem.at[1])
                store.start()
            else:
                relay(j - 1)
            yield
        relay(n - 1)
        store.wait()
        for copy in first + over_y:
            copy.wait_send()
        for copy in to_twin + relayed:
            copy.wait()

    return Job(
        [rows],
        [jax.ShapeDtypeStruct((n, n_ws, count, width), rows.dtype)],
        [pltpu.VMEM((count, width), rows.dtype), DMA((2,)), DMA((n - 1,)), DMA((n - 1,))]
        + [DMA((n,)) for _ in range(6)],
        n,
        body,
        [(k, 0) for k in range(1, n)] + [(0, 1), (0, 2)],
    )


def combine_job(part):
    n, _, count, width = part.shape
    block = (n, count, width)

    def body(
        part, out, mine, core, sum_y, from_y, total, load_sem, c_s, c_r, y_s, y_r, ep_s, ep_r, own_sem
    ):
        e, w = lax.axis_index("ep"), lax.axis_index("ws")
        twin, other, last = flip(w, 1), flip(w, 2), flip(w, 3)
        targets = [flip(e, k) for k in far_first(n)] + [e]
        loads, cores = {}, {}
        for half, near, far in ((1, other, last), (0, w, twin)):
            for j, s in enumerate(targets):
                cores[half, j] = remote(
                    part.at[s, far], core.at[half, j], c_s.at[half, j], c_r.at[half, j], (e, twin)
                )
                cores[half, j].start()
                loads[half, j] = pltpu.make_async_copy(
                    part.at[s, near], mine.at[half, j], load_sem.at[half, j]
                )
                loads[half, j].start()
        over_y, back = [], []

        def send_y(j):
            over_y.append(remote(sum_y.at[j], from_y.at[j], y_s.at[j], y_r.at[j], (e, other)))
            over_y[-1].start()

        def send_back(j):
            back.append(remote(total.at[j], out.at[e], ep_s.at[j], ep_r.at[j], (targets[j], w)))
            back[-1].start()

        for j in range(n):
            loads[1, j].wait()
            cores[1, j].wait_recv()
            sum_y[j] = (mine[1, j].astype(f32) + core[1, j].astype(f32)).astype(bf16)
            if j:
                send_y(j - 1)
        loads[0, 0].wait()
        cores[0, 0].wait_recv()
        send_y(n - 1)
        for j in range(n):
            if j:
                loads[0, j].wait()
                cores[0, j].wait_recv()
            over_y[j].wait_recv()
            total[j] = (
                mine[0, j].astype(f32) + core[0, j].astype(f32) + from_y[j].astype(f32)
            ).astype(bf16)
            if j:
                send_back(j - 1)
            yield
        for copy in over_y + list(cores.values()):
            copy.wait_send()
        keep = pltpu.make_async_copy(total.at[n - 1], out.at[e], own_sem)
        keep.start()
        for copy in back:
            copy.wait()
        keep.wait()

    return Job(
        [part],
        [jax.ShapeDtypeStruct(block, part.dtype)],
        [
            pltpu.VMEM((2,) + block, part.dtype),
            pltpu.VMEM((2,) + block, part.dtype),
            pltpu.VMEM(block, part.dtype),
            pltpu.VMEM(block, part.dtype),
            pltpu.VMEM(block, part.dtype),
            DMA((2, n)),
            DMA((2, n)),
            DMA((2, n)),
            DMA((n,)),
            DMA((n,)),
            DMA((n - 1,)),
            DMA((n - 1,)),
            DMA,
        ],
        n,
        body,
        [(k, 0) for k in range(1, n)] + [(0, 1), (0, 2)],
    )


def exchange_job(rows):
    n = rows.shape[0]

    def body(rows, out, own, load_sem, ep_s, ep_r):
        e, w = lax.axis_index("ep"), lax.axis_index("ws")
        targets = [flip(e, k) for k in far_first(n)]
        copies = []
        for i, s in enumerate(targets):
            copies.append(remote(rows.at[s], out.at[e], ep_s.at[i], ep_r.at[i], (s, w)))
            copies[-1].start()
        load = pltpu.make_async_copy(rows.at[e], own, load_sem.at[0])
        load.start()
        load.wait()
        store = pltpu.make_async_copy(own, out.at[e], load_sem.at[1])
        store.start()
        yield
        store.wait()
        for copy in copies:
            copy.wait()

    return Job(
        [rows],
        [jax.ShapeDtypeStruct(rows.shape, rows.dtype)],
        [pltpu.VMEM(rows.shape[1:], rows.dtype), DMA((2,)), DMA((n - 1,)), DMA((n - 1,))],
        1,
        body,
        [(k, 0) for k in range(1, n)],
    )


def gather_weights_job(mine, normed, n, n_ws):
    rows, block = mine.shape
    routes = [(4, 0), (2, 0), (2, 4)]

    def body(
        mine, normed, out, seq, held, held_rows, load_sem, s_sem, r_sem, x_s, x_r, y_s, y_r, c_s, c_r, t_s, t_r
    ):
        e, w = lax.axis_index("ep"), lax.axis_index("ws")
        twin, other, near = flip(w, 1), flip(w, 2), flip(e, 1)
        copies = {}

        def send(hop, offset, half):
            k = routes.index((hop, offset))
            part = pl.ds(half * (rows // 2), rows // 2)
            at = pl.multiple_of(flip(e, offset) // 2 * block, block)
            place = out.at[part, pl.ds(at, block)]
            copies[hop, offset, half] = remote(
                place if offset else mine.at[part],
                place,
                s_sem.at[k, half],
                r_sem.at[k, half],
                (flip(e, hop), w),
            )
            copies[hop, offset, half].start()

        for half in range(2):
            for route in routes[:2]:
                send(*route, half)
        to_near = remote(normed, seq.at[e % 2, w], x_s, x_r, (near, w))
        to_near.start()
        over_y, to_twin, relays = [], [], []

        def spread_rows(k, half, src):
            place = seq.at[half, w]
            over_y.append(remote(src, place, y_s.at[k], y_r.at[k], (e, other)))
            over_y[k].start()
            to_twin.append(remote(src, place, c_s.at[k], c_r.at[k], (e, twin)))
            to_twin[k].start()

        def relay(k, half):
            over_y[k].wait_recv()
            place = seq.at[half, other]
            relays.append(remote(place, place, t_s.at[k], t_r.at[k], (e, twin)))
            relays[k].start()

        spread_rows(0, e % 2, normed)
        loads = fetch(((mine, held), (normed, held_rows)), load_sem)
        for load in loads:
            load.wait()
        own = out.at[:, pl.ds(pl.multiple_of(e // 2 * block, block), block)]
        stores = fetch(((held, own), (held_rows, seq.at[e % 2, w])), load_sem)
        yield
        to_near.wait_recv()
        spread_rows(1, near % 2, seq.at[near % 2, w])
        yield
        copies[4, 0, 0].wait_recv()
        send(2, 4, 0)
        yield
        relay(0, e % 2)
        copies[4, 0, 1].wait_recv()
        send(2, 4, 1)
        yield
        relay(1, near % 2)
        yield
        for store in stores:
            store.wait()
        for (_, offset, half), copy in copies.items():
            copy.wait_send()
            if (_, offset) != (4, 0):
                copy.wait_recv()
        to_near.wait_send()
        for copy in over_y:
            copy.wait_send()
        for copy in to_twin + relays:
            copy.wait()

    return Job(
        [mine, normed],
        [
            jax.ShapeDtypeStruct((rows, n // 2 * block), bf16),
            jax.ShapeDtypeStruct((2, n_ws) + normed.shape, bf16),
        ],
        [
            pltpu.VMEM(mine.shape, bf16),
            pltpu.VMEM(normed.shape, bf16),
            DMA((2,)),
            DMA((3, 2)),
            DMA((3, 2)),
            DMA,
            DMA,
        ]
        + [DMA((2,)) for _ in range(6)],
        5,
        body,
        [(1, 0), (2, 0), (4, 0), (0, 1), (0, 2)],
    )


def swap_job(blocks):
    def body(blocks, out, held, load_sem, s_sem, r_sem):
        e, w = lax.axis_index("ep"), lax.axis_index("ws")
        near = flip(e, 1)
        copy = remote(blocks.at[near % 2], out.at[e % 2], s_sem, r_sem, (near, w))
        copy.start()
        load = fetch(((blocks.at[e % 2], held),), load_sem)[0]
        load.wait()
        store = fetch(((held, out.at[e % 2]),), load_sem)[0]
        yield
        store.wait()
        copy.wait()

    return Job(
        [blocks],
        [jax.ShapeDtypeStruct(blocks.shape, blocks.dtype)],
        [pltpu.VMEM(blocks.shape[1:], blocks.dtype), DMA((1,)), DMA, DMA],
        1,
        body,
        [(1, 0)],
    )


def add_blocks(out, *refs):
    step = 64 if out.shape[1] > 1024 else 256

    def body(i, carry):
        at = pl.ds(pl.multiple_of(i * step, step), step)
        total = refs[0][at].astype(f32)
        for ref in refs[1:]:
            total = total + ref[at].astype(f32)
        out[at] = total.astype(bf16)
        return carry

    lax.fori_loop(0, out.shape[0] // step, body, 0)


def reduce_weights_job(pieces, part, n):
    rows = pieces.shape[0]
    block = pieces.shape[1] // (n // 2)
    offsets = (4, 0)

    def body(
        pieces, part, out, out_rows, mine, from_z, fourth, last_z, total, own, core, sum_y, from_y, total_near,
        from_near, total_rows, load_sem, z_s, z_r, w_load, c_s, c_r, y_s, y_r, x_s, x_r, sem
    ):
        e, w = lax.axis_index("ep"), lax.axis_index("ws")
        twin, other, last, near = flip(w, 1), flip(w, 2), flip(w, 3), flip(e, 1)

        def columns(s):
            return pieces.at[:, pl.ds(pl.multiple_of(s // 2 * block, block), block)]

        over_z = []
        for i, offset in enumerate(offsets):
            over_z.append(
                remote(columns(flip(e, offset + 2)), from_z.at[i], z_s.at[i], z_r.at[i], (flip(e, 2), w))
            )
            over_z[i].start()
        halves = (near % 2, e % 2)
        cores = {}
        for k, to in enumerate((last, twin)):
            for h, half in enumerate(halves):
                cores[h, k] = remote(
                    part.at[half, to], core.at[h, k], c_s.at[h, k], c_r.at[h, k], (e, twin)
                )
                cores[h, k].start()
        loads = fetch([(columns(flip(e, o)), mine.at[i]) for i, o in enumerate(offsets)], load_sem)
        own_loads = {}
        for h, half in enumerate(halves):
            for k, to in enumerate((other, w)):
                own_loads[h, k] = pltpu.make_async_copy(
                    part.at[half, to], own.at[h, k], w_load.at[h, k]
                )
                own_loads[h, k].start()
        yield
        over_y = []

        def send_y(h):
            over_y.append(remote(sum_y.at[h], from_y.at[h], y_s.at[h], y_r.at[h], (e, other)))
            over_y[h].start()

        for h in range(2):
            own_loads[h, 0].wait()
            cores[h, 0].wait_recv()
            add_blocks(sum_y.at[h], own.at[h, 0], core.at[h, 0])
            if h:
                send_y(0)
        yield
        loads[0].wait()
        over_z[0].wait_recv()
        send_y(1)
        add_blocks(fourth, mine.at[0], from_z.at[0])
        yield
        own_loads[0, 1].wait()
        cores[0, 1].wait_recv()
        over_y[0].wait_recv()
        far = remote(fourth, last_z, z_s.at[2], z_r.at[2], (flip(e, 4), w))
        far.start()
        add_blocks(total_near, own.at[0, 1], core.at[0, 1], from_y.at[0])
        yield
        own_loads[1, 1].wait()
        cores[1, 1].wait_recv()
        over_y[1].wait_recv()
        to_near = remote(total_near, from_near, x_s, x_r, (near, w))
        to_near.start()
        yield
        to_near.wait_recv()
        add_blocks(total_rows, own.at[1, 1], core.at[1, 1], from_y.at[1], from_near)
        loads[1].wait()
        over_z[1].wait_recv()
        far.wait_recv()
        add_blocks(total, mine.at[1], from_z.at[1], last_z)
        stores = fetch(((total_rows, out_rows), (total, out)), sem)
        for copy in over_z + list(cores.values()) + over_y + [far, to_near]:
            copy.wait_send()
        for store in stores:
            store.wait()

    one, rows_one = (rows, block), part.shape[2:]
    return Job(
        [pieces, part],
        [jax.ShapeDtypeStruct(one, bf16), jax.ShapeDtypeStruct(rows_one, bf16)],
        [pltpu.VMEM((2,) + one, bf16) for _ in range(2)]
        + [pltpu.VMEM(one, bf16) for _ in range(3)]
        + [pltpu.VMEM((2, 2) + rows_one, bf16) for _ in range(2)]
        + [pltpu.VMEM((2,) + rows_one, bf16) for _ in range(2)]
        + [pltpu.VMEM(rows_one, bf16) for _ in range(3)]
        + [DMA((2,)), DMA((3,)), DMA((3,)), DMA((2, 2)), DMA((2, 2)), DMA((2, 2))]
        + [DMA((2,)), DMA((2,)), DMA, DMA, DMA((2,))],
        5,
        body,
        [(1, 0), (2, 0), (4, 0), (0, 1), (0, 2)],
    )


def attend_kernel(spans, q_ref, kv_ref, out):
    count, _, slots, part = q_ref.shape
    for w, span in enumerate(spans):

        def head(h, carry, w=w, span=span):
            at = pl.multiple_of(h * HEAD_SIZE, HEAD_SIZE)
            columns = pl.ds(at, HEAD_SIZE)
            q, probs, _, values = head_probs(q_ref, kv_ref, w, span, at)
            mixed = dot(probs.astype(bf16), values)
            out[:, w, :, columns] = mixed.reshape(count, slots, HEAD_SIZE).astype(bf16)
            return carry

        lax.fori_loop(0, part // HEAD_SIZE, head, 0)


def slot_rows(ref, w, at):
    count, _, slots, _ = ref.shape
    rows = ref[:, w, :, pl.ds(at, HEAD_SIZE)].astype(f32)
    return rows.reshape(count * slots, HEAD_SIZE).astype(bf16)


def kv_place(kv, at):
    h = at // HEAD_SIZE
    column = pl.multiple_of(h // 2 * HEAD_SIZE, HEAD_SIZE)
    half = kv.shape[2] // 2
    value_column = pl.multiple_of(half + column, HEAD_SIZE)
    return h % 2, pl.ds(column, HEAD_SIZE), pl.ds(value_column, HEAD_SIZE)


def head_probs(q_ref, kv_ref, w, span, at):
    q = slot_rows(q_ref, w, at)
    side, key_columns, value_columns = kv_place(kv_ref, at)
    keys = kv_ref[side, :span, key_columns]
    values = kv_ref[side, :span, value_columns]
    scores = dot_t(q, keys) * HEAD_SIZE ** (-0.5)
    weight = jnp.exp(scores - jnp.max(scores, -1, keepdims=True))
    probs = weight / jnp.sum(weight, -1, keepdims=True)
    return q, probs, keys, values


def attend_call(queries, kv, spans):
    return pl.pallas_call(
        functools.partial(attend_kernel, spans),
        out_shape=jax.ShapeDtypeStruct(queries.shape, bf16),
        in_specs=[VM, VM],
        out_specs=VM,
        compiler_params=pltpu.CompilerParams(vmem_limit_bytes=VMEM_LIMIT),
        name="attend",
    )(queries, kv)


def attend_back_kernel(spans, q_ref, g_ref, kv_ref, grad_q, grad_kv, total):
    count, _, slots, part = q_ref.shape
    total[...] = jnp.zeros_like(total)
    for w, span in enumerate(spans):

        def head(h, carry, w=w, span=span):
            at = pl.multiple_of(h * HEAD_SIZE, HEAD_SIZE)
            columns = pl.ds(at, HEAD_SIZE)
            q, probs, keys, values = head_probs(q_ref, kv_ref, w, span, at)
            grad = slot_rows(g_ref, w, at)
            grad_probs = dot_t(grad, values)
            centred = jnp.sum(probs * grad_probs, -1, keepdims=True)
            grad_scores = (probs * (grad_probs - centred)).astype(bf16)
            grad_rows = dot(grad_scores, keys) * HEAD_SIZE ** (-0.5)
            grad_q[:, w, :, columns] = grad_rows.reshape(count, slots, HEAD_SIZE).astype(bf16)
            side, key_columns, value_columns = kv_place(kv_ref, at)
            total[side, :span, key_columns] += t_dot(grad_scores, q) * HEAD_SIZE ** (-0.5)
            total[side, :span, value_columns] += t_dot(probs.astype(bf16), grad)
            return carry

        lax.fori_loop(0, part // HEAD_SIZE, head, 0)
    grad_kv[...] = total[...].astype(bf16)


def attend_back_call(queries, grads, kv, spans):
    return pl.pallas_call(
        functools.partial(attend_back_kernel, spans),
        out_shape=[
            jax.ShapeDtypeStruct(queries.shape, bf16),
            jax.ShapeDtypeStruct(kv.shape, bf16),
        ],
        in_specs=[VM, VM, VM],
        out_specs=[VM, VM],
        scratch_shapes=[pltpu.VMEM(kv.shape, f32)],
        compiler_params=pltpu.CompilerParams(vmem_limit_bytes=VMEM_LIMIT),
        name="attend_back",
    )(queries, grads, kv)


def gather_kernel(n, n_ws, own, out, load_sem, w_s, w_r, ep_s, ep_r):
    e, w = lax.axis_index("ep"), lax.axis_index("ws")
    beside = [flip(w, k) for k in range(1, n_ws)]
    across = [flip(e, k) for k in far_first(n)]
    greet([(e, p) for p in beside] + [(s, w) for s in across])
    keep = pltpu.make_async_copy(own, out.at[e, w], load_sem)
    keep.start()
    first = []
    for i, p in enumerate(beside):
        first.append(remote(own, out.at[e, w], w_s.at[i], w_r.at[i], (e, p)))
        first[-1].start()
    keep.wait()
    for copy in first:
        copy.wait()
    second = []
    for i, s in enumerate(across):
        second.append(remote(out.at[e], out.at[e], ep_s.at[i], ep_r.at[i], (s, w)))
        second[-1].start()
    for copy in second:
        copy.wait()


def gather_call(own, n, n_ws):
    return pl.pallas_call(
        functools.partial(gather_kernel, n, n_ws),
        out_shape=jax.ShapeDtypeStruct((n, n_ws) + own.shape, own.dtype),
        in_specs=[VM],
        out_specs=VM,
        scratch_shapes=[DMA, DMA((n_ws - 1,)), DMA((n_ws - 1,)), DMA((n - 1,)), DMA((n - 1,))],
        compiler_params=pltpu.CompilerParams(collective_id=3, has_side_effects=True),
        name="gather_gains",
    )(own)


def reduce_kernel(n, n_ws, parts, out, held, all_parts, load_sem, w_s, w_r, ep_s, ep_r):
    e, w = lax.axis_index("ep"), lax.axis_index("ws")
    beside = [flip(w, k) for k in range(1, n_ws)]
    across = [flip(e, k) for k in far_first(n)]
    greet([(e, p) for p in beside] + [(s, w) for s in across])
    keep = pltpu.make_async_copy(parts.at[:, w], held.at[:, w], load_sem.at[0])
    keep.start()
    first = []
    for i, p in enumerate(beside):
        first.append(remote(parts.at[:, p], held.at[:, w], w_s.at[i], w_r.at[i], (e, p)))
        first[-1].start()
    keep.wait()
    for copy in first:
        copy.wait()
    keep = pltpu.make_async_copy(held.at[e], all_parts.at[e], load_sem.at[1])
    keep.start()
    second = []
    for i, s in enumerate(across):
        second.append(remote(held.at[s], all_parts.at[e], ep_s.at[i], ep_r.at[i], (s, w)))
        second[-1].start()
    keep.wait()
    for copy in second:
        copy.wait()
    out[...] = jnp.sum(jnp.sum(all_parts[...], 0), 0)


def reduce_call(parts):
    n, n_ws = parts.shape[:2]
    return pl.pallas_call(
        functools.partial(reduce_kernel, n, n_ws),
        out_shape=jax.ShapeDtypeStruct(parts.shape[2:], parts.dtype),
        in_specs=[VM],
        out_specs=VM,
        scratch_shapes=[
            pltpu.VMEM(parts.shape, parts.dtype),
            pltpu.VMEM(parts.shape, parts.dtype),
            DMA((2,)),
            DMA((n_ws - 1,)),
            DMA((n_ws - 1,)),
            DMA((n - 1,)),
            DMA((n - 1,)),
        ],
        compiler_params=pltpu.CompilerParams(collective_id=4, has_side_effects=True),
        name="reduce_gains",
    )(parts)


def small(n_ep):
    return n_ep == MIXTURE_EXPERTS and lax.axis_size("ws") == 4


PLAIN = {
    grad_job: lambda a, b: [t_dot(a, b)],
    pair_grad_job: lambda a, b, c: [jnp.stack([t_dot(a, b), t_dot(a, c)], 1)],
    split_job: lambda weight: [weight[:, 0], weight[:, 1]],
    ffn_job: ffn_plain,
    ffn_back_job: ffn_back_plain,
}


def beside(job, plain, arg, fills, collective_id, name):
    if job is None:
        return [plain(arg)] + [out for make, *rest in fills for out in PLAIN[make](*rest)]
    return run_jobs([job(arg)], [make(*rest) for make, *rest in fills], collective_id, name)


def exchange_plain(send):
    return lax.all_to_all(send, "ep", split_axis=0, concat_axis=0, tiled=True)


def exchange(send, *fills, collective_id=2, name="exchange"):
    job = exchange_job if small(send.shape[0]) else None
    return beside(job, exchange_plain, send, fills, collective_id, name)


def spread(rows, group):
    width = rows.shape[-1]
    blocks = rows.reshape(MIXTURE_EXPERTS, 1, ROWS, width)
    return jnp.broadcast_to(blocks, (MIXTURE_EXPERTS, group, ROWS, width)).reshape(
        MIXTURE_EXPERTS * group, ROWS, width
    )


def dispatch(rows, group, *fills, collective_id=0, name="dispatch"):
    width = rows.shape[-1]

    def plain(blocks):
        return lax.all_gather(exchange_plain(blocks), "ws", axis=1, tiled=False)

    job = functools.partial(dispatch_job, n_ws=4) if small(MIXTURE_EXPERTS * group) else None
    out = beside(job, plain, spread(rows, group), fills, collective_id, name)
    return [out[0].reshape(-1, width)] + list(out[1:])


def combine(partial, group, n_ep, n_ws, *fills, collective_id=1, name="combine"):
    width = partial.shape[-1]

    def plain(part):
        part = part.transpose(1, 0, 2, 3).reshape(n_ws * n_ep * ROWS, width)
        own = lax.psum_scatter(part, "ws", scatter_dimension=0, tiled=True)
        return exchange_plain(own.reshape(n_ep, ROWS, width))

    part = partial.reshape(n_ep, n_ws, ROWS, width)
    job = combine_job if small(n_ep) else None
    back, *rest = beside(job, plain, part, fills, collective_id, name)
    if group > 1:
        back = jnp.sum(back.reshape(MIXTURE_EXPERTS, group, ROWS, width).astype(f32), 1).astype(bf16)
    return [back.reshape(MIXTURE_EXPERTS * ROWS, width)] + rest


def slot_tables(routes, slots):
    target = jnp.where(slots < CAP, routes * ROWS + slots, -1)
    places = lax.broadcasted_iota(jnp.int32, (MIXTURE_EXPERTS * ROWS, target.shape[0]), 0)
    return [(places == target[None, :, k]).astype(bf16) for k in range(CHOSEN_EXPERTS)]


def norm_back(grad, unit, inverse, gain):
    gain_grad = jnp.sum(grad * unit, 0)
    scaled = grad * gain
    return (inverse * (scaled - unit * jnp.mean(scaled * unit, -1, keepdims=True)), gain_grad)


def heads_of(rows):
    return rows.reshape(rows.shape[0], -1, HEAD_SIZE)


def local(
    x_in,
    gain_attn,
    gain_ffn,
    key_value_weight,
    w_query,
    w_output,
    w_in,
    w_out,
    gate_attn,
    gate_ffn,
    route_attn,
    slot_attn,
    route_ffn,
    slot_ffn,
    cotangent,
):
    n_ep = lax.axis_size("ep")
    n_ws = lax.axis_size("ws")
    group = n_ep // MIXTURE_EXPERTS
    local_tokens, width = x_in.shape
    key_value_width = KEY_VALUE_HEADS * HEAD_SIZE
    part = w_query.shape[2]
    own_width = group * part
    sequence = n_ws * local_tokens
    place = lax.axis_index("ws")
    scale = HEAD_SIZE ** (-0.5)

    fused = small(n_ep) and key_value_weight.shape[1] == HEAD_SIZE
    short = fused and gain_attn.shape[0] == 64
    if short:
        gains = jnp.concatenate([gain_attn, gain_ffn], 0).astype(f32)[None]
        gains = gather_call(gains, n_ep, n_ws).reshape(n_ep * n_ws, 2, -1)
        gain_one, gain_two = gains[:, 0].reshape(-1), gains[:, 1].reshape(-1)
    else:
        gain_one = lax.all_gather(gain_attn, ("ep", "ws"), axis=0, tiled=True).astype(f32)
        gain_two = lax.all_gather(gain_ffn, ("ep", "ws"), axis=0, tiled=True).astype(f32)
    plain = group == 1 and key_value_weight.shape[1] == HEAD_SIZE
    if plain:
        half = n_ep // 2
        there = [
            (e * n_ws + w, (w + n_ws * (e // half)) * n_ws + e % half)
            for e in range(n_ep)
            for w in range(n_ws)
        ]
        mine = lax.ppermute(key_value_weight, ("ep", "ws"), there)
    else:
        whole = lax.all_gather(key_value_weight, ("ep", "ws"), axis=1, tiled=True)
        whole = whole.reshape(width, 2 * group, n_ws, part)
        kv_own = lax.dynamic_index_in_dim(whole, place, 2, keepdims=False).reshape(width, -1)

    inputs = x_in.astype(f32)
    inverse_one = lax.rsqrt(jnp.mean(inputs * inputs, -1, keepdims=True) + EPS)
    unit_one = inputs * inverse_one
    normed = (unit_one * gain_one).astype(bf16)
    attn_pairs = slot_tables(route_attn, slot_attn)
    ffn_pairs = slot_tables(route_ffn, slot_ffn)
    attn_tokens = attn_pairs[0] + attn_pairs[1]
    ffn_tokens = ffn_pairs[0] + ffn_pairs[1]

    slots_one = dot(attn_tokens, normed).astype(bf16)
    if fused:
        rows_one, kv_own, normed_sequence, gate_weight, up_weight = run_jobs(
            [
                dispatch_job(slots_one.reshape(n_ep, ROWS, width), n_ws),
                gather_weights_job(mine, normed, n_ep, n_ws),
            ],
            [split_job(w_in[0])],
            10,
            "dispatch_weights",
        )
        rows_one = rows_one.reshape(-1, width)
        normed_sequence = normed_sequence.reshape(2 * sequence, width)
    else:
        if plain:
            kv_own = lax.all_gather(mine, "ep", axis=1, tiled=True)
        normed_sequence = lax.all_gather(normed, "ws", axis=0, tiled=True)
        rows_one, gate_weight, up_weight = dispatch(slots_one, group, (split_job, w_in[0]))
    kv = dot(normed_sequence, kv_own).astype(bf16)
    if not fused:
        keys = kv[:, :own_width].reshape(sequence, -1, HEAD_SIZE)
        values = kv[:, own_width:].reshape(sequence, -1, HEAD_SIZE)

    owner_query = dot(rows_one, w_query[0]).astype(bf16)
    owner_query = owner_query.reshape(n_ep, n_ws * ROWS, part)
    if fused:
        queries, kv = run_jobs(
            [exchange_job(owner_query), swap_job(kv.reshape(2, sequence, -1))], [], 13, "exchange_kv"
        )
    else:
        queries = exchange(owner_query)[0]
    queries = queries.reshape(MIXTURE_EXPERTS, group, n_ws, ROWS, part)
    spans = [(w * local_tokens // BLOCK + 1) * BLOCK for w in range(n_ws)]

    def by_block(rows):
        rows = rows.reshape(MIXTURE_EXPERTS, group, n_ws, ROWS, part)
        return [
            rows[:, :, w].transpose(0, 2, 1, 3).reshape(-1, own_width // HEAD_SIZE, HEAD_SIZE)
            for w in range(n_ws)
        ]

    def to_experts(pieces):
        rows = jnp.stack(
            [
                piece.reshape(MIXTURE_EXPERTS, ROWS, group, part).transpose(0, 2, 1, 3)
                for piece in pieces
            ],
            2,
        )
        return rows.reshape(n_ep, n_ws * ROWS, part)

    if fused:
        queries = queries.reshape(n_ep, n_ws, ROWS, part)
        mixed = attend_call(queries, kv, spans).reshape(n_ep, n_ws * ROWS, part)
    else:
        kept = []
        mixed_pieces = []
        for q, span in zip(by_block(queries), spans):
            scores = (
                jnp.einsum("rhd,shd->hrs", q, keys[:span], preferred_element_type=f32) * scale
            )
            probs = jax.nn.softmax(scores, axis=-1)
            mixed = jnp.einsum(
                "hrs,shd->rhd", probs.astype(bf16), values[:span], preferred_element_type=f32
            )
            kept.append((q, probs))
            mixed_pieces.append(mixed.astype(bf16))
        mixed = to_experts(mixed_pieces)
    owner_mixed = exchange(mixed)[0].reshape(-1, part)
    attn_slots = combine(dot(owner_mixed, w_output[0]).astype(bf16), group, n_ep, n_ws, collective_id=11)[0]

    def weighted(pairs, gates, slot_values):
        return sum(gates[:, k : k + 1] * t_dot(pairs[k], slot_values) for k in range(2))

    def to_slots(pairs, gates, values):
        return sum(
            dot(pairs[k], (gates[:, k : k + 1] * values).astype(bf16)) for k in range(2)
        ).astype(bf16)

    hidden_state = inputs + weighted(attn_pairs, gate_attn, attn_slots)
    inverse_two = lax.rsqrt(jnp.mean(hidden_state * hidden_state, -1, keepdims=True) + EPS)
    unit_two = hidden_state * inverse_two
    normed_two = (unit_two * gain_two).astype(bf16)

    grad_out = cotangent.astype(f32)
    grad_slots = to_slots(ffn_pairs, gate_ffn, grad_out)
    expert_rows = dispatch(dot(ffn_tokens, normed_two).astype(bf16), group)[0]
    expert_grad, gate_pre, up_pre, activated, forward_part = dispatch(
        grad_slots,
        group,
        (ffn_job, expert_rows, gate_weight, up_weight, w_out[0]),
        collective_id=5,
        name="dispatch_ffn",
    )
    ffn_slots, grad_gate, grad_up, back_two = combine(
        forward_part,
        group,
        n_ep,
        n_ws,
        (ffn_back_job, expert_grad, gate_pre, up_pre, gate_weight, up_weight, w_out[0]),
        collective_id=1,
        name="combine_ffn_back",
    )
    result = hidden_state + weighted(ffn_pairs, gate_ffn, ffn_slots)
    back_slots, grad_second = combine(
        back_two,
        group,
        n_ep,
        n_ws,
        (grad_job, activated, expert_grad),
        collective_id=6,
        name="combine_grad_out",
    )

    grad_normed_two = t_dot(ffn_tokens, back_slots)
    grad_hidden_norm, grad_gain_two = norm_back(grad_normed_two, unit_two, inverse_two, gain_two)
    grad_hidden = grad_out + grad_hidden_norm
    owner_grad, grad_first = dispatch(
        to_slots(attn_pairs, gate_attn, grad_hidden),
        group,
        (pair_grad_job, expert_rows, grad_gate, grad_up),
        collective_id=7,
        name="dispatch_grad_in",
    )
    back_mixed = dot_t(owner_grad, w_output[0]).astype(bf16)
    mixed_grads, grad_output = exchange(
        back_mixed.reshape(n_ep, n_ws * ROWS, part),
        (grad_job, owner_mixed, owner_grad),
        collective_id=8,
        name="exchange_grad_output",
    )

    if fused:
        mixed_grads = mixed_grads.reshape(n_ep, n_ws, ROWS, part)
        query_grads, grad_kv_rows = attend_back_call(queries, mixed_grads, kv, spans)
        query_grads = query_grads.reshape(n_ep, n_ws * ROWS, part)
    else:
        grad_keys, grad_values, query_pieces = 0.0, 0.0, []
        for (q, probs), grad, span in zip(kept, by_block(mixed_grads), spans):
            grad_probs = jnp.einsum("rhd,shd->hrs", grad, values[:span], preferred_element_type=f32)
            centred = jnp.sum(probs * grad_probs, -1, keepdims=True)
            grad_scores = (probs * (grad_probs - centred)).astype(bf16)
            grad_q = (
                jnp.einsum("hrs,shd->rhd", grad_scores, keys[:span], preferred_element_type=f32)
                * scale
            )
            query_pieces.append(grad_q.astype(bf16))
            pad = ((0, sequence - span), (0, 0), (0, 0))
            piece = jnp.einsum("hrs,rhd->shd", grad_scores, q, preferred_element_type=f32) * scale
            grad_keys = grad_keys + jnp.pad(piece, pad)
            piece = jnp.einsum(
                "hrs,rhd->shd", probs.astype(bf16), grad, preferred_element_type=f32
            )
            grad_values = grad_values + jnp.pad(piece, pad)
        grad_kv_rows = jnp.concatenate(
            [grad_keys.reshape(sequence, -1), grad_values.reshape(sequence, -1)], 1
        ).astype(bf16)
        query_grads = to_experts(query_pieces)
    if fused:
        owner_grad_query, grad_kv_rows = run_jobs(
            [exchange_job(query_grads), swap_job(grad_kv_rows)], [], 14, "exchange_grad_kv"
        )
        owner_grad_query = owner_grad_query.reshape(-1, part)
        grad_kv_rows = grad_kv_rows.reshape(2 * sequence, -1)
    else:
        owner_grad_query = exchange(query_grads)[0].reshape(-1, part)
    grad_kv = t_dot(normed_sequence, grad_kv_rows)
    from_kv = dot_t(grad_kv_rows, kv_own).astype(bf16)
    back_normed = dot_t(owner_grad_query, w_query[0]).astype(bf16)
    if fused:
        normed_back, piece, from_kv, grad_query = run_jobs(
            [
                combine_job(back_normed.reshape(n_ep, n_ws, ROWS, width)),
                reduce_weights_job(
                    grad_kv.astype(bf16), from_kv.reshape(2, n_ws, local_tokens, width), n_ep
                ),
            ],
            [grad_job(rows_one, owner_grad_query)],
            9,
            "combine_weights",
        )
        normed_back = normed_back.reshape(-1, width)
    else:
        normed_back, grad_query = combine(
            back_normed, group, n_ep, n_ws, (grad_job, rows_one, owner_grad_query)
        )
    if fused:
        back = [(b, a) for a, b in there]
        grad_kv_shard = lax.ppermute(piece, ("ep", "ws"), back).astype(f32)
    elif plain:
        pieces = grad_kv.reshape(width, n_ep, HEAD_SIZE).transpose(1, 0, 2).astype(bf16)
        piece = lax.psum_scatter(pieces, "ep", scatter_dimension=0, tiled=False)
        grad_kv_shard = lax.ppermute(piece, ("ep", "ws"), [(b, a) for a, b in there]).astype(f32)
    else:
        mask = (jnp.arange(n_ws) == place)[None, None, :, None]
        pieces = jnp.where(mask, grad_kv.reshape(width, 2 * group, 1, part), 0.0)
        pieces = pieces.reshape(width, 2 * key_value_width).astype(bf16)
        grad_kv_shard = lax.psum_scatter(
            pieces, ("ep", "ws"), scatter_dimension=1, tiled=True
        ).astype(f32)
    if not fused:
        from_kv = lax.psum_scatter(from_kv, "ws", scatter_dimension=0, tiled=True)
    grad_normed = t_dot(attn_tokens, normed_back) + from_kv.astype(f32)
    grad_input_norm, grad_gain_one = norm_back(grad_normed, unit_one, inverse_one, gain_one)
    grad_input = grad_hidden + grad_input_norm
    gain_grads = jnp.stack([grad_gain_one, grad_gain_two], 0)
    if short:
        parts = gain_grads.reshape(2, n_ep, n_ws, -1).transpose(1, 2, 0, 3)
        gain_shards = reduce_call(parts.reshape(n_ep, n_ws, 1, -1)).reshape(2, -1)
    else:
        gain_shards = lax.psum_scatter(
            gain_grads, ("ep", "ws"), scatter_dimension=1, tiled=True
        )
    return (
        result.astype(bf16),
        grad_input,
        gain_shards[0],
        gain_shards[1],
        grad_kv_shard,
        grad_query[None],
        grad_output[None],
        grad_first[None],
        grad_second[None],
    )


def solution(mesh):
    both = ("ep", "ws")
    rows, vector, columns = P(both, None), P(both), P(None, both)
    return jax.shard_map(
        local,
        mesh=mesh,
        in_specs=(
            rows,
            vector,
            vector,
            columns,
            P("ep", None, "ws"),
            P("ep", "ws", None),
            P("ep", None, None, "ws"),
            P("ep", "ws", None),
            rows,
            rows,
            rows,
            rows,
            rows,
            rows,
            rows,
        ),
        out_specs=(
            rows,
            rows,
            vector,
            vector,
            columns,
            P("ep", None, "ws"),
            P("ep", "ws", None),
            P("ep", None, None, "ws"),
            P("ep", "ws", None),
        ),
        check_vma=False,
    )
```

```python
import functools

import jax
import jax.numpy as jnp
from jax import lax
from jax.experimental import pallas as pl
from jax.experimental.pallas import tpu as pltpu
from jax.sharding import PartitionSpec as P

KEY_VALUE_HEADS = 16
HEAD_SIZE = 128
MIXTURE_EXPERTS = 8
CHOSEN_EXPERTS = 2
BLOCK = 256
CAP = 36
ROWS = 40

EPS = 1e-06
very_negative = -1e30
f32 = jnp.float32
bf16 = jnp.bfloat16
MESH = pl.DeviceIdType.MESH
ANY = pl.BlockSpec(memory_space=pl.ANY)
VM = pl.BlockSpec(memory_space=pltpu.VMEM)
DMA = pltpu.SemaphoreType.DMA
STEP = 256
VMEM_LIMIT = 60 << 20


def dot(a, b):
    return jnp.dot(a, b, preferred_element_type=f32)


def dot_t(a, b):
    return lax.dot_general(a, b, (((1,), (1,)), ((), ())), preferred_element_type=f32)


def t_dot(a, b):
    return lax.dot_general(a, b, (((0,), (0,)), ((), ())), preferred_element_type=f32)


def flip(index, bits):
    out, bit = index, 1
    while bit <= bits:
        if bits & bit:
            out = out + bit - 2 * bit * ((index // bit) % 2)
        bit *= 2
    return out


def far_first(n):
    return sorted(range(1, n), key=lambda k: (-((k // 2).bit_length()), k))


def greet(partners):
    barrier = pltpu.get_barrier_semaphore()
    for partner in partners:
        pl.semaphore_signal(barrier, inc=1, device_id=partner, device_id_type=MESH)
    pl.semaphore_wait(barrier, len(partners))


def remote(src, dst, send, recv, device):
    return pltpu.make_async_remote_copy(
        src_ref=src, dst_ref=dst, send_sem=send, recv_sem=recv, device_id=device, device_id_type=MESH
    )


class Job:
    def __init__(self, args, outs, scratch, steps, body, partners=()):
        self.args, self.outs, self.scratch, self.steps, self.body = args, outs, scratch, steps, body
        self.partners = partners


def run_jobs(jobs, fills, collective_id, name):
    whole = jobs + fills
    args = [a for job in whole for a in job.args]
    outs = [o for job in whole for o in job.outs]
    scratch = [x for job in whole for x in job.scratch]
    turns = sorted((k / job.steps, i) for i, job in enumerate(jobs) for k in range(job.steps))
    partners = sorted({p for job in jobs for p in job.partners})

    def kernel(*refs):
        bodies, at = [], [0, len(args), len(args) + len(outs)]
        for job in whole:
            own = []
            for k, part in enumerate((job.args, job.outs, job.scratch)):
                own.append(refs[at[k] : at[k] + len(part)])
                at[k] += len(part)
            bodies.append(job.body(*own[0], *own[1], *own[2]))
        moves, work = bodies[: len(jobs)], bodies[len(jobs) :]
        queue = [g for g, job in zip(work, fills) for _ in range(job.steps)]
        for g in work:
            next(g)
        e, w = lax.axis_index("ep"), lax.axis_index("ws")
        greet([(flip(e, p), flip(w, q)) for p, q in partners])
        done = 0
        for k, (_, i) in enumerate(turns):
            next(moves[i])
            target = (k + 1) * len(queue) // len(turns)
            while done < target:
                next(queue[done])
                done += 1
        for g in moves + work:
            for _ in g:
                pass

    return pl.pallas_call(
        kernel,
        out_shape=outs,
        in_specs=[ANY] * len(args),
        out_specs=[ANY] * len(outs),
        scratch_shapes=scratch,
        compiler_params=pltpu.CompilerParams(
            collective_id=collective_id, has_side_effects=True, vmem_limit_bytes=VMEM_LIMIT
        ),
        name=name,
    )(*args)


def fetch(pairs, sem):
    copies = [
        pltpu.make_async_copy(src, dst, sem.at[i]) for i, (src, dst) in enumerate(pairs)
    ]
    for copy in copies:
        copy.start()
    return copies


def blocks_of(size):
    return [(start, min(STEP, size - start)) for start in range(0, size, STEP)]


def column_tiles(width, tile):
    def body(c, carry):
        tile(pl.multiple_of(c * STEP, STEP), STEP)
        return carry

    lax.fori_loop(0, width // STEP, body, 0)
    if width % STEP:
        tile(width // STEP * STEP, width % STEP)


def grad_job(a, b):
    depth, rows = a.shape
    width = b.shape[1]

    def body(a_hbm, b_hbm, out, a_ref, b_ref, turned, held, load_sem, sem):
        loads = fetch(((a_hbm, a_ref), (b_hbm, b_ref)), load_sem)
        yield
        for load in loads:
            load.wait()
        copies = []
        for i, (start, size) in enumerate(blocks_of(rows)):
            if i >= 2:
                copies[i - 2].wait()
            turned[:size] = a_ref[:, start : start + size].T

            def tile(at, columns, slot=i % 2, size=size):
                held[slot, :size, pl.ds(at, columns)] = jnp.dot(
                    turned[:size], b_ref[:, pl.ds(at, columns)], preferred_element_type=f32
                )

            column_tiles(width, tile)
            copies.append(
                pltpu.make_async_copy(
                    held.at[i % 2, pl.ds(0, size)], out.at[pl.ds(start, size)], sem.at[i % 2]
                )
            )
            copies[i].start()
            yield
        for copy in copies[-2:]:
            copy.wait()

    return Job(
        [a, b],
        [jax.ShapeDtypeStruct((rows, width), f32)],
        [
            pltpu.VMEM(a.shape, bf16),
            pltpu.VMEM(b.shape, bf16),
            pltpu.VMEM((STEP, depth), bf16),
            pltpu.VMEM((2, STEP, width), f32),
            DMA((2,)),
            DMA((2,)),
        ],
        len(blocks_of(rows)),
        body,
    )


def pair_grad_job(a, first, second):
    depth, rows = a.shape
    tiles = first.shape[1] // 128

    def body(a_hbm, f_hbm, s_hbm, out, a_ref, f_ref, s_ref, turned, held, load_sem, sem):
        loads = fetch(((a_hbm, a_ref), (f_hbm, f_ref), (s_hbm, s_ref)), load_sem)
        flat = held.reshape(2 * tiles * STEP * 2, 128)
        yield
        for load in loads:
            load.wait()
        copies = []
        for i, (start, size) in enumerate(blocks_of(rows)):
            if i >= 2:
                for copy in copies[i - 2]:
                    copy.wait()
            turned[:size] = a_ref[:, start : start + size].T

            def tile(at, columns, slot=i % 2, size=size):
                for j, b_ref in enumerate((f_ref, s_ref)):
                    r = jnp.dot(
                        turned[:size], b_ref[:, pl.ds(at, columns)], preferred_element_type=f32
                    )
                    for half in range(columns // 128):
                        base = (slot * tiles + at // 128 + half) * (2 * STEP) + j
                        flat[pl.ds(base, size, stride=2), :] = r[:, half * 128 : half * 128 + 128]

            column_tiles(tiles * 128, tile)
            copies.append(
                [
                    pltpu.make_async_copy(
                        held.at[i % 2, c, pl.ds(0, size)],
                        out.at[pl.ds(start, size), :, pl.ds(c * 128, 128)],
                        sem.at[i % 2, c],
                    )
                    for c in range(tiles)
                ]
            )
            for copy in copies[i]:
                copy.start()
            yield
        for copy in copies[-2] + copies[-1]:
            copy.wait()

    return Job(
        [a, first, second],
        [jax.ShapeDtypeStruct((rows, 2, tiles * 128), f32)],
        [
            pltpu.VMEM(a.shape, bf16),
            pltpu.VMEM(first.shape, bf16),
            pltpu.VMEM(second.shape, bf16),
            pltpu.VMEM((STEP, depth), bf16),
            pltpu.VMEM((2, tiles, STEP, 2, 128), f32),
            DMA((3,)),
            DMA((2, tiles)),
        ],
        len(blocks_of(rows)),
        body,
    )


def split_job(weight):
    rows, _, width = weight.shape

    def body(w_hbm, first, second, block, wide, held, load_sem, sem):
        flat = wide.reshape(2 * STEP, 128)
        steps = rows // STEP

        def load(i):
            return pltpu.make_async_copy(
                w_hbm.at[pl.ds(i * STEP, STEP)], block.at[i % 2], load_sem.at[i % 2]
            )

        load(0).start()
        yield
        copies = []
        for i in range(steps):
            slot = i % 2
            if i + 1 < steps:
                load(i + 1).start()
            load(i).wait()
            if i >= 2:
                for copy in copies[i - 2]:
                    copy.wait()

            def tile(c, carry, slot=slot):
                at = pl.ds(pl.multiple_of(c * 128, 128), 128)
                wide[...] = block[slot, :, :, at].astype(f32)
                for j in range(2):
                    held[slot, j, :, at] = flat[pl.ds(j, STEP, stride=2), :].astype(bf16)
                return carry

            lax.fori_loop(0, width // 128, tile, 0)
            copies.append(
                [
                    pltpu.make_async_copy(
                        held.at[slot, j], out.at[pl.ds(i * STEP, STEP)], sem.at[slot, j]
                    )
                    for j, out in enumerate((first, second))
                ]
            )
            for copy in copies[i]:
                copy.start()
            yield
        for copy in copies[-2] + copies[-1]:
            copy.wait()

    return Job(
        [weight],
        [jax.ShapeDtypeStruct((rows, width), bf16)] * 2,
        [
            pltpu.VMEM((2, STEP, 2, width), bf16),
            pltpu.VMEM((STEP, 2, 128), f32),
            pltpu.VMEM((2, 2, STEP, width), bf16),
            DMA((2,)),
            DMA((2, 2)),
        ],
        rows // STEP,
        body,
    )


def ffn_job(x, gate_weight, up_weight, down_weight):
    rows, width = x.shape
    hidden = gate_weight.shape[1]

    def body(
        x_hbm, g_hbm, u_hbm, d_hbm, gate_out, up_out, act_out, out, x_ref, g_ref, u_ref, d_ref, pre, act, res,
        load_sem, sem
    ):
        loads = fetch(((x_hbm, x_ref), (g_hbm, g_ref), (u_hbm, u_ref), (d_hbm, d_ref)), load_sem)
        yield
        for load in loads:
            load.wait()
        copies = []
        for i, (start, size) in enumerate(blocks_of(rows)):
            slot = i % 2
            here = pl.ds(start, size)
            if i >= 2:
                for copy in copies[i - 2]:
                    copy.wait()

            def tile(at, columns, slot=slot, start=start, size=size):
                part = pl.ds(at, columns)
                left = x_ref[start : start + size]
                gate = dot(left, g_ref[:, part])
                up = dot(left, u_ref[:, part])
                pre[slot, 0, :, part] = gate
                pre[slot, 1, :, part] = up
                act[slot, :, part] = (gate * jax.nn.sigmoid(gate) * up).astype(bf16)

            column_tiles(hidden, tile)
            yield

            def last(at, columns, slot=slot):
                part = pl.ds(at, columns)
                res[slot, :, part] = dot(act[slot], d_ref[:, part]).astype(bf16)

            column_tiles(width, last)
            copies.append(
                [
                    pltpu.make_async_copy(src.at[slot], dst.at[here], sem.at[slot, k])
                    for k, (src, dst) in enumerate(((act, act_out), (res, out)))
                ]
                + [
                    pltpu.make_async_copy(pre.at[slot, k], dst.at[here], sem.at[slot, 2 + k])
                    for k, dst in enumerate((gate_out, up_out))
                ]
            )
            for copy in copies[i]:
                copy.start()
            yield
        for copy in copies[-2] + copies[-1]:
            copy.wait()

    return Job(
        [x, gate_weight, up_weight, down_weight],
        [jax.ShapeDtypeStruct((rows, hidden), f32)] * 2
        + [jax.ShapeDtypeStruct((rows, hidden), bf16), jax.ShapeDtypeStruct((rows, width), bf16)],
        [
            pltpu.VMEM(x.shape, bf16),
            pltpu.VMEM(gate_weight.shape, bf16),
            pltpu.VMEM(up_weight.shape, bf16),
            pltpu.VMEM(down_weight.shape, bf16),
            pltpu.VMEM((2, 2, STEP, hidden), f32),
            pltpu.VMEM((2, STEP, hidden), bf16),
            pltpu.VMEM((2, STEP, width), bf16),
            DMA((4,)),
            DMA((2, 4)),
        ],
        2 * (rows // STEP),
        body,
    )


def ffn_plain(x, gate_weight, up_weight, down_weight):
    gate_pre, up_pre = dot(x, gate_weight), dot(x, up_weight)
    activated = (gate_pre * jax.nn.sigmoid(gate_pre) * up_pre).astype(bf16)
    return gate_pre, up_pre, activated, dot(activated, down_weight).astype(bf16)


def before_activation(grad_act, gate_pre, up_pre):
    sigmoid_gate = jax.nn.sigmoid(gate_pre)
    grad_up = (grad_act * gate_pre * sigmoid_gate).astype(bf16)
    grad_gate = (
        grad_act * up_pre * sigmoid_gate * (1.0 + gate_pre * (1.0 - sigmoid_gate))
    ).astype(bf16)
    return grad_gate, grad_up


def ffn_back_job(grad, gate_pre, up_pre, gate_weight, up_weight, down_weight):
    rows, width = grad.shape
    hidden = gate_weight.shape[1]

    def body(
        x_hbm, gp_hbm, up_hbm, g_hbm, u_hbm, d_hbm, gate_out, up_out, out, x_ref, g_ref, u_ref, d_ref, pre, hid,
        res, load_sem, pre_sem, sem
    ):
        loads = fetch(((x_hbm, x_ref), (g_hbm, g_ref), (u_hbm, u_ref), (d_hbm, d_ref)), load_sem)

        def load_pre(i):
            here = pl.ds(i * STEP, STEP)
            return [
                pltpu.make_async_copy(src.at[here], pre.at[i % 2, k], pre_sem.at[i % 2, k])
                for k, src in enumerate((gp_hbm, up_hbm))
            ]

        for copy in load_pre(0):
            copy.start()
        yield
        for load in loads:
            load.wait()
        copies = []
        steps = rows // STEP
        for i in range(steps):
            slot, start = i % 2, i * STEP
            here = pl.ds(start, STEP)
            if i + 1 < steps:
                for copy in load_pre(i + 1):
                    copy.start()
            for copy in load_pre(i):
                copy.wait()
            if i >= 2:
                for copy in copies[i - 2]:
                    copy.wait()

            def tile(at, columns, slot=slot, start=start):
                part = pl.ds(at, columns)
                grad_act = dot_t(x_ref[start : start + STEP], d_ref[part, :])
                pair = before_activation(grad_act, pre[slot, 0, :, part], pre[slot, 1, :, part])
                hid[slot, 0, :, part], hid[slot, 1, :, part] = pair

            column_tiles(hidden, tile)
            yield

            def last(at, columns, slot=slot):
                part = pl.ds(at, columns)
                total = dot_t(hid[slot, 0], g_ref[part, :]) + dot_t(hid[slot, 1], u_ref[part, :])
                res[slot, :, part] = total.astype(bf16)

            column_tiles(width, last)
            copies.append(
                [pltpu.make_async_copy(res.at[slot], out.at[here], sem.at[slot, 2])]
                + [
                    pltpu.make_async_copy(hid.at[slot, k], dst.at[here], sem.at[slot, k])
                    for k, dst in enumerate((gate_out, up_out))
                ]
            )
            for copy in copies[i]:
                copy.start()
            yield
        for copy in copies[-2] + copies[-1]:
            copy.wait()

    return Job(
        [grad, gate_pre, up_pre, gate_weight, up_weight, down_weight],
        [jax.ShapeDtypeStruct((rows, hidden), bf16)] * 2 + [jax.ShapeDtypeStruct((rows, width), bf16)],
        [
            pltpu.VMEM(grad.shape, bf16),
            pltpu.VMEM(gate_weight.shape, bf16),
            pltpu.VMEM(up_weight.shape, bf16),
            pltpu.VMEM(down_weight.shape, bf16),
            pltpu.VMEM((2, 2, STEP, hidden), f32),
            pltpu.VMEM((2, 2, STEP, hidden), bf16),
            pltpu.VMEM((2, STEP, width), bf16),
            DMA((4,)),
            DMA((2, 2)),
            DMA((2, 3)),
        ],
        2 * (rows // STEP),
        body,
    )


def ffn_back_plain(grad, gate_pre, up_pre, gate_weight, up_weight, down_weight):
    grad_gate, grad_up = before_activation(dot_t(grad, down_weight), gate_pre, up_pre)
    back = dot_t(grad_gate, gate_weight) + dot_t(grad_up, up_weight)
    return grad_gate, grad_up, back.astype(bf16)


def dispatch_job(rows, n_ws):
    n, count, width = rows.shape

    def body(rows, out, own, load_sem, ep_s, ep_r, y_s, y_r, c_s, c_r, x_s, x_r):
        e, w = lax.axis_index("ep"), lax.axis_index("ws")
        twin, other = flip(w, 1), flip(w, 2)
        sources = [e] + [flip(e, k) for k in range(1, n)]
        first = []
        for i, s in enumerate(sources[1:]):
            first.append(remote(rows.at[s], out.at[e, w], ep_s.at[i], ep_r.at[i], (s, w)))
            first[-1].start()
        load = pltpu.make_async_copy(rows.at[e], own, load_sem.at[0])
        load.start()
        over_y, to_twin, relayed = [], [], []

        def relay(j):
            over_y[j].wait_recv()
            block = out.at[sources[j], other]
            relayed.append(remote(block, block, x_s.at[j], x_r.at[j], (e, twin)))
            relayed[-1].start()

        for j, s in enumerate(sources):
            place = out.at[s, w]
            block = rows.at[e] if j == 0 else place
            if j:
                first[j - 1].wait_recv()
            over_y.append(remote(block, place, y_s.at[j], y_r.at[j], (e, other)))
            over_y[-1].start()
            to_twin.append(remote(block, place, c_s.at[j], c_r.at[j], (e, twin)))
            to_twin[-1].start()
            if j == 0:
                load.wait()
                store = pltpu.make_async_copy(own, out.at[e, w], load_sem.at[1])
                store.start()
            else:
                relay(j - 1)
            yield
        relay(n - 1)
        store.wait()
        for copy in first + over_y:
            copy.wait_send()
        for copy in to_twin + relayed:
            copy.wait()

    return Job(
        [rows],
        [jax.ShapeDtypeStruct((n, n_ws, count, width), rows.dtype)],
        [pltpu.VMEM((count, width), rows.dtype), DMA((2,)), DMA((n - 1,)), DMA((n - 1,))]
        + [DMA((n,)) for _ in range(6)],
        n,
        body,
        [(k, 0) for k in range(1, n)] + [(0, 1), (0, 2)],
    )


def combine_job(part):
    n, _, count, width = part.shape
    block = (n, count, width)

    def body(
        part, out, mine, core, sum_y, from_y, total, load_sem, c_s, c_r, y_s, y_r, ep_s, ep_r, own_sem
    ):
        e, w = lax.axis_index("ep"), lax.axis_index("ws")
        twin, other, last = flip(w, 1), flip(w, 2), flip(w, 3)
        targets = [flip(e, k) for k in far_first(n)] + [e]
        loads, cores = {}, {}
        for half, near, far in ((1, other, last), (0, w, twin)):
            for j, s in enumerate(targets):
                cores[half, j] = remote(
                    part.at[s, far], core.at[half, j], c_s.at[half, j], c_r.at[half, j], (e, twin)
                )
                cores[half, j].start()
                loads[half, j] = pltpu.make_async_copy(
                    part.at[s, near], mine.at[half, j], load_sem.at[half, j]
                )
                loads[half, j].start()
        over_y, back = [], []

        def send_y(j):
            over_y.append(remote(sum_y.at[j], from_y.at[j], y_s.at[j], y_r.at[j], (e, other)))
            over_y[-1].start()

        def send_back(j):
            back.append(remote(total.at[j], out.at[e], ep_s.at[j], ep_r.at[j], (targets[j], w)))
            back[-1].start()

        for j in range(n):
            loads[1, j].wait()
            cores[1, j].wait_recv()
            sum_y[j] = (mine[1, j].astype(f32) + core[1, j].astype(f32)).astype(bf16)
            if j:
                send_y(j - 1)
        loads[0, 0].wait()
        cores[0, 0].wait_recv()
        send_y(n - 1)
        for j in range(n):
            if j:
                loads[0, j].wait()
                cores[0, j].wait_recv()
            over_y[j].wait_recv()
            total[j] = (
                mine[0, j].astype(f32) + core[0, j].astype(f32) + from_y[j].astype(f32)
            ).astype(bf16)
            if j:
                send_back(j - 1)
            yield
        for copy in over_y + list(cores.values()):
            copy.wait_send()
        keep = pltpu.make_async_copy(total.at[n - 1], out.at[e], own_sem)
        keep.start()
        for copy in back:
            copy.wait()
        keep.wait()

    return Job(
        [part],
        [jax.ShapeDtypeStruct(block, part.dtype)],
        [
            pltpu.VMEM((2,) + block, part.dtype),
            pltpu.VMEM((2,) + block, part.dtype),
            pltpu.VMEM(block, part.dtype),
            pltpu.VMEM(block, part.dtype),
            pltpu.VMEM(block, part.dtype),
            DMA((2, n)),
            DMA((2, n)),
            DMA((2, n)),
            DMA((n,)),
            DMA((n,)),
            DMA((n - 1,)),
            DMA((n - 1,)),
            DMA,
        ],
        n,
        body,
        [(k, 0) for k in range(1, n)] + [(0, 1), (0, 2)],
    )


def exchange_job(rows):
    n = rows.shape[0]

    def body(rows, out, own, load_sem, ep_s, ep_r):
        e, w = lax.axis_index("ep"), lax.axis_index("ws")
        targets = [flip(e, k) for k in far_first(n)]
        copies = []
        for i, s in enumerate(targets):
            copies.append(remote(rows.at[s], out.at[e], ep_s.at[i], ep_r.at[i], (s, w)))
            copies[-1].start()
        load = pltpu.make_async_copy(rows.at[e], own, load_sem.at[0])
        load.start()
        load.wait()
        store = pltpu.make_async_copy(own, out.at[e], load_sem.at[1])
        store.start()
        yield
        store.wait()
        for copy in copies:
            copy.wait()

    return Job(
        [rows],
        [jax.ShapeDtypeStruct(rows.shape, rows.dtype)],
        [pltpu.VMEM(rows.shape[1:], rows.dtype), DMA((2,)), DMA((n - 1,)), DMA((n - 1,))],
        1,
        body,
        [(k, 0) for k in range(1, n)],
    )


def exchange_combine_job(rows, weight, product, n_ws):
    n, held, depth = rows.shape
    count, width = held // n_ws, max(weight.shape)
    block = (n, count, width)
    turned = weight.shape[0] == width

    def body(
        rows, w_hbm, moved, out, w_ref, here, part, core, sum_y, from_y, total, load_sem, ep_s, ep_r, c_s, c_r,
        y_s, y_r, b_s, b_r
    ):
        e, w = lax.axis_index("ep"), lax.axis_index("ws")
        twin, other, last = flip(w, 1), flip(w, 2), flip(w, 3)
        places = [e] + [flip(e, k) for k in range(1, n)]
        weights = pltpu.make_async_copy(w_hbm, w_ref, load_sem.at[n])
        weights.start()
        arrivals = []
        for i, s in enumerate(places[1:]):
            arrivals.append(remote(rows.at[s], moved.at[e], ep_s.at[i], ep_r.at[i], (s, w)))
            arrivals[i].start()
        cores, over_y, back, stores = {}, [], [], []

        def multiply(j):
            if j:
                arrivals[j - 1].wait_recv()
            src = moved.at[places[j]] if j else rows.at[e]
            load = pltpu.make_async_copy(src, here.at[j], load_sem.at[j])
            load.start()
            load.wait()
            if j == 0:
                stores.append(pltpu.make_async_copy(here.at[0], moved.at[e], load_sem.at[0]))
                stores[0].start()
                weights.wait()

            def tile(at, columns):
                tall = pl.ds(at, columns)
                result = product(here[j], w_ref[tall, :] if turned else w_ref[:, tall])
                part[j, :, :, tall] = result.reshape(n_ws, count, columns).astype(bf16)

            column_tiles(width, tile)

        def send_core(j):
            for half, to in ((1, last), (0, twin)):
                cores[half, j] = remote(
                    part.at[j, to], core.at[half, j], c_s.at[half, j], c_r.at[half, j], (e, twin)
                )
                cores[half, j].start()

        def add_core(j):
            cores[1, j].wait_recv()
            sum_y[j] = (part[j, other].astype(f32) + core[1, j].astype(f32)).astype(bf16)

        def send_y(j):
            over_y.append(remote(sum_y.at[j], from_y.at[j], y_s.at[j], y_r.at[j], (e, other)))
            over_y[j].start()

        def add_all(j):
            cores[0, j].wait_recv()
            over_y[j].wait_recv()
            total[j] = (
                part[j, w].astype(f32) + core[0, j].astype(f32) + from_y[j].astype(f32)
            ).astype(bf16)

        def send_back(j):
            if j:
                back.append(
                    remote(total.at[j], out.at[e], b_s.at[j - 1], b_r.at[j - 1], (places[j], w))
                )
                back[j - 1].start()
            else:
                stores.append(pltpu.make_async_copy(total.at[0], out.at[e], load_sem.at[1]))
                stores[1].start()

        for t in range(n + 4):
            for lag, stage in ((0, multiply), (1, add_core), (3, add_all), (0, send_core), (1, send_y), (4, send_back)):
                if 0 <= t - lag < n:
                    stage(t - lag)
            yield
        for copy in arrivals + list(cores.values()) + over_y:
            copy.wait_send()
        for copy in back + stores:
            copy.wait()

    return Job(
        [rows, weight],
        [jax.ShapeDtypeStruct(rows.shape, bf16), jax.ShapeDtypeStruct(block, bf16)],
        [
            pltpu.VMEM(weight.shape, bf16),
            pltpu.VMEM(rows.shape, bf16),
            pltpu.VMEM((n, n_ws, count, width), bf16),
            pltpu.VMEM((2,) + block, bf16),
            pltpu.VMEM(block, bf16),
            pltpu.VMEM(block, bf16),
            pltpu.VMEM(block, bf16),
            DMA((n + 1,)),
            DMA((n - 1,)),
            DMA((n - 1,)),
            DMA((2, n)),
            DMA((2, n)),
            DMA((n,)),
            DMA((n,)),
            DMA((n - 1,)),
            DMA((n - 1,)),
        ],
        n + 4,
        body,
        [(k, 0) for k in range(1, n)] + [(0, 1), (0, 2)],
    )


def gather_weights_job(mine, normed, n, n_ws):
    rows, block = mine.shape
    routes = [(4, 0), (2, 0), (2, 4)]

    def body(
        mine, normed, out, seq, held, held_rows, load_sem, s_sem, r_sem, x_s, x_r, y_s, y_r, c_s, c_r, t_s, t_r
    ):
        e, w = lax.axis_index("ep"), lax.axis_index("ws")
        twin, other, near = flip(w, 1), flip(w, 2), flip(e, 1)
        copies = {}

        def send(hop, offset, half):
            k = routes.index((hop, offset))
            part = pl.ds(half * (rows // 2), rows // 2)
            at = pl.multiple_of(flip(e, offset) // 2 * block, block)
            place = out.at[part, pl.ds(at, block)]
            copies[hop, offset, half] = remote(
                place if offset else mine.at[part],
                place,
                s_sem.at[k, half],
                r_sem.at[k, half],
                (flip(e, hop), w),
            )
            copies[hop, offset, half].start()

        for half in range(2):
            for route in routes[:2]:
                send(*route, half)
        to_near = remote(normed, seq.at[e % 2, w], x_s, x_r, (near, w))
        to_near.start()
        over_y, to_twin, relays = [], [], []

        def spread_rows(k, half, src):
            place = seq.at[half, w]
            over_y.append(remote(src, place, y_s.at[k], y_r.at[k], (e, other)))
            over_y[k].start()
            to_twin.append(remote(src, place, c_s.at[k], c_r.at[k], (e, twin)))
            to_twin[k].start()

        def relay(k, half):
            over_y[k].wait_recv()
            place = seq.at[half, other]
            relays.append(remote(place, place, t_s.at[k], t_r.at[k], (e, twin)))
            relays[k].start()

        spread_rows(0, e % 2, normed)
        loads = fetch(((mine, held), (normed, held_rows)), load_sem)
        for load in loads:
            load.wait()
        own = out.at[:, pl.ds(pl.multiple_of(e // 2 * block, block), block)]
        stores = fetch(((held, own), (held_rows, seq.at[e % 2, w])), load_sem)
        yield
        to_near.wait_recv()
        spread_rows(1, near % 2, seq.at[near % 2, w])
        yield
        copies[4, 0, 0].wait_recv()
        send(2, 4, 0)
        yield
        relay(0, e % 2)
        copies[4, 0, 1].wait_recv()
        send(2, 4, 1)
        yield
        relay(1, near % 2)
        yield
        for store in stores:
            store.wait()
        for (_, offset, half), copy in copies.items():
            copy.wait_send()
            if (_, offset) != (4, 0):
                copy.wait_recv()
        to_near.wait_send()
        for copy in over_y:
            copy.wait_send()
        for copy in to_twin + relays:
            copy.wait()

    return Job(
        [mine, normed],
        [
            jax.ShapeDtypeStruct((rows, n // 2 * block), bf16),
            jax.ShapeDtypeStruct((2, n_ws) + normed.shape, bf16),
        ],
        [
            pltpu.VMEM(mine.shape, bf16),
            pltpu.VMEM(normed.shape, bf16),
            DMA((2,)),
            DMA((3, 2)),
            DMA((3, 2)),
            DMA,
            DMA,
        ]
        + [DMA((2,)) for _ in range(6)],
        5,
        body,
        [(1, 0), (2, 0), (4, 0), (0, 1), (0, 2)],
    )


def swap_job(blocks):
    def body(blocks, out, held, load_sem, s_sem, r_sem):
        e, w = lax.axis_index("ep"), lax.axis_index("ws")
        near = flip(e, 1)
        copy = remote(blocks.at[near % 2], out.at[e % 2], s_sem, r_sem, (near, w))
        copy.start()
        load = fetch(((blocks.at[e % 2], held),), load_sem)[0]
        load.wait()
        store = fetch(((held, out.at[e % 2]),), load_sem)[0]
        yield
        store.wait()
        copy.wait()

    return Job(
        [blocks],
        [jax.ShapeDtypeStruct(blocks.shape, blocks.dtype)],
        [pltpu.VMEM(blocks.shape[1:], blocks.dtype), DMA((1,)), DMA, DMA],
        1,
        body,
        [(1, 0)],
    )


def add_blocks(out, *refs):
    step = 64 if out.shape[1] > 1024 else 256

    def body(i, carry):
        at = pl.ds(pl.multiple_of(i * step, step), step)
        total = refs[0][at].astype(f32)
        for ref in refs[1:]:
            total = total + ref[at].astype(f32)
        out[at] = total.astype(bf16)
        return carry

    lax.fori_loop(0, out.shape[0] // step, body, 0)


def reduce_weights_job(pieces, part, n):
    rows = pieces.shape[0]
    block = pieces.shape[1] // (n // 2)
    offsets = (4, 0)

    def body(
        pieces, part, out, out_rows, mine, from_z, fourth, last_z, total, own, core, sum_y, from_y, total_near,
        from_near, total_rows, load_sem, z_s, z_r, w_load, c_s, c_r, y_s, y_r, x_s, x_r, sem
    ):
        e, w = lax.axis_index("ep"), lax.axis_index("ws")
        twin, other, last, near = flip(w, 1), flip(w, 2), flip(w, 3), flip(e, 1)

        def columns(s):
            return pieces.at[:, pl.ds(pl.multiple_of(s // 2 * block, block), block)]

        over_z = []
        for i, offset in enumerate(offsets):
            over_z.append(
                remote(columns(flip(e, offset + 2)), from_z.at[i], z_s.at[i], z_r.at[i], (flip(e, 2), w))
            )
            over_z[i].start()
        halves = (near % 2, e % 2)
        cores = {}
        for k, to in enumerate((last, twin)):
            for h, half in enumerate(halves):
                cores[h, k] = remote(
                    part.at[half, to], core.at[h, k], c_s.at[h, k], c_r.at[h, k], (e, twin)
                )
                cores[h, k].start()
        loads = fetch([(columns(flip(e, o)), mine.at[i]) for i, o in enumerate(offsets)], load_sem)
        own_loads = {}
        for h, half in enumerate(halves):
            for k, to in enumerate((other, w)):
                own_loads[h, k] = pltpu.make_async_copy(
                    part.at[half, to], own.at[h, k], w_load.at[h, k]
                )
                own_loads[h, k].start()
        yield
        over_y = []

        def send_y(h):
            over_y.append(remote(sum_y.at[h], from_y.at[h], y_s.at[h], y_r.at[h], (e, other)))
            over_y[h].start()

        for h in range(2):
            own_loads[h, 0].wait()
            cores[h, 0].wait_recv()
            add_blocks(sum_y.at[h], own.at[h, 0], core.at[h, 0])
            if h:
                send_y(0)
        yield
        loads[0].wait()
        over_z[0].wait_recv()
        send_y(1)
        add_blocks(fourth, mine.at[0], from_z.at[0])
        yield
        own_loads[0, 1].wait()
        cores[0, 1].wait_recv()
        over_y[0].wait_recv()
        far = remote(fourth, last_z, z_s.at[2], z_r.at[2], (flip(e, 4), w))
        far.start()
        add_blocks(total_near, own.at[0, 1], core.at[0, 1], from_y.at[0])
        yield
        own_loads[1, 1].wait()
        cores[1, 1].wait_recv()
        over_y[1].wait_recv()
        to_near = remote(total_near, from_near, x_s, x_r, (near, w))
        to_near.start()
        yield
        to_near.wait_recv()
        add_blocks(total_rows, own.at[1, 1], core.at[1, 1], from_y.at[1], from_near)
        loads[1].wait()
        over_z[1].wait_recv()
        far.wait_recv()
        add_blocks(total, mine.at[1], from_z.at[1], last_z)
        stores = fetch(((total_rows, out_rows), (total, out)), sem)
        for copy in over_z + list(cores.values()) + over_y + [far, to_near]:
            copy.wait_send()
        for store in stores:
            store.wait()

    one, rows_one = (rows, block), part.shape[2:]
    return Job(
        [pieces, part],
        [jax.ShapeDtypeStruct(one, bf16), jax.ShapeDtypeStruct(rows_one, bf16)],
        [pltpu.VMEM((2,) + one, bf16) for _ in range(2)]
        + [pltpu.VMEM(one, bf16) for _ in range(3)]
        + [pltpu.VMEM((2, 2) + rows_one, bf16) for _ in range(2)]
        + [pltpu.VMEM((2,) + rows_one, bf16) for _ in range(2)]
        + [pltpu.VMEM(rows_one, bf16) for _ in range(3)]
        + [DMA((2,)), DMA((3,)), DMA((3,)), DMA((2, 2)), DMA((2, 2)), DMA((2, 2))]
        + [DMA((2,)), DMA((2,)), DMA, DMA, DMA((2,))],
        5,
        body,
        [(1, 0), (2, 0), (4, 0), (0, 1), (0, 2)],
    )


def attend_kernel(spans, q_ref, kv_ref, out):
    count, _, slots, part = q_ref.shape
    for w, span in enumerate(spans):

        def head(h, carry, w=w, span=span):
            at = pl.multiple_of(h * HEAD_SIZE, HEAD_SIZE)
            columns = pl.ds(at, HEAD_SIZE)
            q, probs, _, values = head_probs(q_ref, kv_ref, w, span, at)
            mixed = dot(probs.astype(bf16), values)
            out[:, w, :, columns] = mixed.reshape(count, slots, HEAD_SIZE).astype(bf16)
            return carry

        lax.fori_loop(0, part // HEAD_SIZE, head, 0)


def slot_rows(ref, w, at):
    count, _, slots, _ = ref.shape
    rows = ref[:, w, :, pl.ds(at, HEAD_SIZE)].astype(f32)
    return rows.reshape(count * slots, HEAD_SIZE).astype(bf16)


def kv_place(kv, at):
    h = at // HEAD_SIZE
    column = pl.multiple_of(h // 2 * HEAD_SIZE, HEAD_SIZE)
    half = kv.shape[2] // 2
    value_column = pl.multiple_of(half + column, HEAD_SIZE)
    return h % 2, pl.ds(column, HEAD_SIZE), pl.ds(value_column, HEAD_SIZE)


def head_probs(q_ref, kv_ref, w, span, at):
    q = slot_rows(q_ref, w, at)
    side, key_columns, value_columns = kv_place(kv_ref, at)
    keys = kv_ref[side, :span, key_columns]
    values = kv_ref[side, :span, value_columns]
    scores = dot_t(q, keys) * HEAD_SIZE ** (-0.5)
    weight = jnp.exp(scores - jnp.max(scores, -1, keepdims=True))
    probs = weight / jnp.sum(weight, -1, keepdims=True)
    return q, probs, keys, values


def attend_call(queries, kv, spans):
    return pl.pallas_call(
        functools.partial(attend_kernel, spans),
        out_shape=jax.ShapeDtypeStruct(queries.shape, bf16),
        in_specs=[VM, VM],
        out_specs=VM,
        compiler_params=pltpu.CompilerParams(vmem_limit_bytes=VMEM_LIMIT),
        name="attend",
    )(queries, kv)


def attend_back_kernel(spans, q_ref, g_ref, kv_ref, grad_q, grad_kv, total):
    count, _, slots, part = q_ref.shape
    total[...] = jnp.zeros_like(total)
    for w, span in enumerate(spans):

        def head(h, carry, w=w, span=span):
            at = pl.multiple_of(h * HEAD_SIZE, HEAD_SIZE)
            columns = pl.ds(at, HEAD_SIZE)
            q, probs, keys, values = head_probs(q_ref, kv_ref, w, span, at)
            grad = slot_rows(g_ref, w, at)
            grad_probs = dot_t(grad, values)
            centred = jnp.sum(probs * grad_probs, -1, keepdims=True)
            grad_scores = (probs * (grad_probs - centred)).astype(bf16)
            grad_rows = dot(grad_scores, keys) * HEAD_SIZE ** (-0.5)
            grad_q[:, w, :, columns] = grad_rows.reshape(count, slots, HEAD_SIZE).astype(bf16)
            side, key_columns, value_columns = kv_place(kv_ref, at)
            total[side, :span, key_columns] += t_dot(grad_scores, q) * HEAD_SIZE ** (-0.5)
            total[side, :span, value_columns] += t_dot(probs.astype(bf16), grad)
            return carry

        lax.fori_loop(0, part // HEAD_SIZE, head, 0)
    grad_kv[...] = total[...].astype(bf16)


def attend_back_call(queries, grads, kv, spans):
    return pl.pallas_call(
        functools.partial(attend_back_kernel, spans),
        out_shape=[
            jax.ShapeDtypeStruct(queries.shape, bf16),
            jax.ShapeDtypeStruct(kv.shape, bf16),
        ],
        in_specs=[VM, VM, VM],
        out_specs=[VM, VM],
        scratch_shapes=[pltpu.VMEM(kv.shape, f32)],
        compiler_params=pltpu.CompilerParams(vmem_limit_bytes=VMEM_LIMIT),
        name="attend_back",
    )(queries, grads, kv)


def gather_kernel(n, n_ws, own, out, load_sem, w_s, w_r, ep_s, ep_r):
    e, w = lax.axis_index("ep"), lax.axis_index("ws")
    beside = [flip(w, k) for k in range(1, n_ws)]
    across = [flip(e, k) for k in far_first(n)]
    greet([(e, p) for p in beside] + [(s, w) for s in across])
    keep = pltpu.make_async_copy(own, out.at[e, w], load_sem)
    keep.start()
    first = []
    for i, p in enumerate(beside):
        first.append(remote(own, out.at[e, w], w_s.at[i], w_r.at[i], (e, p)))
        first[-1].start()
    keep.wait()
    for copy in first:
        copy.wait()
    second = []
    for i, s in enumerate(across):
        second.append(remote(out.at[e], out.at[e], ep_s.at[i], ep_r.at[i], (s, w)))
        second[-1].start()
    for copy in second:
        copy.wait()


def gather_call(own, n, n_ws):
    return pl.pallas_call(
        functools.partial(gather_kernel, n, n_ws),
        out_shape=jax.ShapeDtypeStruct((n, n_ws) + own.shape, own.dtype),
        in_specs=[VM],
        out_specs=VM,
        scratch_shapes=[DMA, DMA((n_ws - 1,)), DMA((n_ws - 1,)), DMA((n - 1,)), DMA((n - 1,))],
        compiler_params=pltpu.CompilerParams(collective_id=3, has_side_effects=True),
        name="gather_gains",
    )(own)


def reduce_kernel(n, n_ws, parts, out, held, all_parts, load_sem, w_s, w_r, ep_s, ep_r):
    e, w = lax.axis_index("ep"), lax.axis_index("ws")
    beside = [flip(w, k) for k in range(1, n_ws)]
    across = [flip(e, k) for k in far_first(n)]
    greet([(e, p) for p in beside] + [(s, w) for s in across])
    keep = pltpu.make_async_copy(parts.at[:, w], held.at[:, w], load_sem.at[0])
    keep.start()
    first = []
    for i, p in enumerate(beside):
        first.append(remote(parts.at[:, p], held.at[:, w], w_s.at[i], w_r.at[i], (e, p)))
        first[-1].start()
    keep.wait()
    for copy in first:
        copy.wait()
    keep = pltpu.make_async_copy(held.at[e], all_parts.at[e], load_sem.at[1])
    keep.start()
    second = []
    for i, s in enumerate(across):
        second.append(remote(held.at[s], all_parts.at[e], ep_s.at[i], ep_r.at[i], (s, w)))
        second[-1].start()
    keep.wait()
    for copy in second:
        copy.wait()
    out[...] = jnp.sum(jnp.sum(all_parts[...], 0), 0)


def reduce_call(parts):
    n, n_ws = parts.shape[:2]
    return pl.pallas_call(
        functools.partial(reduce_kernel, n, n_ws),
        out_shape=jax.ShapeDtypeStruct(parts.shape[2:], parts.dtype),
        in_specs=[VM],
        out_specs=VM,
        scratch_shapes=[
            pltpu.VMEM(parts.shape, parts.dtype),
            pltpu.VMEM(parts.shape, parts.dtype),
            DMA((2,)),
            DMA((n_ws - 1,)),
            DMA((n_ws - 1,)),
            DMA((n - 1,)),
            DMA((n - 1,)),
        ],
        compiler_params=pltpu.CompilerParams(collective_id=4, has_side_effects=True),
        name="reduce_gains",
    )(parts)


def small(n_ep):
    return n_ep == MIXTURE_EXPERTS and lax.axis_size("ws") == 4


PLAIN = {
    grad_job: lambda a, b: [t_dot(a, b)],
    pair_grad_job: lambda a, b, c: [jnp.stack([t_dot(a, b), t_dot(a, c)], 1)],
    split_job: lambda weight: [weight[:, 0], weight[:, 1]],
    ffn_job: ffn_plain,
    ffn_back_job: ffn_back_plain,
}


def beside(job, plain, arg, fills, collective_id, name):
    if job is None:
        return [plain(arg)] + [out for make, *rest in fills for out in PLAIN[make](*rest)]
    return run_jobs([job(arg)], [make(*rest) for make, *rest in fills], collective_id, name)


def exchange_plain(send):
    return lax.all_to_all(send, "ep", split_axis=0, concat_axis=0, tiled=True)


def exchange(send, *fills, collective_id=2, name="exchange"):
    job = exchange_job if small(send.shape[0]) else None
    return beside(job, exchange_plain, send, fills, collective_id, name)


def spread(rows, group):
    width = rows.shape[-1]
    blocks = rows.reshape(MIXTURE_EXPERTS, 1, ROWS, width)
    return jnp.broadcast_to(blocks, (MIXTURE_EXPERTS, group, ROWS, width)).reshape(
        MIXTURE_EXPERTS * group, ROWS, width
    )


def dispatch(rows, group, *fills, collective_id=0, name="dispatch"):
    width = rows.shape[-1]

    def plain(blocks):
        return lax.all_gather(exchange_plain(blocks), "ws", axis=1, tiled=False)

    job = functools.partial(dispatch_job, n_ws=4) if small(MIXTURE_EXPERTS * group) else None
    out = beside(job, plain, spread(rows, group), fills, collective_id, name)
    return [out[0].reshape(-1, width)] + list(out[1:])


def combine(partial, group, n_ep, n_ws, *fills, collective_id=1, name="combine"):
    width = partial.shape[-1]

    def plain(part):
        part = part.transpose(1, 0, 2, 3).reshape(n_ws * n_ep * ROWS, width)
        own = lax.psum_scatter(part, "ws", scatter_dimension=0, tiled=True)
        return exchange_plain(own.reshape(n_ep, ROWS, width))

    part = partial.reshape(n_ep, n_ws, ROWS, width)
    job = combine_job if small(n_ep) else None
    back, *rest = beside(job, plain, part, fills, collective_id, name)
    if group > 1:
        back = jnp.sum(back.reshape(MIXTURE_EXPERTS, group, ROWS, width).astype(f32), 1).astype(bf16)
    return [back.reshape(MIXTURE_EXPERTS * ROWS, width)] + rest


def slot_tables(routes, slots):
    target = jnp.where(slots < CAP, routes * ROWS + slots, -1)
    places = lax.broadcasted_iota(jnp.int32, (MIXTURE_EXPERTS * ROWS, target.shape[0]), 0)
    return [(places == target[None, :, k]).astype(bf16) for k in range(CHOSEN_EXPERTS)]


def norm_back(grad, unit, inverse, gain):
    gain_grad = jnp.sum(grad * unit, 0)
    scaled = grad * gain
    return (inverse * (scaled - unit * jnp.mean(scaled * unit, -1, keepdims=True)), gain_grad)


def heads_of(rows):
    return rows.reshape(rows.shape[0], -1, HEAD_SIZE)


def local(
    x_in,
    gain_attn,
    gain_ffn,
    key_value_weight,
    w_query,
    w_output,
    w_in,
    w_out,
    gate_attn,
    gate_ffn,
    route_attn,
    slot_attn,
    route_ffn,
    slot_ffn,
    cotangent,
):
    n_ep = lax.axis_size("ep")
    n_ws = lax.axis_size("ws")
    group = n_ep // MIXTURE_EXPERTS
    local_tokens, width = x_in.shape
    key_value_width = KEY_VALUE_HEADS * HEAD_SIZE
    part = w_query.shape[2]
    own_width = group * part
    sequence = n_ws * local_tokens
    place = lax.axis_index("ws")
    scale = HEAD_SIZE ** (-0.5)

    fused = small(n_ep) and key_value_weight.shape[1] == HEAD_SIZE
    short = fused and gain_attn.shape[0] == 64
    if short:
        gains = jnp.concatenate([gain_attn, gain_ffn], 0).astype(f32)[None]
        gains = gather_call(gains, n_ep, n_ws).reshape(n_ep * n_ws, 2, -1)
        gain_one, gain_two = gains[:, 0].reshape(-1), gains[:, 1].reshape(-1)
    else:
        gain_one = lax.all_gather(gain_attn, ("ep", "ws"), axis=0, tiled=True).astype(f32)
        gain_two = lax.all_gather(gain_ffn, ("ep", "ws"), axis=0, tiled=True).astype(f32)
    plain = group == 1 and key_value_weight.shape[1] == HEAD_SIZE
    if plain:
        half = n_ep // 2
        there = [
            (e * n_ws + w, (w + n_ws * (e // half)) * n_ws + e % half)
            for e in range(n_ep)
            for w in range(n_ws)
        ]
        mine = lax.ppermute(key_value_weight, ("ep", "ws"), there)
    else:
        whole = lax.all_gather(key_value_weight, ("ep", "ws"), axis=1, tiled=True)
        whole = whole.reshape(width, 2 * group, n_ws, part)
        kv_own = lax.dynamic_index_in_dim(whole, place, 2, keepdims=False).reshape(width, -1)

    inputs = x_in.astype(f32)
    inverse_one = lax.rsqrt(jnp.mean(inputs * inputs, -1, keepdims=True) + EPS)
    unit_one = inputs * inverse_one
    normed = (unit_one * gain_one).astype(bf16)
    attn_pairs = slot_tables(route_attn, slot_attn)
    ffn_pairs = slot_tables(route_ffn, slot_ffn)
    attn_tokens = attn_pairs[0] + attn_pairs[1]
    ffn_tokens = ffn_pairs[0] + ffn_pairs[1]

    slots_one = dot(attn_tokens, normed).astype(bf16)
    if fused:
        rows_one, kv_own, normed_sequence, gate_weight, up_weight = run_jobs(
            [
                dispatch_job(slots_one.reshape(n_ep, ROWS, width), n_ws),
                gather_weights_job(mine, normed, n_ep, n_ws),
            ],
            [split_job(w_in[0])],
            10,
            "dispatch_weights",
        )
        rows_one = rows_one.reshape(-1, width)
        normed_sequence = normed_sequence.reshape(2 * sequence, width)
    else:
        if plain:
            kv_own = lax.all_gather(mine, "ep", axis=1, tiled=True)
        normed_sequence = lax.all_gather(normed, "ws", axis=0, tiled=True)
        rows_one, gate_weight, up_weight = dispatch(slots_one, group, (split_job, w_in[0]))
    kv = dot(normed_sequence, kv_own).astype(bf16)
    if not fused:
        keys = kv[:, :own_width].reshape(sequence, -1, HEAD_SIZE)
        values = kv[:, own_width:].reshape(sequence, -1, HEAD_SIZE)

    owner_query = dot(rows_one, w_query[0]).astype(bf16)
    owner_query = owner_query.reshape(n_ep, n_ws * ROWS, part)
    if fused:
        queries, kv = run_jobs(
            [exchange_job(owner_query), swap_job(kv.reshape(2, sequence, -1))], [], 13, "exchange_kv"
        )
    else:
        queries = exchange(owner_query)[0]
    queries = queries.reshape(MIXTURE_EXPERTS, group, n_ws, ROWS, part)
    spans = [(w * local_tokens // BLOCK + 1) * BLOCK for w in range(n_ws)]

    def by_block(rows):
        rows = rows.reshape(MIXTURE_EXPERTS, group, n_ws, ROWS, part)
        return [
            rows[:, :, w].transpose(0, 2, 1, 3).reshape(-1, own_width // HEAD_SIZE, HEAD_SIZE)
            for w in range(n_ws)
        ]

    def to_experts(pieces):
        rows = jnp.stack(
            [
                piece.reshape(MIXTURE_EXPERTS, ROWS, group, part).transpose(0, 2, 1, 3)
                for piece in pieces
            ],
            2,
        )
        return rows.reshape(n_ep, n_ws * ROWS, part)

    if fused:
        queries = queries.reshape(n_ep, n_ws, ROWS, part)
        mixed = attend_call(queries, kv, spans).reshape(n_ep, n_ws * ROWS, part)
    else:
        kept = []
        mixed_pieces = []
        for q, span in zip(by_block(queries), spans):
            scores = (
                jnp.einsum("rhd,shd->hrs", q, keys[:span], preferred_element_type=f32) * scale
            )
            probs = jax.nn.softmax(scores, axis=-1)
            mixed = jnp.einsum(
                "hrs,shd->rhd", probs.astype(bf16), values[:span], preferred_element_type=f32
            )
            kept.append((q, probs))
            mixed_pieces.append(mixed.astype(bf16))
        mixed = to_experts(mixed_pieces)
    if fused:
        owner_mixed, attn_slots = run_jobs(
            [exchange_combine_job(mixed, w_output[0], dot, n_ws)], [], 11, "exchange_output"
        )
        owner_mixed, attn_slots = owner_mixed.reshape(-1, part), attn_slots.reshape(-1, width)
    else:
        owner_mixed = exchange(mixed)[0].reshape(-1, part)
        output_part = dot(owner_mixed, w_output[0]).astype(bf16)
        attn_slots = combine(output_part, group, n_ep, n_ws)[0]

    def weighted(pairs, gates, slot_values):
        return sum(gates[:, k : k + 1] * t_dot(pairs[k], slot_values) for k in range(2))

    def to_slots(pairs, gates, values):
        return sum(
            dot(pairs[k], (gates[:, k : k + 1] * values).astype(bf16)) for k in range(2)
        ).astype(bf16)

    hidden_state = inputs + weighted(attn_pairs, gate_attn, attn_slots)
    inverse_two = lax.rsqrt(jnp.mean(hidden_state * hidden_state, -1, keepdims=True) + EPS)
    unit_two = hidden_state * inverse_two
    normed_two = (unit_two * gain_two).astype(bf16)

    grad_out = cotangent.astype(f32)
    grad_slots = to_slots(ffn_pairs, gate_ffn, grad_out)
    expert_rows = dispatch(dot(ffn_tokens, normed_two).astype(bf16), group)[0]
    expert_grad, gate_pre, up_pre, activated, forward_part = dispatch(
        grad_slots,
        group,
        (ffn_job, expert_rows, gate_weight, up_weight, w_out[0]),
        collective_id=5,
        name="dispatch_ffn",
    )
    ffn_slots, grad_gate, grad_up, back_two = combine(
        forward_part,
        group,
        n_ep,
        n_ws,
        (ffn_back_job, expert_grad, gate_pre, up_pre, gate_weight, up_weight, w_out[0]),
        collective_id=1,
        name="combine_ffn_back",
    )
    result = hidden_state + weighted(ffn_pairs, gate_ffn, ffn_slots)
    back_slots, grad_second = combine(
        back_two,
        group,
        n_ep,
        n_ws,
        (grad_job, activated, expert_grad),
        collective_id=6,
        name="combine_grad_out",
    )

    grad_normed_two = t_dot(ffn_tokens, back_slots)
    grad_hidden_norm, grad_gain_two = norm_back(grad_normed_two, unit_two, inverse_two, gain_two)
    grad_hidden = grad_out + grad_hidden_norm
    owner_grad, grad_first = dispatch(
        to_slots(attn_pairs, gate_attn, grad_hidden),
        group,
        (pair_grad_job, expert_rows, grad_gate, grad_up),
        collective_id=7,
        name="dispatch_grad_in",
    )
    back_mixed = dot_t(owner_grad, w_output[0]).astype(bf16)
    mixed_grads, grad_output = exchange(
        back_mixed.reshape(n_ep, n_ws * ROWS, part),
        (grad_job, owner_mixed, owner_grad),
        collective_id=8,
        name="exchange_grad_output",
    )

    if fused:
        mixed_grads = mixed_grads.reshape(n_ep, n_ws, ROWS, part)
        query_grads, grad_kv_rows = attend_back_call(queries, mixed_grads, kv, spans)
        query_grads = query_grads.reshape(n_ep, n_ws * ROWS, part)
    else:
        grad_keys, grad_values, query_pieces = 0.0, 0.0, []
        for (q, probs), grad, span in zip(kept, by_block(mixed_grads), spans):
            grad_probs = jnp.einsum("rhd,shd->hrs", grad, values[:span], preferred_element_type=f32)
            centred = jnp.sum(probs * grad_probs, -1, keepdims=True)
            grad_scores = (probs * (grad_probs - centred)).astype(bf16)
            grad_q = (
                jnp.einsum("hrs,shd->rhd", grad_scores, keys[:span], preferred_element_type=f32)
                * scale
            )
            query_pieces.append(grad_q.astype(bf16))
            pad = ((0, sequence - span), (0, 0), (0, 0))
            piece = jnp.einsum("hrs,rhd->shd", grad_scores, q, preferred_element_type=f32) * scale
            grad_keys = grad_keys + jnp.pad(piece, pad)
            piece = jnp.einsum(
                "hrs,rhd->shd", probs.astype(bf16), grad, preferred_element_type=f32
            )
            grad_values = grad_values + jnp.pad(piece, pad)
        grad_kv_rows = jnp.concatenate(
            [grad_keys.reshape(sequence, -1), grad_values.reshape(sequence, -1)], 1
        ).astype(bf16)
        query_grads = to_experts(query_pieces)
    if fused:
        owner_grad_query, normed_back, grad_kv_rows = run_jobs(
            [exchange_combine_job(query_grads, w_query[0], dot_t, n_ws), swap_job(grad_kv_rows)],
            [],
            14,
            "exchange_back",
        )
        owner_grad_query = owner_grad_query.reshape(-1, part)
        normed_back = normed_back.reshape(-1, width)
        grad_kv_rows = grad_kv_rows.reshape(2 * sequence, -1)
    else:
        owner_grad_query = exchange(query_grads)[0].reshape(-1, part)
    grad_kv = t_dot(normed_sequence, grad_kv_rows)
    from_kv = dot_t(grad_kv_rows, kv_own).astype(bf16)
    if fused:
        piece, from_kv, grad_query = run_jobs(
            [
                reduce_weights_job(
                    grad_kv.astype(bf16), from_kv.reshape(2, n_ws, local_tokens, width), n_ep
                )
            ],
            [grad_job(rows_one, owner_grad_query)],
            9,
            "reduce_weights",
        )
    else:
        back_normed = dot_t(owner_grad_query, w_query[0]).astype(bf16)
        normed_back = combine(back_normed, group, n_ep, n_ws)[0]
        grad_query = t_dot(rows_one, owner_grad_query)
    if fused:
        back = [(b, a) for a, b in there]
        grad_kv_shard = lax.ppermute(piece, ("ep", "ws"), back).astype(f32)
    elif plain:
        pieces = grad_kv.reshape(width, n_ep, HEAD_SIZE).transpose(1, 0, 2).astype(bf16)
        piece = lax.psum_scatter(pieces, "ep", scatter_dimension=0, tiled=False)
        grad_kv_shard = lax.ppermute(piece, ("ep", "ws"), [(b, a) for a, b in there]).astype(f32)
    else:
        mask = (jnp.arange(n_ws) == place)[None, None, :, None]
        pieces = jnp.where(mask, grad_kv.reshape(width, 2 * group, 1, part), 0.0)
        pieces = pieces.reshape(width, 2 * key_value_width).astype(bf16)
        grad_kv_shard = lax.psum_scatter(
            pieces, ("ep", "ws"), scatter_dimension=1, tiled=True
        ).astype(f32)
    if not fused:
        from_kv = lax.psum_scatter(from_kv, "ws", scatter_dimension=0, tiled=True)
    grad_normed = t_dot(attn_tokens, normed_back) + from_kv.astype(f32)
    grad_input_norm, grad_gain_one = norm_back(grad_normed, unit_one, inverse_one, gain_one)
    grad_input = grad_hidden + grad_input_norm
    gain_grads = jnp.stack([grad_gain_one, grad_gain_two], 0)
    if short:
        parts = gain_grads.reshape(2, n_ep, n_ws, -1).transpose(1, 2, 0, 3)
        gain_shards = reduce_call(parts.reshape(n_ep, n_ws, 1, -1)).reshape(2, -1)
    else:
        gain_shards = lax.psum_scatter(
            gain_grads, ("ep", "ws"), scatter_dimension=1, tiled=True
        )
    return (
        result.astype(bf16),
        grad_input,
        gain_shards[0],
        gain_shards[1],
        grad_kv_shard,
        grad_query[None],
        grad_output[None],
        grad_first[None],
        grad_second[None],
    )


def solution(mesh):
    both = ("ep", "ws")
    rows, vector, columns = P(both, None), P(both), P(None, both)
    return jax.shard_map(
        local,
        mesh=mesh,
        in_specs=(
            rows,
            vector,
            vector,
            columns,
            P("ep", None, "ws"),
            P("ep", "ws", None),
            P("ep", None, None, "ws"),
            P("ep", "ws", None),
            rows,
            rows,
            rows,
            rows,
            rows,
            rows,
            rows,
        ),
        out_specs=(
            rows,
            rows,
            vector,
            vector,
            columns,
            P("ep", None, "ws"),
            P("ep", "ws", None),
            P("ep", None, None, "ws"),
            P("ep", "ws", None),
        ),
        check_vma=False,
    )
```

```python
import functools

import jax
import jax.numpy as jnp
from jax import lax
from jax.experimental import pallas as pl
from jax.experimental.pallas import tpu as pltpu
from jax.sharding import PartitionSpec as P

KEY_VALUE_HEADS = 16
HEAD_SIZE = 128
MIXTURE_EXPERTS = 8
CHOSEN_EXPERTS = 2
BLOCK = 256
CAP = 36
ROWS = 40

EPS = 1e-06
very_negative = -1e30
f32 = jnp.float32
bf16 = jnp.bfloat16
MESH = pl.DeviceIdType.MESH
ANY = pl.BlockSpec(memory_space=pl.ANY)
VM = pl.BlockSpec(memory_space=pltpu.VMEM)
DMA = pltpu.SemaphoreType.DMA
STEP = 256
VMEM_LIMIT = 60 << 20


def dot(a, b):
    return jnp.dot(a, b, preferred_element_type=f32)


def dot_t(a, b):
    return lax.dot_general(a, b, (((1,), (1,)), ((), ())), preferred_element_type=f32)


def t_dot(a, b):
    return lax.dot_general(a, b, (((0,), (0,)), ((), ())), preferred_element_type=f32)


def flip(index, bits):
    out, bit = index, 1
    while bit <= bits:
        if bits & bit:
            out = out + bit - 2 * bit * ((index // bit) % 2)
        bit *= 2
    return out


def far_first(n):
    return sorted(range(1, n), key=lambda k: (-((k // 2).bit_length()), k))


def greet(partners):
    barrier = pltpu.get_barrier_semaphore()
    for partner in partners:
        pl.semaphore_signal(barrier, inc=1, device_id=partner, device_id_type=MESH)
    pl.semaphore_wait(barrier, len(partners))


def remote(src, dst, send, recv, device):
    return pltpu.make_async_remote_copy(
        src_ref=src, dst_ref=dst, send_sem=send, recv_sem=recv, device_id=device, device_id_type=MESH
    )


class Job:
    def __init__(self, args, outs, scratch, steps, body, partners=()):
        self.args, self.outs, self.scratch, self.steps, self.body = args, outs, scratch, steps, body
        self.partners = partners


def run_jobs(jobs, fills, collective_id, name):
    whole = jobs + fills
    args = [a for job in whole for a in job.args]
    outs = [o for job in whole for o in job.outs]
    scratch = [x for job in whole for x in job.scratch]
    turns = sorted((k / job.steps, i) for i, job in enumerate(jobs) for k in range(job.steps))
    partners = sorted({p for job in jobs for p in job.partners})

    def kernel(*refs):
        bodies, at = [], [0, len(args), len(args) + len(outs)]
        for job in whole:
            own = []
            for k, part in enumerate((job.args, job.outs, job.scratch)):
                own.append(refs[at[k] : at[k] + len(part)])
                at[k] += len(part)
            bodies.append(job.body(*own[0], *own[1], *own[2]))
        moves, work = bodies[: len(jobs)], bodies[len(jobs) :]
        queue = [g for g, job in zip(work, fills) for _ in range(job.steps)]
        for g in work:
            next(g)
        e, w = lax.axis_index("ep"), lax.axis_index("ws")
        greet([(flip(e, p), flip(w, q)) for p, q in partners])
        done = 0
        for k, (_, i) in enumerate(turns):
            next(moves[i])
            target = (k + 1) * len(queue) // len(turns)
            while done < target:
                next(queue[done])
                done += 1
        for g in moves + work:
            for _ in g:
                pass

    return pl.pallas_call(
        kernel,
        out_shape=outs,
        in_specs=[ANY] * len(args),
        out_specs=[ANY] * len(outs),
        scratch_shapes=scratch,
        compiler_params=pltpu.CompilerParams(
            collective_id=collective_id, has_side_effects=True, vmem_limit_bytes=VMEM_LIMIT
        ),
        name=name,
    )(*args)


def fetch(pairs, sem):
    copies = [
        pltpu.make_async_copy(src, dst, sem.at[i]) for i, (src, dst) in enumerate(pairs)
    ]
    for copy in copies:
        copy.start()
    return copies


def blocks_of(size):
    return [(start, min(STEP, size - start)) for start in range(0, size, STEP)]


def column_tiles(width, tile):
    def body(c, carry):
        tile(pl.multiple_of(c * STEP, STEP), STEP)
        return carry

    lax.fori_loop(0, width // STEP, body, 0)
    if width % STEP:
        tile(width // STEP * STEP, width % STEP)


def grad_job(a, b):
    depth, rows = a.shape
    width = b.shape[1]

    def body(a_hbm, b_hbm, out, a_ref, b_ref, turned, held, load_sem, sem):
        loads = fetch(((a_hbm, a_ref), (b_hbm, b_ref)), load_sem)
        yield
        for load in loads:
            load.wait()
        copies = []
        for i, (start, size) in enumerate(blocks_of(rows)):
            if i >= 2:
                copies[i - 2].wait()
            turned[:size] = a_ref[:, start : start + size].T

            def tile(at, columns, slot=i % 2, size=size):
                held[slot, :size, pl.ds(at, columns)] = jnp.dot(
                    turned[:size], b_ref[:, pl.ds(at, columns)], preferred_element_type=f32
                )

            column_tiles(width, tile)
            copies.append(
                pltpu.make_async_copy(
                    held.at[i % 2, pl.ds(0, size)], out.at[pl.ds(start, size)], sem.at[i % 2]
                )
            )
            copies[i].start()
            yield
        for copy in copies[-2:]:
            copy.wait()

    return Job(
        [a, b],
        [jax.ShapeDtypeStruct((rows, width), f32)],
        [
            pltpu.VMEM(a.shape, bf16),
            pltpu.VMEM(b.shape, bf16),
            pltpu.VMEM((STEP, depth), bf16),
            pltpu.VMEM((2, STEP, width), f32),
            DMA((2,)),
            DMA((2,)),
        ],
        len(blocks_of(rows)),
        body,
    )


def pair_grad_job(a, first, second):
    depth, rows = a.shape
    tiles = first.shape[1] // 128

    def body(a_hbm, f_hbm, s_hbm, out, a_ref, f_ref, s_ref, turned, held, load_sem, sem):
        loads = fetch(((a_hbm, a_ref), (f_hbm, f_ref), (s_hbm, s_ref)), load_sem)
        flat = held.reshape(2 * tiles * STEP * 2, 128)
        yield
        for load in loads:
            load.wait()
        copies = []
        for i, (start, size) in enumerate(blocks_of(rows)):
            if i >= 2:
                for copy in copies[i - 2]:
                    copy.wait()
            turned[:size] = a_ref[:, start : start + size].T

            def tile(at, columns, slot=i % 2, size=size):
                for j, b_ref in enumerate((f_ref, s_ref)):
                    r = jnp.dot(
                        turned[:size], b_ref[:, pl.ds(at, columns)], preferred_element_type=f32
                    )
                    for half in range(columns // 128):
                        base = (slot * tiles + at // 128 + half) * (2 * STEP) + j
                        flat[pl.ds(base, size, stride=2), :] = r[:, half * 128 : half * 128 + 128]

            column_tiles(tiles * 128, tile)
            copies.append(
                [
                    pltpu.make_async_copy(
                        held.at[i % 2, c, pl.ds(0, size)],
                        out.at[pl.ds(start, size), :, pl.ds(c * 128, 128)],
                        sem.at[i % 2, c],
                    )
                    for c in range(tiles)
                ]
            )
            for copy in copies[i]:
                copy.start()
            yield
        for copy in copies[-2] + copies[-1]:
            copy.wait()

    return Job(
        [a, first, second],
        [jax.ShapeDtypeStruct((rows, 2, tiles * 128), f32)],
        [
            pltpu.VMEM(a.shape, bf16),
            pltpu.VMEM(first.shape, bf16),
            pltpu.VMEM(second.shape, bf16),
            pltpu.VMEM((STEP, depth), bf16),
            pltpu.VMEM((2, tiles, STEP, 2, 128), f32),
            DMA((3,)),
            DMA((2, tiles)),
        ],
        len(blocks_of(rows)),
        body,
    )


def split_job(weight):
    rows, _, width = weight.shape

    def body(w_hbm, first, second, block, wide, held, load_sem, sem):
        flat = wide.reshape(2 * STEP, 128)
        steps = rows // STEP

        def load(i):
            return pltpu.make_async_copy(
                w_hbm.at[pl.ds(i * STEP, STEP)], block.at[i % 2], load_sem.at[i % 2]
            )

        load(0).start()
        yield
        copies = []
        for i in range(steps):
            slot = i % 2
            if i + 1 < steps:
                load(i + 1).start()
            load(i).wait()
            if i >= 2:
                for copy in copies[i - 2]:
                    copy.wait()

            def tile(c, carry, slot=slot):
                at = pl.ds(pl.multiple_of(c * 128, 128), 128)
                wide[...] = block[slot, :, :, at].astype(f32)
                for j in range(2):
                    held[slot, j, :, at] = flat[pl.ds(j, STEP, stride=2), :].astype(bf16)
                return carry

            lax.fori_loop(0, width // 128, tile, 0)
            copies.append(
                [
                    pltpu.make_async_copy(
                        held.at[slot, j], out.at[pl.ds(i * STEP, STEP)], sem.at[slot, j]
                    )
                    for j, out in enumerate((first, second))
                ]
            )
            for copy in copies[i]:
                copy.start()
            yield
        for copy in copies[-2] + copies[-1]:
            copy.wait()

    return Job(
        [weight],
        [jax.ShapeDtypeStruct((rows, width), bf16)] * 2,
        [
            pltpu.VMEM((2, STEP, 2, width), bf16),
            pltpu.VMEM((STEP, 2, 128), f32),
            pltpu.VMEM((2, 2, STEP, width), bf16),
            DMA((2,)),
            DMA((2, 2)),
        ],
        rows // STEP,
        body,
    )


def ffn_job(x, gate_weight, up_weight, down_weight):
    rows, width = x.shape
    hidden = gate_weight.shape[1]

    def body(
        x_hbm, g_hbm, u_hbm, d_hbm, gate_out, up_out, act_out, out, x_ref, g_ref, u_ref, d_ref, pre, act, res,
        load_sem, sem
    ):
        loads = fetch(((x_hbm, x_ref), (g_hbm, g_ref), (u_hbm, u_ref), (d_hbm, d_ref)), load_sem)
        yield
        for load in loads:
            load.wait()
        copies = []
        for i, (start, size) in enumerate(blocks_of(rows)):
            slot = i % 2
            here = pl.ds(start, size)
            if i >= 2:
                for copy in copies[i - 2]:
                    copy.wait()

            def tile(at, columns, slot=slot, start=start, size=size):
                part = pl.ds(at, columns)
                left = x_ref[start : start + size]
                gate = dot(left, g_ref[:, part])
                up = dot(left, u_ref[:, part])
                pre[slot, 0, :, part] = gate
                pre[slot, 1, :, part] = up
                act[slot, :, part] = (gate * jax.nn.sigmoid(gate) * up).astype(bf16)

            column_tiles(hidden, tile)
            yield

            def last(at, columns, slot=slot):
                part = pl.ds(at, columns)
                res[slot, :, part] = dot(act[slot], d_ref[:, part]).astype(bf16)

            column_tiles(width, last)
            copies.append(
                [
                    pltpu.make_async_copy(src.at[slot], dst.at[here], sem.at[slot, k])
                    for k, (src, dst) in enumerate(((act, act_out), (res, out)))
                ]
                + [
                    pltpu.make_async_copy(pre.at[slot, k], dst.at[here], sem.at[slot, 2 + k])
                    for k, dst in enumerate((gate_out, up_out))
                ]
            )
            for copy in copies[i]:
                copy.start()
            yield
        for copy in copies[-2] + copies[-1]:
            copy.wait()

    return Job(
        [x, gate_weight, up_weight, down_weight],
        [jax.ShapeDtypeStruct((rows, hidden), f32)] * 2
        + [jax.ShapeDtypeStruct((rows, hidden), bf16), jax.ShapeDtypeStruct((rows, width), bf16)],
        [
            pltpu.VMEM(x.shape, bf16),
            pltpu.VMEM(gate_weight.shape, bf16),
            pltpu.VMEM(up_weight.shape, bf16),
            pltpu.VMEM(down_weight.shape, bf16),
            pltpu.VMEM((2, 2, STEP, hidden), f32),
            pltpu.VMEM((2, STEP, hidden), bf16),
            pltpu.VMEM((2, STEP, width), bf16),
            DMA((4,)),
            DMA((2, 4)),
        ],
        2 * (rows // STEP),
        body,
    )


def ffn_plain(x, gate_weight, up_weight, down_weight):
    gate_pre, up_pre = dot(x, gate_weight), dot(x, up_weight)
    activated = (gate_pre * jax.nn.sigmoid(gate_pre) * up_pre).astype(bf16)
    return gate_pre, up_pre, activated, dot(activated, down_weight).astype(bf16)


def before_activation(grad_act, gate_pre, up_pre):
    sigmoid_gate = jax.nn.sigmoid(gate_pre)
    grad_up = (grad_act * gate_pre * sigmoid_gate).astype(bf16)
    grad_gate = (
        grad_act * up_pre * sigmoid_gate * (1.0 + gate_pre * (1.0 - sigmoid_gate))
    ).astype(bf16)
    return grad_gate, grad_up


def ffn_back_job(grad, gate_pre, up_pre, gate_weight, up_weight, down_weight):
    rows, width = grad.shape
    hidden = gate_weight.shape[1]

    def body(
        x_hbm, gp_hbm, up_hbm, g_hbm, u_hbm, d_hbm, gate_out, up_out, out, x_ref, g_ref, u_ref, d_ref, pre, hid,
        res, load_sem, pre_sem, sem
    ):
        loads = fetch(((x_hbm, x_ref), (g_hbm, g_ref), (u_hbm, u_ref), (d_hbm, d_ref)), load_sem)

        def load_pre(i):
            here = pl.ds(i * STEP, STEP)
            return [
                pltpu.make_async_copy(src.at[here], pre.at[i % 2, k], pre_sem.at[i % 2, k])
                for k, src in enumerate((gp_hbm, up_hbm))
            ]

        for copy in load_pre(0):
            copy.start()
        yield
        for load in loads:
            load.wait()
        copies = []
        steps = rows // STEP
        for i in range(steps):
            slot, start = i % 2, i * STEP
            here = pl.ds(start, STEP)
            if i + 1 < steps:
                for copy in load_pre(i + 1):
                    copy.start()
            for copy in load_pre(i):
                copy.wait()
            if i >= 2:
                for copy in copies[i - 2]:
                    copy.wait()

            def tile(at, columns, slot=slot, start=start):
                part = pl.ds(at, columns)
                grad_act = dot_t(x_ref[start : start + STEP], d_ref[part, :])
                pair = before_activation(grad_act, pre[slot, 0, :, part], pre[slot, 1, :, part])
                hid[slot, 0, :, part], hid[slot, 1, :, part] = pair

            column_tiles(hidden, tile)
            yield

            def last(at, columns, slot=slot):
                part = pl.ds(at, columns)
                total = dot_t(hid[slot, 0], g_ref[part, :]) + dot_t(hid[slot, 1], u_ref[part, :])
                res[slot, :, part] = total.astype(bf16)

            column_tiles(width, last)
            copies.append(
                [pltpu.make_async_copy(res.at[slot], out.at[here], sem.at[slot, 2])]
                + [
                    pltpu.make_async_copy(hid.at[slot, k], dst.at[here], sem.at[slot, k])
                    for k, dst in enumerate((gate_out, up_out))
                ]
            )
            for copy in copies[i]:
                copy.start()
            yield
        for copy in copies[-2] + copies[-1]:
            copy.wait()

    return Job(
        [grad, gate_pre, up_pre, gate_weight, up_weight, down_weight],
        [jax.ShapeDtypeStruct((rows, hidden), bf16)] * 2 + [jax.ShapeDtypeStruct((rows, width), bf16)],
        [
            pltpu.VMEM(grad.shape, bf16),
            pltpu.VMEM(gate_weight.shape, bf16),
            pltpu.VMEM(up_weight.shape, bf16),
            pltpu.VMEM(down_weight.shape, bf16),
            pltpu.VMEM((2, 2, STEP, hidden), f32),
            pltpu.VMEM((2, 2, STEP, hidden), bf16),
            pltpu.VMEM((2, STEP, width), bf16),
            DMA((4,)),
            DMA((2, 2)),
            DMA((2, 3)),
        ],
        2 * (rows // STEP),
        body,
    )


def ffn_back_plain(grad, gate_pre, up_pre, gate_weight, up_weight, down_weight):
    grad_gate, grad_up = before_activation(dot_t(grad, down_weight), gate_pre, up_pre)
    back = dot_t(grad_gate, gate_weight) + dot_t(grad_up, up_weight)
    return grad_gate, grad_up, back.astype(bf16)


def dispatch_job(rows, n_ws):
    n, count, width = rows.shape

    def body(rows, out, own, load_sem, ep_s, ep_r, y_s, y_r, c_s, c_r, x_s, x_r):
        e, w = lax.axis_index("ep"), lax.axis_index("ws")
        twin, other = flip(w, 1), flip(w, 2)
        sources = [e] + [flip(e, k) for k in range(1, n)]
        first = []
        for i, s in enumerate(sources[1:]):
            first.append(remote(rows.at[s], out.at[e, w], ep_s.at[i], ep_r.at[i], (s, w)))
            first[-1].start()
        load = pltpu.make_async_copy(rows.at[e], own, load_sem.at[0])
        load.start()
        over_y, to_twin, relayed = [], [], []

        def relay(j):
            over_y[j].wait_recv()
            block = out.at[sources[j], other]
            relayed.append(remote(block, block, x_s.at[j], x_r.at[j], (e, twin)))
            relayed[-1].start()

        for j, s in enumerate(sources):
            place = out.at[s, w]
            block = rows.at[e] if j == 0 else place
            if j:
                first[j - 1].wait_recv()
            over_y.append(remote(block, place, y_s.at[j], y_r.at[j], (e, other)))
            over_y[-1].start()
            to_twin.append(remote(block, place, c_s.at[j], c_r.at[j], (e, twin)))
            to_twin[-1].start()
            if j == 0:
                load.wait()
                store = pltpu.make_async_copy(own, out.at[e, w], load_sem.at[1])
                store.start()
            else:
                relay(j - 1)
            yield
        relay(n - 1)
        store.wait()
        for copy in first + over_y:
            copy.wait_send()
        for copy in to_twin + relayed:
            copy.wait()

    return Job(
        [rows],
        [jax.ShapeDtypeStruct((n, n_ws, count, width), rows.dtype)],
        [pltpu.VMEM((count, width), rows.dtype), DMA((2,)), DMA((n - 1,)), DMA((n - 1,))]
        + [DMA((n,)) for _ in range(6)],
        n,
        body,
        [(k, 0) for k in range(1, n)] + [(0, 1), (0, 2)],
    )


def combine_job(part):
    n, _, count, width = part.shape
    block = (n, count, width)

    def body(
        part, out, mine, core, sum_y, from_y, total, load_sem, c_s, c_r, y_s, y_r, ep_s, ep_r, own_sem
    ):
        e, w = lax.axis_index("ep"), lax.axis_index("ws")
        twin, other, last = flip(w, 1), flip(w, 2), flip(w, 3)
        targets = [flip(e, k) for k in far_first(n)] + [e]
        loads, cores = {}, {}
        for half, near, far in ((1, other, last), (0, w, twin)):
            for j, s in enumerate(targets):
                cores[half, j] = remote(
                    part.at[s, far], core.at[half, j], c_s.at[half, j], c_r.at[half, j], (e, twin)
                )
                cores[half, j].start()
                loads[half, j] = pltpu.make_async_copy(
                    part.at[s, near], mine.at[half, j], load_sem.at[half, j]
                )
                loads[half, j].start()
        over_y, back = [], []

        def send_y(j):
            over_y.append(remote(sum_y.at[j], from_y.at[j], y_s.at[j], y_r.at[j], (e, other)))
            over_y[-1].start()

        def send_back(j):
            back.append(remote(total.at[j], out.at[e], ep_s.at[j], ep_r.at[j], (targets[j], w)))
            back[-1].start()

        for j in range(n):
            loads[1, j].wait()
            cores[1, j].wait_recv()
            sum_y[j] = (mine[1, j].astype(f32) + core[1, j].astype(f32)).astype(bf16)
            if j:
                send_y(j - 1)
        loads[0, 0].wait()
        cores[0, 0].wait_recv()
        send_y(n - 1)
        for j in range(n):
            if j:
                loads[0, j].wait()
                cores[0, j].wait_recv()
            over_y[j].wait_recv()
            total[j] = (
                mine[0, j].astype(f32) + core[0, j].astype(f32) + from_y[j].astype(f32)
            ).astype(bf16)
            if j:
                send_back(j - 1)
            yield
        for copy in over_y + list(cores.values()):
            copy.wait_send()
        keep = pltpu.make_async_copy(total.at[n - 1], out.at[e], own_sem)
        keep.start()
        for copy in back:
            copy.wait()
        keep.wait()

    return Job(
        [part],
        [jax.ShapeDtypeStruct(block, part.dtype)],
        [
            pltpu.VMEM((2,) + block, part.dtype),
            pltpu.VMEM((2,) + block, part.dtype),
            pltpu.VMEM(block, part.dtype),
            pltpu.VMEM(block, part.dtype),
            pltpu.VMEM(block, part.dtype),
            DMA((2, n)),
            DMA((2, n)),
            DMA((2, n)),
            DMA((n,)),
            DMA((n,)),
            DMA((n - 1,)),
            DMA((n - 1,)),
            DMA,
        ],
        n,
        body,
        [(k, 0) for k in range(1, n)] + [(0, 1), (0, 2)],
    )


def exchange_job(rows):
    n = rows.shape[0]

    def body(rows, out, own, load_sem, ep_s, ep_r):
        e, w = lax.axis_index("ep"), lax.axis_index("ws")
        targets = [flip(e, k) for k in far_first(n)]
        copies = []
        for i, s in enumerate(targets):
            copies.append(remote(rows.at[s], out.at[e], ep_s.at[i], ep_r.at[i], (s, w)))
            copies[-1].start()
        load = pltpu.make_async_copy(rows.at[e], own, load_sem.at[0])
        load.start()
        load.wait()
        store = pltpu.make_async_copy(own, out.at[e], load_sem.at[1])
        store.start()
        yield
        store.wait()
        for copy in copies:
            copy.wait()

    return Job(
        [rows],
        [jax.ShapeDtypeStruct(rows.shape, rows.dtype)],
        [pltpu.VMEM(rows.shape[1:], rows.dtype), DMA((2,)), DMA((n - 1,)), DMA((n - 1,))],
        1,
        body,
        [(k, 0) for k in range(1, n)],
    )


def exchange_combine_job(rows, weight, product, n_ws):
    n, held, depth = rows.shape
    count, width = held // n_ws, max(weight.shape)
    block = (n, count, width)
    turned = weight.shape[0] == width

    def body(
        rows, w_hbm, moved, out, w_ref, here, part, core, sum_y, from_y, total, load_sem, ep_s, ep_r, c_s, c_r,
        y_s, y_r, b_s, b_r
    ):
        e, w = lax.axis_index("ep"), lax.axis_index("ws")
        twin, other, last = flip(w, 1), flip(w, 2), flip(w, 3)
        places = [e] + [flip(e, k) for k in range(1, n)]
        weights = pltpu.make_async_copy(w_hbm, w_ref, load_sem.at[n])
        weights.start()
        arrivals = []
        for i, s in enumerate(places[1:]):
            arrivals.append(remote(rows.at[s], moved.at[e], ep_s.at[i], ep_r.at[i], (s, w)))
            arrivals[i].start()
        cores, over_y, back, stores = {}, [], [], []

        def multiply(j):
            if j:
                arrivals[j - 1].wait_recv()
            src = moved.at[places[j]] if j else rows.at[e]
            load = pltpu.make_async_copy(src, here.at[j], load_sem.at[j])
            load.start()
            load.wait()
            if j == 0:
                stores.append(pltpu.make_async_copy(here.at[0], moved.at[e], load_sem.at[0]))
                stores[0].start()
                weights.wait()

            def tile(at, columns):
                tall = pl.ds(at, columns)
                result = product(here[j], w_ref[tall, :] if turned else w_ref[:, tall])
                part[j, :, :, tall] = result.reshape(n_ws, count, columns).astype(bf16)

            column_tiles(width, tile)

        def send_core(j):
            for half, to in ((1, last), (0, twin)):
                cores[half, j] = remote(
                    part.at[j, to], core.at[half, j], c_s.at[half, j], c_r.at[half, j], (e, twin)
                )
                cores[half, j].start()

        def add_core(j):
            cores[1, j].wait_recv()
            sum_y[j] = (part[j, other].astype(f32) + core[1, j].astype(f32)).astype(bf16)

        def send_y(j):
            over_y.append(remote(sum_y.at[j], from_y.at[j], y_s.at[j], y_r.at[j], (e, other)))
            over_y[j].start()

        def add_all(j):
            cores[0, j].wait_recv()
            over_y[j].wait_recv()
            total[j] = (
                part[j, w].astype(f32) + core[0, j].astype(f32) + from_y[j].astype(f32)
            ).astype(bf16)

        def send_back(j):
            if j:
                back.append(
                    remote(total.at[j], out.at[e], b_s.at[j - 1], b_r.at[j - 1], (places[j], w))
                )
                back[j - 1].start()
            else:
                stores.append(pltpu.make_async_copy(total.at[0], out.at[e], load_sem.at[1]))
                stores[1].start()

        for t in range(n + 4):
            for lag, stage in ((0, multiply), (1, add_core), (3, add_all), (0, send_core), (1, send_y), (4, send_back)):
                if 0 <= t - lag < n:
                    stage(t - lag)
            yield
        for copy in arrivals + list(cores.values()) + over_y:
            copy.wait_send()
        for copy in back + stores:
            copy.wait()

    return Job(
        [rows, weight],
        [jax.ShapeDtypeStruct(rows.shape, bf16), jax.ShapeDtypeStruct(block, bf16)],
        [
            pltpu.VMEM(weight.shape, bf16),
            pltpu.VMEM(rows.shape, bf16),
            pltpu.VMEM((n, n_ws, count, width), bf16),
            pltpu.VMEM((2,) + block, bf16),
            pltpu.VMEM(block, bf16),
            pltpu.VMEM(block, bf16),
            pltpu.VMEM(block, bf16),
            DMA((n + 1,)),
            DMA((n - 1,)),
            DMA((n - 1,)),
            DMA((2, n)),
            DMA((2, n)),
            DMA((n,)),
            DMA((n,)),
            DMA((n - 1,)),
            DMA((n - 1,)),
        ],
        n + 4,
        body,
        [(k, 0) for k in range(1, n)] + [(0, 1), (0, 2)],
    )


def dispatch_exchange_job(rows, weight, product, n_ws):
    n, count, width = rows.shape
    turned = weight.shape[1] == width
    narrow = weight.shape[0] if turned else weight.shape[1]

    def body(
        rows, w_hbm, out, moved, w_ref, own, here, flat, res, load_sem, ep_s, ep_r, y_s, y_r, c_s, c_r, x_s, x_r,
        b_s, b_r
    ):
        e, w = lax.axis_index("ep"), lax.axis_index("ws")
        twin, other = flip(w, 1), flip(w, 2)
        places = [e] + [flip(e, k) for k in range(1, n)]
        weights = pltpu.make_async_copy(w_hbm, w_ref, load_sem.at[2])
        weights.start()
        first, over_y, to_twin, relayed, back, stores = [], [], [], [], [], []
        for i, s in enumerate(places[1:]):
            first.append(remote(rows.at[s], out.at[e, w], ep_s.at[i], ep_r.at[i], (s, w)))
            first[i].start()
        load = pltpu.make_async_copy(rows.at[e], own, load_sem.at[0])
        load.start()

        def arrive(j):
            place = out.at[places[j], w]
            block = place if j else rows.at[e]
            if j:
                first[j - 1].wait_recv()
            over_y.append(remote(block, place, y_s.at[j], y_r.at[j], (e, other)))
            over_y[j].start()
            to_twin.append(remote(block, place, c_s.at[j], c_r.at[j], (e, twin)))
            to_twin[j].start()
            if j == 0:
                load.wait()
                stores.append(pltpu.make_async_copy(own, place, load_sem.at[1]))
                stores[0].start()

        def relay(j):
            over_y[j].wait_recv()
            block = out.at[places[j], other]
            relayed.append(remote(block, block, x_s.at[j], x_r.at[j], (e, twin)))
            relayed[j].start()

        def multiply(j):
            to_twin[j].wait_recv()
            relayed[j].wait_recv()
            if j == 0:
                stores[0].wait()
                weights.wait()
            source = pltpu.make_async_copy(out.at[places[j]], here, load_sem.at[0])
            source.start()
            source.wait()
            flat[...] = here[...].astype(f32).reshape(n_ws * count, width).astype(bf16)

            def tile(at, columns):
                tall = pl.ds(at, columns)
                part = product(flat[...], w_ref[tall, :] if turned else w_ref[:, tall])
                res[j, :, tall] = part.astype(bf16)

            column_tiles(narrow, tile)

        def send(j):
            if j:
                back.append(
                    remote(res.at[j], moved.at[e], b_s.at[j - 1], b_r.at[j - 1], (places[j], w))
                )
                back[j - 1].start()
            else:
                stores.append(pltpu.make_async_copy(res.at[0], moved.at[e], load_sem.at[1]))
                stores[1].start()

        for t in range(n + 3):
            for lag, stage in enumerate((arrive, relay, multiply, send)):
                if 0 <= t - lag < n:
                    stage(t - lag)
            yield
        for copy in first + over_y + to_twin + relayed:
            copy.wait_send()
        for copy in back + stores[1:]:
            copy.wait()

    return Job(
        [rows, weight],
        [
            jax.ShapeDtypeStruct((n, n_ws, count, width), bf16),
            jax.ShapeDtypeStruct((n, n_ws * count, narrow), bf16),
        ],
        [
            pltpu.VMEM(weight.shape, bf16),
            pltpu.VMEM((count, width), bf16),
            pltpu.VMEM((n_ws, count, width), bf16),
            pltpu.VMEM((n_ws * count, width), bf16),
            pltpu.VMEM((n, n_ws * count, narrow), bf16),
            DMA((3,)),
            DMA((n - 1,)),
            DMA((n - 1,)),
        ]
        + [DMA((n,)) for _ in range(6)]
        + [DMA((n - 1,)), DMA((n - 1,))],
        n + 3,
        body,
        [(k, 0) for k in range(1, n)] + [(0, 1), (0, 2)],
    )


def gather_weights_job(mine, normed, n, n_ws):
    rows, block = mine.shape
    routes = [(4, 0), (2, 0), (2, 4)]

    def body(
        mine, normed, out, seq, held, held_rows, load_sem, s_sem, r_sem, x_s, x_r, y_s, y_r, c_s, c_r, t_s, t_r
    ):
        e, w = lax.axis_index("ep"), lax.axis_index("ws")
        twin, other, near = flip(w, 1), flip(w, 2), flip(e, 1)
        copies = {}

        def send(hop, offset, half):
            k = routes.index((hop, offset))
            part = pl.ds(half * (rows // 2), rows // 2)
            at = pl.multiple_of(flip(e, offset) // 2 * block, block)
            place = out.at[part, pl.ds(at, block)]
            copies[hop, offset, half] = remote(
                place if offset else mine.at[part],
                place,
                s_sem.at[k, half],
                r_sem.at[k, half],
                (flip(e, hop), w),
            )
            copies[hop, offset, half].start()

        for half in range(2):
            for route in routes[:2]:
                send(*route, half)
        to_near = remote(normed, seq.at[e % 2, w], x_s, x_r, (near, w))
        to_near.start()
        over_y, to_twin, relays = [], [], []

        def spread_rows(k, half, src):
            place = seq.at[half, w]
            over_y.append(remote(src, place, y_s.at[k], y_r.at[k], (e, other)))
            over_y[k].start()
            to_twin.append(remote(src, place, c_s.at[k], c_r.at[k], (e, twin)))
            to_twin[k].start()

        def relay(k, half):
            over_y[k].wait_recv()
            place = seq.at[half, other]
            relays.append(remote(place, place, t_s.at[k], t_r.at[k], (e, twin)))
            relays[k].start()

        spread_rows(0, e % 2, normed)
        loads = fetch(((mine, held), (normed, held_rows)), load_sem)
        for load in loads:
            load.wait()
        own = out.at[:, pl.ds(pl.multiple_of(e // 2 * block, block), block)]
        stores = fetch(((held, own), (held_rows, seq.at[e % 2, w])), load_sem)
        yield
        to_near.wait_recv()
        spread_rows(1, near % 2, seq.at[near % 2, w])
        yield
        copies[4, 0, 0].wait_recv()
        send(2, 4, 0)
        yield
        relay(0, e % 2)
        copies[4, 0, 1].wait_recv()
        send(2, 4, 1)
        yield
        relay(1, near % 2)
        yield
        for store in stores:
            store.wait()
        for (_, offset, half), copy in copies.items():
            copy.wait_send()
            if (_, offset) != (4, 0):
                copy.wait_recv()
        to_near.wait_send()
        for copy in over_y:
            copy.wait_send()
        for copy in to_twin + relays:
            copy.wait()

    return Job(
        [mine, normed],
        [
            jax.ShapeDtypeStruct((rows, n // 2 * block), bf16),
            jax.ShapeDtypeStruct((2, n_ws) + normed.shape, bf16),
        ],
        [
            pltpu.VMEM(mine.shape, bf16),
            pltpu.VMEM(normed.shape, bf16),
            DMA((2,)),
            DMA((3, 2)),
            DMA((3, 2)),
            DMA,
            DMA,
        ]
        + [DMA((2,)) for _ in range(6)],
        5,
        body,
        [(1, 0), (2, 0), (4, 0), (0, 1), (0, 2)],
    )


def swap_job(blocks):
    def body(blocks, out, held, load_sem, s_sem, r_sem):
        e, w = lax.axis_index("ep"), lax.axis_index("ws")
        near = flip(e, 1)
        copy = remote(blocks.at[near % 2], out.at[e % 2], s_sem, r_sem, (near, w))
        copy.start()
        load = fetch(((blocks.at[e % 2], held),), load_sem)[0]
        load.wait()
        store = fetch(((held, out.at[e % 2]),), load_sem)[0]
        yield
        store.wait()
        copy.wait()

    return Job(
        [blocks],
        [jax.ShapeDtypeStruct(blocks.shape, blocks.dtype)],
        [pltpu.VMEM(blocks.shape[1:], blocks.dtype), DMA((1,)), DMA, DMA],
        1,
        body,
        [(1, 0)],
    )


def add_blocks(out, *refs):
    step = 64 if out.shape[1] > 1024 else 256

    def body(i, carry):
        at = pl.ds(pl.multiple_of(i * step, step), step)
        total = refs[0][at].astype(f32)
        for ref in refs[1:]:
            total = total + ref[at].astype(f32)
        out[at] = total.astype(bf16)
        return carry

    lax.fori_loop(0, out.shape[0] // step, body, 0)


def reduce_weights_job(pieces, part, n):
    rows = pieces.shape[0]
    block = pieces.shape[1] // (n // 2)
    offsets = (4, 0)

    def body(
        pieces, part, out, out_rows, mine, from_z, fourth, last_z, total, own, core, sum_y, from_y, total_near,
        from_near, total_rows, load_sem, z_s, z_r, w_load, c_s, c_r, y_s, y_r, x_s, x_r, sem
    ):
        e, w = lax.axis_index("ep"), lax.axis_index("ws")
        twin, other, last, near = flip(w, 1), flip(w, 2), flip(w, 3), flip(e, 1)

        def columns(s):
            return pieces.at[:, pl.ds(pl.multiple_of(s // 2 * block, block), block)]

        over_z = []
        for i, offset in enumerate(offsets):
            over_z.append(
                remote(columns(flip(e, offset + 2)), from_z.at[i], z_s.at[i], z_r.at[i], (flip(e, 2), w))
            )
            over_z[i].start()
        halves = (near % 2, e % 2)
        cores = {}
        for k, to in enumerate((last, twin)):
            for h, half in enumerate(halves):
                cores[h, k] = remote(
                    part.at[half, to], core.at[h, k], c_s.at[h, k], c_r.at[h, k], (e, twin)
                )
                cores[h, k].start()
        loads = fetch([(columns(flip(e, o)), mine.at[i]) for i, o in enumerate(offsets)], load_sem)
        own_loads = {}
        for h, half in enumerate(halves):
            for k, to in enumerate((other, w)):
                own_loads[h, k] = pltpu.make_async_copy(
                    part.at[half, to], own.at[h, k], w_load.at[h, k]
                )
                own_loads[h, k].start()
        yield
        over_y = []

        def send_y(h):
            over_y.append(remote(sum_y.at[h], from_y.at[h], y_s.at[h], y_r.at[h], (e, other)))
            over_y[h].start()

        for h in range(2):
            own_loads[h, 0].wait()
            cores[h, 0].wait_recv()
            add_blocks(sum_y.at[h], own.at[h, 0], core.at[h, 0])
            if h:
                send_y(0)
        yield
        loads[0].wait()
        over_z[0].wait_recv()
        send_y(1)
        add_blocks(fourth, mine.at[0], from_z.at[0])
        yield
        own_loads[0, 1].wait()
        cores[0, 1].wait_recv()
        over_y[0].wait_recv()
        far = remote(fourth, last_z, z_s.at[2], z_r.at[2], (flip(e, 4), w))
        far.start()
        add_blocks(total_near, own.at[0, 1], core.at[0, 1], from_y.at[0])
        yield
        own_loads[1, 1].wait()
        cores[1, 1].wait_recv()
        over_y[1].wait_recv()
        to_near = remote(total_near, from_near, x_s, x_r, (near, w))
        to_near.start()
        yield
        to_near.wait_recv()
        add_blocks(total_rows, own.at[1, 1], core.at[1, 1], from_y.at[1], from_near)
        loads[1].wait()
        over_z[1].wait_recv()
        far.wait_recv()
        add_blocks(total, mine.at[1], from_z.at[1], last_z)
        stores = fetch(((total_rows, out_rows), (total, out)), sem)
        for copy in over_z + list(cores.values()) + over_y + [far, to_near]:
            copy.wait_send()
        for store in stores:
            store.wait()

    one, rows_one = (rows, block), part.shape[2:]
    return Job(
        [pieces, part],
        [jax.ShapeDtypeStruct(one, bf16), jax.ShapeDtypeStruct(rows_one, bf16)],
        [pltpu.VMEM((2,) + one, bf16) for _ in range(2)]
        + [pltpu.VMEM(one, bf16) for _ in range(3)]
        + [pltpu.VMEM((2, 2) + rows_one, bf16) for _ in range(2)]
        + [pltpu.VMEM((2,) + rows_one, bf16) for _ in range(2)]
        + [pltpu.VMEM(rows_one, bf16) for _ in range(3)]
        + [DMA((2,)), DMA((3,)), DMA((3,)), DMA((2, 2)), DMA((2, 2)), DMA((2, 2))]
        + [DMA((2,)), DMA((2,)), DMA, DMA, DMA((2,))],
        5,
        body,
        [(1, 0), (2, 0), (4, 0), (0, 1), (0, 2)],
    )


def attend_kernel(spans, q_ref, kv_ref, out):
    count, _, slots, part = q_ref.shape
    for w, span in enumerate(spans):

        def head(h, carry, w=w, span=span):
            at = pl.multiple_of(h * HEAD_SIZE, HEAD_SIZE)
            columns = pl.ds(at, HEAD_SIZE)
            q, probs, _, values = head_probs(q_ref, kv_ref, w, span, at)
            mixed = dot(probs.astype(bf16), values)
            out[:, w, :, columns] = mixed.reshape(count, slots, HEAD_SIZE).astype(bf16)
            return carry

        lax.fori_loop(0, part // HEAD_SIZE, head, 0)


def slot_rows(ref, w, at):
    count, _, slots, _ = ref.shape
    rows = ref[:, w, :, pl.ds(at, HEAD_SIZE)].astype(f32)
    return rows.reshape(count * slots, HEAD_SIZE).astype(bf16)


def kv_place(kv, at):
    h = at // HEAD_SIZE
    column = pl.multiple_of(h // 2 * HEAD_SIZE, HEAD_SIZE)
    half = kv.shape[2] // 2
    value_column = pl.multiple_of(half + column, HEAD_SIZE)
    return h % 2, pl.ds(column, HEAD_SIZE), pl.ds(value_column, HEAD_SIZE)


def head_probs(q_ref, kv_ref, w, span, at):
    q = slot_rows(q_ref, w, at)
    side, key_columns, value_columns = kv_place(kv_ref, at)
    keys = kv_ref[side, :span, key_columns]
    values = kv_ref[side, :span, value_columns]
    scores = dot_t(q, keys) * HEAD_SIZE ** (-0.5)
    weight = jnp.exp(scores - jnp.max(scores, -1, keepdims=True))
    probs = weight / jnp.sum(weight, -1, keepdims=True)
    return q, probs, keys, values


def attend_call(queries, kv, spans):
    return pl.pallas_call(
        functools.partial(attend_kernel, spans),
        out_shape=jax.ShapeDtypeStruct(queries.shape, bf16),
        in_specs=[VM, VM],
        out_specs=VM,
        compiler_params=pltpu.CompilerParams(vmem_limit_bytes=VMEM_LIMIT),
        name="attend",
    )(queries, kv)


def attend_back_kernel(spans, q_ref, g_ref, kv_ref, grad_q, grad_kv, total):
    count, _, slots, part = q_ref.shape
    total[...] = jnp.zeros_like(total)
    for w, span in enumerate(spans):

        def head(h, carry, w=w, span=span):
            at = pl.multiple_of(h * HEAD_SIZE, HEAD_SIZE)
            columns = pl.ds(at, HEAD_SIZE)
            q, probs, keys, values = head_probs(q_ref, kv_ref, w, span, at)
            grad = slot_rows(g_ref, w, at)
            grad_probs = dot_t(grad, values)
            centred = jnp.sum(probs * grad_probs, -1, keepdims=True)
            grad_scores = (probs * (grad_probs - centred)).astype(bf16)
            grad_rows = dot(grad_scores, keys) * HEAD_SIZE ** (-0.5)
            grad_q[:, w, :, columns] = grad_rows.reshape(count, slots, HEAD_SIZE).astype(bf16)
            side, key_columns, value_columns = kv_place(kv_ref, at)
            total[side, :span, key_columns] += t_dot(grad_scores, q) * HEAD_SIZE ** (-0.5)
            total[side, :span, value_columns] += t_dot(probs.astype(bf16), grad)
            return carry

        lax.fori_loop(0, part // HEAD_SIZE, head, 0)
    grad_kv[...] = total[...].astype(bf16)


def attend_back_call(queries, grads, kv, spans):
    return pl.pallas_call(
        functools.partial(attend_back_kernel, spans),
        out_shape=[
            jax.ShapeDtypeStruct(queries.shape, bf16),
            jax.ShapeDtypeStruct(kv.shape, bf16),
        ],
        in_specs=[VM, VM, VM],
        out_specs=[VM, VM],
        scratch_shapes=[pltpu.VMEM(kv.shape, f32)],
        compiler_params=pltpu.CompilerParams(vmem_limit_bytes=VMEM_LIMIT),
        name="attend_back",
    )(queries, grads, kv)


def gather_gains_job(own, n, n_ws):
    def body(own, out, held, load_sem, w_s, w_r, ep_s, ep_r):
        e, w = lax.axis_index("ep"), lax.axis_index("ws")
        first = []
        for i in range(n_ws - 1):
            place = (e, flip(w, i + 1))
            first.append(remote(own, out.at[e, w], w_s.at[i], w_r.at[i], place))
            first[i].start()
        load = fetch(((own, held),), load_sem)[0]
        load.wait()
        store = fetch(((held, out.at[e, w]),), load_sem)[0]
        yield
        store.wait()
        for copy in first:
            copy.wait()
        second = []
        for i in range(n - 1):
            place = (flip(e, i + 1), w)
            second.append(remote(out.at[e], out.at[e], ep_s.at[i], ep_r.at[i], place))
            second[i].start()
        yield
        for copy in second:
            copy.wait()

    return Job(
        [own],
        [jax.ShapeDtypeStruct((n, n_ws) + own.shape, own.dtype)],
        [
            pltpu.VMEM(own.shape, own.dtype),
            DMA((1,)),
            DMA((n_ws - 1,)),
            DMA((n_ws - 1,)),
            DMA((n - 1,)),
            DMA((n - 1,)),
        ],
        2,
        body,
        [(k, 0) for k in range(1, n)] + [(0, k) for k in range(1, n_ws)],
    )


def reduce_kernel(n, n_ws, parts, out, held, all_parts, load_sem, w_s, w_r, ep_s, ep_r):
    e, w = lax.axis_index("ep"), lax.axis_index("ws")
    beside = [flip(w, k) for k in range(1, n_ws)]
    across = [flip(e, k) for k in far_first(n)]
    greet([(e, p) for p in beside] + [(s, w) for s in across])
    keep = pltpu.make_async_copy(parts.at[:, w], held.at[:, w], load_sem.at[0])
    keep.start()
    first = []
    for i, p in enumerate(beside):
        first.append(remote(parts.at[:, p], held.at[:, w], w_s.at[i], w_r.at[i], (e, p)))
        first[-1].start()
    keep.wait()
    for copy in first:
        copy.wait()
    keep = pltpu.make_async_copy(held.at[e], all_parts.at[e], load_sem.at[1])
    keep.start()
    second = []
    for i, s in enumerate(across):
        second.append(remote(held.at[s], all_parts.at[e], ep_s.at[i], ep_r.at[i], (s, w)))
        second[-1].start()
    keep.wait()
    for copy in second:
        copy.wait()
    out[...] = jnp.sum(jnp.sum(all_parts[...], 0), 0)


def reduce_call(parts):
    n, n_ws = parts.shape[:2]
    return pl.pallas_call(
        functools.partial(reduce_kernel, n, n_ws),
        out_shape=jax.ShapeDtypeStruct(parts.shape[2:], parts.dtype),
        in_specs=[VM],
        out_specs=VM,
        scratch_shapes=[
            pltpu.VMEM(parts.shape, parts.dtype),
            pltpu.VMEM(parts.shape, parts.dtype),
            DMA((2,)),
            DMA((n_ws - 1,)),
            DMA((n_ws - 1,)),
            DMA((n - 1,)),
            DMA((n - 1,)),
        ],
        compiler_params=pltpu.CompilerParams(collective_id=4, has_side_effects=True),
        name="reduce_gains",
    )(parts)


def small(n_ep):
    return n_ep == MIXTURE_EXPERTS and lax.axis_size("ws") == 4


PLAIN = {
    grad_job: lambda a, b: [t_dot(a, b)],
    pair_grad_job: lambda a, b, c: [jnp.stack([t_dot(a, b), t_dot(a, c)], 1)],
    split_job: lambda weight: [weight[:, 0], weight[:, 1]],
    ffn_job: ffn_plain,
    ffn_back_job: ffn_back_plain,
}


def beside(job, plain, arg, fills, collective_id, name):
    if job is None:
        return [plain(arg)] + [out for make, *rest in fills for out in PLAIN[make](*rest)]
    return run_jobs([job(arg)], [make(*rest) for make, *rest in fills], collective_id, name)


def exchange_plain(send):
    return lax.all_to_all(send, "ep", split_axis=0, concat_axis=0, tiled=True)


def exchange(send, *fills, collective_id=2, name="exchange"):
    job = exchange_job if small(send.shape[0]) else None
    return beside(job, exchange_plain, send, fills, collective_id, name)


def spread(rows, group):
    width = rows.shape[-1]
    blocks = rows.reshape(MIXTURE_EXPERTS, 1, ROWS, width)
    return jnp.broadcast_to(blocks, (MIXTURE_EXPERTS, group, ROWS, width)).reshape(
        MIXTURE_EXPERTS * group, ROWS, width
    )


def dispatch(rows, group, *fills, collective_id=0, name="dispatch"):
    width = rows.shape[-1]

    def plain(blocks):
        return lax.all_gather(exchange_plain(blocks), "ws", axis=1, tiled=False)

    job = functools.partial(dispatch_job, n_ws=4) if small(MIXTURE_EXPERTS * group) else None
    out = beside(job, plain, spread(rows, group), fills, collective_id, name)
    return [out[0].reshape(-1, width)] + list(out[1:])


def combine(partial, group, n_ep, n_ws, *fills, collective_id=1, name="combine"):
    width = partial.shape[-1]

    def plain(part):
        part = part.transpose(1, 0, 2, 3).reshape(n_ws * n_ep * ROWS, width)
        own = lax.psum_scatter(part, "ws", scatter_dimension=0, tiled=True)
        return exchange_plain(own.reshape(n_ep, ROWS, width))

    part = partial.reshape(n_ep, n_ws, ROWS, width)
    job = combine_job if small(n_ep) else None
    back, *rest = beside(job, plain, part, fills, collective_id, name)
    if group > 1:
        back = jnp.sum(back.reshape(MIXTURE_EXPERTS, group, ROWS, width).astype(f32), 1).astype(bf16)
    return [back.reshape(MIXTURE_EXPERTS * ROWS, width)] + rest


def slot_tables(routes, slots):
    target = jnp.where(slots < CAP, routes * ROWS + slots, -1)
    places = lax.broadcasted_iota(jnp.int32, (MIXTURE_EXPERTS * ROWS, target.shape[0]), 0)
    return [(places == target[None, :, k]).astype(bf16) for k in range(CHOSEN_EXPERTS)]


def norm_back(grad, unit, inverse, gain):
    gain_grad = jnp.sum(grad * unit, 0)
    scaled = grad * gain
    return (inverse * (scaled - unit * jnp.mean(scaled * unit, -1, keepdims=True)), gain_grad)


def heads_of(rows):
    return rows.reshape(rows.shape[0], -1, HEAD_SIZE)


def local(
    x_in,
    gain_attn,
    gain_ffn,
    key_value_weight,
    w_query,
    w_output,
    w_in,
    w_out,
    gate_attn,
    gate_ffn,
    route_attn,
    slot_attn,
    route_ffn,
    slot_ffn,
    cotangent,
):
    n_ep = lax.axis_size("ep")
    n_ws = lax.axis_size("ws")
    group = n_ep // MIXTURE_EXPERTS
    local_tokens, width = x_in.shape
    key_value_width = KEY_VALUE_HEADS * HEAD_SIZE
    part = w_query.shape[2]
    own_width = group * part
    sequence = n_ws * local_tokens
    place = lax.axis_index("ws")
    scale = HEAD_SIZE ** (-0.5)

    fused = small(n_ep) and key_value_weight.shape[1] == HEAD_SIZE and gain_attn.shape[0] == 64
    if fused:
        own_gains = jnp.concatenate([gain_attn, gain_ffn], 0).astype(f32)[None]
    else:
        gain_one = lax.all_gather(gain_attn, ("ep", "ws"), axis=0, tiled=True).astype(f32)
        gain_two = lax.all_gather(gain_ffn, ("ep", "ws"), axis=0, tiled=True).astype(f32)
    plain = group == 1 and key_value_weight.shape[1] == HEAD_SIZE
    if plain:
        half = n_ep // 2
        there = [
            (e * n_ws + w, (w + n_ws * (e // half)) * n_ws + e % half)
            for e in range(n_ep)
            for w in range(n_ws)
        ]
        mine = lax.ppermute(key_value_weight, ("ep", "ws"), there)
    else:
        whole = lax.all_gather(key_value_weight, ("ep", "ws"), axis=1, tiled=True)
        whole = whole.reshape(width, 2 * group, n_ws, part)
        kv_own = lax.dynamic_index_in_dim(whole, place, 2, keepdims=False).reshape(width, -1)

    inputs = x_in.astype(f32)
    inverse_one = lax.rsqrt(jnp.mean(inputs * inputs, -1, keepdims=True) + EPS)
    unit_one = inputs * inverse_one
    normed = (unit_one if fused else unit_one * gain_one).astype(bf16)
    attn_pairs = slot_tables(route_attn, slot_attn)
    ffn_pairs = slot_tables(route_ffn, slot_ffn)
    attn_tokens = attn_pairs[0] + attn_pairs[1]
    ffn_tokens = ffn_pairs[0] + ffn_pairs[1]

    slots_one = dot(attn_tokens, normed).astype(bf16)
    if fused:
        rows_one, kv_own, normed_sequence, gains, gate_weight, up_weight = run_jobs(
            [
                dispatch_job(slots_one.reshape(n_ep, ROWS, width), n_ws),
                gather_weights_job(mine, normed, n_ep, n_ws),
                gather_gains_job(own_gains, n_ep, n_ws),
            ],
            [split_job(w_in[0])],
            10,
            "dispatch_weights",
        )
        gains = gains.reshape(n_ep * n_ws, 2, -1)
        gain_one, gain_two = gains[:, 0].reshape(-1), gains[:, 1].reshape(-1)
        rows_one = (rows_one.reshape(-1, width).astype(f32) * gain_one).astype(bf16)
        normed_sequence = normed_sequence.reshape(2 * sequence, width).astype(f32) * gain_one
        normed_sequence = normed_sequence.astype(bf16)
    else:
        if plain:
            kv_own = lax.all_gather(mine, "ep", axis=1, tiled=True)
        normed_sequence = lax.all_gather(normed, "ws", axis=0, tiled=True)
        rows_one, gate_weight, up_weight = dispatch(slots_one, group, (split_job, w_in[0]))
    kv = dot(normed_sequence, kv_own).astype(bf16)
    if not fused:
        keys = kv[:, :own_width].reshape(sequence, -1, HEAD_SIZE)
        values = kv[:, own_width:].reshape(sequence, -1, HEAD_SIZE)

    owner_query = dot(rows_one, w_query[0]).astype(bf16)
    owner_query = owner_query.reshape(n_ep, n_ws * ROWS, part)
    if fused:
        queries, kv = run_jobs(
            [exchange_job(owner_query), swap_job(kv.reshape(2, sequence, -1))], [], 13, "exchange_kv"
        )
    else:
        queries = exchange(owner_query)[0]
    queries = queries.reshape(MIXTURE_EXPERTS, group, n_ws, ROWS, part)
    spans = [(w * local_tokens // BLOCK + 1) * BLOCK for w in range(n_ws)]

    def by_block(rows):
        rows = rows.reshape(MIXTURE_EXPERTS, group, n_ws, ROWS, part)
        return [
            rows[:, :, w].transpose(0, 2, 1, 3).reshape(-1, own_width // HEAD_SIZE, HEAD_SIZE)
            for w in range(n_ws)
        ]

    def to_experts(pieces):
        rows = jnp.stack(
            [
                piece.reshape(MIXTURE_EXPERTS, ROWS, group, part).transpose(0, 2, 1, 3)
                for piece in pieces
            ],
            2,
        )
        return rows.reshape(n_ep, n_ws * ROWS, part)

    if fused:
        queries = queries.reshape(n_ep, n_ws, ROWS, part)
        mixed = attend_call(queries, kv, spans).reshape(n_ep, n_ws * ROWS, part)
    else:
        kept = []
        mixed_pieces = []
        for q, span in zip(by_block(queries), spans):
            scores = (
                jnp.einsum("rhd,shd->hrs", q, keys[:span], preferred_element_type=f32) * scale
            )
            probs = jax.nn.softmax(scores, axis=-1)
            mixed = jnp.einsum(
                "hrs,shd->rhd", probs.astype(bf16), values[:span], preferred_element_type=f32
            )
            kept.append((q, probs))
            mixed_pieces.append(mixed.astype(bf16))
        mixed = to_experts(mixed_pieces)
    if fused:
        owner_mixed, attn_slots = run_jobs(
            [exchange_combine_job(mixed, w_output[0], dot, n_ws)], [], 11, "exchange_output"
        )
        owner_mixed, attn_slots = owner_mixed.reshape(-1, part), attn_slots.reshape(-1, width)
    else:
        owner_mixed = exchange(mixed)[0].reshape(-1, part)
        output_part = dot(owner_mixed, w_output[0]).astype(bf16)
        attn_slots = combine(output_part, group, n_ep, n_ws)[0]

    def weighted(pairs, gates, slot_values):
        return sum(gates[:, k : k + 1] * t_dot(pairs[k], slot_values) for k in range(2))

    def to_slots(pairs, gates, values):
        return sum(
            dot(pairs[k], (gates[:, k : k + 1] * values).astype(bf16)) for k in range(2)
        ).astype(bf16)

    hidden_state = inputs + weighted(attn_pairs, gate_attn, attn_slots)
    inverse_two = lax.rsqrt(jnp.mean(hidden_state * hidden_state, -1, keepdims=True) + EPS)
    unit_two = hidden_state * inverse_two
    normed_two = (unit_two * gain_two).astype(bf16)

    grad_out = cotangent.astype(f32)
    grad_slots = to_slots(ffn_pairs, gate_ffn, grad_out)
    expert_rows = dispatch(dot(ffn_tokens, normed_two).astype(bf16), group)[0]
    expert_grad, gate_pre, up_pre, activated, forward_part = dispatch(
        grad_slots,
        group,
        (ffn_job, expert_rows, gate_weight, up_weight, w_out[0]),
        collective_id=5,
        name="dispatch_ffn",
    )
    ffn_slots, grad_gate, grad_up, back_two = combine(
        forward_part,
        group,
        n_ep,
        n_ws,
        (ffn_back_job, expert_grad, gate_pre, up_pre, gate_weight, up_weight, w_out[0]),
        collective_id=1,
        name="combine_ffn_back",
    )
    result = hidden_state + weighted(ffn_pairs, gate_ffn, ffn_slots)
    back_slots, grad_second = combine(
        back_two,
        group,
        n_ep,
        n_ws,
        (grad_job, activated, expert_grad),
        collective_id=6,
        name="combine_grad_out",
    )

    grad_normed_two = t_dot(ffn_tokens, back_slots)
    grad_hidden_norm, grad_gain_two = norm_back(grad_normed_two, unit_two, inverse_two, gain_two)
    grad_hidden = grad_out + grad_hidden_norm
    attn_grads = to_slots(attn_pairs, gate_attn, grad_hidden)
    if fused:
        owner_grad, mixed_grads, grad_first = run_jobs(
            [dispatch_exchange_job(attn_grads.reshape(n_ep, ROWS, width), w_output[0], dot_t, n_ws)],
            [pair_grad_job(expert_rows, grad_gate, grad_up)],
            7,
            "dispatch_exchange",
        )
        owner_grad = owner_grad.reshape(-1, width)
    else:
        owner_grad = dispatch(attn_grads, group)[0]
        grad_first = jnp.stack([t_dot(expert_rows, grad_gate), t_dot(expert_rows, grad_up)], 1)
        back_mixed = dot_t(owner_grad, w_output[0]).astype(bf16)
        mixed_grads = exchange(back_mixed.reshape(n_ep, n_ws * ROWS, part))[0]
        grad_output = t_dot(owner_mixed, owner_grad)

    if fused:
        mixed_grads = mixed_grads.reshape(n_ep, n_ws, ROWS, part)
        query_grads, grad_kv_rows = attend_back_call(queries, mixed_grads, kv, spans)
        query_grads = query_grads.reshape(n_ep, n_ws * ROWS, part)
    else:
        grad_keys, grad_values, query_pieces = 0.0, 0.0, []
        for (q, probs), grad, span in zip(kept, by_block(mixed_grads), spans):
            grad_probs = jnp.einsum("rhd,shd->hrs", grad, values[:span], preferred_element_type=f32)
            centred = jnp.sum(probs * grad_probs, -1, keepdims=True)
            grad_scores = (probs * (grad_probs - centred)).astype(bf16)
            grad_q = (
                jnp.einsum("hrs,shd->rhd", grad_scores, keys[:span], preferred_element_type=f32)
                * scale
            )
            query_pieces.append(grad_q.astype(bf16))
            pad = ((0, sequence - span), (0, 0), (0, 0))
            piece = jnp.einsum("hrs,rhd->shd", grad_scores, q, preferred_element_type=f32) * scale
            grad_keys = grad_keys + jnp.pad(piece, pad)
            piece = jnp.einsum(
                "hrs,rhd->shd", probs.astype(bf16), grad, preferred_element_type=f32
            )
            grad_values = grad_values + jnp.pad(piece, pad)
        grad_kv_rows = jnp.concatenate(
            [grad_keys.reshape(sequence, -1), grad_values.reshape(sequence, -1)], 1
        ).astype(bf16)
        query_grads = to_experts(query_pieces)
    if fused:
        owner_grad_query, normed_back, grad_kv_rows, grad_output = run_jobs(
            [exchange_combine_job(query_grads, w_query[0], dot_t, n_ws), swap_job(grad_kv_rows)],
            [grad_job(owner_mixed, owner_grad)],
            14,
            "exchange_back",
        )
        owner_grad_query = owner_grad_query.reshape(-1, part)
        normed_back = normed_back.reshape(-1, width)
        grad_kv_rows = grad_kv_rows.reshape(2 * sequence, -1)
    else:
        owner_grad_query = exchange(query_grads)[0].reshape(-1, part)
    grad_kv = t_dot(normed_sequence, grad_kv_rows)
    from_kv = dot_t(grad_kv_rows, kv_own).astype(bf16)
    if fused:
        piece, from_kv, grad_query = run_jobs(
            [
                reduce_weights_job(
                    grad_kv.astype(bf16), from_kv.reshape(2, n_ws, local_tokens, width), n_ep
                )
            ],
            [grad_job(rows_one, owner_grad_query)],
            9,
            "reduce_weights",
        )
    else:
        back_normed = dot_t(owner_grad_query, w_query[0]).astype(bf16)
        normed_back = combine(back_normed, group, n_ep, n_ws)[0]
        grad_query = t_dot(rows_one, owner_grad_query)
    if fused:
        back = [(b, a) for a, b in there]
        grad_kv_shard = lax.ppermute(piece, ("ep", "ws"), back).astype(f32)
    elif plain:
        pieces = grad_kv.reshape(width, n_ep, HEAD_SIZE).transpose(1, 0, 2).astype(bf16)
        piece = lax.psum_scatter(pieces, "ep", scatter_dimension=0, tiled=False)
        grad_kv_shard = lax.ppermute(piece, ("ep", "ws"), [(b, a) for a, b in there]).astype(f32)
    else:
        mask = (jnp.arange(n_ws) == place)[None, None, :, None]
        pieces = jnp.where(mask, grad_kv.reshape(width, 2 * group, 1, part), 0.0)
        pieces = pieces.reshape(width, 2 * key_value_width).astype(bf16)
        grad_kv_shard = lax.psum_scatter(
            pieces, ("ep", "ws"), scatter_dimension=1, tiled=True
        ).astype(f32)
    if not fused:
        from_kv = lax.psum_scatter(from_kv, "ws", scatter_dimension=0, tiled=True)
    grad_normed = t_dot(attn_tokens, normed_back) + from_kv.astype(f32)
    grad_input_norm, grad_gain_one = norm_back(grad_normed, unit_one, inverse_one, gain_one)
    grad_input = grad_hidden + grad_input_norm
    gain_grads = jnp.stack([grad_gain_one, grad_gain_two], 0)
    if fused:
        parts = gain_grads.reshape(2, n_ep, n_ws, -1).transpose(1, 2, 0, 3)
        gain_shards = reduce_call(parts.reshape(n_ep, n_ws, 1, -1)).reshape(2, -1)
    else:
        gain_shards = lax.psum_scatter(
            gain_grads, ("ep", "ws"), scatter_dimension=1, tiled=True
        )
    return (
        result.astype(bf16),
        grad_input,
        gain_shards[0],
        gain_shards[1],
        grad_kv_shard,
        grad_query[None],
        grad_output[None],
        grad_first[None],
        grad_second[None],
    )


def solution(mesh):
    both = ("ep", "ws")
    rows, vector, columns = P(both, None), P(both), P(None, both)
    return jax.shard_map(
        local,
        mesh=mesh,
        in_specs=(
            rows,
            vector,
            vector,
            columns,
            P("ep", None, "ws"),
            P("ep", "ws", None),
            P("ep", None, None, "ws"),
            P("ep", "ws", None),
            rows,
            rows,
            rows,
            rows,
            rows,
            rows,
            rows,
        ),
        out_specs=(
            rows,
            rows,
            vector,
            vector,
            columns,
            P("ep", None, "ws"),
            P("ep", "ws", None),
            P("ep", None, None, "ws"),
            P("ep", "ws", None),
        ),
        check_vma=False,
    )
```

```python
import functools

import jax
import jax.numpy as jnp
from jax import lax
from jax.experimental import pallas as pl
from jax.experimental.pallas import tpu as pltpu
from jax.sharding import PartitionSpec as P

KEY_VALUE_HEADS = 16
HEAD_SIZE = 128
MIXTURE_EXPERTS = 8
CHOSEN_EXPERTS = 2
BLOCK = 256
CAP = 36
ROWS = 40

EPS = 1e-06
very_negative = -1e30
f32 = jnp.float32
bf16 = jnp.bfloat16
MESH = pl.DeviceIdType.MESH
ANY = pl.BlockSpec(memory_space=pl.ANY)
VM = pl.BlockSpec(memory_space=pltpu.VMEM)
DMA = pltpu.SemaphoreType.DMA
STEP = 256
VMEM_LIMIT = 60 << 20


def dot(a, b):
    return jnp.dot(a, b, preferred_element_type=f32)


def dot_t(a, b):
    return lax.dot_general(a, b, (((1,), (1,)), ((), ())), preferred_element_type=f32)


def t_dot(a, b):
    return lax.dot_general(a, b, (((0,), (0,)), ((), ())), preferred_element_type=f32)


def flip(index, bits):
    out, bit = index, 1
    while bit <= bits:
        if bits & bit:
            out = out + bit - 2 * bit * ((index // bit) % 2)
        bit *= 2
    return out


def far_first(n):
    return sorted(range(1, n), key=lambda k: (-((k // 2).bit_length()), k))


def crossed():
    e, w, n_ws = lax.axis_index("ep"), lax.axis_index("ws"), lax.axis_size("ws")
    return (w + n_ws * (e // n_ws), e % n_ws), e % n_ws != w


def greet(partners, crossing=False):
    barrier = pltpu.get_barrier_semaphore()
    for partner in partners:
        pl.semaphore_signal(barrier, inc=1, device_id=partner, device_id_type=MESH)
    if crossing:
        partner, another = crossed()

        @pl.when(another)
        def _():
            pl.semaphore_signal(barrier, inc=1, device_id=partner, device_id_type=MESH)
            pl.semaphore_wait(barrier, len(partners) + 1)

        @pl.when(jnp.logical_not(another))
        def _():
            pl.semaphore_wait(barrier, len(partners))

    else:
        pl.semaphore_wait(barrier, len(partners))


def remote(src, dst, send, recv, device):
    return pltpu.make_async_remote_copy(
        src_ref=src, dst_ref=dst, send_sem=send, recv_sem=recv, device_id=device, device_id_type=MESH
    )


class Job:
    def __init__(self, args, outs, scratch, steps, body, partners=(), crossing=False):
        self.args, self.outs, self.scratch, self.steps, self.body = args, outs, scratch, steps, body
        self.partners, self.crossing = partners, crossing


def run_jobs(jobs, fills, collective_id, name):
    whole = jobs + fills
    args = [a for job in whole for a in job.args]
    outs = [o for job in whole for o in job.outs]
    scratch = [x for job in whole for x in job.scratch]
    turns = sorted((k / job.steps, i) for i, job in enumerate(jobs) for k in range(job.steps))
    partners = sorted({p for job in jobs for p in job.partners})
    crossing = any(job.crossing for job in jobs)

    def kernel(*refs):
        bodies, at = [], [0, len(args), len(args) + len(outs)]
        for job in whole:
            own = []
            for k, part in enumerate((job.args, job.outs, job.scratch)):
                own.append(refs[at[k] : at[k] + len(part)])
                at[k] += len(part)
            bodies.append(job.body(*own[0], *own[1], *own[2]))
        moves, work = bodies[: len(jobs)], bodies[len(jobs) :]
        queue = [g for g, job in zip(work, fills) for _ in range(job.steps)]
        for g in work:
            next(g)
        e, w = lax.axis_index("ep"), lax.axis_index("ws")
        greet([(flip(e, p), flip(w, q)) for p, q in partners], crossing)
        done = 0
        for k, (_, i) in enumerate(turns):
            next(moves[i])
            target = (k + 1) * len(queue) // len(turns)
            while done < target:
                next(queue[done])
                done += 1
        for g in moves + work:
            for _ in g:
                pass

    return pl.pallas_call(
        kernel,
        out_shape=outs,
        in_specs=[ANY] * len(args),
        out_specs=[ANY] * len(outs),
        scratch_shapes=scratch,
        compiler_params=pltpu.CompilerParams(
            collective_id=collective_id, has_side_effects=True, vmem_limit_bytes=VMEM_LIMIT
        ),
        name=name,
    )(*args)


def fetch(pairs, sem):
    copies = [
        pltpu.make_async_copy(src, dst, sem.at[i]) for i, (src, dst) in enumerate(pairs)
    ]
    for copy in copies:
        copy.start()
    return copies


def blocks_of(size):
    return [(start, min(STEP, size - start)) for start in range(0, size, STEP)]


def column_tiles(width, tile):
    def body(c, carry):
        tile(pl.multiple_of(c * STEP, STEP), STEP)
        return carry

    lax.fori_loop(0, width // STEP, body, 0)
    if width % STEP:
        tile(width // STEP * STEP, width % STEP)


def grad_job(a, b):
    depth, rows = a.shape
    width = b.shape[1]

    def body(a_hbm, b_hbm, out, a_ref, b_ref, turned, held, load_sem, sem):
        loads = fetch(((a_hbm, a_ref), (b_hbm, b_ref)), load_sem)
        yield
        for load in loads:
            load.wait()
        copies = []
        for i, (start, size) in enumerate(blocks_of(rows)):
            if i >= 2:
                copies[i - 2].wait()
            turned[:size] = a_ref[:, start : start + size].T

            def tile(at, columns, slot=i % 2, size=size):
                held[slot, :size, pl.ds(at, columns)] = jnp.dot(
                    turned[:size], b_ref[:, pl.ds(at, columns)], preferred_element_type=f32
                )

            column_tiles(width, tile)
            copies.append(
                pltpu.make_async_copy(
                    held.at[i % 2, pl.ds(0, size)], out.at[pl.ds(start, size)], sem.at[i % 2]
                )
            )
            copies[i].start()
            yield
        for copy in copies[-2:]:
            copy.wait()

    return Job(
        [a, b],
        [jax.ShapeDtypeStruct((rows, width), f32)],
        [
            pltpu.VMEM(a.shape, bf16),
            pltpu.VMEM(b.shape, bf16),
            pltpu.VMEM((STEP, depth), bf16),
            pltpu.VMEM((2, STEP, width), f32),
            DMA((2,)),
            DMA((2,)),
        ],
        len(blocks_of(rows)),
        body,
    )


def pair_grad_job(a, first, second):
    depth, rows = a.shape
    tiles = first.shape[1] // 128

    def body(a_hbm, f_hbm, s_hbm, out, a_ref, f_ref, s_ref, turned, held, load_sem, sem):
        loads = fetch(((a_hbm, a_ref), (f_hbm, f_ref), (s_hbm, s_ref)), load_sem)
        flat = held.reshape(2 * tiles * STEP * 2, 128)
        yield
        for load in loads:
            load.wait()
        copies = []
        for i, (start, size) in enumerate(blocks_of(rows)):
            if i >= 2:
                for copy in copies[i - 2]:
                    copy.wait()
            turned[:size] = a_ref[:, start : start + size].T

            def tile(at, columns, slot=i % 2, size=size):
                for j, b_ref in enumerate((f_ref, s_ref)):
                    r = jnp.dot(
                        turned[:size], b_ref[:, pl.ds(at, columns)], preferred_element_type=f32
                    )
                    for half in range(columns // 128):
                        base = (slot * tiles + at // 128 + half) * (2 * STEP) + j
                        flat[pl.ds(base, size, stride=2), :] = r[:, half * 128 : half * 128 + 128]

            column_tiles(tiles * 128, tile)
            copies.append(
                [
                    pltpu.make_async_copy(
                        held.at[i % 2, c, pl.ds(0, size)],
                        out.at[pl.ds(start, size), :, pl.ds(c * 128, 128)],
                        sem.at[i % 2, c],
                    )
                    for c in range(tiles)
                ]
            )
            for copy in copies[i]:
                copy.start()
            yield
        for copy in copies[-2] + copies[-1]:
            copy.wait()

    return Job(
        [a, first, second],
        [jax.ShapeDtypeStruct((rows, 2, tiles * 128), f32)],
        [
            pltpu.VMEM(a.shape, bf16),
            pltpu.VMEM(first.shape, bf16),
            pltpu.VMEM(second.shape, bf16),
            pltpu.VMEM((STEP, depth), bf16),
            pltpu.VMEM((2, tiles, STEP, 2, 128), f32),
            DMA((3,)),
            DMA((2, tiles)),
        ],
        len(blocks_of(rows)),
        body,
    )


def split_job(weight):
    rows, _, width = weight.shape

    def body(w_hbm, first, second, block, wide, held, load_sem, sem):
        flat = wide.reshape(2 * STEP, 128)
        steps = rows // STEP

        def load(i):
            return pltpu.make_async_copy(
                w_hbm.at[pl.ds(i * STEP, STEP)], block.at[i % 2], load_sem.at[i % 2]
            )

        load(0).start()
        yield
        copies = []
        for i in range(steps):
            slot = i % 2
            if i + 1 < steps:
                load(i + 1).start()
            load(i).wait()
            if i >= 2:
                for copy in copies[i - 2]:
                    copy.wait()

            def tile(c, carry, slot=slot):
                at = pl.ds(pl.multiple_of(c * 128, 128), 128)
                wide[...] = block[slot, :, :, at].astype(f32)
                for j in range(2):
                    held[slot, j, :, at] = flat[pl.ds(j, STEP, stride=2), :].astype(bf16)
                return carry

            lax.fori_loop(0, width // 128, tile, 0)
            copies.append(
                [
                    pltpu.make_async_copy(
                        held.at[slot, j], out.at[pl.ds(i * STEP, STEP)], sem.at[slot, j]
                    )
                    for j, out in enumerate((first, second))
                ]
            )
            for copy in copies[i]:
                copy.start()
            yield
        for copy in copies[-2] + copies[-1]:
            copy.wait()

    return Job(
        [weight],
        [jax.ShapeDtypeStruct((rows, width), bf16)] * 2,
        [
            pltpu.VMEM((2, STEP, 2, width), bf16),
            pltpu.VMEM((STEP, 2, 128), f32),
            pltpu.VMEM((2, 2, STEP, width), bf16),
            DMA((2,)),
            DMA((2, 2)),
        ],
        rows // STEP,
        body,
    )


def ffn_job(x, gate_weight, up_weight, down_weight):
    rows, width = x.shape
    hidden = gate_weight.shape[1]

    def body(
        x_hbm, g_hbm, u_hbm, d_hbm, gate_out, up_out, act_out, out, x_ref, g_ref, u_ref, d_ref, pre, act, res,
        load_sem, sem
    ):
        loads = fetch(((x_hbm, x_ref), (g_hbm, g_ref), (u_hbm, u_ref), (d_hbm, d_ref)), load_sem)
        yield
        for load in loads:
            load.wait()
        copies = []
        for i, (start, size) in enumerate(blocks_of(rows)):
            slot = i % 2
            here = pl.ds(start, size)
            if i >= 2:
                for copy in copies[i - 2]:
                    copy.wait()

            def tile(at, columns, slot=slot, start=start, size=size):
                part = pl.ds(at, columns)
                left = x_ref[start : start + size]
                gate = dot(left, g_ref[:, part])
                up = dot(left, u_ref[:, part])
                pre[slot, 0, :, part] = gate
                pre[slot, 1, :, part] = up
                act[slot, :, part] = (gate * jax.nn.sigmoid(gate) * up).astype(bf16)

            column_tiles(hidden, tile)
            yield

            def last(at, columns, slot=slot):
                part = pl.ds(at, columns)
                res[slot, :, part] = dot(act[slot], d_ref[:, part]).astype(bf16)

            column_tiles(width, last)
            copies.append(
                [
                    pltpu.make_async_copy(src.at[slot], dst.at[here], sem.at[slot, k])
                    for k, (src, dst) in enumerate(((act, act_out), (res, out)))
                ]
                + [
                    pltpu.make_async_copy(pre.at[slot, k], dst.at[here], sem.at[slot, 2 + k])
                    for k, dst in enumerate((gate_out, up_out))
                ]
            )
            for copy in copies[i]:
                copy.start()
            yield
        for copy in copies[-2] + copies[-1]:
            copy.wait()

    return Job(
        [x, gate_weight, up_weight, down_weight],
        [jax.ShapeDtypeStruct((rows, hidden), f32)] * 2
        + [jax.ShapeDtypeStruct((rows, hidden), bf16), jax.ShapeDtypeStruct((rows, width), bf16)],
        [
            pltpu.VMEM(x.shape, bf16),
            pltpu.VMEM(gate_weight.shape, bf16),
            pltpu.VMEM(up_weight.shape, bf16),
            pltpu.VMEM(down_weight.shape, bf16),
            pltpu.VMEM((2, 2, STEP, hidden), f32),
            pltpu.VMEM((2, STEP, hidden), bf16),
            pltpu.VMEM((2, STEP, width), bf16),
            DMA((4,)),
            DMA((2, 4)),
        ],
        2 * (rows // STEP),
        body,
    )


def ffn_plain(x, gate_weight, up_weight, down_weight):
    gate_pre, up_pre = dot(x, gate_weight), dot(x, up_weight)
    activated = (gate_pre * jax.nn.sigmoid(gate_pre) * up_pre).astype(bf16)
    return gate_pre, up_pre, activated, dot(activated, down_weight).astype(bf16)


def before_activation(grad_act, gate_pre, up_pre):
    sigmoid_gate = jax.nn.sigmoid(gate_pre)
    grad_up = (grad_act * gate_pre * sigmoid_gate).astype(bf16)
    grad_gate = (
        grad_act * up_pre * sigmoid_gate * (1.0 + gate_pre * (1.0 - sigmoid_gate))
    ).astype(bf16)
    return grad_gate, grad_up


def ffn_back_job(grad, gate_pre, up_pre, gate_weight, up_weight, down_weight):
    rows, width = grad.shape
    hidden = gate_weight.shape[1]

    def body(
        x_hbm, gp_hbm, up_hbm, g_hbm, u_hbm, d_hbm, gate_out, up_out, out, x_ref, g_ref, u_ref, d_ref, pre, hid,
        res, load_sem, pre_sem, sem
    ):
        loads = fetch(((x_hbm, x_ref), (g_hbm, g_ref), (u_hbm, u_ref), (d_hbm, d_ref)), load_sem)

        def load_pre(i):
            here = pl.ds(i * STEP, STEP)
            return [
                pltpu.make_async_copy(src.at[here], pre.at[i % 2, k], pre_sem.at[i % 2, k])
                for k, src in enumerate((gp_hbm, up_hbm))
            ]

        for copy in load_pre(0):
            copy.start()
        yield
        for load in loads:
            load.wait()
        copies = []
        steps = rows // STEP
        for i in range(steps):
            slot, start = i % 2, i * STEP
            here = pl.ds(start, STEP)
            if i + 1 < steps:
                for copy in load_pre(i + 1):
                    copy.start()
            for copy in load_pre(i):
                copy.wait()
            if i >= 2:
                for copy in copies[i - 2]:
                    copy.wait()

            def tile(at, columns, slot=slot, start=start):
                part = pl.ds(at, columns)
                grad_act = dot_t(x_ref[start : start + STEP], d_ref[part, :])
                pair = before_activation(grad_act, pre[slot, 0, :, part], pre[slot, 1, :, part])
                hid[slot, 0, :, part], hid[slot, 1, :, part] = pair

            column_tiles(hidden, tile)
            yield

            def last(at, columns, slot=slot):
                part = pl.ds(at, columns)
                total = dot_t(hid[slot, 0], g_ref[part, :]) + dot_t(hid[slot, 1], u_ref[part, :])
                res[slot, :, part] = total.astype(bf16)

            column_tiles(width, last)
            copies.append(
                [pltpu.make_async_copy(res.at[slot], out.at[here], sem.at[slot, 2])]
                + [
                    pltpu.make_async_copy(hid.at[slot, k], dst.at[here], sem.at[slot, k])
                    for k, dst in enumerate((gate_out, up_out))
                ]
            )
            for copy in copies[i]:
                copy.start()
            yield
        for copy in copies[-2] + copies[-1]:
            copy.wait()

    return Job(
        [grad, gate_pre, up_pre, gate_weight, up_weight, down_weight],
        [jax.ShapeDtypeStruct((rows, hidden), bf16)] * 2 + [jax.ShapeDtypeStruct((rows, width), bf16)],
        [
            pltpu.VMEM(grad.shape, bf16),
            pltpu.VMEM(gate_weight.shape, bf16),
            pltpu.VMEM(up_weight.shape, bf16),
            pltpu.VMEM(down_weight.shape, bf16),
            pltpu.VMEM((2, 2, STEP, hidden), f32),
            pltpu.VMEM((2, 2, STEP, hidden), bf16),
            pltpu.VMEM((2, STEP, width), bf16),
            DMA((4,)),
            DMA((2, 2)),
            DMA((2, 3)),
        ],
        2 * (rows // STEP),
        body,
    )


def ffn_back_plain(grad, gate_pre, up_pre, gate_weight, up_weight, down_weight):
    grad_gate, grad_up = before_activation(dot_t(grad, down_weight), gate_pre, up_pre)
    back = dot_t(grad_gate, gate_weight) + dot_t(grad_up, up_weight)
    return grad_gate, grad_up, back.astype(bf16)


def dispatch_job(rows, n_ws):
    n, count, width = rows.shape

    def body(rows, out, own, load_sem, ep_s, ep_r, y_s, y_r, c_s, c_r, x_s, x_r):
        e, w = lax.axis_index("ep"), lax.axis_index("ws")
        twin, other = flip(w, 1), flip(w, 2)
        sources = [e] + [flip(e, k) for k in range(1, n)]
        first = []
        for i, s in enumerate(sources[1:]):
            first.append(remote(rows.at[s], out.at[e, w], ep_s.at[i], ep_r.at[i], (s, w)))
            first[-1].start()
        load = pltpu.make_async_copy(rows.at[e], own, load_sem.at[0])
        load.start()
        over_y, to_twin, relayed = [], [], []

        def relay(j):
            over_y[j].wait_recv()
            block = out.at[sources[j], other]
            relayed.append(remote(block, block, x_s.at[j], x_r.at[j], (e, twin)))
            relayed[-1].start()

        for j, s in enumerate(sources):
            place = out.at[s, w]
            block = rows.at[e] if j == 0 else place
            if j:
                first[j - 1].wait_recv()
            over_y.append(remote(block, place, y_s.at[j], y_r.at[j], (e, other)))
            over_y[-1].start()
            to_twin.append(remote(block, place, c_s.at[j], c_r.at[j], (e, twin)))
            to_twin[-1].start()
            if j == 0:
                load.wait()
                store = pltpu.make_async_copy(own, out.at[e, w], load_sem.at[1])
                store.start()
            else:
                relay(j - 1)
            yield
        relay(n - 1)
        store.wait()
        for copy in first + over_y:
            copy.wait_send()
        for copy in to_twin + relayed:
            copy.wait()

    return Job(
        [rows],
        [jax.ShapeDtypeStruct((n, n_ws, count, width), rows.dtype)],
        [pltpu.VMEM((count, width), rows.dtype), DMA((2,)), DMA((n - 1,)), DMA((n - 1,))]
        + [DMA((n,)) for _ in range(6)],
        n,
        body,
        [(k, 0) for k in range(1, n)] + [(0, 1), (0, 2)],
    )


def combine_job(part):
    n, _, count, width = part.shape
    block = (n, count, width)

    def body(
        part, out, mine, core, sum_y, from_y, total, load_sem, c_s, c_r, y_s, y_r, ep_s, ep_r, own_sem
    ):
        e, w = lax.axis_index("ep"), lax.axis_index("ws")
        twin, other, last = flip(w, 1), flip(w, 2), flip(w, 3)
        targets = [flip(e, k) for k in far_first(n)] + [e]
        loads, cores = {}, {}
        for half, near, far in ((1, other, last), (0, w, twin)):
            for j, s in enumerate(targets):
                cores[half, j] = remote(
                    part.at[s, far], core.at[half, j], c_s.at[half, j], c_r.at[half, j], (e, twin)
                )
                cores[half, j].start()
                loads[half, j] = pltpu.make_async_copy(
                    part.at[s, near], mine.at[half, j], load_sem.at[half, j]
                )
                loads[half, j].start()
        over_y, back = [], []

        def send_y(j):
            over_y.append(remote(sum_y.at[j], from_y.at[j], y_s.at[j], y_r.at[j], (e, other)))
            over_y[-1].start()

        def send_back(j):
            back.append(remote(total.at[j], out.at[e], ep_s.at[j], ep_r.at[j], (targets[j], w)))
            back[-1].start()

        for j in range(n):
            loads[1, j].wait()
            cores[1, j].wait_recv()
            sum_y[j] = (mine[1, j].astype(f32) + core[1, j].astype(f32)).astype(bf16)
            if j:
                send_y(j - 1)
        loads[0, 0].wait()
        cores[0, 0].wait_recv()
        send_y(n - 1)
        for j in range(n):
            if j:
                loads[0, j].wait()
                cores[0, j].wait_recv()
            over_y[j].wait_recv()
            total[j] = (
                mine[0, j].astype(f32) + core[0, j].astype(f32) + from_y[j].astype(f32)
            ).astype(bf16)
            if j:
                send_back(j - 1)
            yield
        for copy in over_y + list(cores.values()):
            copy.wait_send()
        keep = pltpu.make_async_copy(total.at[n - 1], out.at[e], own_sem)
        keep.start()
        for copy in back:
            copy.wait()
        keep.wait()

    return Job(
        [part],
        [jax.ShapeDtypeStruct(block, part.dtype)],
        [
            pltpu.VMEM((2,) + block, part.dtype),
            pltpu.VMEM((2,) + block, part.dtype),
            pltpu.VMEM(block, part.dtype),
            pltpu.VMEM(block, part.dtype),
            pltpu.VMEM(block, part.dtype),
            DMA((2, n)),
            DMA((2, n)),
            DMA((2, n)),
            DMA((n,)),
            DMA((n,)),
            DMA((n - 1,)),
            DMA((n - 1,)),
            DMA,
        ],
        n,
        body,
        [(k, 0) for k in range(1, n)] + [(0, 1), (0, 2)],
    )


def exchange_job(rows):
    n = rows.shape[0]

    def body(rows, out, own, load_sem, ep_s, ep_r):
        e, w = lax.axis_index("ep"), lax.axis_index("ws")
        targets = [flip(e, k) for k in far_first(n)]
        copies = []
        for i, s in enumerate(targets):
            copies.append(remote(rows.at[s], out.at[e], ep_s.at[i], ep_r.at[i], (s, w)))
            copies[-1].start()
        load = pltpu.make_async_copy(rows.at[e], own, load_sem.at[0])
        load.start()
        load.wait()
        store = pltpu.make_async_copy(own, out.at[e], load_sem.at[1])
        store.start()
        yield
        store.wait()
        for copy in copies:
            copy.wait()

    return Job(
        [rows],
        [jax.ShapeDtypeStruct(rows.shape, rows.dtype)],
        [pltpu.VMEM(rows.shape[1:], rows.dtype), DMA((2,)), DMA((n - 1,)), DMA((n - 1,))],
        1,
        body,
        [(k, 0) for k in range(1, n)],
    )


def exchange_combine_job(rows, weight, product, n_ws):
    n, held, depth = rows.shape
    count, width = held // n_ws, max(weight.shape)
    block = (n, count, width)
    turned = weight.shape[0] == width

    def body(
        rows, w_hbm, moved, out, w_ref, here, part, core, sum_y, from_y, total, load_sem, ep_s, ep_r, c_s, c_r,
        y_s, y_r, b_s, b_r
    ):
        e, w = lax.axis_index("ep"), lax.axis_index("ws")
        twin, other, last = flip(w, 1), flip(w, 2), flip(w, 3)
        places = [e] + [flip(e, k) for k in range(1, n)]
        weights = pltpu.make_async_copy(w_hbm, w_ref, load_sem.at[n])
        weights.start()
        arrivals = []
        for i, s in enumerate(places[1:]):
            arrivals.append(remote(rows.at[s], moved.at[e], ep_s.at[i], ep_r.at[i], (s, w)))
            arrivals[i].start()
        cores, over_y, back, stores = {}, [], [], []

        def multiply(j):
            if j:
                arrivals[j - 1].wait_recv()
            src = moved.at[places[j]] if j else rows.at[e]
            load = pltpu.make_async_copy(src, here.at[j], load_sem.at[j])
            load.start()
            load.wait()
            if j == 0:
                stores.append(pltpu.make_async_copy(here.at[0], moved.at[e], load_sem.at[0]))
                stores[0].start()
                weights.wait()

            def tile(at, columns):
                tall = pl.ds(at, columns)
                result = product(here[j], w_ref[tall, :] if turned else w_ref[:, tall])
                part[j, :, :, tall] = result.reshape(n_ws, count, columns).astype(bf16)

            column_tiles(width, tile)

        def send_core(j):
            for half, to in ((1, last), (0, twin)):
                cores[half, j] = remote(
                    part.at[j, to], core.at[half, j], c_s.at[half, j], c_r.at[half, j], (e, twin)
                )
                cores[half, j].start()

        def add_core(j):
            cores[1, j].wait_recv()
            sum_y[j] = (part[j, other].astype(f32) + core[1, j].astype(f32)).astype(bf16)

        def send_y(j):
            over_y.append(remote(sum_y.at[j], from_y.at[j], y_s.at[j], y_r.at[j], (e, other)))
            over_y[j].start()

        def add_all(j):
            cores[0, j].wait_recv()
            over_y[j].wait_recv()
            total[j] = (
                part[j, w].astype(f32) + core[0, j].astype(f32) + from_y[j].astype(f32)
            ).astype(bf16)

        def send_back(j):
            if j:
                back.append(
                    remote(total.at[j], out.at[e], b_s.at[j - 1], b_r.at[j - 1], (places[j], w))
                )
                back[j - 1].start()
            else:
                stores.append(pltpu.make_async_copy(total.at[0], out.at[e], load_sem.at[1]))
                stores[1].start()

        for t in range(n + 4):
            for lag, stage in ((0, multiply), (1, add_core), (3, add_all), (0, send_core), (1, send_y), (4, send_back)):
                if 0 <= t - lag < n:
                    stage(t - lag)
            yield
        for copy in arrivals + list(cores.values()) + over_y:
            copy.wait_send()
        for copy in back + stores:
            copy.wait()

    return Job(
        [rows, weight],
        [jax.ShapeDtypeStruct(rows.shape, bf16), jax.ShapeDtypeStruct(block, bf16)],
        [
            pltpu.VMEM(weight.shape, bf16),
            pltpu.VMEM(rows.shape, bf16),
            pltpu.VMEM((n, n_ws, count, width), bf16),
            pltpu.VMEM((2,) + block, bf16),
            pltpu.VMEM(block, bf16),
            pltpu.VMEM(block, bf16),
            pltpu.VMEM(block, bf16),
            DMA((n + 1,)),
            DMA((n - 1,)),
            DMA((n - 1,)),
            DMA((2, n)),
            DMA((2, n)),
            DMA((n,)),
            DMA((n,)),
            DMA((n - 1,)),
            DMA((n - 1,)),
        ],
        n + 4,
        body,
        [(k, 0) for k in range(1, n)] + [(0, 1), (0, 2)],
    )


def dispatch_exchange_job(rows, weight, product, n_ws):
    n, count, width = rows.shape
    turned = weight.shape[1] == width
    narrow = weight.shape[0] if turned else weight.shape[1]

    def body(
        rows, w_hbm, out, moved, w_ref, own, here, flat, res, load_sem, ep_s, ep_r, y_s, y_r, c_s, c_r, x_s, x_r,
        b_s, b_r
    ):
        e, w = lax.axis_index("ep"), lax.axis_index("ws")
        twin, other = flip(w, 1), flip(w, 2)
        places = [e] + [flip(e, k) for k in range(1, n)]
        weights = pltpu.make_async_copy(w_hbm, w_ref, load_sem.at[2])
        weights.start()
        first, over_y, to_twin, relayed, back, stores = [], [], [], [], [], []
        for i, s in enumerate(places[1:]):
            first.append(remote(rows.at[s], out.at[e, w], ep_s.at[i], ep_r.at[i], (s, w)))
            first[i].start()
        load = pltpu.make_async_copy(rows.at[e], own, load_sem.at[0])
        load.start()

        def arrive(j):
            place = out.at[places[j], w]
            block = place if j else rows.at[e]
            if j:
                first[j - 1].wait_recv()
            over_y.append(remote(block, place, y_s.at[j], y_r.at[j], (e, other)))
            over_y[j].start()
            to_twin.append(remote(block, place, c_s.at[j], c_r.at[j], (e, twin)))
            to_twin[j].start()
            if j == 0:
                load.wait()
                stores.append(pltpu.make_async_copy(own, place, load_sem.at[1]))
                stores[0].start()

        def relay(j):
            over_y[j].wait_recv()
            block = out.at[places[j], other]
            relayed.append(remote(block, block, x_s.at[j], x_r.at[j], (e, twin)))
            relayed[j].start()

        def multiply(j):
            to_twin[j].wait_recv()
            relayed[j].wait_recv()
            if j == 0:
                stores[0].wait()
                weights.wait()
            source = pltpu.make_async_copy(out.at[places[j]], here, load_sem.at[0])
            source.start()
            source.wait()
            flat[...] = here[...].astype(f32).reshape(n_ws * count, width).astype(bf16)

            def tile(at, columns):
                tall = pl.ds(at, columns)
                part = product(flat[...], w_ref[tall, :] if turned else w_ref[:, tall])
                res[j, :, tall] = part.astype(bf16)

            column_tiles(narrow, tile)

        def send(j):
            if j:
                back.append(
                    remote(res.at[j], moved.at[e], b_s.at[j - 1], b_r.at[j - 1], (places[j], w))
                )
                back[j - 1].start()
            else:
                stores.append(pltpu.make_async_copy(res.at[0], moved.at[e], load_sem.at[1]))
                stores[1].start()

        for t in range(n + 3):
            for lag, stage in enumerate((arrive, relay, multiply, send)):
                if 0 <= t - lag < n:
                    stage(t - lag)
            yield
        for copy in first + over_y + to_twin + relayed:
            copy.wait_send()
        for copy in back + stores[1:]:
            copy.wait()

    return Job(
        [rows, weight],
        [
            jax.ShapeDtypeStruct((n, n_ws, count, width), bf16),
            jax.ShapeDtypeStruct((n, n_ws * count, narrow), bf16),
        ],
        [
            pltpu.VMEM(weight.shape, bf16),
            pltpu.VMEM((count, width), bf16),
            pltpu.VMEM((n_ws, count, width), bf16),
            pltpu.VMEM((n_ws * count, width), bf16),
            pltpu.VMEM((n, n_ws * count, narrow), bf16),
            DMA((3,)),
            DMA((n - 1,)),
            DMA((n - 1,)),
        ]
        + [DMA((n,)) for _ in range(6)]
        + [DMA((n - 1,)), DMA((n - 1,))],
        n + 3,
        body,
        [(k, 0) for k in range(1, n)] + [(0, 1), (0, 2)],
    )


def gather_weights_job(mine, normed, n, n_ws):
    rows, block = mine.shape
    routes = [(4, 0), (2, 0), (2, 4)]

    def body(
        mine, normed, out, seq, held, held_rows, load_sem, s_sem, r_sem, x_s, x_r, y_s, y_r, c_s, c_r, t_s, t_r
    ):
        e, w = lax.axis_index("ep"), lax.axis_index("ws")
        twin, other, near = flip(w, 1), flip(w, 2), flip(e, 1)
        copies = {}

        def send(hop, offset, half):
            k = routes.index((hop, offset))
            part = pl.ds(half * (rows // 2), rows // 2)
            at = pl.multiple_of(flip(e, offset) // 2 * block, block)
            place = out.at[part, pl.ds(at, block)]
            copies[hop, offset, half] = remote(
                place if offset else mine.at[part],
                place,
                s_sem.at[k, half],
                r_sem.at[k, half],
                (flip(e, hop), w),
            )
            copies[hop, offset, half].start()

        for half in range(2):
            for route in routes[:2]:
                send(*route, half)
        to_near = remote(normed, seq.at[e % 2, w], x_s, x_r, (near, w))
        to_near.start()
        over_y, to_twin, relays = [], [], []

        def spread_rows(k, half, src):
            place = seq.at[half, w]
            over_y.append(remote(src, place, y_s.at[k], y_r.at[k], (e, other)))
            over_y[k].start()
            to_twin.append(remote(src, place, c_s.at[k], c_r.at[k], (e, twin)))
            to_twin[k].start()

        def relay(k, half):
            over_y[k].wait_recv()
            place = seq.at[half, other]
            relays.append(remote(place, place, t_s.at[k], t_r.at[k], (e, twin)))
            relays[k].start()

        spread_rows(0, e % 2, normed)
        loads = fetch(((mine, held), (normed, held_rows)), load_sem)
        for load in loads:
            load.wait()
        own = out.at[:, pl.ds(pl.multiple_of(e // 2 * block, block), block)]
        stores = fetch(((held, own), (held_rows, seq.at[e % 2, w])), load_sem)
        yield
        to_near.wait_recv()
        spread_rows(1, near % 2, seq.at[near % 2, w])
        yield
        copies[4, 0, 0].wait_recv()
        send(2, 4, 0)
        yield
        relay(0, e % 2)
        copies[4, 0, 1].wait_recv()
        send(2, 4, 1)
        yield
        relay(1, near % 2)
        yield
        for store in stores:
            store.wait()
        for (_, offset, half), copy in copies.items():
            copy.wait_send()
            if (_, offset) != (4, 0):
                copy.wait_recv()
        to_near.wait_send()
        for copy in over_y:
            copy.wait_send()
        for copy in to_twin + relays:
            copy.wait()

    return Job(
        [mine, normed],
        [
            jax.ShapeDtypeStruct((rows, n // 2 * block), bf16),
            jax.ShapeDtypeStruct((2, n_ws) + normed.shape, bf16),
        ],
        [
            pltpu.VMEM(mine.shape, bf16),
            pltpu.VMEM(normed.shape, bf16),
            DMA((2,)),
            DMA((3, 2)),
            DMA((3, 2)),
            DMA,
            DMA,
        ]
        + [DMA((2,)) for _ in range(6)],
        5,
        body,
        [(1, 0), (2, 0), (4, 0), (0, 1), (0, 2)],
    )


def swap_job(blocks):
    def body(blocks, out, held, load_sem, s_sem, r_sem):
        e, w = lax.axis_index("ep"), lax.axis_index("ws")
        near = flip(e, 1)
        copy = remote(blocks.at[near % 2], out.at[e % 2], s_sem, r_sem, (near, w))
        copy.start()
        load = fetch(((blocks.at[e % 2], held),), load_sem)[0]
        load.wait()
        store = fetch(((held, out.at[e % 2]),), load_sem)[0]
        yield
        store.wait()
        copy.wait()

    return Job(
        [blocks],
        [jax.ShapeDtypeStruct(blocks.shape, blocks.dtype)],
        [pltpu.VMEM(blocks.shape[1:], blocks.dtype), DMA((1,)), DMA, DMA],
        1,
        body,
        [(1, 0)],
    )


def add_blocks(out, *refs):
    step = 64 if out.shape[1] > 1024 else 256

    def body(i, carry):
        at = pl.ds(pl.multiple_of(i * step, step), step)
        total = refs[0][at].astype(f32)
        for ref in refs[1:]:
            total = total + ref[at].astype(f32)
        out[at] = total.astype(bf16)
        return carry

    lax.fori_loop(0, out.shape[0] // step, body, 0)


def reduce_weights_job(pieces, part, n):
    rows = pieces.shape[0]
    block = pieces.shape[1] // (n // 2)
    offsets = (4, 0)

    def body(
        pieces, part, out, out_rows, mine, from_z, fourth, last_z, total, own, core, sum_y, from_y, total_near,
        from_near, total_rows, load_sem, z_s, z_r, w_load, c_s, c_r, y_s, y_r, x_s, x_r, sem, h_s, h_r
    ):
        e, w = lax.axis_index("ep"), lax.axis_index("ws")
        twin, other, last, near = flip(w, 1), flip(w, 2), flip(w, 3), flip(e, 1)

        def columns(s):
            return pieces.at[:, pl.ds(pl.multiple_of(s // 2 * block, block), block)]

        over_z = []
        for i, offset in enumerate(offsets):
            over_z.append(
                remote(columns(flip(e, offset + 2)), from_z.at[i], z_s.at[i], z_r.at[i], (flip(e, 2), w))
            )
            over_z[i].start()
        halves = (near % 2, e % 2)
        cores = {}
        for k, to in enumerate((last, twin)):
            for h, half in enumerate(halves):
                cores[h, k] = remote(
                    part.at[half, to], core.at[h, k], c_s.at[h, k], c_r.at[h, k], (e, twin)
                )
                cores[h, k].start()
        loads = fetch([(columns(flip(e, o)), mine.at[i]) for i, o in enumerate(offsets)], load_sem)
        own_loads = {}
        for h, half in enumerate(halves):
            for k, to in enumerate((other, w)):
                own_loads[h, k] = pltpu.make_async_copy(
                    part.at[half, to], own.at[h, k], w_load.at[h, k]
                )
                own_loads[h, k].start()
        yield
        over_y = []

        def send_y(h):
            over_y.append(remote(sum_y.at[h], from_y.at[h], y_s.at[h], y_r.at[h], (e, other)))
            over_y[h].start()

        for h in range(2):
            own_loads[h, 0].wait()
            cores[h, 0].wait_recv()
            add_blocks(sum_y.at[h], own.at[h, 0], core.at[h, 0])
            if h:
                send_y(0)
        yield
        loads[0].wait()
        over_z[0].wait_recv()
        send_y(1)
        add_blocks(fourth, mine.at[0], from_z.at[0])
        yield
        own_loads[0, 1].wait()
        cores[0, 1].wait_recv()
        over_y[0].wait_recv()
        far = remote(fourth, last_z, z_s.at[2], z_r.at[2], (flip(e, 4), w))
        far.start()
        add_blocks(total_near, own.at[0, 1], core.at[0, 1], from_y.at[0])
        yield
        own_loads[1, 1].wait()
        cores[1, 1].wait_recv()
        over_y[1].wait_recv()
        to_near = remote(total_near, from_near, x_s, x_r, (near, w))
        to_near.start()
        yield
        loads[1].wait()
        over_z[1].wait_recv()
        far.wait_recv()
        add_blocks(total, mine.at[1], from_z.at[1], last_z)
        to_near.wait_recv()
        add_blocks(total_rows, own.at[1, 1], core.at[1, 1], from_y.at[1], from_near)
        partner, another = crossed()
        home = remote(total, out, h_s, h_r, partner)
        keep = pltpu.make_async_copy(total, out, sem.at[1])
        store = pltpu.make_async_copy(total_rows, out_rows, sem.at[0])

        @pl.when(another)
        def _():
            home.start()

        @pl.when(jnp.logical_not(another))
        def _():
            keep.start()

        store.start()
        for copy in over_z + list(cores.values()) + over_y + [far, to_near]:
            copy.wait_send()
        store.wait()

        @pl.when(another)
        def _():
            home.wait()

        @pl.when(jnp.logical_not(another))
        def _():
            keep.wait()

    one, rows_one = (rows, block), part.shape[2:]
    return Job(
        [pieces, part],
        [jax.ShapeDtypeStruct(one, bf16), jax.ShapeDtypeStruct(rows_one, bf16)],
        [pltpu.VMEM((2,) + one, bf16) for _ in range(2)]
        + [pltpu.VMEM(one, bf16) for _ in range(3)]
        + [pltpu.VMEM((2, 2) + rows_one, bf16) for _ in range(2)]
        + [pltpu.VMEM((2,) + rows_one, bf16) for _ in range(2)]
        + [pltpu.VMEM(rows_one, bf16) for _ in range(3)]
        + [DMA((2,)), DMA((3,)), DMA((3,)), DMA((2, 2)), DMA((2, 2)), DMA((2, 2))]
        + [DMA((2,)), DMA((2,)), DMA, DMA, DMA((2,)), DMA, DMA],
        5,
        body,
        [(1, 0), (2, 0), (4, 0), (0, 1), (0, 2)],
        True,
    )


def attend_kernel(spans, q_ref, kv_ref, out):
    count, _, slots, part = q_ref.shape
    for w, span in enumerate(spans):

        def head(h, carry, w=w, span=span):
            at = pl.multiple_of(h * HEAD_SIZE, HEAD_SIZE)
            columns = pl.ds(at, HEAD_SIZE)
            q, probs, _, values = head_probs(q_ref, kv_ref, w, span, at)
            mixed = dot(probs.astype(bf16), values)
            out[:, w, :, columns] = mixed.reshape(count, slots, HEAD_SIZE).astype(bf16)
            return carry

        lax.fori_loop(0, part // HEAD_SIZE, head, 0)


def slot_rows(ref, w, at):
    count, _, slots, _ = ref.shape
    rows = ref[:, w, :, pl.ds(at, HEAD_SIZE)].astype(f32)
    return rows.reshape(count * slots, HEAD_SIZE).astype(bf16)


def kv_place(kv, at):
    h = at // HEAD_SIZE
    column = pl.multiple_of(h // 2 * HEAD_SIZE, HEAD_SIZE)
    half = kv.shape[2] // 2
    value_column = pl.multiple_of(half + column, HEAD_SIZE)
    return h % 2, pl.ds(column, HEAD_SIZE), pl.ds(value_column, HEAD_SIZE)


def head_probs(q_ref, kv_ref, w, span, at):
    q = slot_rows(q_ref, w, at)
    side, key_columns, value_columns = kv_place(kv_ref, at)
    keys = kv_ref[side, :span, key_columns]
    values = kv_ref[side, :span, value_columns]
    scores = dot_t(q, keys) * HEAD_SIZE ** (-0.5)
    weight = jnp.exp(scores - jnp.max(scores, -1, keepdims=True))
    probs = weight / jnp.sum(weight, -1, keepdims=True)
    return q, probs, keys, values


def attend_call(queries, kv, spans):
    return pl.pallas_call(
        functools.partial(attend_kernel, spans),
        out_shape=jax.ShapeDtypeStruct(queries.shape, bf16),
        in_specs=[VM, VM],
        out_specs=VM,
        compiler_params=pltpu.CompilerParams(vmem_limit_bytes=VMEM_LIMIT),
        name="attend",
    )(queries, kv)


def attend_back_kernel(spans, q_ref, g_ref, kv_ref, grad_q, grad_kv, total):
    count, _, slots, part = q_ref.shape
    total[...] = jnp.zeros_like(total)
    for w, span in enumerate(spans):

        def head(h, carry, w=w, span=span):
            at = pl.multiple_of(h * HEAD_SIZE, HEAD_SIZE)
            columns = pl.ds(at, HEAD_SIZE)
            q, probs, keys, values = head_probs(q_ref, kv_ref, w, span, at)
            grad = slot_rows(g_ref, w, at)
            grad_probs = dot_t(grad, values)
            centred = jnp.sum(probs * grad_probs, -1, keepdims=True)
            grad_scores = (probs * (grad_probs - centred)).astype(bf16)
            grad_rows = dot(grad_scores, keys) * HEAD_SIZE ** (-0.5)
            grad_q[:, w, :, columns] = grad_rows.reshape(count, slots, HEAD_SIZE).astype(bf16)
            side, key_columns, value_columns = kv_place(kv_ref, at)
            total[side, :span, key_columns] += t_dot(grad_scores, q) * HEAD_SIZE ** (-0.5)
            total[side, :span, value_columns] += t_dot(probs.astype(bf16), grad)
            return carry

        lax.fori_loop(0, part // HEAD_SIZE, head, 0)
    grad_kv[...] = total[...].astype(bf16)


def attend_back_call(queries, grads, kv, spans):
    return pl.pallas_call(
        functools.partial(attend_back_kernel, spans),
        out_shape=[
            jax.ShapeDtypeStruct(queries.shape, bf16),
            jax.ShapeDtypeStruct(kv.shape, bf16),
        ],
        in_specs=[VM, VM, VM],
        out_specs=[VM, VM],
        scratch_shapes=[pltpu.VMEM(kv.shape, f32)],
        compiler_params=pltpu.CompilerParams(vmem_limit_bytes=VMEM_LIMIT),
        name="attend_back",
    )(queries, grads, kv)


def gather_gains_job(own, n, n_ws):
    def body(own, out, held, load_sem, w_s, w_r, ep_s, ep_r):
        e, w = lax.axis_index("ep"), lax.axis_index("ws")
        first = []
        for i in range(n_ws - 1):
            place = (e, flip(w, i + 1))
            first.append(remote(own, out.at[e, w], w_s.at[i], w_r.at[i], place))
            first[i].start()
        load = fetch(((own, held),), load_sem)[0]
        load.wait()
        store = fetch(((held, out.at[e, w]),), load_sem)[0]
        yield
        store.wait()
        for copy in first:
            copy.wait()
        second = []
        for i in range(n - 1):
            place = (flip(e, i + 1), w)
            second.append(remote(out.at[e], out.at[e], ep_s.at[i], ep_r.at[i], place))
            second[i].start()
        yield
        for copy in second:
            copy.wait()

    return Job(
        [own],
        [jax.ShapeDtypeStruct((n, n_ws) + own.shape, own.dtype)],
        [
            pltpu.VMEM(own.shape, own.dtype),
            DMA((1,)),
            DMA((n_ws - 1,)),
            DMA((n_ws - 1,)),
            DMA((n - 1,)),
            DMA((n - 1,)),
        ],
        2,
        body,
        [(k, 0) for k in range(1, n)] + [(0, k) for k in range(1, n_ws)],
    )


def reduce_kernel(n, n_ws, parts, out, held, all_parts, load_sem, w_s, w_r, ep_s, ep_r):
    e, w = lax.axis_index("ep"), lax.axis_index("ws")
    beside = [flip(w, k) for k in range(1, n_ws)]
    across = [flip(e, k) for k in far_first(n)]
    greet([(e, p) for p in beside] + [(s, w) for s in across])
    keep = pltpu.make_async_copy(parts.at[:, w], held.at[:, w], load_sem.at[0])
    keep.start()
    first = []
    for i, p in enumerate(beside):
        first.append(remote(parts.at[:, p], held.at[:, w], w_s.at[i], w_r.at[i], (e, p)))
        first[-1].start()
    keep.wait()
    for copy in first:
        copy.wait()
    keep = pltpu.make_async_copy(held.at[e], all_parts.at[e], load_sem.at[1])
    keep.start()
    second = []
    for i, s in enumerate(across):
        second.append(remote(held.at[s], all_parts.at[e], ep_s.at[i], ep_r.at[i], (s, w)))
        second[-1].start()
    keep.wait()
    for copy in second:
        copy.wait()
    out[...] = jnp.sum(jnp.sum(all_parts[...], 0), 0)


def reduce_call(parts):
    n, n_ws = parts.shape[:2]
    return pl.pallas_call(
        functools.partial(reduce_kernel, n, n_ws),
        out_shape=jax.ShapeDtypeStruct(parts.shape[2:], parts.dtype),
        in_specs=[VM],
        out_specs=VM,
        scratch_shapes=[
            pltpu.VMEM(parts.shape, parts.dtype),
            pltpu.VMEM(parts.shape, parts.dtype),
            DMA((2,)),
            DMA((n_ws - 1,)),
            DMA((n_ws - 1,)),
            DMA((n - 1,)),
            DMA((n - 1,)),
        ],
        compiler_params=pltpu.CompilerParams(collective_id=4, has_side_effects=True),
        name="reduce_gains",
    )(parts)


def small(n_ep):
    return n_ep == MIXTURE_EXPERTS and lax.axis_size("ws") == 4


PLAIN = {
    grad_job: lambda a, b: [t_dot(a, b)],
    pair_grad_job: lambda a, b, c: [jnp.stack([t_dot(a, b), t_dot(a, c)], 1)],
    split_job: lambda weight: [weight[:, 0], weight[:, 1]],
    ffn_job: ffn_plain,
    ffn_back_job: ffn_back_plain,
}


def beside(job, plain, arg, fills, collective_id, name):
    if job is None:
        return [plain(arg)] + [out for make, *rest in fills for out in PLAIN[make](*rest)]
    return run_jobs([job(arg)], [make(*rest) for make, *rest in fills], collective_id, name)


def exchange_plain(send):
    return lax.all_to_all(send, "ep", split_axis=0, concat_axis=0, tiled=True)


def exchange(send, *fills, collective_id=2, name="exchange"):
    job = exchange_job if small(send.shape[0]) else None
    return beside(job, exchange_plain, send, fills, collective_id, name)


def spread(rows, group):
    width = rows.shape[-1]
    blocks = rows.reshape(MIXTURE_EXPERTS, 1, ROWS, width)
    return jnp.broadcast_to(blocks, (MIXTURE_EXPERTS, group, ROWS, width)).reshape(
        MIXTURE_EXPERTS * group, ROWS, width
    )


def dispatch(rows, group, *fills, collective_id=0, name="dispatch"):
    width = rows.shape[-1]

    def plain(blocks):
        return lax.all_gather(exchange_plain(blocks), "ws", axis=1, tiled=False)

    job = functools.partial(dispatch_job, n_ws=4) if small(MIXTURE_EXPERTS * group) else None
    out = beside(job, plain, spread(rows, group), fills, collective_id, name)
    return [out[0].reshape(-1, width)] + list(out[1:])


def combine(partial, group, n_ep, n_ws, *fills, collective_id=1, name="combine"):
    width = partial.shape[-1]

    def plain(part):
        part = part.transpose(1, 0, 2, 3).reshape(n_ws * n_ep * ROWS, width)
        own = lax.psum_scatter(part, "ws", scatter_dimension=0, tiled=True)
        return exchange_plain(own.reshape(n_ep, ROWS, width))

    part = partial.reshape(n_ep, n_ws, ROWS, width)
    job = combine_job if small(n_ep) else None
    back, *rest = beside(job, plain, part, fills, collective_id, name)
    if group > 1:
        back = jnp.sum(back.reshape(MIXTURE_EXPERTS, group, ROWS, width).astype(f32), 1).astype(bf16)
    return [back.reshape(MIXTURE_EXPERTS * ROWS, width)] + rest


def slot_tables(routes, slots):
    target = jnp.where(slots < CAP, routes * ROWS + slots, -1)
    places = lax.broadcasted_iota(jnp.int32, (MIXTURE_EXPERTS * ROWS, target.shape[0]), 0)
    return [(places == target[None, :, k]).astype(bf16) for k in range(CHOSEN_EXPERTS)]


def norm_back(grad, unit, inverse, gain):
    gain_grad = jnp.sum(grad * unit, 0)
    scaled = grad * gain
    return (inverse * (scaled - unit * jnp.mean(scaled * unit, -1, keepdims=True)), gain_grad)


def heads_of(rows):
    return rows.reshape(rows.shape[0], -1, HEAD_SIZE)


def local(
    x_in,
    gain_attn,
    gain_ffn,
    key_value_weight,
    w_query,
    w_output,
    w_in,
    w_out,
    gate_attn,
    gate_ffn,
    route_attn,
    slot_attn,
    route_ffn,
    slot_ffn,
    cotangent,
):
    n_ep = lax.axis_size("ep")
    n_ws = lax.axis_size("ws")
    group = n_ep // MIXTURE_EXPERTS
    local_tokens, width = x_in.shape
    key_value_width = KEY_VALUE_HEADS * HEAD_SIZE
    part = w_query.shape[2]
    own_width = group * part
    sequence = n_ws * local_tokens
    place = lax.axis_index("ws")
    scale = HEAD_SIZE ** (-0.5)

    fused = small(n_ep) and key_value_weight.shape[1] == HEAD_SIZE and gain_attn.shape[0] == 64
    if fused:
        gains = jnp.concatenate([gain_attn, gain_ffn], 0).astype(f32)[None]
        gains = run_jobs([gather_gains_job(gains, n_ep, n_ws)], [], 3, "gather_gains")[0]
        gains = gains.reshape(n_ep * n_ws, 2, -1)
        gain_one, gain_two = gains[:, 0].reshape(-1), gains[:, 1].reshape(-1)
    else:
        gain_one = lax.all_gather(gain_attn, ("ep", "ws"), axis=0, tiled=True).astype(f32)
        gain_two = lax.all_gather(gain_ffn, ("ep", "ws"), axis=0, tiled=True).astype(f32)
    plain = group == 1 and key_value_weight.shape[1] == HEAD_SIZE
    if plain:
        half = n_ep // 2
        there = [
            (e * n_ws + w, (w + n_ws * (e // half)) * n_ws + e % half)
            for e in range(n_ep)
            for w in range(n_ws)
        ]
        mine = lax.ppermute(key_value_weight, ("ep", "ws"), there)
    else:
        whole = lax.all_gather(key_value_weight, ("ep", "ws"), axis=1, tiled=True)
        whole = whole.reshape(width, 2 * group, n_ws, part)
        kv_own = lax.dynamic_index_in_dim(whole, place, 2, keepdims=False).reshape(width, -1)

    inputs = x_in.astype(f32)
    inverse_one = lax.rsqrt(jnp.mean(inputs * inputs, -1, keepdims=True) + EPS)
    unit_one = inputs * inverse_one
    normed = (unit_one * gain_one).astype(bf16)
    attn_pairs = slot_tables(route_attn, slot_attn)
    ffn_pairs = slot_tables(route_ffn, slot_ffn)
    attn_tokens = attn_pairs[0] + attn_pairs[1]
    ffn_tokens = ffn_pairs[0] + ffn_pairs[1]

    slots_one = dot(attn_tokens, normed).astype(bf16)
    if fused:
        rows_one, kv_own, normed_sequence, gate_weight, up_weight = run_jobs(
            [
                dispatch_job(slots_one.reshape(n_ep, ROWS, width), n_ws),
                gather_weights_job(mine, normed, n_ep, n_ws),
            ],
            [split_job(w_in[0])],
            10,
            "dispatch_weights",
        )
        rows_one = rows_one.reshape(-1, width)
        normed_sequence = normed_sequence.reshape(2 * sequence, width)
    else:
        if plain:
            kv_own = lax.all_gather(mine, "ep", axis=1, tiled=True)
        normed_sequence = lax.all_gather(normed, "ws", axis=0, tiled=True)
        rows_one, gate_weight, up_weight = dispatch(slots_one, group, (split_job, w_in[0]))
    kv = dot(normed_sequence, kv_own).astype(bf16)
    if not fused:
        keys = kv[:, :own_width].reshape(sequence, -1, HEAD_SIZE)
        values = kv[:, own_width:].reshape(sequence, -1, HEAD_SIZE)

    owner_query = dot(rows_one, w_query[0]).astype(bf16)
    owner_query = owner_query.reshape(n_ep, n_ws * ROWS, part)
    if fused:
        queries, kv = run_jobs(
            [exchange_job(owner_query), swap_job(kv.reshape(2, sequence, -1))], [], 13, "exchange_kv"
        )
    else:
        queries = exchange(owner_query)[0]
    queries = queries.reshape(MIXTURE_EXPERTS, group, n_ws, ROWS, part)
    spans = [(w * local_tokens // BLOCK + 1) * BLOCK for w in range(n_ws)]

    def by_block(rows):
        rows = rows.reshape(MIXTURE_EXPERTS, group, n_ws, ROWS, part)
        return [
            rows[:, :, w].transpose(0, 2, 1, 3).reshape(-1, own_width // HEAD_SIZE, HEAD_SIZE)
            for w in range(n_ws)
        ]

    def to_experts(pieces):
        rows = jnp.stack(
            [
                piece.reshape(MIXTURE_EXPERTS, ROWS, group, part).transpose(0, 2, 1, 3)
                for piece in pieces
            ],
            2,
        )
        return rows.reshape(n_ep, n_ws * ROWS, part)

    if fused:
        queries = queries.reshape(n_ep, n_ws, ROWS, part)
        mixed = attend_call(queries, kv, spans).reshape(n_ep, n_ws * ROWS, part)
    else:
        kept = []
        mixed_pieces = []
        for q, span in zip(by_block(queries), spans):
            scores = (
                jnp.einsum("rhd,shd->hrs", q, keys[:span], preferred_element_type=f32) * scale
            )
            probs = jax.nn.softmax(scores, axis=-1)
            mixed = jnp.einsum(
                "hrs,shd->rhd", probs.astype(bf16), values[:span], preferred_element_type=f32
            )
            kept.append((q, probs))
            mixed_pieces.append(mixed.astype(bf16))
        mixed = to_experts(mixed_pieces)
    if fused:
        owner_mixed, attn_slots = run_jobs(
            [exchange_combine_job(mixed, w_output[0], dot, n_ws)], [], 11, "exchange_output"
        )
        owner_mixed, attn_slots = owner_mixed.reshape(-1, part), attn_slots.reshape(-1, width)
    else:
        owner_mixed = exchange(mixed)[0].reshape(-1, part)
        output_part = dot(owner_mixed, w_output[0]).astype(bf16)
        attn_slots = combine(output_part, group, n_ep, n_ws)[0]

    def weighted(pairs, gates, slot_values):
        return sum(gates[:, k : k + 1] * t_dot(pairs[k], slot_values) for k in range(2))

    def to_slots(pairs, gates, values):
        return sum(
            dot(pairs[k], (gates[:, k : k + 1] * values).astype(bf16)) for k in range(2)
        ).astype(bf16)

    hidden_state = inputs + weighted(attn_pairs, gate_attn, attn_slots)
    inverse_two = lax.rsqrt(jnp.mean(hidden_state * hidden_state, -1, keepdims=True) + EPS)
    unit_two = hidden_state * inverse_two
    normed_two = (unit_two * gain_two).astype(bf16)

    grad_out = cotangent.astype(f32)
    grad_slots = to_slots(ffn_pairs, gate_ffn, grad_out)
    expert_rows = dispatch(dot(ffn_tokens, normed_two).astype(bf16), group)[0]
    expert_grad, gate_pre, up_pre, activated, forward_part = dispatch(
        grad_slots,
        group,
        (ffn_job, expert_rows, gate_weight, up_weight, w_out[0]),
        collective_id=5,
        name="dispatch_ffn",
    )
    ffn_slots, grad_gate, grad_up, back_two = combine(
        forward_part,
        group,
        n_ep,
        n_ws,
        (ffn_back_job, expert_grad, gate_pre, up_pre, gate_weight, up_weight, w_out[0]),
        collective_id=1,
        name="combine_ffn_back",
    )
    result = hidden_state + weighted(ffn_pairs, gate_ffn, ffn_slots)
    back_slots, grad_second = combine(
        back_two,
        group,
        n_ep,
        n_ws,
        (grad_job, activated, expert_grad),
        collective_id=6,
        name="combine_grad_out",
    )

    grad_normed_two = t_dot(ffn_tokens, back_slots)
    grad_hidden_norm, grad_gain_two = norm_back(grad_normed_two, unit_two, inverse_two, gain_two)
    grad_hidden = grad_out + grad_hidden_norm
    attn_grads = to_slots(attn_pairs, gate_attn, grad_hidden)
    if fused:
        owner_grad, mixed_grads, grad_first = run_jobs(
            [dispatch_exchange_job(attn_grads.reshape(n_ep, ROWS, width), w_output[0], dot_t, n_ws)],
            [pair_grad_job(expert_rows, grad_gate, grad_up)],
            7,
            "dispatch_exchange",
        )
        owner_grad = owner_grad.reshape(-1, width)
    else:
        owner_grad = dispatch(attn_grads, group)[0]
        grad_first = jnp.stack([t_dot(expert_rows, grad_gate), t_dot(expert_rows, grad_up)], 1)
        back_mixed = dot_t(owner_grad, w_output[0]).astype(bf16)
        mixed_grads = exchange(back_mixed.reshape(n_ep, n_ws * ROWS, part))[0]
        grad_output = t_dot(owner_mixed, owner_grad)

    if fused:
        mixed_grads = mixed_grads.reshape(n_ep, n_ws, ROWS, part)
        query_grads, grad_kv_rows = attend_back_call(queries, mixed_grads, kv, spans)
        query_grads = query_grads.reshape(n_ep, n_ws * ROWS, part)
    else:
        grad_keys, grad_values, query_pieces = 0.0, 0.0, []
        for (q, probs), grad, span in zip(kept, by_block(mixed_grads), spans):
            grad_probs = jnp.einsum("rhd,shd->hrs", grad, values[:span], preferred_element_type=f32)
            centred = jnp.sum(probs * grad_probs, -1, keepdims=True)
            grad_scores = (probs * (grad_probs - centred)).astype(bf16)
            grad_q = (
                jnp.einsum("hrs,shd->rhd", grad_scores, keys[:span], preferred_element_type=f32)
                * scale
            )
            query_pieces.append(grad_q.astype(bf16))
            pad = ((0, sequence - span), (0, 0), (0, 0))
            piece = jnp.einsum("hrs,rhd->shd", grad_scores, q, preferred_element_type=f32) * scale
            grad_keys = grad_keys + jnp.pad(piece, pad)
            piece = jnp.einsum(
                "hrs,rhd->shd", probs.astype(bf16), grad, preferred_element_type=f32
            )
            grad_values = grad_values + jnp.pad(piece, pad)
        grad_kv_rows = jnp.concatenate(
            [grad_keys.reshape(sequence, -1), grad_values.reshape(sequence, -1)], 1
        ).astype(bf16)
        query_grads = to_experts(query_pieces)
    if fused:
        owner_grad_query, normed_back, grad_kv_rows, grad_output = run_jobs(
            [exchange_combine_job(query_grads, w_query[0], dot_t, n_ws), swap_job(grad_kv_rows)],
            [grad_job(owner_mixed, owner_grad)],
            14,
            "exchange_back",
        )
        owner_grad_query = owner_grad_query.reshape(-1, part)
        normed_back = normed_back.reshape(-1, width)
        grad_kv_rows = grad_kv_rows.reshape(2 * sequence, -1)
    else:
        owner_grad_query = exchange(query_grads)[0].reshape(-1, part)
    grad_kv = t_dot(normed_sequence, grad_kv_rows)
    from_kv = dot_t(grad_kv_rows, kv_own).astype(bf16)
    if fused:
        piece, from_kv, grad_query = run_jobs(
            [
                reduce_weights_job(
                    grad_kv.astype(bf16), from_kv.reshape(2, n_ws, local_tokens, width), n_ep
                )
            ],
            [grad_job(rows_one, owner_grad_query)],
            9,
            "reduce_weights",
        )
    else:
        back_normed = dot_t(owner_grad_query, w_query[0]).astype(bf16)
        normed_back = combine(back_normed, group, n_ep, n_ws)[0]
        grad_query = t_dot(rows_one, owner_grad_query)
    if fused:
        grad_kv_shard = piece.astype(f32)
    elif plain:
        pieces = grad_kv.reshape(width, n_ep, HEAD_SIZE).transpose(1, 0, 2).astype(bf16)
        piece = lax.psum_scatter(pieces, "ep", scatter_dimension=0, tiled=False)
        grad_kv_shard = lax.ppermute(piece, ("ep", "ws"), [(b, a) for a, b in there]).astype(f32)
    else:
        mask = (jnp.arange(n_ws) == place)[None, None, :, None]
        pieces = jnp.where(mask, grad_kv.reshape(width, 2 * group, 1, part), 0.0)
        pieces = pieces.reshape(width, 2 * key_value_width).astype(bf16)
        grad_kv_shard = lax.psum_scatter(
            pieces, ("ep", "ws"), scatter_dimension=1, tiled=True
        ).astype(f32)
    if not fused:
        from_kv = lax.psum_scatter(from_kv, "ws", scatter_dimension=0, tiled=True)
    grad_normed = t_dot(attn_tokens, normed_back) + from_kv.astype(f32)
    grad_input_norm, grad_gain_one = norm_back(grad_normed, unit_one, inverse_one, gain_one)
    grad_input = grad_hidden + grad_input_norm
    gain_grads = jnp.stack([grad_gain_one, grad_gain_two], 0)
    if fused:
        parts = gain_grads.reshape(2, n_ep, n_ws, -1).transpose(1, 2, 0, 3)
        gain_shards = reduce_call(parts.reshape(n_ep, n_ws, 1, -1)).reshape(2, -1)
    else:
        gain_shards = lax.psum_scatter(
            gain_grads, ("ep", "ws"), scatter_dimension=1, tiled=True
        )
    return (
        result.astype(bf16),
        grad_input,
        gain_shards[0],
        gain_shards[1],
        grad_kv_shard,
        grad_query[None],
        grad_output[None],
        grad_first[None],
        grad_second[None],
    )


def solution(mesh):
    both = ("ep", "ws")
    rows, vector, columns = P(both, None), P(both), P(None, both)
    return jax.shard_map(
        local,
        mesh=mesh,
        in_specs=(
            rows,
            vector,
            vector,
            columns,
            P("ep", None, "ws"),
            P("ep", "ws", None),
            P("ep", None, None, "ws"),
            P("ep", "ws", None),
            rows,
            rows,
            rows,
            rows,
            rows,
            rows,
            rows,
        ),
        out_specs=(
            rows,
            rows,
            vector,
            vector,
            columns,
            P("ep", None, "ws"),
            P("ep", "ws", None),
            P("ep", None, None, "ws"),
            P("ep", "ws", None),
        ),
        check_vma=False,
    )
```

```python
import functools

import jax
import jax.numpy as jnp
from jax import lax
from jax.experimental import pallas as pl
from jax.experimental.pallas import tpu as pltpu
from jax.sharding import PartitionSpec as P

KEY_VALUE_HEADS = 16
HEAD_SIZE = 128
MIXTURE_EXPERTS = 8
CHOSEN_EXPERTS = 2
BLOCK = 256
CAP = 36
ROWS = 40

EPS = 1e-06
very_negative = -1e30
f32 = jnp.float32
bf16 = jnp.bfloat16
MESH = pl.DeviceIdType.MESH
ANY = pl.BlockSpec(memory_space=pl.ANY)
VM = pl.BlockSpec(memory_space=pltpu.VMEM)
DMA = pltpu.SemaphoreType.DMA
STEP = 256
VMEM_LIMIT = 60 << 20


def dot(a, b):
    return jnp.dot(a, b, preferred_element_type=f32)


def dot_t(a, b):
    return lax.dot_general(a, b, (((1,), (1,)), ((), ())), preferred_element_type=f32)


def t_dot(a, b):
    return lax.dot_general(a, b, (((0,), (0,)), ((), ())), preferred_element_type=f32)


def flip(index, bits):
    out, bit = index, 1
    while bit <= bits:
        if bits & bit:
            out = out + bit - 2 * bit * ((index // bit) % 2)
        bit *= 2
    return out


def far_first(n):
    return sorted(range(1, n), key=lambda k: (-((k // 2).bit_length()), k))


def crossed():
    e, w, n_ws = lax.axis_index("ep"), lax.axis_index("ws"), lax.axis_size("ws")
    return (w + n_ws * (e // n_ws), e % n_ws), e % n_ws != w


def greet(partners, crossing=False):
    barrier = pltpu.get_barrier_semaphore()
    for partner in partners:
        pl.semaphore_signal(barrier, inc=1, device_id=partner, device_id_type=MESH)
    if crossing:
        partner, another = crossed()

        @pl.when(another)
        def _():
            pl.semaphore_signal(barrier, inc=1, device_id=partner, device_id_type=MESH)
            pl.semaphore_wait(barrier, len(partners) + 1)

        @pl.when(jnp.logical_not(another))
        def _():
            pl.semaphore_wait(barrier, len(partners))

    else:
        pl.semaphore_wait(barrier, len(partners))


def remote(src, dst, send, recv, device):
    return pltpu.make_async_remote_copy(
        src_ref=src, dst_ref=dst, send_sem=send, recv_sem=recv, device_id=device, device_id_type=MESH
    )


class Job:
    def __init__(self, args, outs, scratch, steps, body, partners=(), crossing=False):
        self.args, self.outs, self.scratch, self.steps, self.body = args, outs, scratch, steps, body
        self.partners, self.crossing = partners, crossing


def run_jobs(jobs, fills, collective_id, name):
    whole = jobs + fills
    args = [a for job in whole for a in job.args]
    outs = [o for job in whole for o in job.outs]
    scratch = [x for job in whole for x in job.scratch]
    turns = sorted((k / job.steps, i) for i, job in enumerate(jobs) for k in range(job.steps))
    partners = sorted({p for job in jobs for p in job.partners})
    crossing = any(job.crossing for job in jobs)

    def kernel(*refs):
        bodies, at = [], [0, len(args), len(args) + len(outs)]
        for job in whole:
            own = []
            for k, part in enumerate((job.args, job.outs, job.scratch)):
                own.append(refs[at[k] : at[k] + len(part)])
                at[k] += len(part)
            bodies.append(job.body(*own[0], *own[1], *own[2]))
        moves, work = bodies[: len(jobs)], bodies[len(jobs) :]
        queue = [g for g, job in zip(work, fills) for _ in range(job.steps)]
        for g in work:
            next(g)
        e, w = lax.axis_index("ep"), lax.axis_index("ws")
        greet([(flip(e, p), flip(w, q)) for p, q in partners], crossing)
        done = 0
        for k, (_, i) in enumerate(turns):
            next(moves[i])
            target = (k + 1) * len(queue) // len(turns)
            while done < target:
                next(queue[done])
                done += 1
        for g in moves + work:
            for _ in g:
                pass

    return pl.pallas_call(
        kernel,
        out_shape=outs,
        in_specs=[ANY] * len(args),
        out_specs=[ANY] * len(outs),
        scratch_shapes=scratch,
        compiler_params=pltpu.CompilerParams(
            collective_id=collective_id, has_side_effects=True, vmem_limit_bytes=VMEM_LIMIT
        ),
        name=name,
    )(*args)


def fetch(pairs, sem):
    copies = [
        pltpu.make_async_copy(src, dst, sem.at[i]) for i, (src, dst) in enumerate(pairs)
    ]
    for copy in copies:
        copy.start()
    return copies


def blocks_of(size):
    return [(start, min(STEP, size - start)) for start in range(0, size, STEP)]


def column_tiles(width, tile):
    def body(c, carry):
        tile(pl.multiple_of(c * STEP, STEP), STEP)
        return carry

    lax.fori_loop(0, width // STEP, body, 0)
    if width % STEP:
        tile(width // STEP * STEP, width % STEP)


def grad_job(a, b):
    depth, rows = a.shape
    width = b.shape[1]

    def body(a_hbm, b_hbm, out, a_ref, b_ref, turned, held, load_sem, sem):
        loads = fetch(((a_hbm, a_ref), (b_hbm, b_ref)), load_sem)
        yield
        for load in loads:
            load.wait()
        copies = []
        for i, (start, size) in enumerate(blocks_of(rows)):
            if i >= 2:
                copies[i - 2].wait()
            turned[:size] = a_ref[:, start : start + size].T

            def tile(at, columns, slot=i % 2, size=size):
                held[slot, :size, pl.ds(at, columns)] = jnp.dot(
                    turned[:size], b_ref[:, pl.ds(at, columns)], preferred_element_type=f32
                )

            column_tiles(width, tile)
            copies.append(
                pltpu.make_async_copy(
                    held.at[i % 2, pl.ds(0, size)], out.at[pl.ds(start, size)], sem.at[i % 2]
                )
            )
            copies[i].start()
            yield
        for copy in copies[-2:]:
            copy.wait()

    return Job(
        [a, b],
        [jax.ShapeDtypeStruct((rows, width), f32)],
        [
            pltpu.VMEM(a.shape, bf16),
            pltpu.VMEM(b.shape, bf16),
            pltpu.VMEM((STEP, depth), bf16),
            pltpu.VMEM((2, STEP, width), f32),
            DMA((2,)),
            DMA((2,)),
        ],
        len(blocks_of(rows)),
        body,
    )


def pair_grad_job(a, first, second):
    depth, rows = a.shape
    tiles = first.shape[1] // 128

    def body(a_hbm, f_hbm, s_hbm, out, a_ref, f_ref, s_ref, turned, held, load_sem, sem):
        loads = fetch(((a_hbm, a_ref), (f_hbm, f_ref), (s_hbm, s_ref)), load_sem)
        flat = held.reshape(2 * tiles * STEP * 2, 128)
        yield
        for load in loads:
            load.wait()
        copies = []
        for i, (start, size) in enumerate(blocks_of(rows)):
            if i >= 2:
                for copy in copies[i - 2]:
                    copy.wait()
            turned[:size] = a_ref[:, start : start + size].T

            def tile(at, columns, slot=i % 2, size=size):
                for j, b_ref in enumerate((f_ref, s_ref)):
                    r = jnp.dot(
                        turned[:size], b_ref[:, pl.ds(at, columns)], preferred_element_type=f32
                    )
                    for half in range(columns // 128):
                        base = (slot * tiles + at // 128 + half) * (2 * STEP) + j
                        flat[pl.ds(base, size, stride=2), :] = r[:, half * 128 : half * 128 + 128]

            column_tiles(tiles * 128, tile)
            copies.append(
                [
                    pltpu.make_async_copy(
                        held.at[i % 2, c, pl.ds(0, size)],
                        out.at[pl.ds(start, size), :, pl.ds(c * 128, 128)],
                        sem.at[i % 2, c],
                    )
                    for c in range(tiles)
                ]
            )
            for copy in copies[i]:
                copy.start()
            yield
        for copy in copies[-2] + copies[-1]:
            copy.wait()

    return Job(
        [a, first, second],
        [jax.ShapeDtypeStruct((rows, 2, tiles * 128), f32)],
        [
            pltpu.VMEM(a.shape, bf16),
            pltpu.VMEM(first.shape, bf16),
            pltpu.VMEM(second.shape, bf16),
            pltpu.VMEM((STEP, depth), bf16),
            pltpu.VMEM((2, tiles, STEP, 2, 128), f32),
            DMA((3,)),
            DMA((2, tiles)),
        ],
        len(blocks_of(rows)),
        body,
    )


def split_job(weight):
    rows, _, width = weight.shape

    def body(w_hbm, first, second, block, wide, held, load_sem, sem):
        flat = wide.reshape(2 * STEP, 128)
        steps = rows // STEP

        def load(i):
            return pltpu.make_async_copy(
                w_hbm.at[pl.ds(i * STEP, STEP)], block.at[i % 2], load_sem.at[i % 2]
            )

        load(0).start()
        yield
        copies = []
        for i in range(steps):
            slot = i % 2
            if i + 1 < steps:
                load(i + 1).start()
            load(i).wait()
            if i >= 2:
                for copy in copies[i - 2]:
                    copy.wait()

            def tile(c, carry, slot=slot):
                at = pl.ds(pl.multiple_of(c * 128, 128), 128)
                wide[...] = block[slot, :, :, at].astype(f32)
                for j in range(2):
                    held[slot, j, :, at] = flat[pl.ds(j, STEP, stride=2), :].astype(bf16)
                return carry

            lax.fori_loop(0, width // 128, tile, 0)
            copies.append(
                [
                    pltpu.make_async_copy(
                        held.at[slot, j], out.at[pl.ds(i * STEP, STEP)], sem.at[slot, j]
                    )
                    for j, out in enumerate((first, second))
                ]
            )
            for copy in copies[i]:
                copy.start()
            yield
        for copy in copies[-2] + copies[-1]:
            copy.wait()

    return Job(
        [weight],
        [jax.ShapeDtypeStruct((rows, width), bf16)] * 2,
        [
            pltpu.VMEM((2, STEP, 2, width), bf16),
            pltpu.VMEM((STEP, 2, 128), f32),
            pltpu.VMEM((2, 2, STEP, width), bf16),
            DMA((2,)),
            DMA((2, 2)),
        ],
        rows // STEP,
        body,
    )


def ffn_job(x, gate_weight, up_weight, down_weight):
    rows, width = x.shape
    hidden = gate_weight.shape[1]

    def body(
        x_hbm, g_hbm, u_hbm, d_hbm, gate_out, up_out, act_out, out, x_ref, g_ref, u_ref, d_ref, pre, act, res,
        load_sem, sem
    ):
        loads = fetch(((x_hbm, x_ref), (g_hbm, g_ref), (u_hbm, u_ref), (d_hbm, d_ref)), load_sem)
        yield
        for load in loads[:3]:
            load.wait()
        copies = []
        for i, (start, size) in enumerate(blocks_of(rows)):
            slot = i % 2
            here = pl.ds(start, size)
            if i >= 2:
                for copy in copies[i - 2]:
                    copy.wait()

            def tile(at, columns, slot=slot, start=start, size=size):
                part = pl.ds(at, columns)
                left = x_ref[start : start + size]
                gate = dot(left, g_ref[:, part])
                up = dot(left, u_ref[:, part])
                pre[slot, 0, :, part] = gate
                pre[slot, 1, :, part] = up
                act[slot, :, part] = (gate * jax.nn.sigmoid(gate) * up).astype(bf16)

            column_tiles(hidden, tile)
            yield
            if i == 0:
                loads[3].wait()

            def last(at, columns, slot=slot):
                part = pl.ds(at, columns)
                res[slot, :, part] = dot(act[slot], d_ref[:, part]).astype(bf16)

            column_tiles(width, last)
            copies.append(
                [
                    pltpu.make_async_copy(src.at[slot], dst.at[here], sem.at[slot, k])
                    for k, (src, dst) in enumerate(((act, act_out), (res, out)))
                ]
                + [
                    pltpu.make_async_copy(pre.at[slot, k], dst.at[here], sem.at[slot, 2 + k])
                    for k, dst in enumerate((gate_out, up_out))
                ]
            )
            for copy in copies[i]:
                copy.start()
            yield
        for copy in copies[-2] + copies[-1]:
            copy.wait()

    return Job(
        [x, gate_weight, up_weight, down_weight],
        [jax.ShapeDtypeStruct((rows, hidden), f32)] * 2
        + [jax.ShapeDtypeStruct((rows, hidden), bf16), jax.ShapeDtypeStruct((rows, width), bf16)],
        [
            pltpu.VMEM(x.shape, bf16),
            pltpu.VMEM(gate_weight.shape, bf16),
            pltpu.VMEM(up_weight.shape, bf16),
            pltpu.VMEM(down_weight.shape, bf16),
            pltpu.VMEM((2, 2, STEP, hidden), f32),
            pltpu.VMEM((2, STEP, hidden), bf16),
            pltpu.VMEM((2, STEP, width), bf16),
            DMA((4,)),
            DMA((2, 4)),
        ],
        2 * (rows // STEP),
        body,
    )


def ffn_plain(x, gate_weight, up_weight, down_weight):
    gate_pre, up_pre = dot(x, gate_weight), dot(x, up_weight)
    activated = (gate_pre * jax.nn.sigmoid(gate_pre) * up_pre).astype(bf16)
    return gate_pre, up_pre, activated, dot(activated, down_weight).astype(bf16)


def before_activation(grad_act, gate_pre, up_pre):
    sigmoid_gate = jax.nn.sigmoid(gate_pre)
    grad_up = (grad_act * gate_pre * sigmoid_gate).astype(bf16)
    grad_gate = (
        grad_act * up_pre * sigmoid_gate * (1.0 + gate_pre * (1.0 - sigmoid_gate))
    ).astype(bf16)
    return grad_gate, grad_up


def ffn_back_job(grad, gate_pre, up_pre, gate_weight, up_weight, down_weight):
    rows, width = grad.shape
    hidden = gate_weight.shape[1]

    def body(
        x_hbm, gp_hbm, up_hbm, g_hbm, u_hbm, d_hbm, gate_out, up_out, out, x_ref, g_ref, u_ref, d_ref, pre, hid,
        res, load_sem, pre_sem, sem
    ):
        loads = fetch(((x_hbm, x_ref), (d_hbm, d_ref), (g_hbm, g_ref), (u_hbm, u_ref)), load_sem)

        def load_pre(i):
            here = pl.ds(i * STEP, STEP)
            return [
                pltpu.make_async_copy(src.at[here], pre.at[i % 2, k], pre_sem.at[i % 2, k])
                for k, src in enumerate((gp_hbm, up_hbm))
            ]

        for copy in load_pre(0):
            copy.start()
        yield
        for load in loads[:2]:
            load.wait()
        copies = []
        steps = rows // STEP
        for i in range(steps):
            slot, start = i % 2, i * STEP
            here = pl.ds(start, STEP)
            if i + 1 < steps:
                for copy in load_pre(i + 1):
                    copy.start()
            for copy in load_pre(i):
                copy.wait()
            if i >= 2:
                for copy in copies[i - 2]:
                    copy.wait()

            def tile(at, columns, slot=slot, start=start):
                part = pl.ds(at, columns)
                grad_act = dot_t(x_ref[start : start + STEP], d_ref[part, :])
                pair = before_activation(grad_act, pre[slot, 0, :, part], pre[slot, 1, :, part])
                hid[slot, 0, :, part], hid[slot, 1, :, part] = pair

            column_tiles(hidden, tile)
            yield
            if i == 0:
                for load in loads[2:]:
                    load.wait()

            def last(at, columns, slot=slot):
                part = pl.ds(at, columns)
                total = dot_t(hid[slot, 0], g_ref[part, :]) + dot_t(hid[slot, 1], u_ref[part, :])
                res[slot, :, part] = total.astype(bf16)

            column_tiles(width, last)
            copies.append(
                [pltpu.make_async_copy(res.at[slot], out.at[here], sem.at[slot, 2])]
                + [
                    pltpu.make_async_copy(hid.at[slot, k], dst.at[here], sem.at[slot, k])
                    for k, dst in enumerate((gate_out, up_out))
                ]
            )
            for copy in copies[i]:
                copy.start()
            yield
        for copy in copies[-2] + copies[-1]:
            copy.wait()

    return Job(
        [grad, gate_pre, up_pre, gate_weight, up_weight, down_weight],
        [jax.ShapeDtypeStruct((rows, hidden), bf16)] * 2 + [jax.ShapeDtypeStruct((rows, width), bf16)],
        [
            pltpu.VMEM(grad.shape, bf16),
            pltpu.VMEM(gate_weight.shape, bf16),
            pltpu.VMEM(up_weight.shape, bf16),
            pltpu.VMEM(down_weight.shape, bf16),
            pltpu.VMEM((2, 2, STEP, hidden), f32),
            pltpu.VMEM((2, 2, STEP, hidden), bf16),
            pltpu.VMEM((2, STEP, width), bf16),
            DMA((4,)),
            DMA((2, 2)),
            DMA((2, 3)),
        ],
        2 * (rows // STEP),
        body,
    )


def ffn_back_plain(grad, gate_pre, up_pre, gate_weight, up_weight, down_weight):
    grad_gate, grad_up = before_activation(dot_t(grad, down_weight), gate_pre, up_pre)
    back = dot_t(grad_gate, gate_weight) + dot_t(grad_up, up_weight)
    return grad_gate, grad_up, back.astype(bf16)


def dispatch_job(rows, n_ws):
    n, count, width = rows.shape

    def body(rows, out, own, load_sem, ep_s, ep_r, y_s, y_r, c_s, c_r, x_s, x_r):
        e, w = lax.axis_index("ep"), lax.axis_index("ws")
        twin, other = flip(w, 1), flip(w, 2)
        sources = [e] + [flip(e, k) for k in range(1, n)]
        first = []
        for i, s in enumerate(sources[1:]):
            first.append(remote(rows.at[s], out.at[e, w], ep_s.at[i], ep_r.at[i], (s, w)))
            first[-1].start()
        load = pltpu.make_async_copy(rows.at[e], own, load_sem.at[0])
        load.start()
        over_y, to_twin, relayed = [], [], []

        def relay(j):
            over_y[j].wait_recv()
            block = out.at[sources[j], other]
            relayed.append(remote(block, block, x_s.at[j], x_r.at[j], (e, twin)))
            relayed[-1].start()

        for j, s in enumerate(sources):
            place = out.at[s, w]
            block = rows.at[e] if j == 0 else place
            if j:
                first[j - 1].wait_recv()
            over_y.append(remote(block, place, y_s.at[j], y_r.at[j], (e, other)))
            over_y[-1].start()
            to_twin.append(remote(block, place, c_s.at[j], c_r.at[j], (e, twin)))
            to_twin[-1].start()
            if j == 0:
                load.wait()
                store = pltpu.make_async_copy(own, out.at[e, w], load_sem.at[1])
                store.start()
            else:
                relay(j - 1)
            yield
        relay(n - 1)
        store.wait()
        for copy in first + over_y:
            copy.wait_send()
        for copy in to_twin + relayed:
            copy.wait()

    return Job(
        [rows],
        [jax.ShapeDtypeStruct((n, n_ws, count, width), rows.dtype)],
        [pltpu.VMEM((count, width), rows.dtype), DMA((2,)), DMA((n - 1,)), DMA((n - 1,))]
        + [DMA((n,)) for _ in range(6)],
        n,
        body,
        [(k, 0) for k in range(1, n)] + [(0, 1), (0, 2)],
    )


def combine_job(part):
    n, _, count, width = part.shape
    block = (n, count, width)

    def body(
        part, out, mine, core, sum_y, from_y, total, load_sem, c_s, c_r, y_s, y_r, ep_s, ep_r, own_sem
    ):
        e, w = lax.axis_index("ep"), lax.axis_index("ws")
        twin, other, last = flip(w, 1), flip(w, 2), flip(w, 3)
        targets = [flip(e, k) for k in far_first(n)] + [e]
        loads, cores = {}, {}
        for half, near, far in ((1, other, last), (0, w, twin)):
            for j, s in enumerate(targets):
                cores[half, j] = remote(
                    part.at[s, far], core.at[half, j], c_s.at[half, j], c_r.at[half, j], (e, twin)
                )
                cores[half, j].start()
                loads[half, j] = pltpu.make_async_copy(
                    part.at[s, near], mine.at[half, j], load_sem.at[half, j]
                )
                loads[half, j].start()
        over_y, back = [], []

        def send_y(j):
            over_y.append(remote(sum_y.at[j], from_y.at[j], y_s.at[j], y_r.at[j], (e, other)))
            over_y[-1].start()

        def send_back(j):
            back.append(remote(total.at[j], out.at[e], ep_s.at[j], ep_r.at[j], (targets[j], w)))
            back[-1].start()

        for j in range(n):
            loads[1, j].wait()
            cores[1, j].wait_recv()
            sum_y[j] = (mine[1, j].astype(f32) + core[1, j].astype(f32)).astype(bf16)
            if j:
                send_y(j - 1)
        loads[0, 0].wait()
        cores[0, 0].wait_recv()
        send_y(n - 1)
        for j in range(n):
            if j:
                loads[0, j].wait()
                cores[0, j].wait_recv()
            over_y[j].wait_recv()
            total[j] = (
                mine[0, j].astype(f32) + core[0, j].astype(f32) + from_y[j].astype(f32)
            ).astype(bf16)
            if j:
                send_back(j - 1)
            yield
        for copy in over_y + list(cores.values()):
            copy.wait_send()
        keep = pltpu.make_async_copy(total.at[n - 1], out.at[e], own_sem)
        keep.start()
        for copy in back:
            copy.wait()
        keep.wait()

    return Job(
        [part],
        [jax.ShapeDtypeStruct(block, part.dtype)],
        [
            pltpu.VMEM((2,) + block, part.dtype),
            pltpu.VMEM((2,) + block, part.dtype),
            pltpu.VMEM(block, part.dtype),
            pltpu.VMEM(block, part.dtype),
            pltpu.VMEM(block, part.dtype),
            DMA((2, n)),
            DMA((2, n)),
            DMA((2, n)),
            DMA((n,)),
            DMA((n,)),
            DMA((n - 1,)),
            DMA((n - 1,)),
            DMA,
        ],
        n,
        body,
        [(k, 0) for k in range(1, n)] + [(0, 1), (0, 2)],
    )


def exchange_job(rows):
    n = rows.shape[0]

    def body(rows, out, own, load_sem, ep_s, ep_r):
        e, w = lax.axis_index("ep"), lax.axis_index("ws")
        targets = [flip(e, k) for k in far_first(n)]
        copies = []
        for i, s in enumerate(targets):
            copies.append(remote(rows.at[s], out.at[e], ep_s.at[i], ep_r.at[i], (s, w)))
            copies[-1].start()
        load = pltpu.make_async_copy(rows.at[e], own, load_sem.at[0])
        load.start()
        load.wait()
        store = pltpu.make_async_copy(own, out.at[e], load_sem.at[1])
        store.start()
        yield
        store.wait()
        for copy in copies:
            copy.wait()

    return Job(
        [rows],
        [jax.ShapeDtypeStruct(rows.shape, rows.dtype)],
        [pltpu.VMEM(rows.shape[1:], rows.dtype), DMA((2,)), DMA((n - 1,)), DMA((n - 1,))],
        1,
        body,
        [(k, 0) for k in range(1, n)],
    )


def exchange_combine_job(rows, weight, product, n_ws):
    n, held, depth = rows.shape
    count, width = held // n_ws, max(weight.shape)
    block = (n, count, width)
    turned = weight.shape[0] == width

    def body(
        rows, w_hbm, moved, out, w_ref, here, part, core, sum_y, from_y, total, load_sem, ep_s, ep_r, c_s, c_r,
        y_s, y_r, b_s, b_r
    ):
        e, w = lax.axis_index("ep"), lax.axis_index("ws")
        twin, other, last = flip(w, 1), flip(w, 2), flip(w, 3)
        places = [e] + [flip(e, k) for k in range(1, n)]
        weights = pltpu.make_async_copy(w_hbm, w_ref, load_sem.at[n])
        weights.start()
        arrivals = []
        for i, s in enumerate(places[1:]):
            arrivals.append(remote(rows.at[s], moved.at[e], ep_s.at[i], ep_r.at[i], (s, w)))
            arrivals[i].start()
        cores, over_y, back, stores = {}, [], [], []

        def multiply(j):
            if j:
                arrivals[j - 1].wait_recv()
            src = moved.at[places[j]] if j else rows.at[e]
            load = pltpu.make_async_copy(src, here.at[j], load_sem.at[j])
            load.start()
            load.wait()
            if j == 0:
                stores.append(pltpu.make_async_copy(here.at[0], moved.at[e], load_sem.at[0]))
                stores[0].start()
                weights.wait()

            def tile(at, columns):
                tall = pl.ds(at, columns)
                result = product(here[j], w_ref[tall, :] if turned else w_ref[:, tall])
                part[j, :, :, tall] = result.reshape(n_ws, count, columns).astype(bf16)

            column_tiles(width, tile)

        def send_core(j):
            for half, to in ((1, last), (0, twin)):
                cores[half, j] = remote(
                    part.at[j, to], core.at[half, j], c_s.at[half, j], c_r.at[half, j], (e, twin)
                )
                cores[half, j].start()

        def add_core(j):
            cores[1, j].wait_recv()
            sum_y[j] = (part[j, other].astype(f32) + core[1, j].astype(f32)).astype(bf16)

        def send_y(j):
            over_y.append(remote(sum_y.at[j], from_y.at[j], y_s.at[j], y_r.at[j], (e, other)))
            over_y[j].start()

        def add_all(j):
            cores[0, j].wait_recv()
            over_y[j].wait_recv()
            total[j] = (
                part[j, w].astype(f32) + core[0, j].astype(f32) + from_y[j].astype(f32)
            ).astype(bf16)

        def send_back(j):
            if j:
                back.append(
                    remote(total.at[j], out.at[e], b_s.at[j - 1], b_r.at[j - 1], (places[j], w))
                )
                back[j - 1].start()
            else:
                stores.append(pltpu.make_async_copy(total.at[0], out.at[e], load_sem.at[1]))
                stores[1].start()

        for t in range(n + 4):
            for lag, stage in ((0, multiply), (1, add_core), (3, add_all), (0, send_core), (1, send_y), (4, send_back)):
                if 0 <= t - lag < n:
                    stage(t - lag)
            yield
        for copy in arrivals + list(cores.values()) + over_y:
            copy.wait_send()
        for copy in back + stores:
            copy.wait()

    return Job(
        [rows, weight],
        [jax.ShapeDtypeStruct(rows.shape, bf16), jax.ShapeDtypeStruct(block, bf16)],
        [
            pltpu.VMEM(weight.shape, bf16),
            pltpu.VMEM(rows.shape, bf16),
            pltpu.VMEM((n, n_ws, count, width), bf16),
            pltpu.VMEM((2,) + block, bf16),
            pltpu.VMEM(block, bf16),
            pltpu.VMEM(block, bf16),
            pltpu.VMEM(block, bf16),
            DMA((n + 1,)),
            DMA((n - 1,)),
            DMA((n - 1,)),
            DMA((2, n)),
            DMA((2, n)),
            DMA((n,)),
            DMA((n,)),
            DMA((n - 1,)),
            DMA((n - 1,)),
        ],
        n + 4,
        body,
        [(k, 0) for k in range(1, n)] + [(0, 1), (0, 2)],
    )


def dispatch_exchange_job(rows, weight, product, n_ws):
    n, count, width = rows.shape
    turned = weight.shape[1] == width
    narrow = weight.shape[0] if turned else weight.shape[1]

    def body(
        rows, w_hbm, out, moved, w_ref, own, here, flat, res, load_sem, ep_s, ep_r, y_s, y_r, c_s, c_r, x_s, x_r,
        b_s, b_r
    ):
        e, w = lax.axis_index("ep"), lax.axis_index("ws")
        twin, other = flip(w, 1), flip(w, 2)
        places = [e] + [flip(e, k) for k in range(1, n)]
        weights = pltpu.make_async_copy(w_hbm, w_ref, load_sem.at[2])
        weights.start()
        first, over_y, to_twin, relayed, back, stores = [], [], [], [], [], []
        for i, s in enumerate(places[1:]):
            first.append(remote(rows.at[s], out.at[e, w], ep_s.at[i], ep_r.at[i], (s, w)))
            first[i].start()
        load = pltpu.make_async_copy(rows.at[e], own, load_sem.at[0])
        load.start()

        def arrive(j):
            place = out.at[places[j], w]
            block = place if j else rows.at[e]
            if j:
                first[j - 1].wait_recv()
            over_y.append(remote(block, place, y_s.at[j], y_r.at[j], (e, other)))
            over_y[j].start()
            to_twin.append(remote(block, place, c_s.at[j], c_r.at[j], (e, twin)))
            to_twin[j].start()
            if j == 0:
                load.wait()
                stores.append(pltpu.make_async_copy(own, place, load_sem.at[1]))
                stores[0].start()

        def relay(j):
            over_y[j].wait_recv()
            block = out.at[places[j], other]
            relayed.append(remote(block, block, x_s.at[j], x_r.at[j], (e, twin)))
            relayed[j].start()

        def multiply(j):
            to_twin[j].wait_recv()
            relayed[j].wait_recv()
            if j == 0:
                stores[0].wait()
                weights.wait()
            source = pltpu.make_async_copy(out.at[places[j]], here, load_sem.at[0])
            source.start()
            source.wait()
            flat[...] = here[...].astype(f32).reshape(n_ws * count, width).astype(bf16)

            def tile(at, columns):
                tall = pl.ds(at, columns)
                part = product(flat[...], w_ref[tall, :] if turned else w_ref[:, tall])
                res[j, :, tall] = part.astype(bf16)

            column_tiles(narrow, tile)

        def send(j):
            if j:
                back.append(
                    remote(res.at[j], moved.at[e], b_s.at[j - 1], b_r.at[j - 1], (places[j], w))
                )
                back[j - 1].start()
            else:
                stores.append(pltpu.make_async_copy(res.at[0], moved.at[e], load_sem.at[1]))
                stores[1].start()

        for t in range(n + 3):
            for lag, stage in enumerate((arrive, relay, multiply, send)):
                if 0 <= t - lag < n:
                    stage(t - lag)
            yield
        for copy in first + over_y + to_twin + relayed:
            copy.wait_send()
        for copy in back + stores[1:]:
            copy.wait()

    return Job(
        [rows, weight],
        [
            jax.ShapeDtypeStruct((n, n_ws, count, width), bf16),
            jax.ShapeDtypeStruct((n, n_ws * count, narrow), bf16),
        ],
        [
            pltpu.VMEM(weight.shape, bf16),
            pltpu.VMEM((count, width), bf16),
            pltpu.VMEM((n_ws, count, width), bf16),
            pltpu.VMEM((n_ws * count, width), bf16),
            pltpu.VMEM((n, n_ws * count, narrow), bf16),
            DMA((3,)),
            DMA((n - 1,)),
            DMA((n - 1,)),
        ]
        + [DMA((n,)) for _ in range(6)]
        + [DMA((n - 1,)), DMA((n - 1,))],
        n + 3,
        body,
        [(k, 0) for k in range(1, n)] + [(0, 1), (0, 2)],
    )


def gather_weights_job(mine, normed, n, n_ws):
    rows, block = mine.shape
    routes = [(4, 0), (2, 0), (2, 4)]

    def body(
        mine, normed, out, seq, held, held_rows, load_sem, s_sem, r_sem, x_s, x_r, y_s, y_r, c_s, c_r, t_s, t_r
    ):
        e, w = lax.axis_index("ep"), lax.axis_index("ws")
        twin, other, near = flip(w, 1), flip(w, 2), flip(e, 1)
        copies = {}

        def send(hop, offset, half):
            k = routes.index((hop, offset))
            part = pl.ds(half * (rows // 2), rows // 2)
            at = pl.multiple_of(flip(e, offset) // 2 * block, block)
            place = out.at[part, pl.ds(at, block)]
            copies[hop, offset, half] = remote(
                place if offset else mine.at[part],
                place,
                s_sem.at[k, half],
                r_sem.at[k, half],
                (flip(e, hop), w),
            )
            copies[hop, offset, half].start()

        for half in range(2):
            for route in routes[:2]:
                send(*route, half)
        to_near = remote(normed, seq.at[e % 2, w], x_s, x_r, (near, w))
        to_near.start()
        over_y, to_twin, relays = [], [], []

        def spread_rows(k, half, src):
            place = seq.at[half, w]
            over_y.append(remote(src, place, y_s.at[k], y_r.at[k], (e, other)))
            over_y[k].start()
            to_twin.append(remote(src, place, c_s.at[k], c_r.at[k], (e, twin)))
            to_twin[k].start()

        def relay(k, half):
            over_y[k].wait_recv()
            place = seq.at[half, other]
            relays.append(remote(place, place, t_s.at[k], t_r.at[k], (e, twin)))
            relays[k].start()

        spread_rows(0, e % 2, normed)
        loads = fetch(((mine, held), (normed, held_rows)), load_sem)
        for load in loads:
            load.wait()
        own = out.at[:, pl.ds(pl.multiple_of(e // 2 * block, block), block)]
        stores = fetch(((held, own), (held_rows, seq.at[e % 2, w])), load_sem)
        yield
        to_near.wait_recv()
        spread_rows(1, near % 2, seq.at[near % 2, w])
        yield
        copies[4, 0, 0].wait_recv()
        send(2, 4, 0)
        yield
        relay(0, e % 2)
        copies[4, 0, 1].wait_recv()
        send(2, 4, 1)
        yield
        relay(1, near % 2)
        yield
        for store in stores:
            store.wait()
        for (_, offset, half), copy in copies.items():
            copy.wait_send()
            if (_, offset) != (4, 0):
                copy.wait_recv()
        to_near.wait_send()
        for copy in over_y:
            copy.wait_send()
        for copy in to_twin + relays:
            copy.wait()

    return Job(
        [mine, normed],
        [
            jax.ShapeDtypeStruct((rows, n // 2 * block), bf16),
            jax.ShapeDtypeStruct((2, n_ws) + normed.shape, bf16),
        ],
        [
            pltpu.VMEM(mine.shape, bf16),
            pltpu.VMEM(normed.shape, bf16),
            DMA((2,)),
            DMA((3, 2)),
            DMA((3, 2)),
            DMA,
            DMA,
        ]
        + [DMA((2,)) for _ in range(6)],
        5,
        body,
        [(1, 0), (2, 0), (4, 0), (0, 1), (0, 2)],
    )


def swap_job(blocks):
    def body(blocks, out, held, load_sem, s_sem, r_sem):
        e, w = lax.axis_index("ep"), lax.axis_index("ws")
        near = flip(e, 1)
        copy = remote(blocks.at[near % 2], out.at[e % 2], s_sem, r_sem, (near, w))
        copy.start()
        load = fetch(((blocks.at[e % 2], held),), load_sem)[0]
        load.wait()
        store = fetch(((held, out.at[e % 2]),), load_sem)[0]
        yield
        store.wait()
        copy.wait()

    return Job(
        [blocks],
        [jax.ShapeDtypeStruct(blocks.shape, blocks.dtype)],
        [pltpu.VMEM(blocks.shape[1:], blocks.dtype), DMA((1,)), DMA, DMA],
        1,
        body,
        [(1, 0)],
    )


def add_blocks(out, *refs):
    step = 64 if out.shape[1] > 1024 else 256

    def body(i, carry):
        at = pl.ds(pl.multiple_of(i * step, step), step)
        total = refs[0][at].astype(f32)
        for ref in refs[1:]:
            total = total + ref[at].astype(f32)
        out[at] = total.astype(bf16)
        return carry

    lax.fori_loop(0, out.shape[0] // step, body, 0)


def reduce_weights_job(pieces, part, n):
    rows = pieces.shape[0]
    block = pieces.shape[1] // (n // 2)
    offsets = (4, 0)

    def body(
        pieces, part, out, out_rows, mine, from_z, fourth, last_z, total, own, core, sum_y, from_y, total_near,
        from_near, total_rows, load_sem, z_s, z_r, w_load, c_s, c_r, y_s, y_r, x_s, x_r, sem, h_s, h_r
    ):
        e, w = lax.axis_index("ep"), lax.axis_index("ws")
        twin, other, last, near = flip(w, 1), flip(w, 2), flip(w, 3), flip(e, 1)

        def columns(s):
            return pieces.at[:, pl.ds(pl.multiple_of(s // 2 * block, block), block)]

        over_z = []
        for i, offset in enumerate(offsets):
            over_z.append(
                remote(columns(flip(e, offset + 2)), from_z.at[i], z_s.at[i], z_r.at[i], (flip(e, 2), w))
            )
            over_z[i].start()
        halves = (near % 2, e % 2)
        cores = {}
        for k, to in enumerate((last, twin)):
            for h, half in enumerate(halves):
                cores[h, k] = remote(
                    part.at[half, to], core.at[h, k], c_s.at[h, k], c_r.at[h, k], (e, twin)
                )
                cores[h, k].start()
        loads = fetch([(columns(flip(e, o)), mine.at[i]) for i, o in enumerate(offsets)], load_sem)
        own_loads = {}
        for h, half in enumerate(halves):
            for k, to in enumerate((other, w)):
                own_loads[h, k] = pltpu.make_async_copy(
                    part.at[half, to], own.at[h, k], w_load.at[h, k]
                )
                own_loads[h, k].start()
        yield
        over_y = []

        def send_y(h):
            over_y.append(remote(sum_y.at[h], from_y.at[h], y_s.at[h], y_r.at[h], (e, other)))
            over_y[h].start()

        for h in range(2):
            own_loads[h, 0].wait()
            cores[h, 0].wait_recv()
            add_blocks(sum_y.at[h], own.at[h, 0], core.at[h, 0])
            if h:
                send_y(0)
        yield
        loads[0].wait()
        over_z[0].wait_recv()
        send_y(1)
        add_blocks(fourth, mine.at[0], from_z.at[0])
        yield
        own_loads[0, 1].wait()
        cores[0, 1].wait_recv()
        over_y[0].wait_recv()
        far = remote(fourth, last_z, z_s.at[2], z_r.at[2], (flip(e, 4), w))
        far.start()
        add_blocks(total_near, own.at[0, 1], core.at[0, 1], from_y.at[0])
        yield
        own_loads[1, 1].wait()
        cores[1, 1].wait_recv()
        over_y[1].wait_recv()
        to_near = remote(total_near, from_near, x_s, x_r, (near, w))
        to_near.start()
        yield
        loads[1].wait()
        over_z[1].wait_recv()
        far.wait_recv()
        add_blocks(total, mine.at[1], from_z.at[1], last_z)
        to_near.wait_recv()
        add_blocks(total_rows, own.at[1, 1], core.at[1, 1], from_y.at[1], from_near)
        partner, another = crossed()
        home = remote(total, out, h_s, h_r, partner)
        keep = pltpu.make_async_copy(total, out, sem.at[1])
        store = pltpu.make_async_copy(total_rows, out_rows, sem.at[0])

        @pl.when(another)
        def _():
            home.start()

        @pl.when(jnp.logical_not(another))
        def _():
            keep.start()

        store.start()
        for copy in over_z + list(cores.values()) + over_y + [far, to_near]:
            copy.wait_send()
        store.wait()

        @pl.when(another)
        def _():
            home.wait()

        @pl.when(jnp.logical_not(another))
        def _():
            keep.wait()

    one, rows_one = (rows, block), part.shape[2:]
    return Job(
        [pieces, part],
        [jax.ShapeDtypeStruct(one, bf16), jax.ShapeDtypeStruct(rows_one, bf16)],
        [pltpu.VMEM((2,) + one, bf16) for _ in range(2)]
        + [pltpu.VMEM(one, bf16) for _ in range(3)]
        + [pltpu.VMEM((2, 2) + rows_one, bf16) for _ in range(2)]
        + [pltpu.VMEM((2,) + rows_one, bf16) for _ in range(2)]
        + [pltpu.VMEM(rows_one, bf16) for _ in range(3)]
        + [DMA((2,)), DMA((3,)), DMA((3,)), DMA((2, 2)), DMA((2, 2)), DMA((2, 2))]
        + [DMA((2,)), DMA((2,)), DMA, DMA, DMA((2,)), DMA, DMA],
        5,
        body,
        [(1, 0), (2, 0), (4, 0), (0, 1), (0, 2)],
        True,
    )


def attend_kernel(spans, q_ref, kv_ref, out):
    count, _, slots, part = q_ref.shape
    for w, span in enumerate(spans):

        def head(h, carry, w=w, span=span):
            at = pl.multiple_of(h * HEAD_SIZE, HEAD_SIZE)
            columns = pl.ds(at, HEAD_SIZE)
            q, probs, _, values = head_probs(q_ref, kv_ref, w, span, at)
            mixed = dot(probs.astype(bf16), values)
            out[:, w, :, columns] = mixed.reshape(count, slots, HEAD_SIZE).astype(bf16)
            return carry

        lax.fori_loop(0, part // HEAD_SIZE, head, 0)


def slot_rows(ref, w, at):
    count, _, slots, _ = ref.shape
    rows = ref[:, w, :, pl.ds(at, HEAD_SIZE)].astype(f32)
    return rows.reshape(count * slots, HEAD_SIZE).astype(bf16)


def kv_place(kv, at):
    h = at // HEAD_SIZE
    column = pl.multiple_of(h // 2 * HEAD_SIZE, HEAD_SIZE)
    half = kv.shape[2] // 2
    value_column = pl.multiple_of(half + column, HEAD_SIZE)
    return h % 2, pl.ds(column, HEAD_SIZE), pl.ds(value_column, HEAD_SIZE)


def head_probs(q_ref, kv_ref, w, span, at):
    q = slot_rows(q_ref, w, at)
    side, key_columns, value_columns = kv_place(kv_ref, at)
    keys = kv_ref[side, :span, key_columns]
    values = kv_ref[side, :span, value_columns]
    scores = dot_t(q, keys) * HEAD_SIZE ** (-0.5)
    weight = jnp.exp(scores - jnp.max(scores, -1, keepdims=True))
    probs = weight / jnp.sum(weight, -1, keepdims=True)
    return q, probs, keys, values


def attend_call(queries, kv, spans):
    return pl.pallas_call(
        functools.partial(attend_kernel, spans),
        out_shape=jax.ShapeDtypeStruct(queries.shape, bf16),
        in_specs=[VM, VM],
        out_specs=VM,
        compiler_params=pltpu.CompilerParams(vmem_limit_bytes=VMEM_LIMIT),
        name="attend",
    )(queries, kv)


def attend_back_kernel(spans, q_ref, g_ref, kv_ref, grad_q, grad_kv, total):
    count, _, slots, part = q_ref.shape
    total[...] = jnp.zeros_like(total)
    for w, span in enumerate(spans):

        def head(h, carry, w=w, span=span):
            at = pl.multiple_of(h * HEAD_SIZE, HEAD_SIZE)
            columns = pl.ds(at, HEAD_SIZE)
            q, probs, keys, values = head_probs(q_ref, kv_ref, w, span, at)
            grad = slot_rows(g_ref, w, at)
            grad_probs = dot_t(grad, values)
            centred = jnp.sum(probs * grad_probs, -1, keepdims=True)
            grad_scores = (probs * (grad_probs - centred)).astype(bf16)
            grad_rows = dot(grad_scores, keys) * HEAD_SIZE ** (-0.5)
            grad_q[:, w, :, columns] = grad_rows.reshape(count, slots, HEAD_SIZE).astype(bf16)
            side, key_columns, value_columns = kv_place(kv_ref, at)
            total[side, :span, key_columns] += t_dot(grad_scores, q) * HEAD_SIZE ** (-0.5)
            total[side, :span, value_columns] += t_dot(probs.astype(bf16), grad)
            return carry

        lax.fori_loop(0, part // HEAD_SIZE, head, 0)
    grad_kv[...] = total[...].astype(bf16)


def attend_back_call(queries, grads, kv, spans):
    return pl.pallas_call(
        functools.partial(attend_back_kernel, spans),
        out_shape=[
            jax.ShapeDtypeStruct(queries.shape, bf16),
            jax.ShapeDtypeStruct(kv.shape, bf16),
        ],
        in_specs=[VM, VM, VM],
        out_specs=[VM, VM],
        scratch_shapes=[pltpu.VMEM(kv.shape, f32)],
        compiler_params=pltpu.CompilerParams(vmem_limit_bytes=VMEM_LIMIT),
        name="attend_back",
    )(queries, grads, kv)


def gather_gains_job(own, n, n_ws):
    def body(own, out, held, load_sem, w_s, w_r, ep_s, ep_r):
        e, w = lax.axis_index("ep"), lax.axis_index("ws")
        first = []
        for i in range(n_ws - 1):
            place = (e, flip(w, i + 1))
            first.append(remote(own, out.at[e, w], w_s.at[i], w_r.at[i], place))
            first[i].start()
        load = fetch(((own, held),), load_sem)[0]
        load.wait()
        store = fetch(((held, out.at[e, w]),), load_sem)[0]
        yield
        store.wait()
        for copy in first:
            copy.wait()
        second = []
        for i in range(n - 1):
            place = (flip(e, i + 1), w)
            second.append(remote(out.at[e], out.at[e], ep_s.at[i], ep_r.at[i], place))
            second[i].start()
        yield
        for copy in second:
            copy.wait()

    return Job(
        [own],
        [jax.ShapeDtypeStruct((n, n_ws) + own.shape, own.dtype)],
        [
            pltpu.VMEM(own.shape, own.dtype),
            DMA((1,)),
            DMA((n_ws - 1,)),
            DMA((n_ws - 1,)),
            DMA((n - 1,)),
            DMA((n - 1,)),
        ],
        2,
        body,
        [(k, 0) for k in range(1, n)] + [(0, k) for k in range(1, n_ws)],
    )


def reduce_gains_job(parts):
    n, n_ws = parts.shape[:2]

    def body(parts, out, held, every, total, load_sem, w_s, w_r, ep_s, ep_r):
        e, w = lax.axis_index("ep"), lax.axis_index("ws")
        first, second = [], []
        for i in range(n_ws - 1):
            p = flip(w, i + 1)
            first.append(remote(parts.at[:, p], held.at[:, w], w_s.at[i], w_r.at[i], (e, p)))
            first[i].start()
        keep = fetch(((parts.at[:, w], held.at[:, w]),), load_sem)[0]
        yield
        keep.wait()
        for copy in first:
            copy.wait()
        keep = fetch(((held.at[e], every.at[e]),), load_sem)[0]
        for i in range(n - 1):
            p = flip(e, i + 1)
            second.append(remote(held.at[p], every.at[e], ep_s.at[i], ep_r.at[i], (p, w)))
            second[i].start()
        yield
        keep.wait()
        for copy in second:
            copy.wait()
        total[...] = jnp.sum(jnp.sum(every[...], 0), 0)
        store = fetch(((total, out),), load_sem)[0]
        store.wait()

    return Job(
        [parts],
        [jax.ShapeDtypeStruct(parts.shape[2:], parts.dtype)],
        [
            pltpu.VMEM(parts.shape, parts.dtype),
            pltpu.VMEM(parts.shape, parts.dtype),
            pltpu.VMEM(parts.shape[2:], parts.dtype),
            DMA((1,)),
            DMA((n_ws - 1,)),
            DMA((n_ws - 1,)),
            DMA((n - 1,)),
            DMA((n - 1,)),
        ],
        2,
        body,
        [(k, 0) for k in range(1, n)] + [(0, k) for k in range(1, n_ws)],
    )


def small(n_ep):
    return n_ep == MIXTURE_EXPERTS and lax.axis_size("ws") == 4


PLAIN = {
    grad_job: lambda a, b: [t_dot(a, b)],
    pair_grad_job: lambda a, b, c: [jnp.stack([t_dot(a, b), t_dot(a, c)], 1)],
    split_job: lambda weight: [weight[:, 0], weight[:, 1]],
    ffn_job: ffn_plain,
    ffn_back_job: ffn_back_plain,
}


def beside(job, plain, arg, fills, collective_id, name):
    if job is None:
        return [plain(arg)] + [out for make, *rest in fills for out in PLAIN[make](*rest)]
    return run_jobs([job(arg)], [make(*rest) for make, *rest in fills], collective_id, name)


def exchange_plain(send):
    return lax.all_to_all(send, "ep", split_axis=0, concat_axis=0, tiled=True)


def exchange(send, *fills, collective_id=2, name="exchange"):
    job = exchange_job if small(send.shape[0]) else None
    return beside(job, exchange_plain, send, fills, collective_id, name)


def spread(rows, group):
    width = rows.shape[-1]
    blocks = rows.reshape(MIXTURE_EXPERTS, 1, ROWS, width)
    return jnp.broadcast_to(blocks, (MIXTURE_EXPERTS, group, ROWS, width)).reshape(
        MIXTURE_EXPERTS * group, ROWS, width
    )


def dispatch(rows, group, *fills, collective_id=0, name="dispatch"):
    width = rows.shape[-1]

    def plain(blocks):
        return lax.all_gather(exchange_plain(blocks), "ws", axis=1, tiled=False)

    job = functools.partial(dispatch_job, n_ws=4) if small(MIXTURE_EXPERTS * group) else None
    out = beside(job, plain, spread(rows, group), fills, collective_id, name)
    return [out[0].reshape(-1, width)] + list(out[1:])


def combine(partial, group, n_ep, n_ws, *fills, collective_id=1, name="combine"):
    width = partial.shape[-1]

    def plain(part):
        part = part.transpose(1, 0, 2, 3).reshape(n_ws * n_ep * ROWS, width)
        own = lax.psum_scatter(part, "ws", scatter_dimension=0, tiled=True)
        return exchange_plain(own.reshape(n_ep, ROWS, width))

    part = partial.reshape(n_ep, n_ws, ROWS, width)
    job = combine_job if small(n_ep) else None
    back, *rest = beside(job, plain, part, fills, collective_id, name)
    if group > 1:
        back = jnp.sum(back.reshape(MIXTURE_EXPERTS, group, ROWS, width).astype(f32), 1).astype(bf16)
    return [back.reshape(MIXTURE_EXPERTS * ROWS, width)] + rest


def slot_tables(routes, slots):
    target = jnp.where(slots < CAP, routes * ROWS + slots, -1)
    places = lax.broadcasted_iota(jnp.int32, (MIXTURE_EXPERTS * ROWS, target.shape[0]), 0)
    return [(places == target[None, :, k]).astype(bf16) for k in range(CHOSEN_EXPERTS)]


def norm_back(grad, unit, inverse, gain):
    gain_grad = jnp.sum(grad * unit, 0)
    scaled = grad * gain
    return (inverse * (scaled - unit * jnp.mean(scaled * unit, -1, keepdims=True)), gain_grad)


def heads_of(rows):
    return rows.reshape(rows.shape[0], -1, HEAD_SIZE)


def local(
    x_in,
    gain_attn,
    gain_ffn,
    key_value_weight,
    w_query,
    w_output,
    w_in,
    w_out,
    gate_attn,
    gate_ffn,
    route_attn,
    slot_attn,
    route_ffn,
    slot_ffn,
    cotangent,
):
    n_ep = lax.axis_size("ep")
    n_ws = lax.axis_size("ws")
    group = n_ep // MIXTURE_EXPERTS
    local_tokens, width = x_in.shape
    key_value_width = KEY_VALUE_HEADS * HEAD_SIZE
    part = w_query.shape[2]
    own_width = group * part
    sequence = n_ws * local_tokens
    place = lax.axis_index("ws")
    scale = HEAD_SIZE ** (-0.5)

    fused = small(n_ep) and key_value_weight.shape[1] == HEAD_SIZE and gain_attn.shape[0] == 64
    if fused:
        gains = jnp.concatenate([gain_attn, gain_ffn], 0).astype(f32)[None]
        gains = run_jobs([gather_gains_job(gains, n_ep, n_ws)], [], 3, "gather_gains")[0]
        gains = gains.reshape(n_ep * n_ws, 2, -1)
        gain_one, gain_two = gains[:, 0].reshape(-1), gains[:, 1].reshape(-1)
    else:
        gain_one = lax.all_gather(gain_attn, ("ep", "ws"), axis=0, tiled=True).astype(f32)
        gain_two = lax.all_gather(gain_ffn, ("ep", "ws"), axis=0, tiled=True).astype(f32)
    plain = group == 1 and key_value_weight.shape[1] == HEAD_SIZE
    if plain:
        half = n_ep // 2
        there = [
            (e * n_ws + w, (w + n_ws * (e // half)) * n_ws + e % half)
            for e in range(n_ep)
            for w in range(n_ws)
        ]
        mine = lax.ppermute(key_value_weight, ("ep", "ws"), there)
    else:
        whole = lax.all_gather(key_value_weight, ("ep", "ws"), axis=1, tiled=True)
        whole = whole.reshape(width, 2 * group, n_ws, part)
        kv_own = lax.dynamic_index_in_dim(whole, place, 2, keepdims=False).reshape(width, -1)

    inputs = x_in.astype(f32)
    inverse_one = lax.rsqrt(jnp.mean(inputs * inputs, -1, keepdims=True) + EPS)
    unit_one = inputs * inverse_one
    normed = (unit_one * gain_one).astype(bf16)
    attn_pairs = slot_tables(route_attn, slot_attn)
    ffn_pairs = slot_tables(route_ffn, slot_ffn)
    attn_tokens = attn_pairs[0] + attn_pairs[1]
    ffn_tokens = ffn_pairs[0] + ffn_pairs[1]

    slots_one = dot(attn_tokens, normed).astype(bf16)
    if fused:
        rows_one, kv_own, normed_sequence, gate_weight, up_weight = run_jobs(
            [
                dispatch_job(slots_one.reshape(n_ep, ROWS, width), n_ws),
                gather_weights_job(mine, normed, n_ep, n_ws),
            ],
            [split_job(w_in[0])],
            10,
            "dispatch_weights",
        )
        rows_one = rows_one.reshape(-1, width)
        normed_sequence = normed_sequence.reshape(2 * sequence, width)
    else:
        if plain:
            kv_own = lax.all_gather(mine, "ep", axis=1, tiled=True)
        normed_sequence = lax.all_gather(normed, "ws", axis=0, tiled=True)
        rows_one, gate_weight, up_weight = dispatch(slots_one, group, (split_job, w_in[0]))
    kv = dot(normed_sequence, kv_own).astype(bf16)
    if not fused:
        keys = kv[:, :own_width].reshape(sequence, -1, HEAD_SIZE)
        values = kv[:, own_width:].reshape(sequence, -1, HEAD_SIZE)

    owner_query = dot(rows_one, w_query[0]).astype(bf16)
    owner_query = owner_query.reshape(n_ep, n_ws * ROWS, part)
    if fused:
        queries, kv = run_jobs(
            [exchange_job(owner_query), swap_job(kv.reshape(2, sequence, -1))], [], 13, "exchange_kv"
        )
    else:
        queries = exchange(owner_query)[0]
    queries = queries.reshape(MIXTURE_EXPERTS, group, n_ws, ROWS, part)
    spans = [(w * local_tokens // BLOCK + 1) * BLOCK for w in range(n_ws)]

    def by_block(rows):
        rows = rows.reshape(MIXTURE_EXPERTS, group, n_ws, ROWS, part)
        return [
            rows[:, :, w].transpose(0, 2, 1, 3).reshape(-1, own_width // HEAD_SIZE, HEAD_SIZE)
            for w in range(n_ws)
        ]

    def to_experts(pieces):
        rows = jnp.stack(
            [
                piece.reshape(MIXTURE_EXPERTS, ROWS, group, part).transpose(0, 2, 1, 3)
                for piece in pieces
            ],
            2,
        )
        return rows.reshape(n_ep, n_ws * ROWS, part)

    if fused:
        queries = queries.reshape(n_ep, n_ws, ROWS, part)
        mixed = attend_call(queries, kv, spans).reshape(n_ep, n_ws * ROWS, part)
    else:
        kept = []
        mixed_pieces = []
        for q, span in zip(by_block(queries), spans):
            scores = (
                jnp.einsum("rhd,shd->hrs", q, keys[:span], preferred_element_type=f32) * scale
            )
            probs = jax.nn.softmax(scores, axis=-1)
            mixed = jnp.einsum(
                "hrs,shd->rhd", probs.astype(bf16), values[:span], preferred_element_type=f32
            )
            kept.append((q, probs))
            mixed_pieces.append(mixed.astype(bf16))
        mixed = to_experts(mixed_pieces)
    if fused:
        owner_mixed, attn_slots = run_jobs(
            [exchange_combine_job(mixed, w_output[0], dot, n_ws)], [], 11, "exchange_output"
        )
        owner_mixed, attn_slots = owner_mixed.reshape(-1, part), attn_slots.reshape(-1, width)
    else:
        owner_mixed = exchange(mixed)[0].reshape(-1, part)
        output_part = dot(owner_mixed, w_output[0]).astype(bf16)
        attn_slots = combine(output_part, group, n_ep, n_ws)[0]

    def weighted(pairs, gates, slot_values):
        return sum(gates[:, k : k + 1] * t_dot(pairs[k], slot_values) for k in range(2))

    def to_slots(pairs, gates, values):
        return sum(
            dot(pairs[k], (gates[:, k : k + 1] * values).astype(bf16)) for k in range(2)
        ).astype(bf16)

    hidden_state = inputs + weighted(attn_pairs, gate_attn, attn_slots)
    inverse_two = lax.rsqrt(jnp.mean(hidden_state * hidden_state, -1, keepdims=True) + EPS)
    unit_two = hidden_state * inverse_two
    normed_two = (unit_two * gain_two).astype(bf16)

    grad_out = cotangent.astype(f32)
    grad_slots = to_slots(ffn_pairs, gate_ffn, grad_out)
    expert_rows = dispatch(dot(ffn_tokens, normed_two).astype(bf16), group)[0]
    expert_grad, gate_pre, up_pre, activated, forward_part = dispatch(
        grad_slots,
        group,
        (ffn_job, expert_rows, gate_weight, up_weight, w_out[0]),
        collective_id=5,
        name="dispatch_ffn",
    )
    ffn_slots, grad_gate, grad_up, back_two = combine(
        forward_part,
        group,
        n_ep,
        n_ws,
        (ffn_back_job, expert_grad, gate_pre, up_pre, gate_weight, up_weight, w_out[0]),
        collective_id=1,
        name="combine_ffn_back",
    )
    result = hidden_state + weighted(ffn_pairs, gate_ffn, ffn_slots)
    back_slots, grad_second = combine(
        back_two,
        group,
        n_ep,
        n_ws,
        (grad_job, activated, expert_grad),
        collective_id=6,
        name="combine_grad_out",
    )

    grad_normed_two = t_dot(ffn_tokens, back_slots)
    grad_hidden_norm, grad_gain_two = norm_back(grad_normed_two, unit_two, inverse_two, gain_two)
    grad_hidden = grad_out + grad_hidden_norm
    attn_grads = to_slots(attn_pairs, gate_attn, grad_hidden)
    if fused:
        owner_grad, mixed_grads, grad_first = run_jobs(
            [dispatch_exchange_job(attn_grads.reshape(n_ep, ROWS, width), w_output[0], dot_t, n_ws)],
            [pair_grad_job(expert_rows, grad_gate, grad_up)],
            7,
            "dispatch_exchange",
        )
        owner_grad = owner_grad.reshape(-1, width)
    else:
        owner_grad = dispatch(attn_grads, group)[0]
        grad_first = jnp.stack([t_dot(expert_rows, grad_gate), t_dot(expert_rows, grad_up)], 1)
        back_mixed = dot_t(owner_grad, w_output[0]).astype(bf16)
        mixed_grads = exchange(back_mixed.reshape(n_ep, n_ws * ROWS, part))[0]
        grad_output = t_dot(owner_mixed, owner_grad)

    if fused:
        mixed_grads = mixed_grads.reshape(n_ep, n_ws, ROWS, part)
        query_grads, grad_kv_rows = attend_back_call(queries, mixed_grads, kv, spans)
        query_grads = query_grads.reshape(n_ep, n_ws * ROWS, part)
    else:
        grad_keys, grad_values, query_pieces = 0.0, 0.0, []
        for (q, probs), grad, span in zip(kept, by_block(mixed_grads), spans):
            grad_probs = jnp.einsum("rhd,shd->hrs", grad, values[:span], preferred_element_type=f32)
            centred = jnp.sum(probs * grad_probs, -1, keepdims=True)
            grad_scores = (probs * (grad_probs - centred)).astype(bf16)
            grad_q = (
                jnp.einsum("hrs,shd->rhd", grad_scores, keys[:span], preferred_element_type=f32)
                * scale
            )
            query_pieces.append(grad_q.astype(bf16))
            pad = ((0, sequence - span), (0, 0), (0, 0))
            piece = jnp.einsum("hrs,rhd->shd", grad_scores, q, preferred_element_type=f32) * scale
            grad_keys = grad_keys + jnp.pad(piece, pad)
            piece = jnp.einsum(
                "hrs,rhd->shd", probs.astype(bf16), grad, preferred_element_type=f32
            )
            grad_values = grad_values + jnp.pad(piece, pad)
        grad_kv_rows = jnp.concatenate(
            [grad_keys.reshape(sequence, -1), grad_values.reshape(sequence, -1)], 1
        ).astype(bf16)
        query_grads = to_experts(query_pieces)
    if fused:
        owner_grad_query, normed_back, grad_kv_rows, grad_output = run_jobs(
            [exchange_combine_job(query_grads, w_query[0], dot_t, n_ws), swap_job(grad_kv_rows)],
            [grad_job(owner_mixed, owner_grad)],
            14,
            "exchange_back",
        )
        owner_grad_query = owner_grad_query.reshape(-1, part)
        normed_back = normed_back.reshape(-1, width)
        grad_kv_rows = grad_kv_rows.reshape(2 * sequence, -1)
    else:
        owner_grad_query = exchange(query_grads)[0].reshape(-1, part)
    grad_kv = t_dot(normed_sequence, grad_kv_rows)
    from_kv = dot_t(grad_kv_rows, kv_own).astype(bf16)
    if fused:
        slot_share = t_dot(attn_tokens, normed_back)
        kv_share = jnp.sum(from_kv.astype(f32) * normed_sequence.astype(f32), 0) / gain_one
        gain_parts = jnp.stack([jnp.sum(slot_share * unit_one, 0) + kv_share, grad_gain_two], 0)
        gain_parts = gain_parts.reshape(2, n_ep, n_ws, -1).transpose(1, 2, 0, 3)
        piece, from_kv, gain_shards, grad_query = run_jobs(
            [
                reduce_weights_job(
                    grad_kv.astype(bf16), from_kv.reshape(2, n_ws, local_tokens, width), n_ep
                ),
                reduce_gains_job(gain_parts.reshape(n_ep, n_ws, 1, -1)),
            ],
            [grad_job(rows_one, owner_grad_query)],
            9,
            "reduce_weights",
        )
    else:
        back_normed = dot_t(owner_grad_query, w_query[0]).astype(bf16)
        normed_back = combine(back_normed, group, n_ep, n_ws)[0]
        grad_query = t_dot(rows_one, owner_grad_query)
    if fused:
        grad_kv_shard = piece.astype(f32)
    elif plain:
        pieces = grad_kv.reshape(width, n_ep, HEAD_SIZE).transpose(1, 0, 2).astype(bf16)
        piece = lax.psum_scatter(pieces, "ep", scatter_dimension=0, tiled=False)
        grad_kv_shard = lax.ppermute(piece, ("ep", "ws"), [(b, a) for a, b in there]).astype(f32)
    else:
        mask = (jnp.arange(n_ws) == place)[None, None, :, None]
        pieces = jnp.where(mask, grad_kv.reshape(width, 2 * group, 1, part), 0.0)
        pieces = pieces.reshape(width, 2 * key_value_width).astype(bf16)
        grad_kv_shard = lax.psum_scatter(
            pieces, ("ep", "ws"), scatter_dimension=1, tiled=True
        ).astype(f32)
    if not fused:
        from_kv = lax.psum_scatter(from_kv, "ws", scatter_dimension=0, tiled=True)
    grad_normed = t_dot(attn_tokens, normed_back) + from_kv.astype(f32)
    grad_input_norm, grad_gain_one = norm_back(grad_normed, unit_one, inverse_one, gain_one)
    grad_input = grad_hidden + grad_input_norm
    if fused:
        gain_shards = gain_shards.reshape(2, -1)
    else:
        gain_shards = lax.psum_scatter(
            jnp.stack([grad_gain_one, grad_gain_two], 0),
            ("ep", "ws"),
            scatter_dimension=1,
            tiled=True,
        )
    return (
        result.astype(bf16),
        grad_input,
        gain_shards[0],
        gain_shards[1],
        grad_kv_shard,
        grad_query[None],
        grad_output[None],
        grad_first[None],
        grad_second[None],
    )


def solution(mesh):
    both = ("ep", "ws")
    rows, vector, columns = P(both, None), P(both), P(None, both)
    return jax.shard_map(
        local,
        mesh=mesh,
        in_specs=(
            rows,
            vector,
            vector,
            columns,
            P("ep", None, "ws"),
            P("ep", "ws", None),
            P("ep", None, None, "ws"),
            P("ep", "ws", None),
            rows,
            rows,
            rows,
            rows,
            rows,
            rows,
            rows,
        ),
        out_specs=(
            rows,
            rows,
            vector,
            vector,
            columns,
            P("ep", None, "ws"),
            P("ep", "ws", None),
            P("ep", None, None, "ws"),
            P("ep", "ws", None),
        ),
        check_vma=False,
    )
```

```python
import functools

import jax
import jax.numpy as jnp
from jax import lax
from jax.experimental import pallas as pl
from jax.experimental.pallas import tpu as pltpu
from jax.sharding import PartitionSpec as P

KEY_VALUE_HEADS = 16
HEAD_SIZE = 128
MIXTURE_EXPERTS = 8
CHOSEN_EXPERTS = 2
BLOCK = 256
CAP = 36
ROWS = 40

EPS = 1e-06
very_negative = -1e30
f32 = jnp.float32
bf16 = jnp.bfloat16
MESH = pl.DeviceIdType.MESH
ANY = pl.BlockSpec(memory_space=pl.ANY)
VM = pl.BlockSpec(memory_space=pltpu.VMEM)
DMA = pltpu.SemaphoreType.DMA
STEP = 256
VMEM_LIMIT = 60 << 20


def dot(a, b):
    return jnp.dot(a, b, preferred_element_type=f32)


def dot_t(a, b):
    return lax.dot_general(a, b, (((1,), (1,)), ((), ())), preferred_element_type=f32)


def t_dot(a, b):
    return lax.dot_general(a, b, (((0,), (0,)), ((), ())), preferred_element_type=f32)


def flip(index, bits):
    out, bit = index, 1
    while bit <= bits:
        if bits & bit:
            out = out + bit - 2 * bit * ((index // bit) % 2)
        bit *= 2
    return out


def far_first(n):
    return sorted(range(1, n), key=lambda k: (-((k // 2).bit_length()), k))


def crossed():
    e, w, n_ws = lax.axis_index("ep"), lax.axis_index("ws"), lax.axis_size("ws")
    return (w + n_ws * (e // n_ws), e % n_ws), e % n_ws != w


def greet(partners, crossing=False):
    barrier = pltpu.get_barrier_semaphore()
    for partner in partners:
        pl.semaphore_signal(barrier, inc=1, device_id=partner, device_id_type=MESH)
    if crossing:
        partner, another = crossed()

        @pl.when(another)
        def _():
            pl.semaphore_signal(barrier, inc=1, device_id=partner, device_id_type=MESH)
            pl.semaphore_wait(barrier, len(partners) + 1)

        @pl.when(jnp.logical_not(another))
        def _():
            pl.semaphore_wait(barrier, len(partners))

    else:
        pl.semaphore_wait(barrier, len(partners))


def remote(src, dst, send, recv, device):
    return pltpu.make_async_remote_copy(
        src_ref=src, dst_ref=dst, send_sem=send, recv_sem=recv, device_id=device, device_id_type=MESH
    )


class Job:
    def __init__(self, args, outs, scratch, steps, body, partners=(), crossing=False):
        self.args, self.outs, self.scratch, self.steps, self.body = args, outs, scratch, steps, body
        self.partners, self.crossing = partners, crossing


def run_jobs(jobs, fills, collective_id, name):
    whole = jobs + fills
    args = [a for job in whole for a in job.args]
    outs = [o for job in whole for o in job.outs]
    scratch = [x for job in whole for x in job.scratch]
    turns = sorted((k / job.steps, i) for i, job in enumerate(jobs) for k in range(job.steps))
    partners = sorted({p for job in jobs for p in job.partners})
    crossing = any(job.crossing for job in jobs)

    def kernel(*refs):
        bodies, at = [], [0, len(args), len(args) + len(outs)]
        for job in whole:
            own = []
            for k, part in enumerate((job.args, job.outs, job.scratch)):
                own.append(refs[at[k] : at[k] + len(part)])
                at[k] += len(part)
            bodies.append(job.body(*own[0], *own[1], *own[2]))
        moves, work = bodies[: len(jobs)], bodies[len(jobs) :]
        queue = [g for g, job in zip(work, fills) for _ in range(job.steps)]
        for g in work:
            next(g)
        e, w = lax.axis_index("ep"), lax.axis_index("ws")
        greet([(flip(e, p), flip(w, q)) for p, q in partners], crossing)
        done = 0
        for k, (_, i) in enumerate(turns):
            next(moves[i])
            target = (k + 1) * len(queue) // len(turns)
            while done < target:
                next(queue[done])
                done += 1
        for g in moves + work:
            for _ in g:
                pass

    return pl.pallas_call(
        kernel,
        out_shape=outs,
        in_specs=[ANY] * len(args),
        out_specs=[ANY] * len(outs),
        scratch_shapes=scratch,
        compiler_params=pltpu.CompilerParams(
            collective_id=collective_id, has_side_effects=True, vmem_limit_bytes=VMEM_LIMIT
        ),
        name=name,
    )(*args)


def fetch(pairs, sem):
    copies = [
        pltpu.make_async_copy(src, dst, sem.at[i]) for i, (src, dst) in enumerate(pairs)
    ]
    for copy in copies:
        copy.start()
    return copies


def blocks_of(size):
    return [(start, min(STEP, size - start)) for start in range(0, size, STEP)]


def column_tiles(width, tile):
    def body(c, carry):
        tile(pl.multiple_of(c * STEP, STEP), STEP)
        return carry

    lax.fori_loop(0, width // STEP, body, 0)
    if width % STEP:
        tile(width // STEP * STEP, width % STEP)


def grad_job(a, b):
    depth, rows = a.shape
    width = b.shape[1]

    def body(a_hbm, b_hbm, out, a_ref, b_ref, turned, held, load_sem, sem):
        loads = fetch(((a_hbm, a_ref), (b_hbm, b_ref)), load_sem)
        yield
        for load in loads:
            load.wait()
        copies = []
        for i, (start, size) in enumerate(blocks_of(rows)):
            if i >= 2:
                copies[i - 2].wait()
            turned[:size] = a_ref[:, start : start + size].T

            def tile(at, columns, slot=i % 2, size=size):
                held[slot, :size, pl.ds(at, columns)] = jnp.dot(
                    turned[:size], b_ref[:, pl.ds(at, columns)], preferred_element_type=f32
                )

            column_tiles(width, tile)
            copies.append(
                pltpu.make_async_copy(
                    held.at[i % 2, pl.ds(0, size)], out.at[pl.ds(start, size)], sem.at[i % 2]
                )
            )
            copies[i].start()
            yield
        for copy in copies[-2:]:
            copy.wait()

    return Job(
        [a, b],
        [jax.ShapeDtypeStruct((rows, width), f32)],
        [
            pltpu.VMEM(a.shape, bf16),
            pltpu.VMEM(b.shape, bf16),
            pltpu.VMEM((STEP, depth), bf16),
            pltpu.VMEM((2, STEP, width), f32),
            DMA((2,)),
            DMA((2,)),
        ],
        len(blocks_of(rows)),
        body,
    )


def pair_grad_job(a, first, second):
    depth, rows = a.shape
    tiles = first.shape[1] // 128

    def body(a_hbm, f_hbm, s_hbm, out, a_ref, f_ref, s_ref, turned, held, load_sem, sem):
        loads = fetch(((a_hbm, a_ref), (f_hbm, f_ref), (s_hbm, s_ref)), load_sem)
        flat = held.reshape(2 * tiles * STEP * 2, 128)
        yield
        for load in loads:
            load.wait()
        copies = []
        for i, (start, size) in enumerate(blocks_of(rows)):
            if i >= 2:
                for copy in copies[i - 2]:
                    copy.wait()
            turned[:size] = a_ref[:, start : start + size].T

            def tile(at, columns, slot=i % 2, size=size):
                for j, b_ref in enumerate((f_ref, s_ref)):
                    r = jnp.dot(
                        turned[:size], b_ref[:, pl.ds(at, columns)], preferred_element_type=f32
                    )
                    for half in range(columns // 128):
                        base = (slot * tiles + at // 128 + half) * (2 * STEP) + j
                        flat[pl.ds(base, size, stride=2), :] = r[:, half * 128 : half * 128 + 128]

            column_tiles(tiles * 128, tile)
            copies.append(
                [
                    pltpu.make_async_copy(
                        held.at[i % 2, c, pl.ds(0, size)],
                        out.at[pl.ds(start, size), :, pl.ds(c * 128, 128)],
                        sem.at[i % 2, c],
                    )
                    for c in range(tiles)
                ]
            )
            for copy in copies[i]:
                copy.start()
            yield
        for copy in copies[-2] + copies[-1]:
            copy.wait()

    return Job(
        [a, first, second],
        [jax.ShapeDtypeStruct((rows, 2, tiles * 128), f32)],
        [
            pltpu.VMEM(a.shape, bf16),
            pltpu.VMEM(first.shape, bf16),
            pltpu.VMEM(second.shape, bf16),
            pltpu.VMEM((STEP, depth), bf16),
            pltpu.VMEM((2, tiles, STEP, 2, 128), f32),
            DMA((3,)),
            DMA((2, tiles)),
        ],
        len(blocks_of(rows)),
        body,
    )


def split_job(weight):
    rows, _, width = weight.shape

    def body(w_hbm, first, second, block, wide, held, load_sem, sem):
        flat = wide.reshape(2 * STEP, 128)
        steps = rows // STEP

        def load(i):
            return pltpu.make_async_copy(
                w_hbm.at[pl.ds(i * STEP, STEP)], block.at[i % 2], load_sem.at[i % 2]
            )

        load(0).start()
        yield
        copies = []
        for i in range(steps):
            slot = i % 2
            if i + 1 < steps:
                load(i + 1).start()
            load(i).wait()
            if i >= 2:
                for copy in copies[i - 2]:
                    copy.wait()

            def tile(c, carry, slot=slot):
                at = pl.ds(pl.multiple_of(c * 128, 128), 128)
                wide[...] = block[slot, :, :, at].astype(f32)
                for j in range(2):
                    held[slot, j, :, at] = flat[pl.ds(j, STEP, stride=2), :].astype(bf16)
                return carry

            lax.fori_loop(0, width // 128, tile, 0)
            copies.append(
                [
                    pltpu.make_async_copy(
                        held.at[slot, j], out.at[pl.ds(i * STEP, STEP)], sem.at[slot, j]
                    )
                    for j, out in enumerate((first, second))
                ]
            )
            for copy in copies[i]:
                copy.start()
            yield
        for copy in copies[-2] + copies[-1]:
            copy.wait()

    return Job(
        [weight],
        [jax.ShapeDtypeStruct((rows, width), bf16)] * 2,
        [
            pltpu.VMEM((2, STEP, 2, width), bf16),
            pltpu.VMEM((STEP, 2, 128), f32),
            pltpu.VMEM((2, 2, STEP, width), bf16),
            DMA((2,)),
            DMA((2, 2)),
        ],
        rows // STEP,
        body,
    )


def ffn_job(x, gate_weight, up_weight, down_weight):
    rows, width = x.shape
    hidden = gate_weight.shape[1]

    def body(
        x_hbm, g_hbm, u_hbm, d_hbm, gate_out, up_out, act_out, out, x_ref, g_ref, u_ref, d_ref, pre, act, res,
        load_sem, sem
    ):
        loads = fetch(((x_hbm, x_ref), (g_hbm, g_ref), (u_hbm, u_ref), (d_hbm, d_ref)), load_sem)
        yield
        for load in loads[:3]:
            load.wait()
        copies = []
        for i, (start, size) in enumerate(blocks_of(rows)):
            slot = i % 2
            here = pl.ds(start, size)
            if i >= 2:
                for copy in copies[i - 2]:
                    copy.wait()

            def tile(at, columns, slot=slot, start=start, size=size):
                part = pl.ds(at, columns)
                left = x_ref[start : start + size]
                gate = dot(left, g_ref[:, part])
                up = dot(left, u_ref[:, part])
                pre[slot, 0, :, part] = gate
                pre[slot, 1, :, part] = up
                act[slot, :, part] = (gate * jax.nn.sigmoid(gate) * up).astype(bf16)

            column_tiles(hidden, tile)
            yield
            if i == 0:
                loads[3].wait()

            def last(at, columns, slot=slot):
                part = pl.ds(at, columns)
                res[slot, :, part] = dot(act[slot], d_ref[:, part]).astype(bf16)

            column_tiles(width, last)
            copies.append(
                [
                    pltpu.make_async_copy(src.at[slot], dst.at[here], sem.at[slot, k])
                    for k, (src, dst) in enumerate(((act, act_out), (res, out)))
                ]
                + [
                    pltpu.make_async_copy(pre.at[slot, k], dst.at[here], sem.at[slot, 2 + k])
                    for k, dst in enumerate((gate_out, up_out))
                ]
            )
            for copy in copies[i]:
                copy.start()
            yield
        for copy in copies[-2] + copies[-1]:
            copy.wait()

    return Job(
        [x, gate_weight, up_weight, down_weight],
        [jax.ShapeDtypeStruct((rows, hidden), f32)] * 2
        + [jax.ShapeDtypeStruct((rows, hidden), bf16), jax.ShapeDtypeStruct((rows, width), bf16)],
        [
            pltpu.VMEM(x.shape, bf16),
            pltpu.VMEM(gate_weight.shape, bf16),
            pltpu.VMEM(up_weight.shape, bf16),
            pltpu.VMEM(down_weight.shape, bf16),
            pltpu.VMEM((2, 2, STEP, hidden), f32),
            pltpu.VMEM((2, STEP, hidden), bf16),
            pltpu.VMEM((2, STEP, width), bf16),
            DMA((4,)),
            DMA((2, 4)),
        ],
        2 * (rows // STEP),
        body,
    )


def ffn_plain(x, gate_weight, up_weight, down_weight):
    gate_pre, up_pre = dot(x, gate_weight), dot(x, up_weight)
    activated = (gate_pre * jax.nn.sigmoid(gate_pre) * up_pre).astype(bf16)
    return gate_pre, up_pre, activated, dot(activated, down_weight).astype(bf16)


def before_activation(grad_act, gate_pre, up_pre):
    sigmoid_gate = jax.nn.sigmoid(gate_pre)
    grad_up = (grad_act * gate_pre * sigmoid_gate).astype(bf16)
    grad_gate = (
        grad_act * up_pre * sigmoid_gate * (1.0 + gate_pre * (1.0 - sigmoid_gate))
    ).astype(bf16)
    return grad_gate, grad_up


def ffn_back_job(grad, gate_pre, up_pre, gate_weight, up_weight, down_weight):
    rows, width = grad.shape
    hidden = gate_weight.shape[1]

    def body(
        x_hbm, gp_hbm, up_hbm, g_hbm, u_hbm, d_hbm, gate_out, up_out, out, x_ref, g_ref, u_ref, d_ref, pre, hid,
        res, load_sem, pre_sem, sem
    ):
        loads = fetch(((x_hbm, x_ref), (d_hbm, d_ref), (g_hbm, g_ref), (u_hbm, u_ref)), load_sem)

        def load_pre(i):
            here = pl.ds(i * STEP, STEP)
            return [
                pltpu.make_async_copy(src.at[here], pre.at[i % 2, k], pre_sem.at[i % 2, k])
                for k, src in enumerate((gp_hbm, up_hbm))
            ]

        for copy in load_pre(0):
            copy.start()
        yield
        for load in loads[:2]:
            load.wait()
        copies = []
        steps = rows // STEP
        for i in range(steps):
            slot, start = i % 2, i * STEP
            here = pl.ds(start, STEP)
            if i + 1 < steps:
                for copy in load_pre(i + 1):
                    copy.start()
            for copy in load_pre(i):
                copy.wait()
            if i >= 2:
                for copy in copies[i - 2]:
                    copy.wait()

            def tile(at, columns, slot=slot, start=start):
                part = pl.ds(at, columns)
                grad_act = dot_t(x_ref[start : start + STEP], d_ref[part, :])
                pair = before_activation(grad_act, pre[slot, 0, :, part], pre[slot, 1, :, part])
                hid[slot, 0, :, part], hid[slot, 1, :, part] = pair

            column_tiles(hidden, tile)
            yield
            if i == 0:
                for load in loads[2:]:
                    load.wait()

            def last(at, columns, slot=slot):
                part = pl.ds(at, columns)
                total = dot_t(hid[slot, 0], g_ref[part, :]) + dot_t(hid[slot, 1], u_ref[part, :])
                res[slot, :, part] = total.astype(bf16)

            column_tiles(width, last)
            copies.append(
                [pltpu.make_async_copy(res.at[slot], out.at[here], sem.at[slot, 2])]
                + [
                    pltpu.make_async_copy(hid.at[slot, k], dst.at[here], sem.at[slot, k])
                    for k, dst in enumerate((gate_out, up_out))
                ]
            )
            for copy in copies[i]:
                copy.start()
            yield
        for copy in copies[-2] + copies[-1]:
            copy.wait()

    return Job(
        [grad, gate_pre, up_pre, gate_weight, up_weight, down_weight],
        [jax.ShapeDtypeStruct((rows, hidden), bf16)] * 2 + [jax.ShapeDtypeStruct((rows, width), bf16)],
        [
            pltpu.VMEM(grad.shape, bf16),
            pltpu.VMEM(gate_weight.shape, bf16),
            pltpu.VMEM(up_weight.shape, bf16),
            pltpu.VMEM(down_weight.shape, bf16),
            pltpu.VMEM((2, 2, STEP, hidden), f32),
            pltpu.VMEM((2, 2, STEP, hidden), bf16),
            pltpu.VMEM((2, STEP, width), bf16),
            DMA((4,)),
            DMA((2, 2)),
            DMA((2, 3)),
        ],
        2 * (rows // STEP),
        body,
    )


def ffn_back_plain(grad, gate_pre, up_pre, gate_weight, up_weight, down_weight):
    grad_gate, grad_up = before_activation(dot_t(grad, down_weight), gate_pre, up_pre)
    back = dot_t(grad_gate, gate_weight) + dot_t(grad_up, up_weight)
    return grad_gate, grad_up, back.astype(bf16)


def dispatch_job(rows, n_ws):
    n, count, width = rows.shape

    def body(rows, out, own, load_sem, ep_s, ep_r, y_s, y_r, c_s, c_r, x_s, x_r):
        e, w = lax.axis_index("ep"), lax.axis_index("ws")
        twin, other = flip(w, 1), flip(w, 2)
        sources = [e] + [flip(e, k) for k in range(1, n)]
        first = []
        for i, s in enumerate(sources[1:]):
            first.append(remote(rows.at[s], out.at[e, w], ep_s.at[i], ep_r.at[i], (s, w)))
            first[-1].start()
        load = pltpu.make_async_copy(rows.at[e], own, load_sem.at[0])
        load.start()
        over_y, to_twin, relayed = [], [], []

        def relay(j):
            over_y[j].wait_recv()
            block = out.at[sources[j], other]
            relayed.append(remote(block, block, x_s.at[j], x_r.at[j], (e, twin)))
            relayed[-1].start()

        for j, s in enumerate(sources):
            place = out.at[s, w]
            block = rows.at[e] if j == 0 else place
            if j:
                first[j - 1].wait_recv()
            over_y.append(remote(block, place, y_s.at[j], y_r.at[j], (e, other)))
            over_y[-1].start()
            to_twin.append(remote(block, place, c_s.at[j], c_r.at[j], (e, twin)))
            to_twin[-1].start()
            if j == 0:
                load.wait()
                store = pltpu.make_async_copy(own, out.at[e, w], load_sem.at[1])
                store.start()
            else:
                relay(j - 1)
            yield
        relay(n - 1)
        store.wait()
        for copy in first + over_y:
            copy.wait_send()
        for copy in to_twin + relayed:
            copy.wait()

    return Job(
        [rows],
        [jax.ShapeDtypeStruct((n, n_ws, count, width), rows.dtype)],
        [pltpu.VMEM((count, width), rows.dtype), DMA((2,)), DMA((n - 1,)), DMA((n - 1,))]
        + [DMA((n,)) for _ in range(6)],
        n,
        body,
        [(k, 0) for k in range(1, n)] + [(0, 1), (0, 2)],
    )


def combine_job(part):
    n, _, count, width = part.shape
    block = (n, count, width)

    def body(
        part, out, mine, core, sum_y, from_y, total, load_sem, c_s, c_r, y_s, y_r, ep_s, ep_r, own_sem
    ):
        e, w = lax.axis_index("ep"), lax.axis_index("ws")
        twin, other, last = flip(w, 1), flip(w, 2), flip(w, 3)
        targets = [flip(e, k) for k in far_first(n)] + [e]
        loads, cores = {}, {}
        for half, near, far in ((1, other, last), (0, w, twin)):
            for j, s in enumerate(targets):
                cores[half, j] = remote(
                    part.at[s, far], core.at[half, j], c_s.at[half, j], c_r.at[half, j], (e, twin)
                )
                cores[half, j].start()
                loads[half, j] = pltpu.make_async_copy(
                    part.at[s, near], mine.at[half, j], load_sem.at[half, j]
                )
                loads[half, j].start()
        over_y, back = [], []

        def send_y(j):
            over_y.append(remote(sum_y.at[j], from_y.at[j], y_s.at[j], y_r.at[j], (e, other)))
            over_y[-1].start()

        def send_back(j):
            back.append(remote(total.at[j], out.at[e], ep_s.at[j], ep_r.at[j], (targets[j], w)))
            back[-1].start()

        for j in range(n):
            loads[1, j].wait()
            cores[1, j].wait_recv()
            sum_y[j] = (mine[1, j].astype(f32) + core[1, j].astype(f32)).astype(bf16)
            if j:
                send_y(j - 1)
        loads[0, 0].wait()
        cores[0, 0].wait_recv()
        send_y(n - 1)
        for j in range(n):
            if j:
                loads[0, j].wait()
                cores[0, j].wait_recv()
            over_y[j].wait_recv()
            total[j] = (
                mine[0, j].astype(f32) + core[0, j].astype(f32) + from_y[j].astype(f32)
            ).astype(bf16)
            if j:
                send_back(j - 1)
            yield
        for copy in over_y + list(cores.values()):
            copy.wait_send()
        keep = pltpu.make_async_copy(total.at[n - 1], out.at[e], own_sem)
        keep.start()
        for copy in back:
            copy.wait()
        keep.wait()

    return Job(
        [part],
        [jax.ShapeDtypeStruct(block, part.dtype)],
        [
            pltpu.VMEM((2,) + block, part.dtype),
            pltpu.VMEM((2,) + block, part.dtype),
            pltpu.VMEM(block, part.dtype),
            pltpu.VMEM(block, part.dtype),
            pltpu.VMEM(block, part.dtype),
            DMA((2, n)),
            DMA((2, n)),
            DMA((2, n)),
            DMA((n,)),
            DMA((n,)),
            DMA((n - 1,)),
            DMA((n - 1,)),
            DMA,
        ],
        n,
        body,
        [(k, 0) for k in range(1, n)] + [(0, 1), (0, 2)],
    )


def exchange_job(rows):
    n = rows.shape[0]

    def body(rows, out, own, load_sem, ep_s, ep_r):
        e, w = lax.axis_index("ep"), lax.axis_index("ws")
        targets = [flip(e, k) for k in far_first(n)]
        copies = []
        for i, s in enumerate(targets):
            copies.append(remote(rows.at[s], out.at[e], ep_s.at[i], ep_r.at[i], (s, w)))
            copies[-1].start()
        load = pltpu.make_async_copy(rows.at[e], own, load_sem.at[0])
        load.start()
        load.wait()
        store = pltpu.make_async_copy(own, out.at[e], load_sem.at[1])
        store.start()
        yield
        store.wait()
        for copy in copies:
            copy.wait()

    return Job(
        [rows],
        [jax.ShapeDtypeStruct(rows.shape, rows.dtype)],
        [pltpu.VMEM(rows.shape[1:], rows.dtype), DMA((2,)), DMA((n - 1,)), DMA((n - 1,))],
        1,
        body,
        [(k, 0) for k in range(1, n)],
    )


def exchange_combine_job(rows, weight, product, n_ws):
    n, held, depth = rows.shape
    count, width = held // n_ws, max(weight.shape)
    block = (n, count, width)
    turned = weight.shape[0] == width

    def body(
        rows, w_hbm, moved, out, w_ref, here, part, core, sum_y, from_y, total, load_sem, ep_s, ep_r, c_s, c_r,
        y_s, y_r, b_s, b_r
    ):
        e, w = lax.axis_index("ep"), lax.axis_index("ws")
        twin, other, last = flip(w, 1), flip(w, 2), flip(w, 3)
        places = [e] + [flip(e, k) for k in range(1, n)]
        weights = pltpu.make_async_copy(w_hbm, w_ref, load_sem.at[n])
        weights.start()
        arrivals = []
        for i, s in enumerate(places[1:]):
            arrivals.append(remote(rows.at[s], moved.at[e], ep_s.at[i], ep_r.at[i], (s, w)))
            arrivals[i].start()
        cores, over_y, back, stores = {}, [], [], []

        def multiply(j):
            if j:
                arrivals[j - 1].wait_recv()
            src = moved.at[places[j]] if j else rows.at[e]
            load = pltpu.make_async_copy(src, here.at[j], load_sem.at[j])
            load.start()
            load.wait()
            if j == 0:
                stores.append(pltpu.make_async_copy(here.at[0], moved.at[e], load_sem.at[0]))
                stores[0].start()
                weights.wait()

            def tile(at, columns):
                tall = pl.ds(at, columns)
                result = product(here[j], w_ref[tall, :] if turned else w_ref[:, tall])
                part[j, :, :, tall] = result.reshape(n_ws, count, columns).astype(bf16)

            column_tiles(width, tile)

        def send_core(j):
            for half, to in ((1, last), (0, twin)):
                cores[half, j] = remote(
                    part.at[j, to], core.at[half, j], c_s.at[half, j], c_r.at[half, j], (e, twin)
                )
                cores[half, j].start()

        def add_core(j):
            cores[1, j].wait_recv()
            sum_y[j] = (part[j, other].astype(f32) + core[1, j].astype(f32)).astype(bf16)

        def send_y(j):
            over_y.append(remote(sum_y.at[j], from_y.at[j], y_s.at[j], y_r.at[j], (e, other)))
            over_y[j].start()

        def add_all(j):
            cores[0, j].wait_recv()
            over_y[j].wait_recv()
            total[j] = (
                part[j, w].astype(f32) + core[0, j].astype(f32) + from_y[j].astype(f32)
            ).astype(bf16)

        def send_back(j):
            if j:
                back.append(
                    remote(total.at[j], out.at[e], b_s.at[j - 1], b_r.at[j - 1], (places[j], w))
                )
                back[j - 1].start()
            else:
                stores.append(pltpu.make_async_copy(total.at[0], out.at[e], load_sem.at[1]))
                stores[1].start()

        for t in range(n + 4):
            for lag, stage in ((0, multiply), (1, add_core), (3, add_all), (0, send_core), (1, send_y), (4, send_back)):
                if 0 <= t - lag < n:
                    stage(t - lag)
            yield
        for copy in arrivals + list(cores.values()) + over_y:
            copy.wait_send()
        for copy in back + stores:
            copy.wait()

    return Job(
        [rows, weight],
        [jax.ShapeDtypeStruct(rows.shape, bf16), jax.ShapeDtypeStruct(block, bf16)],
        [
            pltpu.VMEM(weight.shape, bf16),
            pltpu.VMEM(rows.shape, bf16),
            pltpu.VMEM((n, n_ws, count, width), bf16),
            pltpu.VMEM((2,) + block, bf16),
            pltpu.VMEM(block, bf16),
            pltpu.VMEM(block, bf16),
            pltpu.VMEM(block, bf16),
            DMA((n + 1,)),
            DMA((n - 1,)),
            DMA((n - 1,)),
            DMA((2, n)),
            DMA((2, n)),
            DMA((n,)),
            DMA((n,)),
            DMA((n - 1,)),
            DMA((n - 1,)),
        ],
        n + 4,
        body,
        [(k, 0) for k in range(1, n)] + [(0, 1), (0, 2)],
    )


def dispatch_exchange_job(rows, weight, product, n_ws):
    n, count, width = rows.shape
    turned = weight.shape[1] == width
    narrow = weight.shape[0] if turned else weight.shape[1]

    def body(
        rows, w_hbm, out, moved, w_ref, own, here, flat, res, load_sem, ep_s, ep_r, y_s, y_r, c_s, c_r, x_s, x_r,
        b_s, b_r
    ):
        e, w = lax.axis_index("ep"), lax.axis_index("ws")
        twin, other = flip(w, 1), flip(w, 2)
        places = [e] + [flip(e, k) for k in range(1, n)]
        weights = pltpu.make_async_copy(w_hbm, w_ref, load_sem.at[2])
        weights.start()
        first, over_y, to_twin, relayed, back, stores = [], [], [], [], [], []
        for i, s in enumerate(places[1:]):
            first.append(remote(rows.at[s], out.at[e, w], ep_s.at[i], ep_r.at[i], (s, w)))
            first[i].start()
        load = pltpu.make_async_copy(rows.at[e], own, load_sem.at[0])
        load.start()

        def arrive(j):
            place = out.at[places[j], w]
            block = place if j else rows.at[e]
            if j:
                first[j - 1].wait_recv()
            over_y.append(remote(block, place, y_s.at[j], y_r.at[j], (e, other)))
            over_y[j].start()
            to_twin.append(remote(block, place, c_s.at[j], c_r.at[j], (e, twin)))
            to_twin[j].start()
            if j == 0:
                load.wait()
                stores.append(pltpu.make_async_copy(own, place, load_sem.at[1]))
                stores[0].start()

        def relay(j):
            over_y[j].wait_recv()
            block = out.at[places[j], other]
            relayed.append(remote(block, block, x_s.at[j], x_r.at[j], (e, twin)))
            relayed[j].start()

        def multiply(j):
            to_twin[j].wait_recv()
            relayed[j].wait_recv()
            if j == 0:
                stores[0].wait()
                weights.wait()
            source = pltpu.make_async_copy(out.at[places[j]], here, load_sem.at[0])
            source.start()
            source.wait()
            flat[...] = here[...].astype(f32).reshape(n_ws * count, width).astype(bf16)

            def tile(at, columns):
                tall = pl.ds(at, columns)
                part = product(flat[...], w_ref[tall, :] if turned else w_ref[:, tall])
                res[j, :, tall] = part.astype(bf16)

            column_tiles(narrow, tile)

        def send(j):
            if j:
                back.append(
                    remote(res.at[j], moved.at[e], b_s.at[j - 1], b_r.at[j - 1], (places[j], w))
                )
                back[j - 1].start()
            else:
                stores.append(pltpu.make_async_copy(res.at[0], moved.at[e], load_sem.at[1]))
                stores[1].start()

        for t in range(n + 3):
            for lag, stage in enumerate((arrive, relay, multiply, send)):
                if 0 <= t - lag < n:
                    stage(t - lag)
            yield
        for copy in first + over_y + to_twin + relayed:
            copy.wait_send()
        for copy in back + stores[1:]:
            copy.wait()

    return Job(
        [rows, weight],
        [
            jax.ShapeDtypeStruct((n, n_ws, count, width), bf16),
            jax.ShapeDtypeStruct((n, n_ws * count, narrow), bf16),
        ],
        [
            pltpu.VMEM(weight.shape, bf16),
            pltpu.VMEM((count, width), bf16),
            pltpu.VMEM((n_ws, count, width), bf16),
            pltpu.VMEM((n_ws * count, width), bf16),
            pltpu.VMEM((n, n_ws * count, narrow), bf16),
            DMA((3,)),
            DMA((n - 1,)),
            DMA((n - 1,)),
        ]
        + [DMA((n,)) for _ in range(6)]
        + [DMA((n - 1,)), DMA((n - 1,))],
        n + 3,
        body,
        [(k, 0) for k in range(1, n)] + [(0, 1), (0, 2)],
    )


def gather_weights_job(mine, normed, n, n_ws):
    rows, block = mine.shape
    routes = [(4, 0), (2, 0), (2, 4)]

    def body(
        mine, normed, out, seq, held, held_rows, load_sem, s_sem, r_sem, x_s, x_r, y_s, y_r, c_s, c_r, t_s, t_r
    ):
        e, w = lax.axis_index("ep"), lax.axis_index("ws")
        twin, other, near = flip(w, 1), flip(w, 2), flip(e, 1)
        copies = {}

        def send(hop, offset, half):
            k = routes.index((hop, offset))
            part = pl.ds(half * (rows // 2), rows // 2)
            at = pl.multiple_of(flip(e, offset) // 2 * block, block)
            place = out.at[part, pl.ds(at, block)]
            copies[hop, offset, half] = remote(
                place if offset else mine.at[part],
                place,
                s_sem.at[k, half],
                r_sem.at[k, half],
                (flip(e, hop), w),
            )
            copies[hop, offset, half].start()

        for half in range(2):
            for route in routes[:2]:
                send(*route, half)
        to_near = remote(normed, seq.at[e % 2, w], x_s, x_r, (near, w))
        to_near.start()
        over_y, to_twin, relays = [], [], []

        def spread_rows(k, half, src):
            place = seq.at[half, w]
            over_y.append(remote(src, place, y_s.at[k], y_r.at[k], (e, other)))
            over_y[k].start()
            to_twin.append(remote(src, place, c_s.at[k], c_r.at[k], (e, twin)))
            to_twin[k].start()

        def relay(k, half):
            over_y[k].wait_recv()
            place = seq.at[half, other]
            relays.append(remote(place, place, t_s.at[k], t_r.at[k], (e, twin)))
            relays[k].start()

        spread_rows(0, e % 2, normed)
        loads = fetch(((mine, held), (normed, held_rows)), load_sem)
        for load in loads:
            load.wait()
        own = out.at[:, pl.ds(pl.multiple_of(e // 2 * block, block), block)]
        stores = fetch(((held, own), (held_rows, seq.at[e % 2, w])), load_sem)
        yield
        to_near.wait_recv()
        spread_rows(1, near % 2, seq.at[near % 2, w])
        yield
        copies[4, 0, 0].wait_recv()
        send(2, 4, 0)
        yield
        relay(0, e % 2)
        copies[4, 0, 1].wait_recv()
        send(2, 4, 1)
        yield
        relay(1, near % 2)
        yield
        for store in stores:
            store.wait()
        for (_, offset, half), copy in copies.items():
            copy.wait_send()
            if (_, offset) != (4, 0):
                copy.wait_recv()
        to_near.wait_send()
        for copy in over_y:
            copy.wait_send()
        for copy in to_twin + relays:
            copy.wait()

    return Job(
        [mine, normed],
        [
            jax.ShapeDtypeStruct((rows, n // 2 * block), bf16),
            jax.ShapeDtypeStruct((2, n_ws) + normed.shape, bf16),
        ],
        [
            pltpu.VMEM(mine.shape, bf16),
            pltpu.VMEM(normed.shape, bf16),
            DMA((2,)),
            DMA((3, 2)),
            DMA((3, 2)),
            DMA,
            DMA,
        ]
        + [DMA((2,)) for _ in range(6)],
        5,
        body,
        [(1, 0), (2, 0), (4, 0), (0, 1), (0, 2)],
    )


def swap_job(blocks):
    def body(blocks, out, held, load_sem, s_sem, r_sem):
        e, w = lax.axis_index("ep"), lax.axis_index("ws")
        near = flip(e, 1)
        copy = remote(blocks.at[near % 2], out.at[e % 2], s_sem, r_sem, (near, w))
        copy.start()
        load = fetch(((blocks.at[e % 2], held),), load_sem)[0]
        load.wait()
        store = fetch(((held, out.at[e % 2]),), load_sem)[0]
        yield
        store.wait()
        copy.wait()

    return Job(
        [blocks],
        [jax.ShapeDtypeStruct(blocks.shape, blocks.dtype)],
        [pltpu.VMEM(blocks.shape[1:], blocks.dtype), DMA((1,)), DMA, DMA],
        1,
        body,
        [(1, 0)],
    )


def add_blocks(out, *refs):
    step = 64 if out.shape[1] > 1024 else 256

    def body(i, carry):
        at = pl.ds(pl.multiple_of(i * step, step), step)
        total = refs[0][at].astype(f32)
        for ref in refs[1:]:
            total = total + ref[at].astype(f32)
        out[at] = total.astype(bf16)
        return carry

    lax.fori_loop(0, out.shape[0] // step, body, 0)


def reduce_weights_job(pieces, part, n):
    rows = pieces.shape[0]
    block = pieces.shape[1] // (n // 2)
    offsets = (4, 0)

    def body(
        pieces, part, out, out_rows, mine, from_z, fourth, last_z, total, own, core, sum_y, from_y, total_near,
        from_near, total_rows, load_sem, z_s, z_r, w_load, c_s, c_r, y_s, y_r, x_s, x_r, sem, h_s, h_r
    ):
        e, w = lax.axis_index("ep"), lax.axis_index("ws")
        twin, other, last, near = flip(w, 1), flip(w, 2), flip(w, 3), flip(e, 1)

        def columns(s):
            return pieces.at[:, pl.ds(pl.multiple_of(s // 2 * block, block), block)]

        over_z = []
        for i, offset in enumerate(offsets):
            over_z.append(
                remote(columns(flip(e, offset + 2)), from_z.at[i], z_s.at[i], z_r.at[i], (flip(e, 2), w))
            )
            over_z[i].start()
        halves = (near % 2, e % 2)
        cores = {}
        for k, to in enumerate((last, twin)):
            for h, half in enumerate(halves):
                cores[h, k] = remote(
                    part.at[half, to], core.at[h, k], c_s.at[h, k], c_r.at[h, k], (e, twin)
                )
                cores[h, k].start()
        loads = fetch([(columns(flip(e, o)), mine.at[i]) for i, o in enumerate(offsets)], load_sem)
        own_loads = {}
        for h, half in enumerate(halves):
            for k, to in enumerate((other, w)):
                own_loads[h, k] = pltpu.make_async_copy(
                    part.at[half, to], own.at[h, k], w_load.at[h, k]
                )
                own_loads[h, k].start()
        yield
        over_y = []

        def send_y(h):
            over_y.append(remote(sum_y.at[h], from_y.at[h], y_s.at[h], y_r.at[h], (e, other)))
            over_y[h].start()

        for h in range(2):
            own_loads[h, 0].wait()
            cores[h, 0].wait_recv()
            add_blocks(sum_y.at[h], own.at[h, 0], core.at[h, 0])
            if h:
                send_y(0)
        yield
        loads[0].wait()
        over_z[0].wait_recv()
        send_y(1)
        add_blocks(fourth, mine.at[0], from_z.at[0])
        yield
        own_loads[0, 1].wait()
        cores[0, 1].wait_recv()
        over_y[0].wait_recv()
        far = remote(fourth, last_z, z_s.at[2], z_r.at[2], (flip(e, 4), w))
        far.start()
        add_blocks(total_near, own.at[0, 1], core.at[0, 1], from_y.at[0])
        yield
        own_loads[1, 1].wait()
        cores[1, 1].wait_recv()
        over_y[1].wait_recv()
        to_near = remote(total_near, from_near, x_s, x_r, (near, w))
        to_near.start()
        loads[1].wait()
        over_z[1].wait_recv()
        far.wait_recv()
        add_blocks(total, mine.at[1], from_z.at[1], last_z)
        yield
        partner, another = crossed()
        home = remote(total, out, h_s, h_r, partner)
        keep = pltpu.make_async_copy(total, out, sem.at[1])
        store = pltpu.make_async_copy(total_rows, out_rows, sem.at[0])

        @pl.when(another)
        def _():
            home.start()

        @pl.when(jnp.logical_not(another))
        def _():
            keep.start()

        to_near.wait_recv()
        add_blocks(total_rows, own.at[1, 1], core.at[1, 1], from_y.at[1], from_near)
        store.start()
        for copy in over_z + list(cores.values()) + over_y + [far, to_near]:
            copy.wait_send()
        store.wait()

        @pl.when(another)
        def _():
            home.wait()

        @pl.when(jnp.logical_not(another))
        def _():
            keep.wait()

    one, rows_one = (rows, block), part.shape[2:]
    return Job(
        [pieces, part],
        [jax.ShapeDtypeStruct(one, bf16), jax.ShapeDtypeStruct(rows_one, bf16)],
        [pltpu.VMEM((2,) + one, bf16) for _ in range(2)]
        + [pltpu.VMEM(one, bf16) for _ in range(3)]
        + [pltpu.VMEM((2, 2) + rows_one, bf16) for _ in range(2)]
        + [pltpu.VMEM((2,) + rows_one, bf16) for _ in range(2)]
        + [pltpu.VMEM(rows_one, bf16) for _ in range(3)]
        + [DMA((2,)), DMA((3,)), DMA((3,)), DMA((2, 2)), DMA((2, 2)), DMA((2, 2))]
        + [DMA((2,)), DMA((2,)), DMA, DMA, DMA((2,)), DMA, DMA],
        5,
        body,
        [(1, 0), (2, 0), (4, 0), (0, 1), (0, 2)],
        True,
    )


def attend_kernel(spans, q_ref, kv_ref, out):
    count, _, slots, part = q_ref.shape
    for w, span in enumerate(spans):

        def head(h, carry, w=w, span=span):
            at = pl.multiple_of(h * HEAD_SIZE, HEAD_SIZE)
            columns = pl.ds(at, HEAD_SIZE)
            q, probs, _, values = head_probs(q_ref, kv_ref, w, span, at)
            mixed = dot(probs.astype(bf16), values)
            out[:, w, :, columns] = mixed.reshape(count, slots, HEAD_SIZE).astype(bf16)
            return carry

        lax.fori_loop(0, part // HEAD_SIZE, head, 0)


def slot_rows(ref, w, at):
    count, _, slots, _ = ref.shape
    rows = ref[:, w, :, pl.ds(at, HEAD_SIZE)].astype(f32)
    return rows.reshape(count * slots, HEAD_SIZE).astype(bf16)


def kv_place(kv, at):
    h = at // HEAD_SIZE
    column = pl.multiple_of(h // 2 * HEAD_SIZE, HEAD_SIZE)
    half = kv.shape[2] // 2
    value_column = pl.multiple_of(half + column, HEAD_SIZE)
    return h % 2, pl.ds(column, HEAD_SIZE), pl.ds(value_column, HEAD_SIZE)


def head_probs(q_ref, kv_ref, w, span, at):
    q = slot_rows(q_ref, w, at)
    side, key_columns, value_columns = kv_place(kv_ref, at)
    keys = kv_ref[side, :span, key_columns]
    values = kv_ref[side, :span, value_columns]
    scores = dot_t(q, keys) * HEAD_SIZE ** (-0.5)
    weight = jnp.exp(scores - jnp.max(scores, -1, keepdims=True))
    probs = weight / jnp.sum(weight, -1, keepdims=True)
    return q, probs, keys, values


def attend_call(queries, kv, spans):
    return pl.pallas_call(
        functools.partial(attend_kernel, spans),
        out_shape=jax.ShapeDtypeStruct(queries.shape, bf16),
        in_specs=[VM, VM],
        out_specs=VM,
        compiler_params=pltpu.CompilerParams(vmem_limit_bytes=VMEM_LIMIT),
        name="attend",
    )(queries, kv)


def attend_back_kernel(spans, q_ref, g_ref, kv_ref, grad_q, grad_kv, total):
    count, _, slots, part = q_ref.shape
    total[...] = jnp.zeros_like(total)
    for w, span in enumerate(spans):

        def head(h, carry, w=w, span=span):
            at = pl.multiple_of(h * HEAD_SIZE, HEAD_SIZE)
            columns = pl.ds(at, HEAD_SIZE)
            q, probs, keys, values = head_probs(q_ref, kv_ref, w, span, at)
            grad = slot_rows(g_ref, w, at)
            grad_probs = dot_t(grad, values)
            centred = jnp.sum(probs * grad_probs, -1, keepdims=True)
            grad_scores = (probs * (grad_probs - centred)).astype(bf16)
            grad_rows = dot(grad_scores, keys) * HEAD_SIZE ** (-0.5)
            grad_q[:, w, :, columns] = grad_rows.reshape(count, slots, HEAD_SIZE).astype(bf16)
            side, key_columns, value_columns = kv_place(kv_ref, at)
            total[side, :span, key_columns] += t_dot(grad_scores, q) * HEAD_SIZE ** (-0.5)
            total[side, :span, value_columns] += t_dot(probs.astype(bf16), grad)
            return carry

        lax.fori_loop(0, part // HEAD_SIZE, head, 0)
    grad_kv[...] = total[...].astype(bf16)


def attend_back_call(queries, grads, kv, spans):
    return pl.pallas_call(
        functools.partial(attend_back_kernel, spans),
        out_shape=[
            jax.ShapeDtypeStruct(queries.shape, bf16),
            jax.ShapeDtypeStruct(kv.shape, bf16),
        ],
        in_specs=[VM, VM, VM],
        out_specs=[VM, VM],
        scratch_shapes=[pltpu.VMEM(kv.shape, f32)],
        compiler_params=pltpu.CompilerParams(vmem_limit_bytes=VMEM_LIMIT),
        name="attend_back",
    )(queries, grads, kv)


def gather_gains_job(own, n, n_ws):
    def body(own, out, held, load_sem, w_s, w_r, ep_s, ep_r):
        e, w = lax.axis_index("ep"), lax.axis_index("ws")
        first = []
        for i in range(n_ws - 1):
            place = (e, flip(w, i + 1))
            first.append(remote(own, out.at[e, w], w_s.at[i], w_r.at[i], place))
            first[i].start()
        load = fetch(((own, held),), load_sem)[0]
        load.wait()
        store = fetch(((held, out.at[e, w]),), load_sem)[0]
        yield
        store.wait()
        for copy in first:
            copy.wait()
        second = []
        for i in range(n - 1):
            place = (flip(e, i + 1), w)
            second.append(remote(out.at[e], out.at[e], ep_s.at[i], ep_r.at[i], place))
            second[i].start()
        yield
        for copy in second:
            copy.wait()

    return Job(
        [own],
        [jax.ShapeDtypeStruct((n, n_ws) + own.shape, own.dtype)],
        [
            pltpu.VMEM(own.shape, own.dtype),
            DMA((1,)),
            DMA((n_ws - 1,)),
            DMA((n_ws - 1,)),
            DMA((n - 1,)),
            DMA((n - 1,)),
        ],
        2,
        body,
        [(k, 0) for k in range(1, n)] + [(0, k) for k in range(1, n_ws)],
    )


def reduce_gains_job(parts):
    n, n_ws = parts.shape[:2]

    def body(parts, out, held, every, total, load_sem, w_s, w_r, ep_s, ep_r):
        e, w = lax.axis_index("ep"), lax.axis_index("ws")
        first, second = [], []
        for i in range(n_ws - 1):
            p = flip(w, i + 1)
            first.append(remote(parts.at[:, p], held.at[:, w], w_s.at[i], w_r.at[i], (e, p)))
            first[i].start()
        keep = fetch(((parts.at[:, w], held.at[:, w]),), load_sem)[0]
        yield
        keep.wait()
        for copy in first:
            copy.wait()
        keep = fetch(((held.at[e], every.at[e]),), load_sem)[0]
        for i in range(n - 1):
            p = flip(e, i + 1)
            second.append(remote(held.at[p], every.at[e], ep_s.at[i], ep_r.at[i], (p, w)))
            second[i].start()
        yield
        keep.wait()
        for copy in second:
            copy.wait()
        total[...] = jnp.sum(jnp.sum(every[...], 0), 0)
        store = fetch(((total, out),), load_sem)[0]
        store.wait()

    return Job(
        [parts],
        [jax.ShapeDtypeStruct(parts.shape[2:], parts.dtype)],
        [
            pltpu.VMEM(parts.shape, parts.dtype),
            pltpu.VMEM(parts.shape, parts.dtype),
            pltpu.VMEM(parts.shape[2:], parts.dtype),
            DMA((1,)),
            DMA((n_ws - 1,)),
            DMA((n_ws - 1,)),
            DMA((n - 1,)),
            DMA((n - 1,)),
        ],
        2,
        body,
        [(k, 0) for k in range(1, n)] + [(0, k) for k in range(1, n_ws)],
    )


def small(n_ep):
    return n_ep == MIXTURE_EXPERTS and lax.axis_size("ws") == 4


PLAIN = {
    grad_job: lambda a, b: [t_dot(a, b)],
    pair_grad_job: lambda a, b, c: [jnp.stack([t_dot(a, b), t_dot(a, c)], 1)],
    split_job: lambda weight: [weight[:, 0], weight[:, 1]],
    ffn_job: ffn_plain,
    ffn_back_job: ffn_back_plain,
}


def beside(job, plain, arg, fills, collective_id, name):
    if job is None:
        return [plain(arg)] + [out for make, *rest in fills for out in PLAIN[make](*rest)]
    return run_jobs([job(arg)], [make(*rest) for make, *rest in fills], collective_id, name)


def exchange_plain(send):
    return lax.all_to_all(send, "ep", split_axis=0, concat_axis=0, tiled=True)


def exchange(send, *fills, collective_id=2, name="exchange"):
    job = exchange_job if small(send.shape[0]) else None
    return beside(job, exchange_plain, send, fills, collective_id, name)


def spread(rows, group):
    width = rows.shape[-1]
    blocks = rows.reshape(MIXTURE_EXPERTS, 1, ROWS, width)
    return jnp.broadcast_to(blocks, (MIXTURE_EXPERTS, group, ROWS, width)).reshape(
        MIXTURE_EXPERTS * group, ROWS, width
    )


def dispatch(rows, group, *fills, collective_id=0, name="dispatch"):
    width = rows.shape[-1]

    def plain(blocks):
        return lax.all_gather(exchange_plain(blocks), "ws", axis=1, tiled=False)

    job = functools.partial(dispatch_job, n_ws=4) if small(MIXTURE_EXPERTS * group) else None
    out = beside(job, plain, spread(rows, group), fills, collective_id, name)
    return [out[0].reshape(-1, width)] + list(out[1:])


def combine(partial, group, n_ep, n_ws, *fills, collective_id=1, name="combine"):
    width = partial.shape[-1]

    def plain(part):
        part = part.transpose(1, 0, 2, 3).reshape(n_ws * n_ep * ROWS, width)
        own = lax.psum_scatter(part, "ws", scatter_dimension=0, tiled=True)
        return exchange_plain(own.reshape(n_ep, ROWS, width))

    part = partial.reshape(n_ep, n_ws, ROWS, width)
    job = combine_job if small(n_ep) else None
    back, *rest = beside(job, plain, part, fills, collective_id, name)
    if group > 1:
        back = jnp.sum(back.reshape(MIXTURE_EXPERTS, group, ROWS, width).astype(f32), 1).astype(bf16)
    return [back.reshape(MIXTURE_EXPERTS * ROWS, width)] + rest


def slot_tables(routes, slots):
    target = jnp.where(slots < CAP, routes * ROWS + slots, -1)
    places = lax.broadcasted_iota(jnp.int32, (MIXTURE_EXPERTS * ROWS, target.shape[0]), 0)
    return [(places == target[None, :, k]).astype(bf16) for k in range(CHOSEN_EXPERTS)]


def norm_back(grad, unit, inverse, gain):
    gain_grad = jnp.sum(grad * unit, 0)
    scaled = grad * gain
    return (inverse * (scaled - unit * jnp.mean(scaled * unit, -1, keepdims=True)), gain_grad)


def heads_of(rows):
    return rows.reshape(rows.shape[0], -1, HEAD_SIZE)


def local(
    x_in,
    gain_attn,
    gain_ffn,
    key_value_weight,
    w_query,
    w_output,
    w_in,
    w_out,
    gate_attn,
    gate_ffn,
    route_attn,
    slot_attn,
    route_ffn,
    slot_ffn,
    cotangent,
):
    n_ep = lax.axis_size("ep")
    n_ws = lax.axis_size("ws")
    group = n_ep // MIXTURE_EXPERTS
    local_tokens, width = x_in.shape
    key_value_width = KEY_VALUE_HEADS * HEAD_SIZE
    part = w_query.shape[2]
    own_width = group * part
    sequence = n_ws * local_tokens
    place = lax.axis_index("ws")
    scale = HEAD_SIZE ** (-0.5)

    fused = small(n_ep) and key_value_weight.shape[1] == HEAD_SIZE and gain_attn.shape[0] == 64
    if fused:
        gains = jnp.concatenate([gain_attn, gain_ffn], 0).astype(f32)[None]
        gains = run_jobs([gather_gains_job(gains, n_ep, n_ws)], [], 3, "gather_gains")[0]
        gains = gains.reshape(n_ep * n_ws, 2, -1)
        gain_one, gain_two = gains[:, 0].reshape(-1), gains[:, 1].reshape(-1)
    else:
        gain_one = lax.all_gather(gain_attn, ("ep", "ws"), axis=0, tiled=True).astype(f32)
        gain_two = lax.all_gather(gain_ffn, ("ep", "ws"), axis=0, tiled=True).astype(f32)
    plain = group == 1 and key_value_weight.shape[1] == HEAD_SIZE
    if plain:
        half = n_ep // 2
        there = [
            (e * n_ws + w, (w + n_ws * (e // half)) * n_ws + e % half)
            for e in range(n_ep)
            for w in range(n_ws)
        ]
        mine = lax.ppermute(key_value_weight, ("ep", "ws"), there)
    else:
        whole = lax.all_gather(key_value_weight, ("ep", "ws"), axis=1, tiled=True)
        whole = whole.reshape(width, 2 * group, n_ws, part)
        kv_own = lax.dynamic_index_in_dim(whole, place, 2, keepdims=False).reshape(width, -1)

    inputs = x_in.astype(f32)
    inverse_one = lax.rsqrt(jnp.mean(inputs * inputs, -1, keepdims=True) + EPS)
    unit_one = inputs * inverse_one
    normed = (unit_one * gain_one).astype(bf16)
    attn_pairs = slot_tables(route_attn, slot_attn)
    ffn_pairs = slot_tables(route_ffn, slot_ffn)
    attn_tokens = attn_pairs[0] + attn_pairs[1]
    ffn_tokens = ffn_pairs[0] + ffn_pairs[1]

    slots_one = dot(attn_tokens, normed).astype(bf16)
    if fused:
        rows_one, kv_own, normed_sequence, gate_weight, up_weight = run_jobs(
            [
                dispatch_job(slots_one.reshape(n_ep, ROWS, width), n_ws),
                gather_weights_job(mine, normed, n_ep, n_ws),
            ],
            [split_job(w_in[0])],
            10,
            "dispatch_weights",
        )
        rows_one = rows_one.reshape(-1, width)
        normed_sequence = normed_sequence.reshape(2 * sequence, width)
    else:
        if plain:
            kv_own = lax.all_gather(mine, "ep", axis=1, tiled=True)
        normed_sequence = lax.all_gather(normed, "ws", axis=0, tiled=True)
        rows_one, gate_weight, up_weight = dispatch(slots_one, group, (split_job, w_in[0]))
    kv = dot(normed_sequence, kv_own).astype(bf16)
    if not fused:
        keys = kv[:, :own_width].reshape(sequence, -1, HEAD_SIZE)
        values = kv[:, own_width:].reshape(sequence, -1, HEAD_SIZE)

    owner_query = dot(rows_one, w_query[0]).astype(bf16)
    owner_query = owner_query.reshape(n_ep, n_ws * ROWS, part)
    if fused:
        queries, kv = run_jobs(
            [exchange_job(owner_query), swap_job(kv.reshape(2, sequence, -1))], [], 13, "exchange_kv"
        )
    else:
        queries = exchange(owner_query)[0]
    queries = queries.reshape(MIXTURE_EXPERTS, group, n_ws, ROWS, part)
    spans = [(w * local_tokens // BLOCK + 1) * BLOCK for w in range(n_ws)]

    def by_block(rows):
        rows = rows.reshape(MIXTURE_EXPERTS, group, n_ws, ROWS, part)
        return [
            rows[:, :, w].transpose(0, 2, 1, 3).reshape(-1, own_width // HEAD_SIZE, HEAD_SIZE)
            for w in range(n_ws)
        ]

    def to_experts(pieces):
        rows = jnp.stack(
            [
                piece.reshape(MIXTURE_EXPERTS, ROWS, group, part).transpose(0, 2, 1, 3)
                for piece in pieces
            ],
            2,
        )
        return rows.reshape(n_ep, n_ws * ROWS, part)

    if fused:
        queries = queries.reshape(n_ep, n_ws, ROWS, part)
        mixed = attend_call(queries, kv, spans).reshape(n_ep, n_ws * ROWS, part)
    else:
        kept = []
        mixed_pieces = []
        for q, span in zip(by_block(queries), spans):
            scores = (
                jnp.einsum("rhd,shd->hrs", q, keys[:span], preferred_element_type=f32) * scale
            )
            probs = jax.nn.softmax(scores, axis=-1)
            mixed = jnp.einsum(
                "hrs,shd->rhd", probs.astype(bf16), values[:span], preferred_element_type=f32
            )
            kept.append((q, probs))
            mixed_pieces.append(mixed.astype(bf16))
        mixed = to_experts(mixed_pieces)
    if fused:
        owner_mixed, attn_slots = run_jobs(
            [exchange_combine_job(mixed, w_output[0], dot, n_ws)], [], 11, "exchange_output"
        )
        owner_mixed, attn_slots = owner_mixed.reshape(-1, part), attn_slots.reshape(-1, width)
    else:
        owner_mixed = exchange(mixed)[0].reshape(-1, part)
        output_part = dot(owner_mixed, w_output[0]).astype(bf16)
        attn_slots = combine(output_part, group, n_ep, n_ws)[0]

    def weighted(pairs, gates, slot_values):
        return sum(gates[:, k : k + 1] * t_dot(pairs[k], slot_values) for k in range(2))

    def to_slots(pairs, gates, values):
        return sum(
            dot(pairs[k], (gates[:, k : k + 1] * values).astype(bf16)) for k in range(2)
        ).astype(bf16)

    hidden_state = inputs + weighted(attn_pairs, gate_attn, attn_slots)
    inverse_two = lax.rsqrt(jnp.mean(hidden_state * hidden_state, -1, keepdims=True) + EPS)
    unit_two = hidden_state * inverse_two
    normed_two = (unit_two * gain_two).astype(bf16)

    grad_out = cotangent.astype(f32)
    grad_slots = to_slots(ffn_pairs, gate_ffn, grad_out)
    expert_rows = dispatch(dot(ffn_tokens, normed_two).astype(bf16), group)[0]
    expert_grad, gate_pre, up_pre, activated, forward_part = dispatch(
        grad_slots,
        group,
        (ffn_job, expert_rows, gate_weight, up_weight, w_out[0]),
        collective_id=5,
        name="dispatch_ffn",
    )
    ffn_slots, grad_gate, grad_up, back_two = combine(
        forward_part,
        group,
        n_ep,
        n_ws,
        (ffn_back_job, expert_grad, gate_pre, up_pre, gate_weight, up_weight, w_out[0]),
        collective_id=1,
        name="combine_ffn_back",
    )
    result = hidden_state + weighted(ffn_pairs, gate_ffn, ffn_slots)
    back_slots, grad_second = combine(
        back_two,
        group,
        n_ep,
        n_ws,
        (grad_job, activated, expert_grad),
        collective_id=6,
        name="combine_grad_out",
    )

    grad_normed_two = t_dot(ffn_tokens, back_slots)
    grad_hidden_norm, grad_gain_two = norm_back(grad_normed_two, unit_two, inverse_two, gain_two)
    grad_hidden = grad_out + grad_hidden_norm
    attn_grads = to_slots(attn_pairs, gate_attn, grad_hidden)
    if fused:
        owner_grad, mixed_grads, grad_first = run_jobs(
            [dispatch_exchange_job(attn_grads.reshape(n_ep, ROWS, width), w_output[0], dot_t, n_ws)],
            [pair_grad_job(expert_rows, grad_gate, grad_up)],
            7,
            "dispatch_exchange",
        )
        owner_grad = owner_grad.reshape(-1, width)
    else:
        owner_grad = dispatch(attn_grads, group)[0]
        grad_first = jnp.stack([t_dot(expert_rows, grad_gate), t_dot(expert_rows, grad_up)], 1)
        back_mixed = dot_t(owner_grad, w_output[0]).astype(bf16)
        mixed_grads = exchange(back_mixed.reshape(n_ep, n_ws * ROWS, part))[0]
        grad_output = t_dot(owner_mixed, owner_grad)

    if fused:
        mixed_grads = mixed_grads.reshape(n_ep, n_ws, ROWS, part)
        query_grads, grad_kv_rows = attend_back_call(queries, mixed_grads, kv, spans)
        query_grads = query_grads.reshape(n_ep, n_ws * ROWS, part)
    else:
        grad_keys, grad_values, query_pieces = 0.0, 0.0, []
        for (q, probs), grad, span in zip(kept, by_block(mixed_grads), spans):
            grad_probs = jnp.einsum("rhd,shd->hrs", grad, values[:span], preferred_element_type=f32)
            centred = jnp.sum(probs * grad_probs, -1, keepdims=True)
            grad_scores = (probs * (grad_probs - centred)).astype(bf16)
            grad_q = (
                jnp.einsum("hrs,shd->rhd", grad_scores, keys[:span], preferred_element_type=f32)
                * scale
            )
            query_pieces.append(grad_q.astype(bf16))
            pad = ((0, sequence - span), (0, 0), (0, 0))
            piece = jnp.einsum("hrs,rhd->shd", grad_scores, q, preferred_element_type=f32) * scale
            grad_keys = grad_keys + jnp.pad(piece, pad)
            piece = jnp.einsum(
                "hrs,rhd->shd", probs.astype(bf16), grad, preferred_element_type=f32
            )
            grad_values = grad_values + jnp.pad(piece, pad)
        grad_kv_rows = jnp.concatenate(
            [grad_keys.reshape(sequence, -1), grad_values.reshape(sequence, -1)], 1
        ).astype(bf16)
        query_grads = to_experts(query_pieces)
    if fused:
        owner_grad_query, normed_back, grad_kv_rows, grad_output = run_jobs(
            [exchange_combine_job(query_grads, w_query[0], dot_t, n_ws), swap_job(grad_kv_rows)],
            [grad_job(owner_mixed, owner_grad)],
            14,
            "exchange_back",
        )
        owner_grad_query = owner_grad_query.reshape(-1, part)
        normed_back = normed_back.reshape(-1, width)
        grad_kv_rows = grad_kv_rows.reshape(2 * sequence, -1)
    else:
        owner_grad_query = exchange(query_grads)[0].reshape(-1, part)
    grad_kv = t_dot(normed_sequence, grad_kv_rows)
    from_kv = dot_t(grad_kv_rows, kv_own).astype(bf16)
    if fused:
        slot_share = t_dot(attn_tokens, normed_back)
        kv_share = jnp.sum(from_kv.astype(f32) * normed_sequence.astype(f32), 0) / gain_one
        gain_parts = jnp.stack([jnp.sum(slot_share * unit_one, 0) + kv_share, grad_gain_two], 0)
        gain_parts = gain_parts.reshape(2, n_ep, n_ws, -1).transpose(1, 2, 0, 3)
        piece, from_kv, gain_shards, grad_query = run_jobs(
            [
                reduce_weights_job(
                    grad_kv.astype(bf16), from_kv.reshape(2, n_ws, local_tokens, width), n_ep
                ),
                reduce_gains_job(gain_parts.reshape(n_ep, n_ws, 1, -1)),
            ],
            [grad_job(rows_one, owner_grad_query)],
            9,
            "reduce_weights",
        )
    else:
        back_normed = dot_t(owner_grad_query, w_query[0]).astype(bf16)
        normed_back = combine(back_normed, group, n_ep, n_ws)[0]
        grad_query = t_dot(rows_one, owner_grad_query)
    if fused:
        grad_kv_shard = piece.astype(f32)
    elif plain:
        pieces = grad_kv.reshape(width, n_ep, HEAD_SIZE).transpose(1, 0, 2).astype(bf16)
        piece = lax.psum_scatter(pieces, "ep", scatter_dimension=0, tiled=False)
        grad_kv_shard = lax.ppermute(piece, ("ep", "ws"), [(b, a) for a, b in there]).astype(f32)
    else:
        mask = (jnp.arange(n_ws) == place)[None, None, :, None]
        pieces = jnp.where(mask, grad_kv.reshape(width, 2 * group, 1, part), 0.0)
        pieces = pieces.reshape(width, 2 * key_value_width).astype(bf16)
        grad_kv_shard = lax.psum_scatter(
            pieces, ("ep", "ws"), scatter_dimension=1, tiled=True
        ).astype(f32)
    if not fused:
        from_kv = lax.psum_scatter(from_kv, "ws", scatter_dimension=0, tiled=True)
    grad_normed = t_dot(attn_tokens, normed_back) + from_kv.astype(f32)
    grad_input_norm, grad_gain_one = norm_back(grad_normed, unit_one, inverse_one, gain_one)
    grad_input = grad_hidden + grad_input_norm
    if fused:
        gain_shards = gain_shards.reshape(2, -1)
    else:
        gain_shards = lax.psum_scatter(
            jnp.stack([grad_gain_one, grad_gain_two], 0),
            ("ep", "ws"),
            scatter_dimension=1,
            tiled=True,
        )
    return (
        result.astype(bf16),
        grad_input,
        gain_shards[0],
        gain_shards[1],
        grad_kv_shard,
        grad_query[None],
        grad_output[None],
        grad_first[None],
        grad_second[None],
    )


def solution(mesh):
    both = ("ep", "ws")
    rows, vector, columns = P(both, None), P(both), P(None, both)
    return jax.shard_map(
        local,
        mesh=mesh,
        in_specs=(
            rows,
            vector,
            vector,
            columns,
            P("ep", None, "ws"),
            P("ep", "ws", None),
            P("ep", None, None, "ws"),
            P("ep", "ws", None),
            rows,
            rows,
            rows,
            rows,
            rows,
            rows,
            rows,
        ),
        out_specs=(
            rows,
            rows,
            vector,
            vector,
            columns,
            P("ep", None, "ws"),
            P("ep", "ws", None),
            P("ep", None, None, "ws"),
            P("ep", "ws", None),
        ),
        check_vma=False,
    )
```
